32 devices in a mesh: dp: 16 (over z, x, core), seq: 2 (over y).
Axes of the slice: x: 2, y: 2, z: 4, core: 2. Of those that a mesh axis runs over, the one named last changes fastest.
Arguments:
- tokens: bfloat16 [16, 512, 1152], P('dp', 'seq'), may hold values from -6 to 6
- segment_ids: int32 [16, 512], P('dp'), may hold values from 0 to 3, never falling along the last dimension, each value on 1 to 256 neighbouring positions
- cotangent: bfloat16 [16, 512, 1152], P('dp', 'seq'), may hold values from -6 to 6
- query_weight: bfloat16 [1152, 1024], P(('dp', 'seq')), may hold values from -0.1875 to 0.1875
- key_weight: bfloat16 [1152, 256], P(('dp', 'seq')), may hold values from -0.1875 to 0.1875
- value_weight: bfloat16 [1152, 256], P(('dp', 'seq')), may hold values from -0.1875 to 0.1875
- output_weight: bfloat16 [1024, 1152], P(('dp', 'seq')), may hold values from -0.1875 to 0.1875
- gate_weight: bfloat16 [1152, 6912], P(('dp', 'seq')), may hold values from -0.1875 to 0.1875
- up_weight: bfloat16 [1152, 6912], P(('dp', 'seq')), may hold values from -0.1875 to 0.1875
- down_weight: bfloat16 [6912, 1152], P(('dp', 'seq')), may hold values from -0.078125 to 0.078125
- input_gain: bfloat16 [1152], P(('dp', 'seq')), may hold values from 0.25 to 1.75
- query_gain: bfloat16 [256], P(('dp', 'seq')), may hold values from 0.25 to 1.75
- key_gain: bfloat16 [256], P(('dp', 'seq')), may hold values from 0.25 to 1.75
- attnout_gain: bfloat16 [1152], P(('dp', 'seq')), may hold values from 0.25 to 1.75
- ffnin_gain: bfloat16 [1152], P(('dp', 'seq')), may hold values from 0.25 to 1.75
- ffnout_gain: bfloat16 [1152], P(('dp', 'seq')), may hold values from 0.25 to 1.75
Outputs:
- output: bfloat16 [16, 512, 1152], P('dp', 'seq')
- input_grad: float32 [16, 512, 1152], P('dp', 'seq')
- grad_query: float32 [1152, 1024], P(('dp', 'seq'))
- grad_key: float32 [1152, 256], P(('dp', 'seq'))
- grad_value: float32 [1152, 256], P(('dp', 'seq'))
- grad_output: float32 [1024, 1152], P(('dp', 'seq'))
- grad_gate: float32 [1152, 6912], P(('dp', 'seq'))
- grad_up: float32 [1152, 6912], P(('dp', 'seq'))
- grad_down: float32 [6912, 1152], P(('dp', 'seq'))
- grad_input_gain: float32 [1152], P(('dp', 'seq'))
- grad_query_gain: float32 [256], P(('dp', 'seq'))
- grad_key_gain: float32 [256], P(('dp', 'seq'))
- grad_attnout_gain: float32 [1152], P(('dp', 'seq'))
- grad_ffnin_gain: float32 [1152], P(('dp', 'seq'))
- grad_ffnout_gain: float32 [1152], P(('dp', 'seq'))
The draws below stay inside these ranges and needn't reach their ends.
Inputs may be any that keep to these rules, and one draw needn't show every extreme that they name: `segment_ids`: in each row the ids never fall and every id occurs; each document spans 1 to 256 positions, one exactly 256.
All inputs are finite; a program needn't handle non-finite values.
Results may differ from the reference program's by a relative error of at most 0.019.
Values may be sent and summed in bfloat16 or wider, within the bound.
A program may use at most 448 MiB of HBM per device.

```python
import math
import jax
import jax.numpy as jnp
import numpy as np
from jax import lax

D = 1152
HEADS = 4
HEAD_DIM = 256
FF = 6912
DOCS = 4
ROWS = 16
LEN = 512


def with_spikes(entries, own_key, source, target, parts, factor):
    def block_of(axis_at):
        return (jnp.arange(entries.shape[axis_at]) // (entries.shape[axis_at] // parts)).reshape((-1,) + (1,) * (entries.ndim - 1 - axis_at))

    one_side = jax.random.permutation(own_key, parts)[block_of(target)]
    far = (block_of(target) + parts // 2) % parts
    return jnp.where((block_of(source) == one_side) | (block_of(source) == far), factor * entries, entries)


def levels(stream_key, shape, split, smallest, high):
    loudness = 1.0
    for position, blocks in split:
        steps = jax.random.uniform(jax.random.fold_in(jax.random.fold_in(stream_key, 6), position), (blocks,), jnp.float32, smallest / len(split), high / len(split))
        loudness = loudness * jnp.repeat(jnp.exp(steps), shape[position] // blocks).reshape((-1,) + (1,) * (len(shape) - 1 - position))
    return loudness


def profile(number_of, total, most, lean):
    loads = [(1 << 20) // math.isqrt(rank ** lean) + 1 for rank in range(2, number_of + 1)]
    rest, counts = total - most - (number_of - 1), [1] * (number_of - 1)
    while rest > 0:
        candidates = [i for i in range(number_of - 1) if counts[i] < most]
        pool, budget = sum([loads[i] for i in candidates]), rest
        for i in candidates:
            more = min(most - counts[i], max(1, budget * loads[i] // pool), rest)
            counts[i] = counts[i] + more
            rest = rest - more
    return np.array([most] + counts)


def uneven_parts(rng, amount, total, reach, skew):
    if amount == 2:
        one = jax.random.randint(rng, (), max(1, total - reach), min(reach, total - 1) + 1)
        return jnp.stack([one, total - one])
    lengths = jnp.asarray(profile(amount, total, reach, skew), jnp.int32)
    couples = (amount - 1) // 2
    source_of, taker = lengths[1:1 + 2 * couples:2], lengths[2:2 + 2 * couples:2]
    slack = jnp.minimum(source_of - 1, reach - taker)
    moved = jax.random.randint(jax.random.fold_in(rng, 1), (couples,), 0, 1 << 20) % (slack + 1)
    lengths = lengths.at[1:1 + 2 * couples:2].set(source_of - moved).at[2:2 + 2 * couples:2].set(taker + moved)
    return lengths[jax.random.permutation(jax.random.fold_in(rng, 2), amount)]


def gaussian(stream_key, extent, spread, limit, shards=(), held_as=jnp.bfloat16):
    array = spread * jax.random.normal(stream_key, extent, jnp.float32)
    if shards:
        array = array * levels(stream_key, extent, shards, -0.22, 0.18)
    return jnp.clip(array, -limit, limit).astype(held_as)


def heavy_noise(own_key, shape, spread, most, split, heavy, kind=jnp.bfloat16):
    drawn = spread * jax.random.normal(own_key, shape, jnp.float32)
    if split:
        drawn = drawn * levels(own_key, shape, split, -0.22, 0.18)
    return jnp.clip(with_spikes(drawn, jax.random.fold_in(own_key, 3), *heavy), -most, most).astype(kind)


def setup_inputs(seed: int = 0) -> dict:
    seeds = jax.random.split(jax.random.key(seed), 17)
    return {
        "tokens": heavy_noise(seeds[0], (ROWS, LEN, D), 1.0, 6.0, ((0, 16), (1, 2)), (0, 2, 16, 2.0)),
        "segment_ids": jax.vmap(lambda own: jnp.searchsorted(jnp.cumsum(uneven_parts(own, DOCS, LEN, LEN // 2, 1)), jnp.arange(LEN), side="right"))(jax.random.split(seeds[1], ROWS)).reshape((ROWS, LEN)).astype(jnp.int32),
        "cotangent": gaussian(seeds[2], (ROWS, LEN, D), 1.0, 6.0, ((0, 16), (1, 2))),
        "query_weight": gaussian(seeds[3], (D, HEADS * HEAD_DIM), D ** -0.5, 0.1875, ((0, 32),)),
        "key_weight": gaussian(seeds[4], (D, HEAD_DIM), D ** -0.5, 0.1875, ((0, 32),)),
        "value_weight": gaussian(seeds[5], (D, HEAD_DIM), D ** -0.5, 0.1875, ((0, 32),)),
        "output_weight": gaussian(seeds[6], (HEADS * HEAD_DIM, D), (HEADS * HEAD_DIM) ** -0.5, 0.1875, ((0, 32),)),
        "gate_weight": gaussian(seeds[7], (D, FF), D ** -0.5, 0.1875, ((0, 32),)),
        "up_weight": gaussian(seeds[8], (D, FF), D ** -0.5, 0.1875, ((0, 32),)),
        "down_weight": gaussian(seeds[9], (FF, D), FF ** -0.5, 0.078125, ((0, 32),)),
        "input_gain": jnp.clip(1.0 + 0.15 * jax.random.normal(seeds[10], (D,), jnp.float32), 0.25, 1.75).astype(jnp.bfloat16),
        "query_gain": jnp.clip(1.0 + 0.15 * jax.random.normal(seeds[11], (HEAD_DIM,), jnp.float32), 0.25, 1.75).astype(jnp.bfloat16),
        "key_gain": jnp.clip(1.0 + 0.15 * jax.random.normal(seeds[12], (HEAD_DIM,), jnp.float32), 0.25, 1.75).astype(jnp.bfloat16),
        "attnout_gain": jnp.clip(1.0 + 0.15 * jax.random.normal(seeds[13], (D,), jnp.float32), 0.25, 1.75).astype(jnp.bfloat16),
        "ffnin_gain": jnp.clip(1.0 + 0.15 * jax.random.normal(seeds[14], (D,), jnp.float32), 0.25, 1.75).astype(jnp.bfloat16),
        "ffnout_gain": jnp.clip(1.0 + 0.15 * jax.random.normal(seeds[15], (D,), jnp.float32), 0.25, 1.75).astype(jnp.bfloat16),
    }


epsilon = 1e-06
rope_base = 1000000.0
masked_score = -1e+30

@jax.custom_vjp
def low(v):
    return lax.optimization_barrier(v.astype(jnp.bfloat16)).astype(jnp.float32)

@jax.custom_vjp
def low_back(v):
    return v

def low_keep(v):
    return (low(v), None)

def low_pass(kept, grad):
    return (grad,)

def back_keep(v):
    return (v, None)

def back_low(kept, grad):
    return (low(grad),)
low.defvjp(low_keep, low_pass)
low_back.defvjp(back_keep, back_low)

def matmul_exact(left, right):
    return jnp.matmul(left, right, precision=lax.Precision.HIGHEST, preferred_element_type=jnp.float32)

def rms_gain(values, gain):
    return values * lax.rsqrt(lax.optimization_barrier(jnp.mean(values * values, axis=-1, keepdims=True)) + epsilon) * gain

def doc_positions(segments):
    length = segments.shape[-1]
    places = jnp.arange(length, dtype=jnp.int32)
    earlier = jnp.concatenate([segments[:, :1] - 1, segments[:, :-1]], axis=1)
    starts = jnp.where(segments != earlier, places[None, :], jnp.zeros_like(segments))
    return (places[None, :] - lax.cummax(starts, axis=1)).astype(jnp.float32)

def rope_tables(positions, head_width):
    half_width = head_width // 2
    frequency = rope_base ** (-(2.0 / head_width) * jnp.arange(half_width, dtype=jnp.float32))
    angles = positions[..., None] * frequency
    return (jnp.cos(angles), jnp.sin(angles))

def rotate(values, cos_table, sin_table):
    half_width = values.shape[-1] // 2
    first_half = values[..., :half_width]
    second_half = values[..., half_width:]
    return jnp.concatenate([first_half * cos_table - second_half * sin_table, second_half * cos_table + first_half * sin_table], axis=-1)

def attend_row(pieces):
    queries, key_rows, values, allowed = pieces
    scores = low_back(jnp.einsum('qhd,kd->hqk', queries, key_rows, precision=lax.Precision.HIGHEST))
    scores = jnp.where(allowed[None], scores, masked_score)
    weights = low(jax.nn.softmax(scores, axis=-1))
    return jnp.einsum('hqk,kd->qhd', weights, values, precision=lax.Precision.HIGHEST)

def layer_forward(params, hidden, cos_table, sin_table, allowed):
    query_weight, key_weight, value_weight, output_weight, gate_weight, up_weight, down_weight, input_gain, query_gain, key_gain, attnout_gain, ffnin_gain, ffnout_gain = params
    row_count, seq_length, width = hidden.shape
    normed = low(rms_gain(hidden, input_gain))
    query_raw = low_back(matmul_exact(normed, query_weight)).reshape(row_count, seq_length, HEADS, HEAD_DIM)
    key_raw = low_back(matmul_exact(normed, key_weight))
    value_raw = low_back(matmul_exact(normed, value_weight))
    queries = low(rotate(rms_gain(query_raw, query_gain), cos_table[:, :, None, :], sin_table[:, :, None, :]) * HEAD_DIM ** (-0.5))
    key_rows = low(rotate(rms_gain(key_raw, key_gain), cos_table, sin_table))
    values = low(value_raw)
    attn_mix = lax.map(jax.checkpoint(attend_row), (queries, key_rows, values, allowed))
    attn_mix = low(low_back(attn_mix)).reshape(row_count, seq_length, HEADS * HEAD_DIM)
    attn_out = rms_gain(low_back(matmul_exact(attn_mix, output_weight)), attnout_gain)
    middle = hidden + attn_out
    ffn_in = low(rms_gain(middle, ffnin_gain))
    gate_proj = low_back(matmul_exact(ffn_in, gate_weight))
    up_proj = low_back(matmul_exact(ffn_in, up_weight))
    activated = low(jax.nn.gelu(gate_proj, approximate=True) * up_proj)
    ffn_out = rms_gain(low_back(matmul_exact(activated, down_weight)), ffnout_gain)
    return middle + ffn_out

def reference(tokens, segment_ids, cotangent, query_weight, key_weight, value_weight, output_weight, gate_weight, up_weight, down_weight, input_gain, query_gain, key_gain, attnout_gain, ffnin_gain, ffnout_gain):
    params = tuple((array_in.astype(jnp.float32) for array_in in (query_weight, key_weight, value_weight, output_weight, gate_weight, up_weight, down_weight, input_gain, query_gain, key_gain, attnout_gain, ffnin_gain, ffnout_gain)))
    group_rows = math.gcd(ROWS, max(1, 4096 // LEN))
    group_count = ROWS // group_rows
    cos_table, sin_table = rope_tables(doc_positions(segment_ids), HEAD_DIM)
    places = jnp.arange(LEN, dtype=jnp.int32)
    causal = places[:, None] >= places[None, :]

    def regroup(array_in):
        return array_in.reshape((group_count, group_rows) + array_in.shape[1:])

    def one_group(running, pieces):
        hidden, segments, incoming, cos_rows, sin_rows = pieces
        allowed = (segments[:, :, None] == segments[:, None, :]) & causal[None]

        def run_layer(weights_now, hidden_now):
            return layer_forward(weights_now, hidden_now, cos_rows, sin_rows, allowed)
        output, pull_back = jax.vjp(run_layer, params, hidden)
        weight_grads, hidden_grad = pull_back(incoming)
        running = tuple((before + gradient for before, gradient in zip(running, weight_grads)))
        return (running, (output.astype(jnp.bfloat16), hidden_grad))
    initial = tuple((jnp.zeros_like(array_in) for array_in in params))
    inputs = (regroup(tokens.astype(jnp.float32)), regroup(segment_ids), regroup(cotangent.astype(jnp.float32)), regroup(cos_table), regroup(sin_table))
    totals, (outputs, input_grads) = lax.scan(one_group, initial, inputs)
    return (outputs.reshape(ROWS, LEN, D), input_grads.reshape(ROWS, LEN, D), totals[0], totals[1], totals[2], totals[3], totals[4], totals[5], totals[6], totals[7], totals[8], totals[9], totals[10], totals[11], totals[12])
```

```python
import jax
import jax.numpy as jnp
from jax import lax
from jax.sharding import Mesh
from jax.sharding import PartitionSpec as P

epsilon = 1e-06
rope_base = 1000000.0
masked_score = -1e30


def inverse_rms(values):
    return lax.rsqrt(jnp.mean(values * values, axis=-1, keepdims=True) + epsilon)


def rms_back(grad_normed, normed, inverse):
    return inverse * (grad_normed - normed * jnp.mean(grad_normed * normed, axis=-1, keepdims=True))


def doc_positions(segments):
    length = segments.shape[0]
    smaller = segments[None, :] < segments[:, None]
    starts = jnp.sum(smaller.astype(jnp.int32), axis=1)
    return (jnp.arange(length, dtype=jnp.int32) - starts).astype(jnp.float32)


def rope_tables(positions, head_width):
    half_width = head_width // 2
    frequency = rope_base ** (-(2.0 / head_width) * jnp.arange(half_width, dtype=jnp.float32))
    angles = positions[..., None] * frequency
    return (jnp.cos(angles), jnp.sin(angles))


def rotate(values, cos_table, sin_table):
    half_width = values.shape[-1] // 2
    first_half = values[..., :half_width]
    second_half = values[..., half_width:]
    return jnp.concatenate(
        [
            first_half * cos_table - second_half * sin_table,
            second_half * cos_table + first_half * sin_table,
        ],
        axis=-1,
    )


def matmul(left, right):
    return jnp.dot(left, right, preferred_element_type=jnp.float32)


def contract_rows(left, right):
    return lax.dot_general(
        left, right, (((0,), (0,)), ((), ())), preferred_element_type=jnp.float32
    )


def contract_cols(left, right):
    return lax.dot_general(
        left, right, (((1,), (1,)), ((), ())), preferred_element_type=jnp.float32
    )


def gelu_pair(gate_proj, up_proj):
    return jax.nn.gelu(gate_proj, approximate=True) * up_proj


ALL = ("z", "x", "core", "seq")
PLANE = ("x", "core", "seq")


def exchange(blocks, axes):
    return lax.all_to_all(blocks, axes, split_axis=0, concat_axis=0, tiled=True)


def plane_gather(local):
    return lax.all_gather(local, PLANE, axis=0, tiled=True)


def plane_scatter_sum(partial):
    members = lax.axis_size(PLANE)
    terms = exchange(partial.reshape((members, -1) + partial.shape[1:]), PLANE)
    return jnp.sum(terms.astype(jnp.float32), axis=0)


def body(
    tokens,
    segment_ids,
    cotangent,
    query_weight,
    key_weight,
    value_weight,
    output_weight,
    gate_weight,
    up_weight,
    down_weight,
    input_gain,
    query_gain,
    key_gain,
    attnout_gain,
    ffnin_gain,
    ffnout_gain,
):
    bf16, f32 = jnp.bfloat16, jnp.float32
    devices = lax.axis_size(ALL)
    members = lax.axis_size(PLANE)
    planes = lax.axis_size("z")
    seq_count = lax.axis_size("seq")
    width_rows = query_weight.shape[0]
    hidden_rows = down_weight.shape[0]
    head_width = key_weight.shape[1]
    query_width = query_weight.shape[1]
    head_count = query_width // head_width
    qkv_width = query_width + 2 * head_width
    mix_rows = output_weight.shape[0]
    padded = (width_rows + 1 + 7) // 8 * 8

    gains = (input_gain, query_gain, key_gain, attnout_gain, ffnin_gain, ffnout_gain)
    gain_row = jnp.concatenate(gains)
    gain_widths = [g.shape[0] for g in gains]
    gain_row = jnp.pad(gain_row, (0, qkv_width - gain_row.shape[0]))
    qkv_local = jnp.concatenate([query_weight, key_weight, value_weight], axis=1)
    packed = jnp.concatenate([qkv_local, gain_row[None]], axis=0)
    packed = jnp.pad(packed, ((0, padded - width_rows - 1), (0, 0)))
    packed_all = lax.all_gather(packed, ALL, axis=0, tiled=False)
    qkv_full = packed_all[:, :width_rows].reshape(devices * width_rows, qkv_width)
    scales, at = [], 0
    for width in gain_widths:
        scales.append(packed_all[:, width_rows, at : at + width].reshape(-1).astype(f32))
        at += width
    input_scale, query_scale, key_scale, attnout_scale, ffnin_scale, ffnout_scale = scales
    output_full = lax.all_gather(output_weight, ALL, axis=0, tiled=True)

    def column_blocks(weight):
        pieces = weight.reshape(width_rows, planes, members, hidden_rows)
        return pieces.transpose(2, 0, 1, 3).reshape(members, width_rows, planes * hidden_rows)

    gate_up = jnp.concatenate([column_blocks(gate_weight), column_blocks(up_weight)], axis=1)
    gate_up = jnp.broadcast_to(gate_up[None], (planes,) + gate_up.shape)
    gate_up = exchange(gate_up.reshape((devices,) + gate_up.shape[2:]), ALL)
    gate_full = gate_up[:, :width_rows].reshape(devices * width_rows, planes * hidden_rows)
    up_full = gate_up[:, width_rows:].reshape(devices * width_rows, planes * hidden_rows)
    down_full = exchange(jnp.broadcast_to(down_weight[None], (planes,) + down_weight.shape), "z")
    down_full = down_full.reshape(planes * hidden_rows, down_weight.shape[1])

    hidden = tokens[0].astype(f32)
    incoming = cotangent[0].astype(f32)
    local_rows = hidden.shape[0]
    full_length = local_rows * seq_count
    offset = lax.axis_index("seq") * local_rows
    segment_row = segment_ids[0]

    def mine(rows):
        return lax.dynamic_slice_in_dim(rows, offset, local_rows)

    my_segments = mine(segment_row)
    cos_full, sin_full = rope_tables(doc_positions(segment_row), head_width)
    cos_table, sin_table = mine(cos_full), mine(sin_full)
    scale = head_width ** (-0.5)

    row_hidden = lax.all_gather(tokens[0], "seq", axis=0, tiled=True).astype(f32)
    row_normed = (row_hidden * inverse_rms(row_hidden) * input_scale).astype(bf16)
    key_value_raw = matmul(row_normed, qkv_full[:, query_width:])
    row_key_raw = key_value_raw[:, :head_width]
    value_rows = key_value_raw[:, head_width:].astype(bf16)
    key_rows = rotate(
        row_key_raw * inverse_rms(row_key_raw) * key_scale, cos_full, sin_full
    ).astype(bf16)

    inv_input = inverse_rms(hidden)
    norm_input = hidden * inv_input
    normed = (norm_input * input_scale).astype(bf16)
    query_raw = matmul(normed, qkv_full[:, :query_width]).reshape(
        local_rows, head_count, head_width
    )
    inv_query = inverse_rms(query_raw)
    norm_query = query_raw * inv_query
    queries = (
        rotate(norm_query * query_scale, cos_table[:, None, :], sin_table[:, None, :]) * scale
    ).astype(bf16)
    key_raw = mine(row_key_raw)
    inv_key = inverse_rms(key_raw)
    norm_key = key_raw * inv_key

    query_places = offset + jnp.arange(local_rows, dtype=jnp.int32)
    key_places = jnp.arange(full_length, dtype=jnp.int32)
    allowed = (my_segments[:, None] == segment_row[None, :]) & (
        query_places[:, None] >= key_places[None, :]
    )
    raw_scores = jnp.einsum("qhd,kd->hqk", queries, key_rows, preferred_element_type=f32)
    scores = jnp.where(allowed[None], raw_scores, masked_score)
    peak = jnp.max(scores, axis=-1, keepdims=True)
    log_total = peak + jnp.log(jnp.sum(jnp.exp(scores - peak), axis=-1, keepdims=True))
    probs = jnp.exp(scores - log_total)
    probs_low = probs.astype(bf16)
    attn_mix = jnp.einsum("hqk,kd->qhd", probs_low, value_rows, preferred_element_type=f32)
    attn_flat = attn_mix.astype(bf16).reshape(local_rows, query_width)
    attn_raw = matmul(attn_flat, output_full)
    inv_attn = inverse_rms(attn_raw)
    norm_attn = attn_raw * inv_attn
    middle = hidden + norm_attn * attnout_scale
    inv_middle = inverse_rms(middle)
    norm_middle = middle * inv_middle
    ffn_in = (norm_middle * ffnin_scale).astype(bf16)

    plane_in = plane_gather(ffn_in)
    gate_proj = matmul(plane_in, gate_full)
    up_proj = matmul(plane_in, up_full)
    activated, gelu_back = jax.vjp(gelu_pair, gate_proj, up_proj)
    activated_low = activated.astype(bf16)
    ffn_raw = plane_scatter_sum(matmul(activated_low, down_full).astype(bf16))
    inv_ffn = inverse_rms(ffn_raw)
    norm_ffn = ffn_raw * inv_ffn
    result = middle + norm_ffn * ffnout_scale
    ffnout_gain_grad = jnp.sum(incoming * norm_ffn, axis=0)
    ffn_raw_grad = rms_back(incoming * ffnout_scale, norm_ffn, inv_ffn).astype(bf16)

    plane_grad = plane_gather(ffn_raw_grad)
    act_grad = contract_cols(plane_grad, down_full)
    gate_grad, up_grad = gelu_back(act_grad)
    gate_low = gate_grad.astype(bf16)
    up_low = up_grad.astype(bf16)
    ffn_in_grad = plane_scatter_sum(
        (contract_cols(gate_low, gate_full) + contract_cols(up_low, up_full)).astype(bf16)
    )
    down_terms = exchange(
        contract_rows(activated_low, plane_grad)
        .astype(bf16)
        .reshape(planes, hidden_rows, down_weight.shape[1]),
        "z",
    )
    down_wgrad = jnp.sum(down_terms.astype(f32), axis=0)

    def row_blocks(grad):
        return grad.astype(bf16).reshape(devices, width_rows, planes * hidden_rows)

    gate_up_terms = exchange(
        jnp.concatenate(
            [
                row_blocks(contract_rows(plane_in, gate_low)),
                row_blocks(contract_rows(plane_in, up_low)),
            ],
            axis=1,
        ),
        ALL,
    )
    gate_up_sum = jnp.sum(
        gate_up_terms.astype(f32).reshape(
            planes, members, 2, width_rows, planes, hidden_rows
        ),
        axis=0,
    )
    gate_up_sum = gate_up_sum.transpose(1, 2, 3, 0, 4).reshape(
        2, width_rows, planes * members * hidden_rows
    )
    gate_wgrad, up_wgrad = gate_up_sum[0], gate_up_sum[1]

    ffnin_gain_grad = jnp.sum(ffn_in_grad * norm_middle, axis=0)
    middle_grad = incoming + rms_back(ffn_in_grad * ffnin_scale, norm_middle, inv_middle)
    attnout_gain_grad = jnp.sum(middle_grad * norm_attn, axis=0)
    attn_raw_grad = rms_back(middle_grad * attnout_scale, norm_attn, inv_attn).astype(bf16)
    output_wgrad = contract_rows(attn_flat, attn_raw_grad)
    mix_grad = (
        contract_cols(attn_raw_grad, output_full)
        .astype(bf16)
        .reshape(local_rows, head_count, head_width)
    )
    prob_grad = jnp.einsum("qhd,kd->hqk", mix_grad, value_rows, preferred_element_type=f32)
    row_delta = jnp.sum(prob_grad * probs, axis=-1, keepdims=True)
    score_grad = (probs * (prob_grad - row_delta)).astype(bf16)
    value_grad_rows = jnp.einsum("hqk,qhd->kd", probs_low, mix_grad, preferred_element_type=f32)
    key_grad_rows = jnp.einsum("hqk,qhd->kd", score_grad, queries, preferred_element_type=f32)
    query_grad = jnp.einsum("hqk,kd->qhd", score_grad, key_rows, preferred_element_type=f32)
    key_value_terms = exchange(
        jnp.concatenate([key_grad_rows, value_grad_rows], axis=1)
        .astype(bf16)
        .reshape(seq_count, local_rows, 2 * head_width),
        "seq",
    )
    key_value_grad = jnp.sum(key_value_terms.astype(f32), axis=0)
    key_grad, value_grad = key_value_grad[:, :head_width], key_value_grad[:, head_width:]
    query_norm_grad = rotate(query_grad * scale, cos_table[:, None, :], -sin_table[:, None, :])
    query_gain_grad = jnp.sum(query_norm_grad * norm_query, axis=(0, 1))
    query_raw_low = (
        rms_back(query_norm_grad * query_scale, norm_query, inv_query)
        .astype(bf16)
        .reshape(local_rows, query_width)
    )
    key_norm_grad = rotate(key_grad, cos_table, -sin_table)
    key_gain_grad = jnp.sum(key_norm_grad * norm_key, axis=0)
    key_raw_low = rms_back(key_norm_grad * key_scale, norm_key, inv_key).astype(bf16)
    qkv_raw_low = jnp.concatenate([query_raw_low, key_raw_low, value_grad.astype(bf16)], axis=1)
    qkv_wgrad = contract_rows(normed, qkv_raw_low)
    normed_grad = contract_cols(qkv_raw_low, qkv_full)
    input_gain_grad = jnp.sum(normed_grad * norm_input, axis=0)
    input_grad = middle_grad + rms_back(normed_grad * input_scale, norm_input, inv_input)

    def to_owners(grad):
        rows, columns = grad.shape[0] // devices, grad.shape[1]
        blocks = grad.astype(bf16).reshape(planes, members, rows, columns)
        terms = exchange(blocks.transpose(1, 0, 2, 3), PLANE)
        summed = jnp.sum(terms.astype(f32), axis=0).astype(bf16)
        return jnp.sum(exchange(summed, "z").astype(f32), axis=0)

    output_share = to_owners(output_wgrad)
    gain_grads = (
        input_gain_grad,
        query_gain_grad,
        key_gain_grad,
        attnout_gain_grad,
        ffnin_gain_grad,
        ffnout_gain_grad,
    )
    gain_rows = jnp.concatenate([g.reshape(devices, -1) for g in gain_grads], axis=1)
    gain_rows = jnp.pad(gain_rows, ((0, 0), (0, qkv_width - gain_rows.shape[1])))
    qkv_blocks = jnp.concatenate(
        [qkv_wgrad.reshape(devices, width_rows, qkv_width), gain_rows[:, None]], axis=1
    )
    qkv_blocks = jnp.pad(qkv_blocks, ((0, 0), (0, padded - width_rows - 1), (0, 0)))
    qkv_share = to_owners(qkv_blocks.reshape(devices * padded, qkv_width))
    gain_shares, at = [], 0
    for width in gain_widths:
        gain_shares.append(qkv_share[width_rows, at : at + width])
        at += width
    return (
        result.astype(bf16)[None],
        input_grad[None],
        qkv_share[:width_rows, :query_width],
        qkv_share[:width_rows, query_width : query_width + head_width],
        qkv_share[:width_rows, query_width + head_width :],
        output_share,
        gate_wgrad,
        up_wgrad,
        down_wgrad,
        *gain_shares,
    )


def solution(mesh):
    dp, seq = mesh.shape["dp"], mesh.shape["seq"]
    split = Mesh(mesh.devices.reshape(dp // 4, 2, 2, seq), ALL)
    rows = P(("z", "x", "core"), "seq", None)
    matrix, vector = P(ALL, None), P(ALL)
    return jax.shard_map(
        body,
        mesh=split,
        in_specs=(rows, P(("z", "x", "core"), None), rows) + (matrix,) * 7 + (vector,) * 6,
        out_specs=(rows, rows) + (matrix,) * 7 + (vector,) * 6,
        check_vma=False,
    )
```

```python
import functools

import jax
import jax.numpy as jnp
from jax import lax
from jax.experimental import pallas as pl
from jax.experimental.pallas import tpu as pltpu
from jax.sharding import Mesh
from jax.sharding import PartitionSpec as P

epsilon = 1e-06
rope_base = 1000000.0
masked_score = -1e30


def inverse_rms(values):
    return lax.rsqrt(jnp.mean(values * values, axis=-1, keepdims=True) + epsilon)


def rms_back(grad_normed, normed, inverse):
    return inverse * (grad_normed - normed * jnp.mean(grad_normed * normed, axis=-1, keepdims=True))


def doc_positions(segments):
    length = segments.shape[0]
    smaller = segments[None, :] < segments[:, None]
    starts = jnp.sum(smaller.astype(jnp.int32), axis=1)
    return (jnp.arange(length, dtype=jnp.int32) - starts).astype(jnp.float32)


def rope_tables(positions, head_width):
    half_width = head_width // 2
    frequency = rope_base ** (-(2.0 / head_width) * jnp.arange(half_width, dtype=jnp.float32))
    angles = positions[..., None] * frequency
    return (jnp.cos(angles), jnp.sin(angles))


def rotate(values, cos_table, sin_table):
    half_width = values.shape[-1] // 2
    first_half = values[..., :half_width]
    second_half = values[..., half_width:]
    return jnp.concatenate(
        [
            first_half * cos_table - second_half * sin_table,
            second_half * cos_table + first_half * sin_table,
        ],
        axis=-1,
    )


def matmul(left, right):
    return jnp.dot(left, right, preferred_element_type=jnp.float32)


def contract_rows(left, right):
    return lax.dot_general(
        left, right, (((0,), (0,)), ((), ())), preferred_element_type=jnp.float32
    )


def contract_cols(left, right):
    return lax.dot_general(
        left, right, (((1,), (1,)), ((), ())), preferred_element_type=jnp.float32
    )


def gelu_pair(gate_proj, up_proj):
    return jax.nn.gelu(gate_proj, approximate=True) * up_proj


ALL = ("z", "x", "core", "seq")
PLANE = ("x", "core", "seq")

MESH_ID = pl.DeviceIdType.MESH
VMEM_BYTES = 48 * 2**20


def exchange(blocks, axes):
    return lax.all_to_all(blocks, axes, split_axis=0, concat_axis=0, tiled=True)


def busy(microseconds):
    return pl.CostEstimate(flops=0, bytes_accessed=microseconds * 3_000_000, transcendentals=0)


def plane_places():
    z, x, core, seq = (lax.axis_index(name) for name in ALL)
    sibling = (z, x, 1 - core, seq)
    along_x = (z, 1 - x, core, seq)
    along_y = (z, x, core, 1 - seq)

    def member(other_x, other_core, other_y):
        at_x = 1 - x if other_x else x
        at_core = 1 - core if other_core else core
        at_y = 1 - seq if other_y else seq
        return (at_x * 2 + at_core) * 2 + at_y

    return sibling, along_x, along_y, member


def greet(places):
    barrier = pltpu.get_barrier_semaphore()
    for place in places:
        pl.semaphore_signal(barrier, inc=1, device_id=place, device_id_type=MESH_ID)
    pl.semaphore_wait(barrier, len(places))


def sender(send_sems, recv_sems):
    def send(kind, source, target, place):
        copy = pltpu.make_async_remote_copy(
            src_ref=source,
            dst_ref=target,
            send_sem=send_sems.at[kind],
            recv_sem=recv_sems.at[kind],
            device_id=place,
            device_id_type=MESH_ID,
        )
        copy.start()
        return copy

    return send


def plane_spread(own_ref, out_ref, send_sems, recv_sems, local_sem):
    sibling, along_x, along_y, member = plane_places()
    half = own_ref.shape[0] // 2
    top, bottom = pl.ds(0, half), pl.ds(half, half)
    me = member(0, 0, 0)
    keep = pltpu.make_async_copy(own_ref, out_ref.at[me], local_sem)
    keep.start()
    send = sender(send_sems, recv_sems)

    def forward(kind, block, rows, place):
        return send(kind, out_ref.at[block, rows], out_ref.at[block, rows], place)

    own_x_top = send(1, own_ref.at[top], out_ref.at[me, top], along_x)
    own_y_bottom = send(3, own_ref.at[bottom], out_ref.at[me, bottom], along_y)
    own_sibling = send(0, own_ref, out_ref.at[me], sibling)
    own_x_bottom = send(2, own_ref.at[bottom], out_ref.at[me, bottom], along_x)
    own_y_top = send(4, own_ref.at[top], out_ref.at[me, top], along_y)
    x_block, y_block, diagonal = member(1, 0, 0), member(0, 0, 1), member(1, 0, 1)
    own_x_top.wait_recv()
    diagonal_top = forward(5, x_block, top, along_y)
    x_top = forward(7, x_block, top, sibling)
    own_y_bottom.wait_recv()
    diagonal_bottom = forward(6, y_block, bottom, along_x)
    y_bottom = forward(9, y_block, bottom, sibling)
    own_x_bottom.wait_recv()
    x_bottom = forward(8, x_block, bottom, sibling)
    own_y_top.wait_recv()
    y_top = forward(10, y_block, top, sibling)
    diagonal_top.wait_recv()
    far_top = forward(11, diagonal, top, sibling)
    diagonal_bottom.wait_recv()
    far_bottom = forward(12, diagonal, bottom, sibling)
    for copy in (own_sibling, x_top, y_bottom, x_bottom, y_top, far_top, far_bottom):
        copy.wait_recv()
    for copy in (
        own_x_top,
        own_y_bottom,
        own_sibling,
        own_x_bottom,
        own_y_top,
        diagonal_top,
        diagonal_bottom,
        x_top,
        y_bottom,
        x_bottom,
        y_top,
        far_top,
        far_bottom,
    ):
        copy.wait_send()
    keep.wait()


def gather_kernel(own_ref, out_ref, *sems):
    greet(plane_places()[:3])
    plane_spread(own_ref, out_ref, *sems)


def wide_gather_kernel(planes, own_ref, out_ref, held, z_send, z_recv, own_sem, *sems):
    z, x, core, seq = (lax.axis_index(name) for name in ALL)
    others = [(lax.rem(z + k, planes), x, core, seq) for k in range(1, planes)]
    greet((*plane_places()[:3], *others))
    slot = held.at[z]
    keep = pltpu.make_async_copy(own_ref, slot, own_sem)
    keep.start()
    send = sender(z_send, z_recv)
    copies = [send(k, own_ref, slot, place) for k, place in enumerate(others)]
    for copy in copies:
        copy.wait_recv()
    keep.wait()
    plane_spread(held, out_ref, *sems)
    for copy in copies:
        copy.wait_send()


GATHER_SEMS = [
    pltpu.SemaphoreType.DMA((13,)),
    pltpu.SemaphoreType.DMA((13,)),
    pltpu.SemaphoreType.DMA,
]


def wide_gather(local, planes, collective_id):
    rows, columns = local.shape
    members = 8
    return pl.pallas_call(
        functools.partial(wide_gather_kernel, planes),
        out_shape=jax.ShapeDtypeStruct((members, planes, rows, columns), local.dtype),
        in_specs=[pl.BlockSpec(memory_space=pltpu.VMEM)],
        out_specs=pl.BlockSpec(memory_space=pl.ANY),
        scratch_shapes=[
            pltpu.VMEM((planes, rows, columns), local.dtype),
            pltpu.SemaphoreType.DMA((planes - 1,)),
            pltpu.SemaphoreType.DMA((planes - 1,)),
            pltpu.SemaphoreType.DMA,
            *GATHER_SEMS,
        ],
        cost_estimate=busy(35),
        compiler_params=pltpu.CompilerParams(
            collective_id=collective_id, has_side_effects=True, vmem_limit_bytes=VMEM_BYTES
        ),
    )(local)


def plane_gather(local, collective_id):
    rows, columns = local.shape
    members = 8
    out = pl.pallas_call(
        gather_kernel,
        out_shape=jax.ShapeDtypeStruct((members, rows // 16, 16, columns), local.dtype),
        in_specs=[pl.BlockSpec(memory_space=pl.ANY)],
        out_specs=pl.BlockSpec(memory_space=pl.ANY),
        scratch_shapes=GATHER_SEMS,
        cost_estimate=busy(25),
        compiler_params=pltpu.CompilerParams(
            collective_id=collective_id, has_side_effects=True, vmem_limit_bytes=VMEM_BYTES
        ),
    )(local.reshape(rows // 16, 16, columns))
    return out.reshape(members * rows, columns)


def add_rows(target, sources, start, count):
    def one(i, carry):
        total = sources[0][i].astype(jnp.float32)
        for source in sources[1:]:
            total = total + source[i].astype(jnp.float32)
        target[i] = total.astype(target.dtype)
        return carry

    lax.fori_loop(start, start + count, one, 0)


def plane_sum(part_ref, own_sum, near, sums, from_x, from_y, far_x, far_y, send_sems, recv_sems):
    sibling, along_x, along_y, member = plane_places()
    rows = own_sum.shape[0]
    half = rows // 2
    top, bottom = pl.ds(0, half), pl.ds(half, half)
    send = sender(send_sems, recv_sems)
    chips = ((1, 1), (1, 0), (0, 1), (0, 0))
    mine = [part_ref.at[member(at_x, 0, at_y)] for at_x, at_y in chips]
    to_sibling = [
        send(k, part_ref.at[member(at_x, 1, at_y)], near.at[k], sibling)
        for k, (at_x, at_y) in enumerate(chips)
    ]
    to_sibling[0].wait_recv()
    add_rows(sums.at[0], (mine[0], near.at[0]), 0, rows)
    diagonal_x = send(4, sums.at[0, bottom], far_x.at[bottom], along_x)
    diagonal_y = send(5, sums.at[0, top], far_y.at[top], along_y)
    to_sibling[1].wait_recv()
    add_rows(sums.at[1], (mine[1], near.at[1]), half, half)
    direct_x = send(6, sums.at[1, bottom], from_x.at[bottom], along_x)
    to_sibling[2].wait_recv()
    add_rows(sums.at[2], (mine[2], near.at[2]), 0, half)
    direct_y = send(7, sums.at[2, top], from_y.at[top], along_y)
    to_sibling[3].wait_recv()
    diagonal_y.wait_recv()
    add_rows(sums.at[1], (mine[1], near.at[1], far_y), 0, half)
    joint_x = send(8, sums.at[1, top], from_x.at[top], along_x)
    diagonal_x.wait_recv()
    add_rows(sums.at[2], (mine[2], near.at[2], far_x), half, half)
    joint_y = send(9, sums.at[2, bottom], from_y.at[bottom], along_y)
    direct_x.wait_recv()
    direct_y.wait_recv()
    joint_x.wait_recv()
    joint_y.wait_recv()
    add_rows(own_sum, (mine[3], near.at[3], from_x, from_y), 0, rows)
    for copy in (*to_sibling, diagonal_x, diagonal_y, direct_x, direct_y, joint_x, joint_y):
        copy.wait_send()


def plane_sum_kernel(part_ref, out_ref, *scratch):
    sibling, along_x, along_y, _ = plane_places()
    greet((sibling, along_x, along_y))
    plane_sum(part_ref, out_ref, *scratch)


def plane_sum_scratch(shape, dtype):
    block = pltpu.VMEM(shape, dtype)
    return [
        pltpu.VMEM((4, *shape), dtype),
        pltpu.VMEM((3, *shape), dtype),
        block,
        block,
        block,
        block,
        pltpu.SemaphoreType.DMA((10,)),
        pltpu.SemaphoreType.DMA((10,)),
    ]


def plane_scatter_sum(partial, collective_id):
    members = 8
    rows, columns = partial.shape[0] // members, partial.shape[1]
    shape = (rows // 16, 16, columns)
    out = pl.pallas_call(
        plane_sum_kernel,
        out_shape=jax.ShapeDtypeStruct(shape, jnp.float32),
        in_specs=[pl.BlockSpec(memory_space=pltpu.VMEM)],
        out_specs=pl.BlockSpec(memory_space=pltpu.VMEM),
        scratch_shapes=plane_sum_scratch(shape, partial.dtype),
        cost_estimate=busy(25),
        compiler_params=pltpu.CompilerParams(
            collective_id=collective_id, has_side_effects=True, vmem_limit_bytes=VMEM_BYTES
        ),
    )(partial.reshape(members, *shape))
    return out.reshape(rows, columns)


def owner_sum_kernel(planes, part_ref, out_ref, own_sum, leaving, arriving, z_send, z_recv, *scratch):
    sibling, along_x, along_y, _ = plane_places()
    z, x, core, seq = (lax.axis_index(name) for name in ALL)
    others = [(lax.rem(z + k, planes), x, core, seq) for k in range(1, planes)]
    greet((sibling, along_x, along_y, *others))
    plane_sum(part_ref, own_sum, *scratch)
    send = sender(z_send, z_recv)

    def narrow(i, carry):
        leaving[i] = own_sum[i].astype(leaving.dtype)
        return carry

    lax.fori_loop(0, planes, narrow, 0)
    copies = [
        send(k, leaving.at[place[0]], arriving.at[k], place) for k, place in enumerate(others)
    ]
    for copy in copies:
        copy.wait_recv()

    value = own_sum[z]
    for k in range(planes - 1):
        value = value + arriving[k].astype(jnp.float32)
    out_ref[...] = value
    for copy in copies:
        copy.wait_send()


def owner_sum(blocks, collective_id):
    members, planes, rows, columns = blocks.shape
    return pl.pallas_call(
        functools.partial(owner_sum_kernel, planes),
        out_shape=jax.ShapeDtypeStruct((rows, columns), jnp.float32),
        in_specs=[pl.BlockSpec(memory_space=pltpu.VMEM)],
        out_specs=pl.BlockSpec(memory_space=pltpu.VMEM),
        scratch_shapes=[
            pltpu.VMEM((planes, rows, columns), jnp.float32),
            pltpu.VMEM((planes, rows, columns), blocks.dtype),
            pltpu.VMEM((planes - 1, rows, columns), blocks.dtype),
            pltpu.SemaphoreType.DMA((planes - 1,)),
            pltpu.SemaphoreType.DMA((planes - 1,)),
            *plane_sum_scratch((planes, rows, columns), blocks.dtype),
        ],
        cost_estimate=busy(35),
        compiler_params=pltpu.CompilerParams(
            collective_id=collective_id, has_side_effects=True, vmem_limit_bytes=VMEM_BYTES
        ),
    )(blocks)


def body(
    tokens,
    segment_ids,
    cotangent,
    query_weight,
    key_weight,
    value_weight,
    output_weight,
    gate_weight,
    up_weight,
    down_weight,
    input_gain,
    query_gain,
    key_gain,
    attnout_gain,
    ffnin_gain,
    ffnout_gain,
):
    bf16, f32 = jnp.bfloat16, jnp.float32
    devices = lax.axis_size(ALL)
    members = lax.axis_size(PLANE)
    planes = lax.axis_size("z")
    seq_count = lax.axis_size("seq")
    width_rows = query_weight.shape[0]
    hidden_rows = down_weight.shape[0]
    head_width = key_weight.shape[1]
    query_width = query_weight.shape[1]
    head_count = query_width // head_width
    qkv_width = query_width + 2 * head_width
    mix_rows = output_weight.shape[0]
    padded = (width_rows + 1 + 7) // 8 * 8

    gains = (input_gain, query_gain, key_gain, attnout_gain, ffnin_gain, ffnout_gain)
    gain_row = jnp.concatenate(gains)
    gain_widths = [g.shape[0] for g in gains]
    gain_row = jnp.pad(gain_row, (0, qkv_width - gain_row.shape[0]))
    qkv_local = jnp.concatenate([query_weight, key_weight, value_weight], axis=1)
    packed = jnp.concatenate([qkv_local, gain_row[None]], axis=0)
    packed = jnp.pad(packed, ((0, padded - width_rows - 1), (0, 0)))
    packed_all = wide_gather(packed, planes, 0).transpose(1, 0, 2, 3)
    packed_all = packed_all.reshape(devices, padded, qkv_width)
    qkv_full = packed_all[:, :width_rows].reshape(devices * width_rows, qkv_width)
    scales, at = [], 0
    for width in gain_widths:
        scales.append(packed_all[:, width_rows, at : at + width].reshape(-1).astype(f32))
        at += width
    input_scale, query_scale, key_scale, attnout_scale, ffnin_scale, ffnout_scale = scales
    output_full = lax.all_gather(output_weight, ALL, axis=0, tiled=True)

    def column_blocks(weight):
        pieces = weight.reshape(width_rows, planes, members, hidden_rows)
        return pieces.transpose(2, 0, 1, 3).reshape(members, width_rows, planes * hidden_rows)

    gate_up = jnp.concatenate([column_blocks(gate_weight), column_blocks(up_weight)], axis=1)
    gate_up = jnp.broadcast_to(gate_up[None], (planes,) + gate_up.shape)
    gate_up = exchange(gate_up.reshape((devices,) + gate_up.shape[2:]), ALL)
    gate_full = gate_up[:, :width_rows].reshape(devices * width_rows, planes * hidden_rows)
    up_full = gate_up[:, width_rows:].reshape(devices * width_rows, planes * hidden_rows)
    down_full = lax.all_gather(down_weight, "z", axis=0, tiled=True)

    hidden = tokens[0].astype(f32)
    incoming = cotangent[0].astype(f32)
    local_rows = hidden.shape[0]
    full_length = local_rows * seq_count
    offset = lax.axis_index("seq") * local_rows
    segment_row = segment_ids[0]

    def mine(rows):
        return lax.dynamic_slice_in_dim(rows, offset, local_rows)

    my_segments = mine(segment_row)
    cos_full, sin_full = rope_tables(doc_positions(segment_row), head_width)
    cos_table, sin_table = mine(cos_full), mine(sin_full)
    scale = head_width ** (-0.5)

    other_half = [(0, 1), (1, 0)]
    first = lax.axis_index("seq") == 0
    other_tokens = lax.ppermute(tokens[0], "seq", other_half)
    row_hidden = jnp.concatenate(
        [
            jnp.where(first, tokens[0], other_tokens),
            jnp.where(first, other_tokens, tokens[0]),
        ]
    ).astype(f32)
    row_normed = (row_hidden * inverse_rms(row_hidden) * input_scale).astype(bf16)
    key_value_raw = matmul(row_normed, qkv_full[:, query_width:])
    row_key_raw = key_value_raw[:, :head_width]
    value_rows = key_value_raw[:, head_width:].astype(bf16)
    key_rows = rotate(
        row_key_raw * inverse_rms(row_key_raw) * key_scale, cos_full, sin_full
    ).astype(bf16)

    inv_input = inverse_rms(hidden)
    norm_input = hidden * inv_input
    normed = (norm_input * input_scale).astype(bf16)
    query_raw = matmul(normed, qkv_full[:, :query_width]).reshape(
        local_rows, head_count, head_width
    )
    inv_query = inverse_rms(query_raw)
    norm_query = query_raw * inv_query
    queries = (
        rotate(norm_query * query_scale, cos_table[:, None, :], sin_table[:, None, :]) * scale
    ).astype(bf16)
    key_raw = mine(row_key_raw)
    inv_key = inverse_rms(key_raw)
    norm_key = key_raw * inv_key

    query_places = offset + jnp.arange(local_rows, dtype=jnp.int32)
    key_places = jnp.arange(full_length, dtype=jnp.int32)
    allowed = (my_segments[:, None] == segment_row[None, :]) & (
        query_places[:, None] >= key_places[None, :]
    )
    raw_scores = jnp.einsum("qhd,kd->hqk", queries, key_rows, preferred_element_type=f32)
    scores = jnp.where(allowed[None], raw_scores, masked_score)
    peak = jnp.max(scores, axis=-1, keepdims=True)
    log_total = peak + jnp.log(jnp.sum(jnp.exp(scores - peak), axis=-1, keepdims=True))
    probs = jnp.exp(scores - log_total)
    probs_low = probs.astype(bf16)
    attn_mix = jnp.einsum("hqk,kd->qhd", probs_low, value_rows, preferred_element_type=f32)
    attn_flat = attn_mix.astype(bf16).reshape(local_rows, query_width)
    attn_raw = matmul(attn_flat, output_full)
    inv_attn = inverse_rms(attn_raw)
    norm_attn = attn_raw * inv_attn
    middle = hidden + norm_attn * attnout_scale
    inv_middle = inverse_rms(middle)
    norm_middle = middle * inv_middle
    ffn_in = (norm_middle * ffnin_scale).astype(bf16)

    plane_in = plane_gather(ffn_in, 1)
    gate_proj = matmul(plane_in, gate_full)
    up_proj = matmul(plane_in, up_full)
    activated, gelu_back = jax.vjp(gelu_pair, gate_proj, up_proj)
    activated_low = activated.astype(bf16)
    ffn_raw = plane_scatter_sum(matmul(activated_low, down_full).astype(bf16), 2)
    inv_ffn = inverse_rms(ffn_raw)
    norm_ffn = ffn_raw * inv_ffn
    result = middle + norm_ffn * ffnout_scale
    ffnout_gain_grad = jnp.sum(incoming * norm_ffn, axis=0)
    ffn_raw_grad = rms_back(incoming * ffnout_scale, norm_ffn, inv_ffn).astype(bf16)

    plane_grad = plane_gather(ffn_raw_grad, 3)
    act_grad = contract_cols(plane_grad, down_full)
    gate_grad, up_grad = gelu_back(act_grad)
    gate_low = gate_grad.astype(bf16)
    up_low = up_grad.astype(bf16)
    ffn_in_grad = plane_scatter_sum(
        (contract_cols(gate_low, gate_full) + contract_cols(up_low, up_full)).astype(bf16), 4
    )
    down_terms = exchange(
        contract_rows(activated_low, plane_grad)
        .astype(bf16)
        .reshape(planes, hidden_rows, down_weight.shape[1]),
        "z",
    )
    down_wgrad = jnp.sum(down_terms.astype(f32), axis=0)

    def row_blocks(grad):
        return grad.astype(bf16).reshape(devices, width_rows, planes * hidden_rows)

    gate_up_terms = exchange(
        jnp.concatenate(
            [
                row_blocks(contract_rows(plane_in, gate_low)),
                row_blocks(contract_rows(plane_in, up_low)),
            ],
            axis=1,
        ),
        ALL,
    )
    gate_up_sum = jnp.sum(
        gate_up_terms.astype(f32).reshape(
            planes, members, 2 * width_rows, planes * hidden_rows
        ),
        axis=0,
    )
    gate_up_sum = gate_up_sum.reshape(members, 2, width_rows, planes, hidden_rows)
    gate_up_sum = gate_up_sum.transpose(1, 2, 3, 0, 4).reshape(
        2, width_rows, planes * members * hidden_rows
    )
    gate_wgrad, up_wgrad = gate_up_sum[0], gate_up_sum[1]

    ffnin_gain_grad = jnp.sum(ffn_in_grad * norm_middle, axis=0)
    middle_grad = incoming + rms_back(ffn_in_grad * ffnin_scale, norm_middle, inv_middle)
    attnout_gain_grad = jnp.sum(middle_grad * norm_attn, axis=0)
    attn_raw_grad = rms_back(middle_grad * attnout_scale, norm_attn, inv_attn).astype(bf16)
    output_wgrad = contract_rows(attn_flat, attn_raw_grad)
    mix_grad = (
        contract_cols(attn_raw_grad, output_full)
        .astype(bf16)
        .reshape(local_rows, head_count, head_width)
    )
    prob_grad = jnp.einsum("qhd,kd->hqk", mix_grad, value_rows, preferred_element_type=f32)
    row_delta = jnp.sum(prob_grad * probs, axis=-1, keepdims=True)
    score_grad = (probs * (prob_grad - row_delta)).astype(bf16)
    value_grad_rows = jnp.einsum("hqk,qhd->kd", probs_low, mix_grad, preferred_element_type=f32)
    key_grad_rows = jnp.einsum("hqk,qhd->kd", score_grad, queries, preferred_element_type=f32)
    query_grad = jnp.einsum("hqk,kd->qhd", score_grad, key_rows, preferred_element_type=f32)
    key_value_rows = jnp.concatenate([key_grad_rows, value_grad_rows], axis=1)
    theirs = lax.dynamic_slice_in_dim(key_value_rows, local_rows - offset, local_rows)
    key_value_grad = mine(key_value_rows) + lax.ppermute(
        theirs.astype(bf16), "seq", other_half
    ).astype(f32)
    key_grad, value_grad = key_value_grad[:, :head_width], key_value_grad[:, head_width:]
    query_norm_grad = rotate(query_grad * scale, cos_table[:, None, :], -sin_table[:, None, :])
    query_gain_grad = jnp.sum(query_norm_grad * norm_query, axis=(0, 1))
    query_raw_low = (
        rms_back(query_norm_grad * query_scale, norm_query, inv_query)
        .astype(bf16)
        .reshape(local_rows, query_width)
    )
    key_norm_grad = rotate(key_grad, cos_table, -sin_table)
    key_gain_grad = jnp.sum(key_norm_grad * norm_key, axis=0)
    key_raw_low = rms_back(key_norm_grad * key_scale, norm_key, inv_key).astype(bf16)
    qkv_raw_low = jnp.concatenate([query_raw_low, key_raw_low, value_grad.astype(bf16)], axis=1)
    qkv_wgrad = contract_rows(normed, qkv_raw_low)
    normed_grad = contract_cols(qkv_raw_low, qkv_full)
    input_gain_grad = jnp.sum(normed_grad * norm_input, axis=0)
    input_grad = middle_grad + rms_back(normed_grad * input_scale, norm_input, inv_input)

    def to_owners(grad, collective_id):
        rows, columns = grad.shape[0] // devices, grad.shape[1]
        blocks = grad.astype(bf16).reshape(planes, members, rows, columns)
        return owner_sum(blocks.transpose(1, 0, 2, 3), collective_id)

    output_share = to_owners(output_wgrad, 5)
    gain_grads = (
        input_gain_grad,
        query_gain_grad,
        key_gain_grad,
        attnout_gain_grad,
        ffnin_gain_grad,
        ffnout_gain_grad,
    )
    gain_rows = jnp.concatenate([g.reshape(devices, -1) for g in gain_grads], axis=1)
    gain_rows = jnp.pad(gain_rows, ((0, 0), (0, qkv_width - gain_rows.shape[1])))
    qkv_blocks = jnp.concatenate(
        [qkv_wgrad.reshape(devices, width_rows, qkv_width), gain_rows[:, None]], axis=1
    )
    qkv_blocks = jnp.pad(qkv_blocks, ((0, 0), (0, padded - width_rows - 1), (0, 0)))
    qkv_share = to_owners(qkv_blocks.reshape(devices * padded, qkv_width), 6)
    gain_shares, at = [], 0
    for width in gain_widths:
        gain_shares.append(qkv_share[width_rows, at : at + width])
        at += width
    return (
        result.astype(bf16)[None],
        input_grad[None],
        qkv_share[:width_rows, :query_width],
        qkv_share[:width_rows, query_width : query_width + head_width],
        qkv_share[:width_rows, query_width + head_width :],
        output_share,
        gate_wgrad,
        up_wgrad,
        down_wgrad,
        *gain_shares,
    )


def solution(mesh):
    dp, seq = mesh.shape["dp"], mesh.shape["seq"]
    split = Mesh(mesh.devices.reshape(dp // 4, 2, 2, seq), ALL)
    rows = P(("z", "x", "core"), "seq", None)
    matrix, vector = P(ALL, None), P(ALL)
    return jax.shard_map(
        body,
        mesh=split,
        in_specs=(rows, P(("z", "x", "core"), None), rows) + (matrix,) * 7 + (vector,) * 6,
        out_specs=(rows, rows) + (matrix,) * 7 + (vector,) * 6,
        check_vma=False,
    )
```

```python
import functools

import jax
import jax.numpy as jnp
from jax import lax
from jax.experimental import pallas as pl
from jax.experimental.pallas import tpu as pltpu
from jax.sharding import Mesh
from jax.sharding import PartitionSpec as P

epsilon = 1e-06
rope_base = 1000000.0
masked_score = -1e30


def inverse_rms(values):
    return lax.rsqrt(jnp.mean(values * values, axis=-1, keepdims=True) + epsilon)


def rms_back(grad_normed, normed, inverse):
    return inverse * (grad_normed - normed * jnp.mean(grad_normed * normed, axis=-1, keepdims=True))


def doc_positions(segments):
    length = segments.shape[0]
    smaller = segments[None, :] < segments[:, None]
    starts = jnp.sum(smaller.astype(jnp.int32), axis=1)
    return (jnp.arange(length, dtype=jnp.int32) - starts).astype(jnp.float32)


def rope_tables(positions, head_width):
    half_width = head_width // 2
    frequency = rope_base ** (-(2.0 / head_width) * jnp.arange(half_width, dtype=jnp.float32))
    angles = positions[..., None] * frequency
    return (jnp.cos(angles), jnp.sin(angles))


def rotate(values, cos_table, sin_table):
    half_width = values.shape[-1] // 2
    first_half = values[..., :half_width]
    second_half = values[..., half_width:]
    return jnp.concatenate(
        [
            first_half * cos_table - second_half * sin_table,
            second_half * cos_table + first_half * sin_table,
        ],
        axis=-1,
    )


def matmul(left, right):
    return jnp.dot(left, right, preferred_element_type=jnp.float32)


def contract_rows(left, right):
    return lax.dot_general(
        left, right, (((0,), (0,)), ((), ())), preferred_element_type=jnp.float32
    )


def contract_cols(left, right):
    return lax.dot_general(
        left, right, (((1,), (1,)), ((), ())), preferred_element_type=jnp.float32
    )


def gelu_pair(gate_proj, up_proj):
    return jax.nn.gelu(gate_proj, approximate=True) * up_proj


ALL = ("z", "x", "core", "seq")
PLANE = ("x", "core", "seq")

MESH_ID = pl.DeviceIdType.MESH
VMEM_BYTES = 48 * 2**20


def exchange(blocks, axes):
    return lax.all_to_all(blocks, axes, split_axis=0, concat_axis=0, tiled=True)


def busy(microseconds):
    return pl.CostEstimate(flops=0, bytes_accessed=microseconds * 3_000_000, transcendentals=0)


def plane_places():
    z, x, core, seq = (lax.axis_index(name) for name in ALL)
    sibling = (z, x, 1 - core, seq)
    along_x = (z, 1 - x, core, seq)
    along_y = (z, x, core, 1 - seq)

    def member(other_x, other_core, other_y):
        at_x = 1 - x if other_x else x
        at_core = 1 - core if other_core else core
        at_y = 1 - seq if other_y else seq
        return (at_x * 2 + at_core) * 2 + at_y

    return sibling, along_x, along_y, member


def greet(places):
    barrier = pltpu.get_barrier_semaphore()
    for place in places:
        pl.semaphore_signal(barrier, inc=1, device_id=place, device_id_type=MESH_ID)
    pl.semaphore_wait(barrier, len(places))


def sender(send_sems, recv_sems):
    def send(kind, source, target, place):
        copy = pltpu.make_async_remote_copy(
            src_ref=source,
            dst_ref=target,
            send_sem=send_sems.at[kind],
            recv_sem=recv_sems.at[kind],
            device_id=place,
            device_id_type=MESH_ID,
        )
        copy.start()
        return copy

    return send


def plane_spread(own_ref, out_ref, send_sems, recv_sems, local_sem):
    sibling, along_x, along_y, member = plane_places()
    half = own_ref.shape[0] // 2
    top, bottom = pl.ds(0, half), pl.ds(half, half)
    me = member(0, 0, 0)
    keep = pltpu.make_async_copy(own_ref, out_ref.at[me], local_sem)
    keep.start()
    send = sender(send_sems, recv_sems)

    def forward(kind, block, rows, place):
        return send(kind, out_ref.at[block, rows], out_ref.at[block, rows], place)

    own_x_top = send(1, own_ref.at[top], out_ref.at[me, top], along_x)
    own_y_bottom = send(3, own_ref.at[bottom], out_ref.at[me, bottom], along_y)
    own_sibling = send(0, own_ref, out_ref.at[me], sibling)
    own_x_bottom = send(2, own_ref.at[bottom], out_ref.at[me, bottom], along_x)
    own_y_top = send(4, own_ref.at[top], out_ref.at[me, top], along_y)
    x_block, y_block, diagonal = member(1, 0, 0), member(0, 0, 1), member(1, 0, 1)
    own_x_top.wait_recv()
    diagonal_top = forward(5, x_block, top, along_y)
    x_top = forward(7, x_block, top, sibling)
    own_y_bottom.wait_recv()
    diagonal_bottom = forward(6, y_block, bottom, along_x)
    y_bottom = forward(9, y_block, bottom, sibling)
    own_x_bottom.wait_recv()
    x_bottom = forward(8, x_block, bottom, sibling)
    own_y_top.wait_recv()
    y_top = forward(10, y_block, top, sibling)
    diagonal_top.wait_recv()
    far_top = forward(11, diagonal, top, sibling)
    diagonal_bottom.wait_recv()
    far_bottom = forward(12, diagonal, bottom, sibling)
    for copy in (own_sibling, x_top, y_bottom, x_bottom, y_top, far_top, far_bottom):
        copy.wait_recv()
    for copy in (
        own_x_top,
        own_y_bottom,
        own_sibling,
        own_x_bottom,
        own_y_top,
        diagonal_top,
        diagonal_bottom,
        x_top,
        y_bottom,
        x_bottom,
        y_top,
        far_top,
        far_bottom,
    ):
        copy.wait_send()
    keep.wait()


def gather_kernel(own_ref, out_ref, *sems):
    greet(plane_places()[:3])
    plane_spread(own_ref, out_ref, *sems)


def wide_gather_kernel(planes, own_ref, out_ref, held, z_send, z_recv, own_sem, *sems):
    z, x, core, seq = (lax.axis_index(name) for name in ALL)
    others = [(lax.rem(z + k, planes), x, core, seq) for k in range(1, planes)]
    greet((*plane_places()[:3], *others))
    slot = held.at[z]
    keep = pltpu.make_async_copy(own_ref, slot, own_sem)
    keep.start()
    send = sender(z_send, z_recv)
    copies = [send(k, own_ref, slot, place) for k, place in enumerate(others)]
    for copy in copies:
        copy.wait_recv()
    keep.wait()
    plane_spread(held, out_ref, *sems)
    for copy in copies:
        copy.wait_send()


GATHER_SEMS = [
    pltpu.SemaphoreType.DMA((13,)),
    pltpu.SemaphoreType.DMA((13,)),
    pltpu.SemaphoreType.DMA,
]


def wide_gather(local, planes, collective_id):
    rows, columns = local.shape
    members = 8
    return pl.pallas_call(
        functools.partial(wide_gather_kernel, planes),
        out_shape=jax.ShapeDtypeStruct((members, planes, rows, columns), local.dtype),
        in_specs=[pl.BlockSpec(memory_space=pltpu.VMEM)],
        out_specs=pl.BlockSpec(memory_space=pl.ANY),
        scratch_shapes=[
            pltpu.VMEM((planes, rows, columns), local.dtype),
            pltpu.SemaphoreType.DMA((planes - 1,)),
            pltpu.SemaphoreType.DMA((planes - 1,)),
            pltpu.SemaphoreType.DMA,
            *GATHER_SEMS,
        ],
        cost_estimate=busy(35),
        compiler_params=pltpu.CompilerParams(
            collective_id=collective_id, has_side_effects=True, vmem_limit_bytes=VMEM_BYTES
        ),
    )(local)


def plane_gather(local, collective_id):
    rows, columns = local.shape
    members = 8
    out = pl.pallas_call(
        gather_kernel,
        out_shape=jax.ShapeDtypeStruct((members, rows // 16, 16, columns), local.dtype),
        in_specs=[pl.BlockSpec(memory_space=pl.ANY)],
        out_specs=pl.BlockSpec(memory_space=pl.ANY),
        scratch_shapes=GATHER_SEMS,
        cost_estimate=busy(25),
        compiler_params=pltpu.CompilerParams(
            collective_id=collective_id, has_side_effects=True, vmem_limit_bytes=VMEM_BYTES
        ),
    )(local.reshape(rows // 16, 16, columns))
    return out.reshape(members * rows, columns)


def add_rows(target, sources, start, count):
    def one(i, carry):
        total = sources[0][i].astype(jnp.float32)
        for source in sources[1:]:
            total = total + source[i].astype(jnp.float32)
        target[i] = total.astype(target.dtype)
        return carry

    lax.fori_loop(start, start + count, one, 0)


def plane_sum(part_ref, own_sum, near, sums, from_x, from_y, far_x, far_y, send_sems, recv_sems):
    sibling, along_x, along_y, member = plane_places()
    rows = own_sum.shape[0]
    half = rows // 2
    top, bottom = pl.ds(0, half), pl.ds(half, half)
    send = sender(send_sems, recv_sems)
    chips = ((1, 1), (1, 0), (0, 1), (0, 0))
    mine = [part_ref.at[member(at_x, 0, at_y)] for at_x, at_y in chips]
    to_sibling = [
        send(k, part_ref.at[member(at_x, 1, at_y)], near.at[k], sibling)
        for k, (at_x, at_y) in enumerate(chips)
    ]
    to_sibling[0].wait_recv()
    add_rows(sums.at[0], (mine[0], near.at[0]), 0, rows)
    diagonal_x = send(4, sums.at[0, bottom], far_x.at[bottom], along_x)
    diagonal_y = send(5, sums.at[0, top], far_y.at[top], along_y)
    to_sibling[1].wait_recv()
    add_rows(sums.at[1], (mine[1], near.at[1]), half, half)
    direct_x = send(6, sums.at[1, bottom], from_x.at[bottom], along_x)
    to_sibling[2].wait_recv()
    add_rows(sums.at[2], (mine[2], near.at[2]), 0, half)
    direct_y = send(7, sums.at[2, top], from_y.at[top], along_y)
    to_sibling[3].wait_recv()
    diagonal_y.wait_recv()
    add_rows(sums.at[1], (mine[1], near.at[1], far_y), 0, half)
    joint_x = send(8, sums.at[1, top], from_x.at[top], along_x)
    diagonal_x.wait_recv()
    add_rows(sums.at[2], (mine[2], near.at[2], far_x), half, half)
    joint_y = send(9, sums.at[2, bottom], from_y.at[bottom], along_y)
    direct_x.wait_recv()
    direct_y.wait_recv()
    joint_x.wait_recv()
    joint_y.wait_recv()
    add_rows(own_sum, (mine[3], near.at[3], from_x, from_y), 0, rows)
    for copy in (*to_sibling, diagonal_x, diagonal_y, direct_x, direct_y, joint_x, joint_y):
        copy.wait_send()


def plane_sum_kernel(part_ref, out_ref, *scratch):
    sibling, along_x, along_y, _ = plane_places()
    greet((sibling, along_x, along_y))
    plane_sum(part_ref, out_ref, *scratch)


def plane_sum_scratch(shape, dtype):
    block = pltpu.VMEM(shape, dtype)
    return [
        pltpu.VMEM((4, *shape), dtype),
        pltpu.VMEM((3, *shape), dtype),
        block,
        block,
        block,
        block,
        pltpu.SemaphoreType.DMA((10,)),
        pltpu.SemaphoreType.DMA((10,)),
    ]


def plane_scatter_sum(partial, collective_id):
    members = 8
    rows, columns = partial.shape[0] // members, partial.shape[1]
    shape = (rows // 16, 16, columns)
    out = pl.pallas_call(
        plane_sum_kernel,
        out_shape=jax.ShapeDtypeStruct(shape, jnp.float32),
        in_specs=[pl.BlockSpec(memory_space=pltpu.VMEM)],
        out_specs=pl.BlockSpec(memory_space=pltpu.VMEM),
        scratch_shapes=plane_sum_scratch(shape, partial.dtype),
        cost_estimate=busy(25),
        compiler_params=pltpu.CompilerParams(
            collective_id=collective_id, has_side_effects=True, vmem_limit_bytes=VMEM_BYTES
        ),
    )(partial.reshape(members, *shape))
    return out.reshape(rows, columns)


def owner_sum_kernel(planes, part_ref, out_ref, own_sum, leaving, arriving, z_send, z_recv, *scratch):
    sibling, along_x, along_y, _ = plane_places()
    z, x, core, seq = (lax.axis_index(name) for name in ALL)
    others = [(lax.rem(z + k, planes), x, core, seq) for k in range(1, planes)]
    greet((sibling, along_x, along_y, *others))
    plane_sum(part_ref, own_sum, *scratch)
    send = sender(z_send, z_recv)

    def narrow(i, carry):
        leaving[i] = own_sum[i].astype(leaving.dtype)
        return carry

    lax.fori_loop(0, planes, narrow, 0)
    copies = [
        send(k, leaving.at[place[0]], arriving.at[k], place) for k, place in enumerate(others)
    ]
    for copy in copies:
        copy.wait_recv()

    value = own_sum[z]
    for k in range(planes - 1):
        value = value + arriving[k].astype(jnp.float32)
    out_ref[...] = value
    for copy in copies:
        copy.wait_send()


def owner_sum(blocks, collective_id):
    members, planes, rows, columns = blocks.shape
    return pl.pallas_call(
        functools.partial(owner_sum_kernel, planes),
        out_shape=jax.ShapeDtypeStruct((rows, columns), jnp.float32),
        in_specs=[pl.BlockSpec(memory_space=pltpu.VMEM)],
        out_specs=pl.BlockSpec(memory_space=pltpu.VMEM),
        scratch_shapes=[
            pltpu.VMEM((planes, rows, columns), jnp.float32),
            pltpu.VMEM((planes, rows, columns), blocks.dtype),
            pltpu.VMEM((planes - 1, rows, columns), blocks.dtype),
            pltpu.SemaphoreType.DMA((planes - 1,)),
            pltpu.SemaphoreType.DMA((planes - 1,)),
            *plane_sum_scratch((planes, rows, columns), blocks.dtype),
        ],
        cost_estimate=busy(35),
        compiler_params=pltpu.CompilerParams(
            collective_id=collective_id, has_side_effects=True, vmem_limit_bytes=VMEM_BYTES
        ),
    )(blocks)


def body(
    tokens,
    segment_ids,
    cotangent,
    query_weight,
    key_weight,
    value_weight,
    output_weight,
    gate_weight,
    up_weight,
    down_weight,
    input_gain,
    query_gain,
    key_gain,
    attnout_gain,
    ffnin_gain,
    ffnout_gain,
):
    bf16, f32 = jnp.bfloat16, jnp.float32
    devices = lax.axis_size(ALL)
    members = lax.axis_size(PLANE)
    planes = lax.axis_size("z")
    seq_count = lax.axis_size("seq")
    width_rows = query_weight.shape[0]
    hidden_rows = down_weight.shape[0]
    head_width = key_weight.shape[1]
    query_width = query_weight.shape[1]
    head_count = query_width // head_width
    qkv_width = query_width + 2 * head_width
    mix_rows = output_weight.shape[0]
    padded = (width_rows + 1 + 7) // 8 * 8

    def column_blocks(weight):
        pieces = weight.reshape(width_rows, planes, members, hidden_rows)
        return pieces.transpose(2, 0, 1, 3).reshape(members, width_rows, planes * hidden_rows)

    gate_up = jnp.concatenate([column_blocks(gate_weight), column_blocks(up_weight)], axis=1)
    gate_up = jnp.broadcast_to(gate_up[None], (planes,) + gate_up.shape)
    gate_up = gate_up.reshape((devices,) + gate_up.shape[2:])

    gains = (input_gain, query_gain, key_gain, attnout_gain, ffnin_gain, ffnout_gain)
    gain_row = jnp.concatenate(gains)
    gain_widths = [g.shape[0] for g in gains]
    gain_row = jnp.pad(gain_row, (0, qkv_width - gain_row.shape[0]))
    qkv_local = jnp.concatenate([query_weight, key_weight, value_weight], axis=1)
    packed = jnp.concatenate([qkv_local, gain_row[None]], axis=0)
    packed = jnp.pad(packed, ((0, padded - width_rows - 1), (0, 0)))
    output_wide = jnp.pad(output_weight, ((0, 0), (0, qkv_width - output_weight.shape[1])))
    packed = jnp.concatenate([packed, output_wide], axis=0)
    packed_all = wide_gather(packed, planes, 0)
    gate_up, down_local, packed_all = lax.optimization_barrier(
        (gate_up, down_weight, packed_all)
    )
    gate_up = exchange(gate_up, ALL)
    gate_full = gate_up[:, :width_rows].reshape(devices * width_rows, planes * hidden_rows)
    up_full = gate_up[:, width_rows:].reshape(devices * width_rows, planes * hidden_rows)
    down_full = lax.all_gather(down_local, "z", axis=0, tiled=True)
    packed_all = packed_all.transpose(1, 0, 2, 3)
    packed_all = packed_all.reshape(devices, padded + mix_rows, qkv_width)
    qkv_full = packed_all[:, :width_rows].reshape(devices * width_rows, qkv_width)
    output_full = packed_all[:, padded:, : output_weight.shape[1]]
    output_full = output_full.reshape(devices * mix_rows, output_weight.shape[1])
    scales, at = [], 0
    for width in gain_widths:
        scales.append(packed_all[:, width_rows, at : at + width].reshape(-1).astype(f32))
        at += width
    input_scale, query_scale, key_scale, attnout_scale, ffnin_scale, ffnout_scale = scales

    hidden = tokens[0].astype(f32)
    incoming = cotangent[0].astype(f32)
    local_rows = hidden.shape[0]
    full_length = local_rows * seq_count
    offset = lax.axis_index("seq") * local_rows
    segment_row = segment_ids[0]

    def mine(rows):
        return lax.dynamic_slice_in_dim(rows, offset, local_rows)

    my_segments = mine(segment_row)
    cos_full, sin_full = rope_tables(doc_positions(segment_row), head_width)
    cos_table, sin_table = mine(cos_full), mine(sin_full)
    scale = head_width ** (-0.5)

    other_half = [(0, 1), (1, 0)]
    first = lax.axis_index("seq") == 0
    other_tokens = lax.ppermute(tokens[0], "seq", other_half)
    row_hidden = jnp.concatenate(
        [
            jnp.where(first, tokens[0], other_tokens),
            jnp.where(first, other_tokens, tokens[0]),
        ]
    ).astype(f32)
    row_normed = (row_hidden * inverse_rms(row_hidden) * input_scale).astype(bf16)
    key_value_raw = matmul(row_normed, qkv_full[:, query_width:])
    row_key_raw = key_value_raw[:, :head_width]
    value_rows = key_value_raw[:, head_width:].astype(bf16)
    key_rows = rotate(
        row_key_raw * inverse_rms(row_key_raw) * key_scale, cos_full, sin_full
    ).astype(bf16)

    inv_input = inverse_rms(hidden)
    norm_input = hidden * inv_input
    normed = (norm_input * input_scale).astype(bf16)
    query_raw = matmul(normed, qkv_full[:, :query_width]).reshape(
        local_rows, head_count, head_width
    )
    inv_query = inverse_rms(query_raw)
    norm_query = query_raw * inv_query
    queries = (
        rotate(norm_query * query_scale, cos_table[:, None, :], sin_table[:, None, :]) * scale
    ).astype(bf16)
    key_raw = mine(row_key_raw)
    inv_key = inverse_rms(key_raw)
    norm_key = key_raw * inv_key

    query_places = offset + jnp.arange(local_rows, dtype=jnp.int32)
    key_places = jnp.arange(full_length, dtype=jnp.int32)
    allowed = (my_segments[:, None] == segment_row[None, :]) & (
        query_places[:, None] >= key_places[None, :]
    )
    raw_scores = jnp.einsum("qhd,kd->hqk", queries, key_rows, preferred_element_type=f32)
    scores = jnp.where(allowed[None], raw_scores, masked_score)
    peak = jnp.max(scores, axis=-1, keepdims=True)
    log_total = peak + jnp.log(jnp.sum(jnp.exp(scores - peak), axis=-1, keepdims=True))
    probs = jnp.exp(scores - log_total)
    probs_low = probs.astype(bf16)
    attn_mix = jnp.einsum("hqk,kd->qhd", probs_low, value_rows, preferred_element_type=f32)
    attn_flat = attn_mix.astype(bf16).reshape(local_rows, query_width)
    attn_raw = matmul(attn_flat, output_full)
    inv_attn = inverse_rms(attn_raw)
    norm_attn = attn_raw * inv_attn
    middle = hidden + norm_attn * attnout_scale
    inv_middle = inverse_rms(middle)
    norm_middle = middle * inv_middle
    ffn_in = (norm_middle * ffnin_scale).astype(bf16)

    plane_in = plane_gather(ffn_in, 1)
    gate_proj = matmul(plane_in, gate_full)
    up_proj = matmul(plane_in, up_full)
    activated, gelu_back = jax.vjp(gelu_pair, gate_proj, up_proj)
    activated_low = activated.astype(bf16)
    ffn_raw = plane_scatter_sum(matmul(activated_low, down_full).astype(bf16), 2)
    inv_ffn = inverse_rms(ffn_raw)
    norm_ffn = ffn_raw * inv_ffn
    result = middle + norm_ffn * ffnout_scale
    ffnout_gain_grad = jnp.sum(incoming * norm_ffn, axis=0)
    ffn_raw_grad = rms_back(incoming * ffnout_scale, norm_ffn, inv_ffn).astype(bf16)

    plane_grad = plane_gather(ffn_raw_grad, 3)
    act_grad = contract_cols(plane_grad, down_full)
    gate_grad, up_grad = gelu_back(act_grad)
    gate_low = gate_grad.astype(bf16)
    up_low = up_grad.astype(bf16)
    down_blocks = contract_rows(activated_low, plane_grad).reshape(
        planes, hidden_rows, down_weight.shape[1]
    )
    plane = lax.axis_index("z")
    down_wgrad = lax.dynamic_index_in_dim(down_blocks, plane, 0, keepdims=False)
    down_low = down_blocks.astype(bf16)
    for k in range(1, planes):
        leaving = lax.dynamic_index_in_dim(down_low, lax.rem(plane + k, planes), 0, keepdims=False)
        shift = [(i, (i + k) % planes) for i in range(planes)]
        down_wgrad = down_wgrad + lax.ppermute(leaving, "z", shift).astype(f32)

    def row_blocks(grad):
        return grad.astype(bf16).reshape(devices, width_rows, planes * hidden_rows)

    gate_up_blocks = jnp.concatenate(
        [
            row_blocks(contract_rows(plane_in, gate_low)),
            row_blocks(contract_rows(plane_in, up_low)),
        ],
        axis=1,
    )
    ffn_in_part = (contract_cols(gate_low, gate_full) + contract_cols(up_low, up_full)).astype(bf16)
    gate_up_blocks, ffn_in_part = lax.optimization_barrier((gate_up_blocks, ffn_in_part))
    gate_up_terms = exchange(gate_up_blocks, ALL)
    ffn_in_grad = plane_scatter_sum(ffn_in_part, 4)
    ffnin_gain_grad = jnp.sum(ffn_in_grad * norm_middle, axis=0)
    middle_grad = incoming + rms_back(ffn_in_grad * ffnin_scale, norm_middle, inv_middle)
    attnout_gain_grad = jnp.sum(middle_grad * norm_attn, axis=0)
    attn_raw_grad = rms_back(middle_grad * attnout_scale, norm_attn, inv_attn).astype(bf16)
    output_wgrad = contract_rows(attn_flat, attn_raw_grad)
    mix_grad = (
        contract_cols(attn_raw_grad, output_full)
        .astype(bf16)
        .reshape(local_rows, head_count, head_width)
    )
    prob_grad = jnp.einsum("qhd,kd->hqk", mix_grad, value_rows, preferred_element_type=f32)
    row_delta = jnp.sum(prob_grad * probs, axis=-1, keepdims=True)
    score_grad = (probs * (prob_grad - row_delta)).astype(bf16)
    value_grad_rows = jnp.einsum("hqk,qhd->kd", probs_low, mix_grad, preferred_element_type=f32)
    key_grad_rows = jnp.einsum("hqk,qhd->kd", score_grad, queries, preferred_element_type=f32)
    query_grad = jnp.einsum("hqk,kd->qhd", score_grad, key_rows, preferred_element_type=f32)
    key_value_rows = jnp.concatenate([key_grad_rows, value_grad_rows], axis=1)
    theirs = lax.dynamic_slice_in_dim(key_value_rows, local_rows - offset, local_rows)
    key_value_grad = mine(key_value_rows) + lax.ppermute(
        theirs.astype(bf16), "seq", other_half
    ).astype(f32)
    key_grad, value_grad = key_value_grad[:, :head_width], key_value_grad[:, head_width:]
    query_norm_grad = rotate(query_grad * scale, cos_table[:, None, :], -sin_table[:, None, :])
    query_gain_grad = jnp.sum(query_norm_grad * norm_query, axis=(0, 1))
    query_raw_low = (
        rms_back(query_norm_grad * query_scale, norm_query, inv_query)
        .astype(bf16)
        .reshape(local_rows, query_width)
    )
    key_norm_grad = rotate(key_grad, cos_table, -sin_table)
    key_gain_grad = jnp.sum(key_norm_grad * norm_key, axis=0)
    key_raw_low = rms_back(key_norm_grad * key_scale, norm_key, inv_key).astype(bf16)
    qkv_raw_low = jnp.concatenate([query_raw_low, key_raw_low, value_grad.astype(bf16)], axis=1)
    qkv_wgrad = contract_rows(normed, qkv_raw_low)
    normed_grad = contract_cols(qkv_raw_low, qkv_full)
    input_gain_grad = jnp.sum(normed_grad * norm_input, axis=0)
    input_grad = middle_grad + rms_back(normed_grad * input_scale, norm_input, inv_input)

    gain_grads = (
        input_gain_grad,
        query_gain_grad,
        key_gain_grad,
        attnout_gain_grad,
        ffnin_gain_grad,
        ffnout_gain_grad,
    )
    gain_rows = jnp.concatenate([g.reshape(devices, -1) for g in gain_grads], axis=1)
    gain_rows = jnp.pad(gain_rows, ((0, 0), (0, qkv_width - gain_rows.shape[1])))
    blocks = jnp.concatenate(
        [qkv_wgrad.reshape(devices, width_rows, qkv_width), gain_rows[:, None]], axis=1
    )
    blocks = jnp.pad(blocks.astype(bf16), ((0, 0), (0, padded - width_rows - 1), (0, 0)))
    output_blocks = output_wgrad.astype(bf16).reshape(devices, mix_rows, -1)
    output_blocks = jnp.pad(
        output_blocks, ((0, 0), (0, 0), (0, qkv_width - output_blocks.shape[2]))
    )
    blocks = jnp.concatenate([blocks, output_blocks], axis=1)
    blocks = blocks.reshape(planes, members, padded + mix_rows, qkv_width)
    blocks, gate_up_terms = lax.optimization_barrier((blocks, gate_up_terms))
    share = owner_sum(blocks.transpose(1, 0, 2, 3), 5)
    gate_up_sum = jnp.sum(
        gate_up_terms.astype(f32).reshape(
            planes, members, 2 * width_rows, planes * hidden_rows
        ),
        axis=0,
    )
    gate_up_sum = gate_up_sum.reshape(members, 2, width_rows, planes, hidden_rows)
    gate_up_sum = gate_up_sum.transpose(1, 2, 3, 0, 4).reshape(
        2, width_rows, planes * members * hidden_rows
    )
    gate_wgrad, up_wgrad = gate_up_sum[0], gate_up_sum[1]

    qkv_share, output_share = share[:padded], share[padded:, : output_weight.shape[1]]
    gain_shares, at = [], 0
    for width in gain_widths:
        gain_shares.append(qkv_share[width_rows, at : at + width])
        at += width
    return (
        result.astype(bf16)[None],
        input_grad[None],
        qkv_share[:width_rows, :query_width],
        qkv_share[:width_rows, query_width : query_width + head_width],
        qkv_share[:width_rows, query_width + head_width :],
        output_share,
        gate_wgrad,
        up_wgrad,
        down_wgrad,
        *gain_shares,
    )


def solution(mesh):
    dp, seq = mesh.shape["dp"], mesh.shape["seq"]
    split = Mesh(mesh.devices.reshape(dp // 4, 2, 2, seq), ALL)
    rows = P(("z", "x", "core"), "seq", None)
    matrix, vector = P(ALL, None), P(ALL)
    return jax.shard_map(
        body,
        mesh=split,
        in_specs=(rows, P(("z", "x", "core"), None), rows) + (matrix,) * 7 + (vector,) * 6,
        out_specs=(rows, rows) + (matrix,) * 7 + (vector,) * 6,
        check_vma=False,
    )
```

```python
import functools

import jax
import jax.numpy as jnp
from jax import lax
from jax.experimental import pallas as pl
from jax.experimental.pallas import tpu as pltpu
from jax.sharding import Mesh
from jax.sharding import PartitionSpec as P

epsilon = 1e-06
rope_base = 1000000.0
masked_score = -1e30


def inverse_rms(values):
    return lax.rsqrt(jnp.mean(values * values, axis=-1, keepdims=True) + epsilon)


def rms_back(grad_normed, normed, inverse):
    return inverse * (grad_normed - normed * jnp.mean(grad_normed * normed, axis=-1, keepdims=True))


def doc_positions(segments):
    length = segments.shape[0]
    smaller = segments[None, :] < segments[:, None]
    starts = jnp.sum(smaller.astype(jnp.int32), axis=1)
    return (jnp.arange(length, dtype=jnp.int32) - starts).astype(jnp.float32)


def rope_tables(positions, head_width):
    half_width = head_width // 2
    frequency = rope_base ** (-(2.0 / head_width) * jnp.arange(half_width, dtype=jnp.float32))
    angles = positions[..., None] * frequency
    return (jnp.cos(angles), jnp.sin(angles))


def rotate(values, cos_table, sin_table):
    half_width = values.shape[-1] // 2
    first_half = values[..., :half_width]
    second_half = values[..., half_width:]
    return jnp.concatenate(
        [
            first_half * cos_table - second_half * sin_table,
            second_half * cos_table + first_half * sin_table,
        ],
        axis=-1,
    )


def matmul(left, right):
    return jnp.dot(left, right, preferred_element_type=jnp.float32)


def contract_rows(left, right):
    return lax.dot_general(
        left, right, (((0,), (0,)), ((), ())), preferred_element_type=jnp.float32
    )


def contract_cols(left, right):
    return lax.dot_general(
        left, right, (((1,), (1,)), ((), ())), preferred_element_type=jnp.float32
    )


def gelu_pair(gate_proj, up_proj):
    return jax.nn.gelu(gate_proj, approximate=True) * up_proj


ALL = ("z", "x", "core", "seq")
PLANE = ("x", "core", "seq")

MESH_ID = pl.DeviceIdType.MESH
VMEM_BYTES = 48 * 2**20


def exchange(blocks, axes):
    return lax.all_to_all(blocks, axes, split_axis=0, concat_axis=0, tiled=True)


def busy(microseconds):
    return pl.CostEstimate(flops=0, bytes_accessed=microseconds * 3_000_000, transcendentals=0)


def plane_places():
    z, x, core, seq = (lax.axis_index(name) for name in ALL)
    sibling = (z, x, 1 - core, seq)
    along_x = (z, 1 - x, core, seq)
    along_y = (z, x, core, 1 - seq)

    def member(other_x, other_core, other_y):
        at_x = 1 - x if other_x else x
        at_core = 1 - core if other_core else core
        at_y = 1 - seq if other_y else seq
        return (at_x * 2 + at_core) * 2 + at_y

    return sibling, along_x, along_y, member


def greet(places):
    barrier = pltpu.get_barrier_semaphore()
    for place in places:
        pl.semaphore_signal(barrier, inc=1, device_id=place, device_id_type=MESH_ID)
    pl.semaphore_wait(barrier, len(places))


def sender(send_sems, recv_sems):
    def send(kind, source, target, place):
        copy = pltpu.make_async_remote_copy(
            src_ref=source,
            dst_ref=target,
            send_sem=send_sems.at[kind],
            recv_sem=recv_sems.at[kind],
            device_id=place,
            device_id_type=MESH_ID,
        )
        copy.start()
        return copy

    return send


def plane_spread(own_ref, out_ref, send_sems, recv_sems, local_sem):
    sibling, along_x, along_y, member = plane_places()
    half = own_ref.shape[0] // 2
    top, bottom = pl.ds(0, half), pl.ds(half, half)
    me = member(0, 0, 0)
    keep = pltpu.make_async_copy(own_ref, out_ref.at[me], local_sem)
    keep.start()
    send = sender(send_sems, recv_sems)

    def forward(kind, block, rows, place):
        return send(kind, out_ref.at[block, rows], out_ref.at[block, rows], place)

    own_x_top = send(1, own_ref.at[top], out_ref.at[me, top], along_x)
    own_y_bottom = send(3, own_ref.at[bottom], out_ref.at[me, bottom], along_y)
    own_sibling = send(0, own_ref, out_ref.at[me], sibling)
    own_x_bottom = send(2, own_ref.at[bottom], out_ref.at[me, bottom], along_x)
    own_y_top = send(4, own_ref.at[top], out_ref.at[me, top], along_y)
    x_block, y_block, diagonal = member(1, 0, 0), member(0, 0, 1), member(1, 0, 1)
    own_x_top.wait_recv()
    diagonal_top = forward(5, x_block, top, along_y)
    x_top = forward(7, x_block, top, sibling)
    own_y_bottom.wait_recv()
    diagonal_bottom = forward(6, y_block, bottom, along_x)
    y_bottom = forward(9, y_block, bottom, sibling)
    own_x_bottom.wait_recv()
    x_bottom = forward(8, x_block, bottom, sibling)
    own_y_top.wait_recv()
    y_top = forward(10, y_block, top, sibling)
    diagonal_top.wait_recv()
    far_top = forward(11, diagonal, top, sibling)
    diagonal_bottom.wait_recv()
    far_bottom = forward(12, diagonal, bottom, sibling)
    for copy in (own_sibling, x_top, y_bottom, x_bottom, y_top, far_top, far_bottom):
        copy.wait_recv()
    for copy in (
        own_x_top,
        own_y_bottom,
        own_sibling,
        own_x_bottom,
        own_y_top,
        diagonal_top,
        diagonal_bottom,
        x_top,
        y_bottom,
        x_bottom,
        y_top,
        far_top,
        far_bottom,
    ):
        copy.wait_send()
    keep.wait()


def gather_kernel(own_ref, out_ref, *sems):
    greet(plane_places()[:3])
    plane_spread(own_ref, out_ref, *sems)


def z_gather_kernel(planes, own_ref, out_ref, send_sems, recv_sems, own_sem):
    z, x, core, seq = (lax.axis_index(name) for name in ALL)
    others = [(lax.rem(z + k, planes), x, core, seq) for k in range(1, planes)]
    greet(others)
    keep = pltpu.make_async_copy(own_ref, out_ref.at[z], own_sem)
    keep.start()
    send = sender(send_sems, recv_sems)
    copies = [send(k, own_ref, out_ref.at[z], place) for k, place in enumerate(others)]
    for copy in copies:
        copy.wait_recv()
    for copy in copies:
        copy.wait_send()
    keep.wait()


GATHER_SEMS = [
    pltpu.SemaphoreType.DMA((13,)),
    pltpu.SemaphoreType.DMA((13,)),
    pltpu.SemaphoreType.DMA,
]


def z_gather(local, planes, collective_id):
    return pl.pallas_call(
        functools.partial(z_gather_kernel, planes),
        out_shape=jax.ShapeDtypeStruct((planes, *local.shape), local.dtype),
        in_specs=[pl.BlockSpec(memory_space=pltpu.VMEM)],
        out_specs=pl.BlockSpec(memory_space=pl.ANY),
        scratch_shapes=[
            pltpu.SemaphoreType.DMA((planes - 1,)),
            pltpu.SemaphoreType.DMA((planes - 1,)),
            pltpu.SemaphoreType.DMA,
        ],
        cost_estimate=busy(20),
        compiler_params=pltpu.CompilerParams(
            collective_id=collective_id, has_side_effects=True, vmem_limit_bytes=VMEM_BYTES
        ),
    )(local)


def plane_gather(local, collective_id):
    members = 8
    return pl.pallas_call(
        gather_kernel,
        out_shape=jax.ShapeDtypeStruct((members, *local.shape), local.dtype),
        in_specs=[pl.BlockSpec(memory_space=pl.ANY)],
        out_specs=pl.BlockSpec(memory_space=pl.ANY),
        scratch_shapes=GATHER_SEMS,
        cost_estimate=busy(25),
        compiler_params=pltpu.CompilerParams(
            collective_id=collective_id, has_side_effects=True, vmem_limit_bytes=VMEM_BYTES
        ),
    )(local)


def gather_rows(local, collective_id):
    rows, columns = local.shape
    out = plane_gather(local.reshape(rows // 16, 16, columns), collective_id)
    return out.reshape(-1, columns)


def add_rows(target, sources, start, count):
    def one(i, carry):
        total = sources[0][i].astype(jnp.float32)
        for source in sources[1:]:
            total = total + source[i].astype(jnp.float32)
        target[i] = total.astype(target.dtype)
        return carry

    lax.fori_loop(start, start + count, one, 0)


def plane_sum(part_ref, own_sum, near, sums, from_x, from_y, far_x, far_y, send_sems, recv_sems):
    sibling, along_x, along_y, member = plane_places()
    rows = own_sum.shape[0]
    half = rows // 2
    top, bottom = pl.ds(0, half), pl.ds(half, half)
    send = sender(send_sems, recv_sems)
    chips = ((1, 1), (1, 0), (0, 1), (0, 0))
    mine = [part_ref.at[member(at_x, 0, at_y)] for at_x, at_y in chips]
    to_sibling = [
        send(k, part_ref.at[member(at_x, 1, at_y)], near.at[k], sibling)
        for k, (at_x, at_y) in enumerate(chips)
    ]
    to_sibling[0].wait_recv()
    add_rows(sums.at[0], (mine[0], near.at[0]), 0, rows)
    diagonal_x = send(4, sums.at[0, bottom], far_x.at[bottom], along_x)
    diagonal_y = send(5, sums.at[0, top], far_y.at[top], along_y)
    to_sibling[1].wait_recv()
    add_rows(sums.at[1], (mine[1], near.at[1]), half, half)
    direct_x = send(6, sums.at[1, bottom], from_x.at[bottom], along_x)
    to_sibling[2].wait_recv()
    add_rows(sums.at[2], (mine[2], near.at[2]), 0, half)
    direct_y = send(7, sums.at[2, top], from_y.at[top], along_y)
    to_sibling[3].wait_recv()
    diagonal_y.wait_recv()
    add_rows(sums.at[1], (mine[1], near.at[1], far_y), 0, half)
    joint_x = send(8, sums.at[1, top], from_x.at[top], along_x)
    diagonal_x.wait_recv()
    add_rows(sums.at[2], (mine[2], near.at[2], far_x), half, half)
    joint_y = send(9, sums.at[2, bottom], from_y.at[bottom], along_y)
    direct_x.wait_recv()
    direct_y.wait_recv()
    joint_x.wait_recv()
    joint_y.wait_recv()
    add_rows(own_sum, (mine[3], near.at[3], from_x, from_y), 0, rows)
    for copy in (*to_sibling, diagonal_x, diagonal_y, direct_x, direct_y, joint_x, joint_y):
        copy.wait_send()


def plane_sum_kernel(part_ref, out_ref, *scratch):
    sibling, along_x, along_y, _ = plane_places()
    greet((sibling, along_x, along_y))
    plane_sum(part_ref, out_ref, *scratch)


def plane_sum_scratch(shape, dtype):
    block = pltpu.VMEM(shape, dtype)
    return [
        pltpu.VMEM((4, *shape), dtype),
        pltpu.VMEM((3, *shape), dtype),
        block,
        block,
        block,
        block,
        pltpu.SemaphoreType.DMA((10,)),
        pltpu.SemaphoreType.DMA((10,)),
    ]


def plane_scatter_sum(partial, collective_id):
    members = 8
    rows, columns = partial.shape[0] // members, partial.shape[1]
    shape = (rows // 16, 16, columns)
    out = pl.pallas_call(
        plane_sum_kernel,
        out_shape=jax.ShapeDtypeStruct(shape, jnp.float32),
        in_specs=[pl.BlockSpec(memory_space=pltpu.VMEM)],
        out_specs=pl.BlockSpec(memory_space=pltpu.VMEM),
        scratch_shapes=plane_sum_scratch(shape, partial.dtype),
        cost_estimate=busy(25),
        compiler_params=pltpu.CompilerParams(
            collective_id=collective_id, has_side_effects=True, vmem_limit_bytes=VMEM_BYTES
        ),
    )(partial.reshape(members, *shape))
    return out.reshape(rows, columns)


def owner_sum_kernel(planes, part_ref, out_ref, own_sum, leaving, arriving, z_send, z_recv, *scratch):
    sibling, along_x, along_y, _ = plane_places()
    z, x, core, seq = (lax.axis_index(name) for name in ALL)
    others = [(lax.rem(z + k, planes), x, core, seq) for k in range(1, planes)]
    greet((sibling, along_x, along_y, *others))
    plane_sum(part_ref, own_sum, *scratch)
    send = sender(z_send, z_recv)

    def narrow(i, carry):
        leaving[i] = own_sum[i].astype(leaving.dtype)
        return carry

    lax.fori_loop(0, planes, narrow, 0)
    copies = [
        send(k, leaving.at[place[0]], arriving.at[k], place) for k, place in enumerate(others)
    ]
    for copy in copies:
        copy.wait_recv()

    value = own_sum[z]
    for k in range(planes - 1):
        value = value + arriving[k].astype(jnp.float32)
    out_ref[...] = value
    for copy in copies:
        copy.wait_send()


def owner_sum(blocks, collective_id):
    members, planes, rows, columns = blocks.shape
    return pl.pallas_call(
        functools.partial(owner_sum_kernel, planes),
        out_shape=jax.ShapeDtypeStruct((rows, columns), jnp.float32),
        in_specs=[pl.BlockSpec(memory_space=pltpu.VMEM)],
        out_specs=pl.BlockSpec(memory_space=pltpu.VMEM),
        scratch_shapes=[
            pltpu.VMEM((planes, rows, columns), jnp.float32),
            pltpu.VMEM((planes, rows, columns), blocks.dtype),
            pltpu.VMEM((planes - 1, rows, columns), blocks.dtype),
            pltpu.SemaphoreType.DMA((planes - 1,)),
            pltpu.SemaphoreType.DMA((planes - 1,)),
            *plane_sum_scratch((planes, rows, columns), blocks.dtype),
        ],
        cost_estimate=busy(35),
        compiler_params=pltpu.CompilerParams(
            collective_id=collective_id, has_side_effects=True, vmem_limit_bytes=VMEM_BYTES
        ),
    )(blocks)


def body(
    tokens,
    segment_ids,
    cotangent,
    query_weight,
    key_weight,
    value_weight,
    output_weight,
    gate_weight,
    up_weight,
    down_weight,
    input_gain,
    query_gain,
    key_gain,
    attnout_gain,
    ffnin_gain,
    ffnout_gain,
):
    bf16, f32 = jnp.bfloat16, jnp.float32
    devices = lax.axis_size(ALL)
    members = lax.axis_size(PLANE)
    planes = lax.axis_size("z")
    seq_count = lax.axis_size("seq")
    width_rows = query_weight.shape[0]
    hidden_rows = down_weight.shape[0]
    head_width = key_weight.shape[1]
    query_width = query_weight.shape[1]
    head_count = query_width // head_width
    qkv_width = query_width + 2 * head_width
    mix_rows = output_weight.shape[0]
    padded = (width_rows + 1 + 7) // 8 * 8

    def column_blocks(weight):
        pieces = weight.reshape(width_rows, planes, members, hidden_rows)
        return pieces.transpose(2, 0, 1, 3).reshape(members, width_rows, planes * hidden_rows)

    gate_up = jnp.concatenate([column_blocks(gate_weight), column_blocks(up_weight)], axis=1)
    gate_up = jnp.broadcast_to(gate_up[None], (planes,) + gate_up.shape)
    gate_up = gate_up.reshape((devices,) + gate_up.shape[2:])

    gains = (input_gain, query_gain, key_gain, attnout_gain, ffnin_gain, ffnout_gain)
    gain_row = jnp.concatenate(gains)
    gain_widths = [g.shape[0] for g in gains]
    gain_row = jnp.pad(gain_row, (0, qkv_width - gain_row.shape[0]))
    qkv_local = jnp.concatenate([query_weight, key_weight, value_weight], axis=1)
    packed = jnp.concatenate([qkv_local, gain_row[None]], axis=0)
    packed = jnp.pad(packed, ((0, padded - width_rows - 1), (0, 0)))
    output_wide = jnp.pad(output_weight, ((0, 0), (0, qkv_width - output_weight.shape[1])))
    packed = jnp.concatenate([packed, output_wide], axis=0)
    packed_all = z_gather(packed, planes, 0)
    gate_up, down_local, packed_all = lax.optimization_barrier(
        (gate_up, down_weight, packed_all)
    )
    packed_all = plane_gather(packed_all, 6)
    gate_up = exchange(gate_up, ALL)
    gate_full = gate_up[:, :width_rows].reshape(devices * width_rows, planes * hidden_rows)
    up_full = gate_up[:, width_rows:].reshape(devices * width_rows, planes * hidden_rows)
    down_full = lax.all_gather(down_local, "z", axis=0, tiled=True)
    packed_all = packed_all.transpose(1, 0, 2, 3)
    packed_all = packed_all.reshape(devices, padded + mix_rows, qkv_width)
    qkv_full = packed_all[:, :width_rows].reshape(devices * width_rows, qkv_width)
    output_full = packed_all[:, padded:, : output_weight.shape[1]]
    output_full = output_full.reshape(devices * mix_rows, output_weight.shape[1])
    scales, at = [], 0
    for width in gain_widths:
        scales.append(packed_all[:, width_rows, at : at + width].reshape(-1).astype(f32))
        at += width
    input_scale, query_scale, key_scale, attnout_scale, ffnin_scale, ffnout_scale = scales

    hidden = tokens[0].astype(f32)
    incoming = cotangent[0].astype(f32)
    local_rows = hidden.shape[0]
    full_length = local_rows * seq_count
    offset = lax.axis_index("seq") * local_rows
    segment_row = segment_ids[0]

    def mine(rows):
        return lax.dynamic_slice_in_dim(rows, offset, local_rows)

    my_segments = mine(segment_row)
    cos_full, sin_full = rope_tables(doc_positions(segment_row), head_width)
    cos_table, sin_table = mine(cos_full), mine(sin_full)
    scale = head_width ** (-0.5)

    other_half = [(0, 1), (1, 0)]
    first = lax.axis_index("seq") == 0
    other_tokens = lax.ppermute(tokens[0], "seq", other_half)
    row_hidden = jnp.concatenate(
        [
            jnp.where(first, tokens[0], other_tokens),
            jnp.where(first, other_tokens, tokens[0]),
        ]
    ).astype(f32)
    row_normed = (row_hidden * inverse_rms(row_hidden) * input_scale).astype(bf16)
    key_value_raw = matmul(row_normed, qkv_full[:, query_width:])
    row_key_raw = key_value_raw[:, :head_width]
    value_rows = key_value_raw[:, head_width:].astype(bf16)
    key_rows = rotate(
        row_key_raw * inverse_rms(row_key_raw) * key_scale, cos_full, sin_full
    ).astype(bf16)

    inv_input = inverse_rms(hidden)
    norm_input = hidden * inv_input
    normed = (norm_input * input_scale).astype(bf16)
    query_raw = matmul(normed, qkv_full[:, :query_width]).reshape(
        local_rows, head_count, head_width
    )
    inv_query = inverse_rms(query_raw)
    norm_query = query_raw * inv_query
    queries = (
        rotate(norm_query * query_scale, cos_table[:, None, :], sin_table[:, None, :]) * scale
    ).astype(bf16)
    key_raw = mine(row_key_raw)
    inv_key = inverse_rms(key_raw)
    norm_key = key_raw * inv_key

    query_places = offset + jnp.arange(local_rows, dtype=jnp.int32)
    key_places = jnp.arange(full_length, dtype=jnp.int32)
    allowed = (my_segments[:, None] == segment_row[None, :]) & (
        query_places[:, None] >= key_places[None, :]
    )
    raw_scores = jnp.einsum("qhd,kd->hqk", queries, key_rows, preferred_element_type=f32)
    scores = jnp.where(allowed[None], raw_scores, masked_score)
    peak = jnp.max(scores, axis=-1, keepdims=True)
    log_total = peak + jnp.log(jnp.sum(jnp.exp(scores - peak), axis=-1, keepdims=True))
    probs = jnp.exp(scores - log_total)
    probs_low = probs.astype(bf16)
    attn_mix = jnp.einsum("hqk,kd->qhd", probs_low, value_rows, preferred_element_type=f32)
    attn_flat = attn_mix.astype(bf16).reshape(local_rows, query_width)
    attn_raw = matmul(attn_flat, output_full)
    inv_attn = inverse_rms(attn_raw)
    norm_attn = attn_raw * inv_attn
    middle = hidden + norm_attn * attnout_scale
    inv_middle = inverse_rms(middle)
    norm_middle = middle * inv_middle
    ffn_in = (norm_middle * ffnin_scale).astype(bf16)

    plane_in = gather_rows(ffn_in, 1)
    gate_proj = matmul(plane_in, gate_full)
    up_proj = matmul(plane_in, up_full)
    activated, gelu_back = jax.vjp(gelu_pair, gate_proj, up_proj)
    activated_low = activated.astype(bf16)
    ffn_raw = plane_scatter_sum(matmul(activated_low, down_full).astype(bf16), 2)
    inv_ffn = inverse_rms(ffn_raw)
    norm_ffn = ffn_raw * inv_ffn
    result = middle + norm_ffn * ffnout_scale
    ffnout_gain_grad = jnp.sum(incoming * norm_ffn, axis=0)
    ffn_raw_grad = rms_back(incoming * ffnout_scale, norm_ffn, inv_ffn).astype(bf16)

    plane_grad = gather_rows(ffn_raw_grad, 3)
    act_grad = contract_cols(plane_grad, down_full)
    gate_grad, up_grad = gelu_back(act_grad)
    gate_low = gate_grad.astype(bf16)
    up_low = up_grad.astype(bf16)
    down_blocks = contract_rows(activated_low, plane_grad).reshape(
        planes, hidden_rows, down_weight.shape[1]
    )
    plane = lax.axis_index("z")
    down_wgrad = lax.dynamic_index_in_dim(down_blocks, plane, 0, keepdims=False)
    down_low = down_blocks.astype(bf16)
    for k in range(1, planes):
        leaving = lax.dynamic_index_in_dim(down_low, lax.rem(plane + k, planes), 0, keepdims=False)
        shift = [(i, (i + k) % planes) for i in range(planes)]
        down_wgrad = down_wgrad + lax.ppermute(leaving, "z", shift).astype(f32)

    def row_blocks(grad):
        return grad.astype(bf16).reshape(devices, width_rows, planes * hidden_rows)

    gate_up_blocks = jnp.concatenate(
        [
            row_blocks(contract_rows(plane_in, gate_low)),
            row_blocks(contract_rows(plane_in, up_low)),
        ],
        axis=1,
    )
    ffn_in_part = (contract_cols(gate_low, gate_full) + contract_cols(up_low, up_full)).astype(bf16)
    gate_up_blocks, ffn_in_part = lax.optimization_barrier((gate_up_blocks, ffn_in_part))
    gate_up_terms = exchange(gate_up_blocks, ALL)
    ffn_in_grad = plane_scatter_sum(ffn_in_part, 4)
    ffnin_gain_grad = jnp.sum(ffn_in_grad * norm_middle, axis=0)
    middle_grad = incoming + rms_back(ffn_in_grad * ffnin_scale, norm_middle, inv_middle)
    attnout_gain_grad = jnp.sum(middle_grad * norm_attn, axis=0)
    attn_raw_grad = rms_back(middle_grad * attnout_scale, norm_attn, inv_attn).astype(bf16)
    output_wgrad = contract_rows(attn_flat, attn_raw_grad)
    mix_grad = (
        contract_cols(attn_raw_grad, output_full)
        .astype(bf16)
        .reshape(local_rows, head_count, head_width)
    )
    prob_grad = jnp.einsum("qhd,kd->hqk", mix_grad, value_rows, preferred_element_type=f32)
    row_delta = jnp.sum(prob_grad * probs, axis=-1, keepdims=True)
    score_grad = (probs * (prob_grad - row_delta)).astype(bf16)
    value_grad_rows = jnp.einsum("hqk,qhd->kd", probs_low, mix_grad, preferred_element_type=f32)
    key_grad_rows = jnp.einsum("hqk,qhd->kd", score_grad, queries, preferred_element_type=f32)
    query_grad = jnp.einsum("hqk,kd->qhd", score_grad, key_rows, preferred_element_type=f32)
    key_value_rows = jnp.concatenate([key_grad_rows, value_grad_rows], axis=1)
    theirs = lax.dynamic_slice_in_dim(key_value_rows, local_rows - offset, local_rows)
    key_value_grad = mine(key_value_rows) + lax.ppermute(
        theirs.astype(bf16), "seq", other_half
    ).astype(f32)
    key_grad, value_grad = key_value_grad[:, :head_width], key_value_grad[:, head_width:]
    query_norm_grad = rotate(query_grad * scale, cos_table[:, None, :], -sin_table[:, None, :])
    query_gain_grad = jnp.sum(query_norm_grad * norm_query, axis=(0, 1))
    query_raw_low = (
        rms_back(query_norm_grad * query_scale, norm_query, inv_query)
        .astype(bf16)
        .reshape(local_rows, query_width)
    )
    key_norm_grad = rotate(key_grad, cos_table, -sin_table)
    key_gain_grad = jnp.sum(key_norm_grad * norm_key, axis=0)
    key_raw_low = rms_back(key_norm_grad * key_scale, norm_key, inv_key).astype(bf16)
    qkv_raw_low = jnp.concatenate([query_raw_low, key_raw_low, value_grad.astype(bf16)], axis=1)
    qkv_wgrad = contract_rows(normed, qkv_raw_low)
    normed_grad = contract_cols(qkv_raw_low, qkv_full)
    input_gain_grad = jnp.sum(normed_grad * norm_input, axis=0)
    input_grad = middle_grad + rms_back(normed_grad * input_scale, norm_input, inv_input)

    gain_grads = (
        input_gain_grad,
        query_gain_grad,
        key_gain_grad,
        attnout_gain_grad,
        ffnin_gain_grad,
        ffnout_gain_grad,
    )
    gain_rows = jnp.concatenate([g.reshape(devices, -1) for g in gain_grads], axis=1)
    gain_rows = jnp.pad(gain_rows, ((0, 0), (0, qkv_width - gain_rows.shape[1])))
    blocks = jnp.concatenate(
        [qkv_wgrad.reshape(devices, width_rows, qkv_width), gain_rows[:, None]], axis=1
    )
    blocks = jnp.pad(blocks.astype(bf16), ((0, 0), (0, padded - width_rows - 1), (0, 0)))
    output_blocks = output_wgrad.astype(bf16).reshape(devices, mix_rows, -1)
    output_blocks = jnp.pad(
        output_blocks, ((0, 0), (0, 0), (0, qkv_width - output_blocks.shape[2]))
    )
    blocks = jnp.concatenate([blocks, output_blocks], axis=1)
    blocks = blocks.reshape(planes, members, padded + mix_rows, qkv_width)
    share = owner_sum(blocks.transpose(1, 0, 2, 3), 5)
    gate_up_sum = jnp.sum(
        gate_up_terms.astype(f32).reshape(
            planes, members, 2 * width_rows, planes * hidden_rows
        ),
        axis=0,
    )
    gate_up_sum = gate_up_sum.reshape(members, 2, width_rows, planes, hidden_rows)
    gate_up_sum = gate_up_sum.transpose(1, 2, 3, 0, 4).reshape(
        2, width_rows, planes * members * hidden_rows
    )
    gate_wgrad, up_wgrad = gate_up_sum[0], gate_up_sum[1]

    qkv_share, output_share = share[:padded], share[padded:, : output_weight.shape[1]]
    gain_shares, at = [], 0
    for width in gain_widths:
        gain_shares.append(qkv_share[width_rows, at : at + width])
        at += width
    return (
        result.astype(bf16)[None],
        input_grad[None],
        qkv_share[:width_rows, :query_width],
        qkv_share[:width_rows, query_width : query_width + head_width],
        qkv_share[:width_rows, query_width + head_width :],
        output_share,
        gate_wgrad,
        up_wgrad,
        down_wgrad,
        *gain_shares,
    )


def solution(mesh):
    dp, seq = mesh.shape["dp"], mesh.shape["seq"]
    split = Mesh(mesh.devices.reshape(dp // 4, 2, 2, seq), ALL)
    rows = P(("z", "x", "core"), "seq", None)
    matrix, vector = P(ALL, None), P(ALL)
    return jax.shard_map(
        body,
        mesh=split,
        in_specs=(rows, P(("z", "x", "core"), None), rows) + (matrix,) * 7 + (vector,) * 6,
        out_specs=(rows, rows) + (matrix,) * 7 + (vector,) * 6,
        check_vma=False,
    )
```

```python
import functools

import jax
import jax.numpy as jnp
from jax import lax
from jax.experimental import pallas as pl
from jax.experimental.pallas import tpu as pltpu
from jax.sharding import Mesh
from jax.sharding import PartitionSpec as P

epsilon = 1e-06
rope_base = 1000000.0
masked_score = -1e30


def inverse_rms(values):
    return lax.rsqrt(jnp.mean(values * values, axis=-1, keepdims=True) + epsilon)


def rms_back(grad_normed, normed, inverse):
    return inverse * (grad_normed - normed * jnp.mean(grad_normed * normed, axis=-1, keepdims=True))


def doc_positions(segments):
    length = segments.shape[0]
    smaller = segments[None, :] < segments[:, None]
    starts = jnp.sum(smaller.astype(jnp.int32), axis=1)
    return (jnp.arange(length, dtype=jnp.int32) - starts).astype(jnp.float32)


def rope_tables(positions, head_width):
    half_width = head_width // 2
    frequency = rope_base ** (-(2.0 / head_width) * jnp.arange(half_width, dtype=jnp.float32))
    angles = positions[..., None] * frequency
    return (jnp.cos(angles), jnp.sin(angles))


def rotate(values, cos_table, sin_table):
    half_width = values.shape[-1] // 2
    first_half = values[..., :half_width]
    second_half = values[..., half_width:]
    return jnp.concatenate(
        [
            first_half * cos_table - second_half * sin_table,
            second_half * cos_table + first_half * sin_table,
        ],
        axis=-1,
    )


def matmul(left, right):
    return jnp.dot(left, right, preferred_element_type=jnp.float32)


def contract_rows(left, right):
    return lax.dot_general(
        left, right, (((0,), (0,)), ((), ())), preferred_element_type=jnp.float32
    )


def contract_cols(left, right):
    return lax.dot_general(
        left, right, (((1,), (1,)), ((), ())), preferred_element_type=jnp.float32
    )


def gelu_pair(gate_proj, up_proj):
    return jax.nn.gelu(gate_proj, approximate=True) * up_proj


ALL = ("z", "x", "core", "seq")


def up_to(size, multiple):
    return (size + multiple - 1) // multiple * multiple


def place_columns(blocks, members, planes, rows, padded, by_member):
    source = lax.broadcasted_iota(jnp.int32, (blocks * rows, blocks * padded), 0)
    target = lax.broadcasted_iota(jnp.int32, (blocks * rows, blocks * padded), 1)
    block = source // rows
    if by_member:
        block = block % members * planes + block // members
    return (target == block * padded + source % rows).astype(jnp.bfloat16)


def take_back(padded_values, placing):
    high = lax.reduce_precision(padded_values, 8, 7)
    terms = jnp.concatenate([high, padded_values - high], axis=0).astype(jnp.bfloat16)
    both = contract_cols(terms, placing)
    rows = padded_values.shape[0]
    return both[:rows] + both[rows:]


PLANE = ("x", "core", "seq")

MESH_ID = pl.DeviceIdType.MESH
VMEM_BYTES = 48 * 2**20


def exchange(blocks, axes):
    return lax.all_to_all(blocks, axes, split_axis=0, concat_axis=0, tiled=True)


def busy(microseconds):
    return pl.CostEstimate(flops=0, bytes_accessed=microseconds * 3_000_000, transcendentals=0)


def plane_places():
    z, x, core, seq = (lax.axis_index(name) for name in ALL)
    sibling = (z, x, 1 - core, seq)
    along_x = (z, 1 - x, core, seq)
    along_y = (z, x, core, 1 - seq)

    def member(other_x, other_core, other_y):
        at_x = 1 - x if other_x else x
        at_core = 1 - core if other_core else core
        at_y = 1 - seq if other_y else seq
        return (at_x * 2 + at_core) * 2 + at_y

    return sibling, along_x, along_y, member


def greet(places):
    barrier = pltpu.get_barrier_semaphore()
    for place in places:
        pl.semaphore_signal(barrier, inc=1, device_id=place, device_id_type=MESH_ID)
    pl.semaphore_wait(barrier, len(places))


def sender(send_sems, recv_sems):
    def send(kind, source, target, place):
        copy = pltpu.make_async_remote_copy(
            src_ref=source,
            dst_ref=target,
            send_sem=send_sems.at[kind],
            recv_sem=recv_sems.at[kind],
            device_id=place,
            device_id_type=MESH_ID,
        )
        copy.start()
        return copy

    return send


def plane_spread(own_ref, out_ref, send_sems, recv_sems, local_sem):
    sibling, along_x, along_y, member = plane_places()
    half = own_ref.shape[0] // 2
    top, bottom = pl.ds(0, half), pl.ds(half, half)
    me = member(0, 0, 0)
    keep = pltpu.make_async_copy(own_ref, out_ref.at[me], local_sem)
    keep.start()
    send = sender(send_sems, recv_sems)

    def forward(kind, block, rows, place):
        return send(kind, out_ref.at[block, rows], out_ref.at[block, rows], place)

    own_x_top = send(1, own_ref.at[top], out_ref.at[me, top], along_x)
    own_y_bottom = send(3, own_ref.at[bottom], out_ref.at[me, bottom], along_y)
    own_sibling = send(0, own_ref, out_ref.at[me], sibling)
    own_x_bottom = send(2, own_ref.at[bottom], out_ref.at[me, bottom], along_x)
    own_y_top = send(4, own_ref.at[top], out_ref.at[me, top], along_y)
    x_block, y_block, diagonal = member(1, 0, 0), member(0, 0, 1), member(1, 0, 1)
    own_x_top.wait_recv()
    diagonal_top = forward(5, x_block, top, along_y)
    x_top = forward(7, x_block, top, sibling)
    own_y_bottom.wait_recv()
    diagonal_bottom = forward(6, y_block, bottom, along_x)
    y_bottom = forward(9, y_block, bottom, sibling)
    own_x_bottom.wait_recv()
    x_bottom = forward(8, x_block, bottom, sibling)
    own_y_top.wait_recv()
    y_top = forward(10, y_block, top, sibling)
    diagonal_top.wait_recv()
    far_top = forward(11, diagonal, top, sibling)
    diagonal_bottom.wait_recv()
    far_bottom = forward(12, diagonal, bottom, sibling)
    for copy in (own_sibling, x_top, y_bottom, x_bottom, y_top, far_top, far_bottom):
        copy.wait_recv()
    for copy in (
        own_x_top,
        own_y_bottom,
        own_sibling,
        own_x_bottom,
        own_y_top,
        diagonal_top,
        diagonal_bottom,
        x_top,
        y_bottom,
        x_bottom,
        y_top,
        far_top,
        far_bottom,
    ):
        copy.wait_send()
    keep.wait()


def gather_kernel(own_ref, out_ref, *sems):
    greet(plane_places()[:3])
    plane_spread(own_ref, out_ref, *sems)


def z_gather_kernel(planes, own_ref, out_ref, send_sems, recv_sems, own_sem):
    z, x, core, seq = (lax.axis_index(name) for name in ALL)
    others = [(lax.rem(z + k, planes), x, core, seq) for k in range(1, planes)]
    greet(others)
    keep = pltpu.make_async_copy(own_ref, out_ref.at[z], own_sem)
    keep.start()
    send = sender(send_sems, recv_sems)
    copies = [send(k, own_ref, out_ref.at[z], place) for k, place in enumerate(others)]
    for copy in copies:
        copy.wait_recv()
    for copy in copies:
        copy.wait_send()
    keep.wait()


GATHER_SEMS = [
    pltpu.SemaphoreType.DMA((13,)),
    pltpu.SemaphoreType.DMA((13,)),
    pltpu.SemaphoreType.DMA,
]


def z_gather(local, planes, collective_id):
    return pl.pallas_call(
        functools.partial(z_gather_kernel, planes),
        out_shape=jax.ShapeDtypeStruct((planes, *local.shape), local.dtype),
        in_specs=[pl.BlockSpec(memory_space=pltpu.VMEM)],
        out_specs=pl.BlockSpec(memory_space=pl.ANY),
        scratch_shapes=[
            pltpu.SemaphoreType.DMA((planes - 1,)),
            pltpu.SemaphoreType.DMA((planes - 1,)),
            pltpu.SemaphoreType.DMA,
        ],
        cost_estimate=busy(20),
        compiler_params=pltpu.CompilerParams(
            collective_id=collective_id, has_side_effects=True, vmem_limit_bytes=VMEM_BYTES
        ),
    )(local)


def plane_gather(local, collective_id):
    members = 8
    return pl.pallas_call(
        gather_kernel,
        out_shape=jax.ShapeDtypeStruct((members, *local.shape), local.dtype),
        in_specs=[pl.BlockSpec(memory_space=pl.ANY)],
        out_specs=pl.BlockSpec(memory_space=pl.ANY),
        scratch_shapes=GATHER_SEMS,
        cost_estimate=busy(25),
        compiler_params=pltpu.CompilerParams(
            collective_id=collective_id, has_side_effects=True, vmem_limit_bytes=VMEM_BYTES
        ),
    )(local)


def gather_rows(local, collective_id):
    rows, columns = local.shape
    out = plane_gather(local.reshape(rows // 16, 16, columns), collective_id)
    return out.reshape(-1, columns)


def add_rows(target, sources, start, count):
    def one(i, carry):
        total = sources[0][i].astype(jnp.float32)
        for source in sources[1:]:
            total = total + source[i].astype(jnp.float32)
        target[i] = total.astype(target.dtype)
        return carry

    lax.fori_loop(start, start + count, one, 0)


def plane_sum(part_ref, own_sum, near, sums, from_x, from_y, far_x, far_y, send_sems, recv_sems):
    sibling, along_x, along_y, member = plane_places()
    rows = own_sum.shape[0]
    half = rows // 2
    top, bottom = pl.ds(0, half), pl.ds(half, half)
    send = sender(send_sems, recv_sems)
    chips = ((1, 1), (1, 0), (0, 1), (0, 0))
    mine = [part_ref.at[member(at_x, 0, at_y)] for at_x, at_y in chips]
    to_sibling = [
        send(k, part_ref.at[member(at_x, 1, at_y)], near.at[k], sibling)
        for k, (at_x, at_y) in enumerate(chips)
    ]
    to_sibling[0].wait_recv()
    add_rows(sums.at[0], (mine[0], near.at[0]), 0, rows)
    diagonal_x = send(4, sums.at[0, bottom], far_x.at[bottom], along_x)
    diagonal_y = send(5, sums.at[0, top], far_y.at[top], along_y)
    to_sibling[1].wait_recv()
    add_rows(sums.at[1], (mine[1], near.at[1]), half, half)
    direct_x = send(6, sums.at[1, bottom], from_x.at[bottom], along_x)
    to_sibling[2].wait_recv()
    add_rows(sums.at[2], (mine[2], near.at[2]), 0, half)
    direct_y = send(7, sums.at[2, top], from_y.at[top], along_y)
    to_sibling[3].wait_recv()
    diagonal_y.wait_recv()
    add_rows(sums.at[1], (mine[1], near.at[1], far_y), 0, half)
    joint_x = send(8, sums.at[1, top], from_x.at[top], along_x)
    diagonal_x.wait_recv()
    add_rows(sums.at[2], (mine[2], near.at[2], far_x), half, half)
    joint_y = send(9, sums.at[2, bottom], from_y.at[bottom], along_y)
    direct_x.wait_recv()
    direct_y.wait_recv()
    joint_x.wait_recv()
    joint_y.wait_recv()
    add_rows(own_sum, (mine[3], near.at[3], from_x, from_y), 0, rows)
    for copy in (*to_sibling, diagonal_x, diagonal_y, direct_x, direct_y, joint_x, joint_y):
        copy.wait_send()


def plane_sum_kernel(part_ref, out_ref, *scratch):
    sibling, along_x, along_y, _ = plane_places()
    greet((sibling, along_x, along_y))
    plane_sum(part_ref, out_ref, *scratch)


def plane_sum_scratch(shape, dtype):
    block = pltpu.VMEM(shape, dtype)
    return [
        pltpu.VMEM((4, *shape), dtype),
        pltpu.VMEM((3, *shape), dtype),
        block,
        block,
        block,
        block,
        pltpu.SemaphoreType.DMA((10,)),
        pltpu.SemaphoreType.DMA((10,)),
    ]


def plane_scatter_sum(partial, collective_id):
    members = 8
    rows, columns = partial.shape[0] // members, partial.shape[1]
    shape = (rows // 16, 16, columns)
    out = pl.pallas_call(
        plane_sum_kernel,
        out_shape=jax.ShapeDtypeStruct(shape, jnp.float32),
        in_specs=[pl.BlockSpec(memory_space=pltpu.VMEM)],
        out_specs=pl.BlockSpec(memory_space=pltpu.VMEM),
        scratch_shapes=plane_sum_scratch(shape, partial.dtype),
        cost_estimate=busy(25),
        compiler_params=pltpu.CompilerParams(
            collective_id=collective_id, has_side_effects=True, vmem_limit_bytes=VMEM_BYTES
        ),
    )(partial.reshape(members, *shape))
    return out.reshape(rows, columns)


def owner_sum_kernel(planes, part_ref, out_ref, own_sum, leaving, arriving, z_send, z_recv, *scratch):
    sibling, along_x, along_y, _ = plane_places()
    z, x, core, seq = (lax.axis_index(name) for name in ALL)
    others = [(lax.rem(z + k, planes), x, core, seq) for k in range(1, planes)]
    greet((sibling, along_x, along_y, *others))
    plane_sum(part_ref, own_sum, *scratch)
    send = sender(z_send, z_recv)

    def narrow(i, carry):
        leaving[i] = own_sum[i].astype(leaving.dtype)
        return carry

    lax.fori_loop(0, planes, narrow, 0)
    copies = [
        send(k, leaving.at[place[0]], arriving.at[k], place) for k, place in enumerate(others)
    ]
    for copy in copies:
        copy.wait_recv()

    value = own_sum[z]
    for k in range(planes - 1):
        value = value + arriving[k].astype(jnp.float32)
    out_ref[...] = value
    for copy in copies:
        copy.wait_send()


def owner_sum(blocks, collective_id):
    members, planes, rows, columns = blocks.shape
    return pl.pallas_call(
        functools.partial(owner_sum_kernel, planes),
        out_shape=jax.ShapeDtypeStruct((rows, columns), jnp.float32),
        in_specs=[pl.BlockSpec(memory_space=pltpu.VMEM)],
        out_specs=pl.BlockSpec(memory_space=pltpu.VMEM),
        scratch_shapes=[
            pltpu.VMEM((planes, rows, columns), jnp.float32),
            pltpu.VMEM((planes, rows, columns), blocks.dtype),
            pltpu.VMEM((planes - 1, rows, columns), blocks.dtype),
            pltpu.SemaphoreType.DMA((planes - 1,)),
            pltpu.SemaphoreType.DMA((planes - 1,)),
            *plane_sum_scratch((planes, rows, columns), blocks.dtype),
        ],
        cost_estimate=busy(35),
        compiler_params=pltpu.CompilerParams(
            collective_id=collective_id, has_side_effects=True, vmem_limit_bytes=VMEM_BYTES
        ),
    )(blocks)


def body(
    tokens,
    segment_ids,
    cotangent,
    query_weight,
    key_weight,
    value_weight,
    output_weight,
    gate_weight,
    up_weight,
    down_weight,
    input_gain,
    query_gain,
    key_gain,
    attnout_gain,
    ffnin_gain,
    ffnout_gain,
):
    bf16, f32 = jnp.bfloat16, jnp.float32
    devices = lax.axis_size(ALL)
    members = lax.axis_size(PLANE)
    planes = lax.axis_size("z")
    seq_count = lax.axis_size("seq")
    width_rows = query_weight.shape[0]
    hidden_rows = down_weight.shape[0]
    head_width = key_weight.shape[1]
    query_width = query_weight.shape[1]
    head_count = query_width // head_width
    qkv_width = query_width + 2 * head_width
    mix_rows = output_weight.shape[0]
    padded = up_to(width_rows + 1, 8)
    width = devices * width_rows
    unit_count = planes * hidden_rows
    unit_pad = up_to(unit_count, 128)
    by_device = place_columns(devices, members, planes, width_rows, padded, False)
    by_member = place_columns(devices, members, planes, width_rows, padded, True)

    def column_blocks(weight):
        pieces = weight.reshape(width_rows, planes, members, hidden_rows)
        pieces = pieces.transpose(2, 0, 1, 3).reshape(members, width_rows, unit_count)
        return jnp.pad(
            pieces, ((0, 0), (0, padded - width_rows), (0, unit_pad - unit_count))
        )

    gate_up = jnp.concatenate([column_blocks(gate_weight), column_blocks(up_weight)], axis=2)
    gate_up = jnp.broadcast_to(gate_up[None], (planes,) + gate_up.shape)
    gate_up = gate_up.reshape((devices,) + gate_up.shape[2:])

    gains = (input_gain, query_gain, key_gain, attnout_gain, ffnin_gain, ffnout_gain)
    gain_row = jnp.concatenate(gains)
    gain_widths = [g.shape[0] for g in gains]
    gain_row = jnp.pad(gain_row, (0, qkv_width - gain_row.shape[0]))
    qkv_local = jnp.concatenate([query_weight, key_weight, value_weight], axis=1)
    packed = jnp.concatenate([qkv_local, gain_row[None]], axis=0)
    packed = jnp.pad(packed, ((0, padded - width_rows - 1), (0, 0)))
    output_wide = jnp.pad(output_weight, ((0, 0), (0, qkv_width - output_weight.shape[1])))
    packed = jnp.concatenate([packed, output_wide], axis=0)
    packed_all = z_gather(packed, planes, 0)
    gate_up, down_local, packed_all = lax.optimization_barrier(
        (gate_up, down_weight, packed_all)
    )
    packed_all = plane_gather(packed_all, 6)
    gate_up_full = exchange(gate_up, ALL).reshape(devices * padded, 2 * unit_pad)
    down_full = lax.all_gather(down_local, "z", axis=0, tiled=True)
    qkv_full = packed_all[:, :, :padded].reshape(devices * padded, qkv_width)
    output_full = packed_all[:, :, padded:, : output_weight.shape[1]].transpose(1, 0, 2, 3)
    output_full = output_full.reshape(devices * mix_rows, output_weight.shape[1])
    gain_rows = packed_all[:, :, width_rows, :].astype(f32)
    scales, at = [], 0
    for count in gain_widths:
        scales.append(gain_rows[:, :, at : at + count].transpose(1, 0, 2).reshape(-1))
        at += count
    padded_input_scale = jnp.pad(
        gain_rows[:, :, :width_rows], ((0, 0), (0, 0), (0, padded - width_rows))
    ).reshape(-1)
    _, query_scale, key_scale, attnout_scale, ffnin_scale, ffnout_scale = scales

    hidden = tokens[0].astype(f32)
    incoming = cotangent[0].astype(f32)
    local_rows = hidden.shape[0]
    full_length = local_rows * seq_count
    offset = lax.axis_index("seq") * local_rows
    segment_row = segment_ids[0]

    def mine(rows):
        return lax.dynamic_slice_in_dim(rows, offset, local_rows)

    my_segments = mine(segment_row)
    cos_full, sin_full = rope_tables(doc_positions(segment_row), head_width)
    cos_table, sin_table = mine(cos_full), mine(sin_full)
    scale = head_width ** (-0.5)

    other_half = [(0, 1), (1, 0)]
    first = lax.axis_index("seq") == 0
    other_tokens = lax.ppermute(tokens[0], "seq", other_half)
    row_tokens = jnp.concatenate(
        [
            jnp.where(first, tokens[0], other_tokens),
            jnp.where(first, other_tokens, tokens[0]),
        ]
    )
    row_hidden = matmul(row_tokens, by_member)
    row_inverse = lax.rsqrt(jnp.sum(row_hidden * row_hidden, axis=-1, keepdims=True) / width + epsilon)
    row_norm = row_hidden * row_inverse
    row_normed = (row_norm * padded_input_scale).astype(bf16)
    key_value_raw = matmul(row_normed, qkv_full[:, query_width:])
    row_key_raw = key_value_raw[:, :head_width]
    value_rows = key_value_raw[:, head_width:].astype(bf16)
    key_rows = rotate(
        row_key_raw * inverse_rms(row_key_raw) * key_scale, cos_full, sin_full
    ).astype(bf16)

    inv_input = mine(row_inverse)
    norm_input = mine(row_norm)
    normed = mine(row_normed)
    query_raw = matmul(normed, qkv_full[:, :query_width]).reshape(
        local_rows, head_count, head_width
    )
    inv_query = inverse_rms(query_raw)
    norm_query = query_raw * inv_query
    queries = (
        rotate(norm_query * query_scale, cos_table[:, None, :], sin_table[:, None, :]) * scale
    ).astype(bf16)
    key_raw = mine(row_key_raw)
    inv_key = inverse_rms(key_raw)
    norm_key = key_raw * inv_key

    query_places = offset + jnp.arange(local_rows, dtype=jnp.int32)
    key_places = jnp.arange(full_length, dtype=jnp.int32)
    allowed = (my_segments[:, None] == segment_row[None, :]) & (
        query_places[:, None] >= key_places[None, :]
    )
    raw_scores = jnp.einsum("qhd,kd->hqk", queries, key_rows, preferred_element_type=f32)
    scores = jnp.where(allowed[None], raw_scores, masked_score)
    peak = jnp.max(scores, axis=-1, keepdims=True)
    log_total = peak + jnp.log(jnp.sum(jnp.exp(scores - peak), axis=-1, keepdims=True))
    probs = jnp.exp(scores - log_total)
    probs_low = probs.astype(bf16)
    attn_mix = jnp.einsum("hqk,kd->qhd", probs_low, value_rows, preferred_element_type=f32)
    attn_flat = attn_mix.astype(bf16).reshape(local_rows, query_width)
    attn_raw = matmul(attn_flat, output_full)
    inv_attn = inverse_rms(attn_raw)
    norm_attn = attn_raw * inv_attn
    middle = hidden + norm_attn * attnout_scale
    inv_middle = inverse_rms(middle)
    norm_middle = middle * inv_middle
    ffn_in = (norm_middle * ffnin_scale).astype(bf16)

    plane_in = gather_rows(matmul(ffn_in, by_device).astype(bf16), 1)
    gate_up_proj = matmul(plane_in, gate_up_full)
    activated, gelu_back = jax.vjp(
        lambda proj: gelu_pair(proj[:, :unit_pad], proj[:, unit_pad:]), gate_up_proj
    )
    activated_low = activated.astype(bf16)
    ffn_raw = plane_scatter_sum(matmul(activated_low[:, :unit_count], down_full).astype(bf16), 2)
    inv_ffn = inverse_rms(ffn_raw)
    norm_ffn = ffn_raw * inv_ffn
    result = middle + norm_ffn * ffnout_scale
    ffnout_gain_grad = jnp.sum(incoming * norm_ffn, axis=0)
    ffn_raw_grad = rms_back(incoming * ffnout_scale, norm_ffn, inv_ffn).astype(bf16)

    plane_grad = gather_rows(ffn_raw_grad, 3)
    act_grad = contract_cols(plane_grad, down_full)
    act_grad = jnp.pad(act_grad, ((0, 0), (0, unit_pad - unit_count)))
    gate_up_low = gelu_back(act_grad)[0].astype(bf16)
    down_blocks = contract_rows(activated_low[:, :unit_count], plane_grad).reshape(
        planes, hidden_rows, down_weight.shape[1]
    )
    plane = lax.axis_index("z")
    down_wgrad = lax.dynamic_index_in_dim(down_blocks, plane, 0, keepdims=False)
    down_low = down_blocks.astype(bf16)
    for k in range(1, planes):
        leaving = lax.dynamic_index_in_dim(down_low, lax.rem(plane + k, planes), 0, keepdims=False)
        shift = [(i, (i + k) % planes) for i in range(planes)]
        down_wgrad = down_wgrad + lax.ppermute(leaving, "z", shift).astype(f32)

    gate_up_blocks = contract_rows(plane_in, gate_up_low).astype(bf16)
    gate_up_blocks = gate_up_blocks.reshape(devices, padded, 2 * unit_pad)
    ffn_in_part = contract_cols(gate_up_low, gate_up_full).astype(bf16)
    gate_up_blocks, ffn_in_part = lax.optimization_barrier((gate_up_blocks, ffn_in_part))
    gate_up_terms = exchange(gate_up_blocks, ALL)
    ffn_in_grad = take_back(plane_scatter_sum(ffn_in_part, 4), by_device)
    ffnin_gain_grad = jnp.sum(ffn_in_grad * norm_middle, axis=0)
    middle_grad = incoming + rms_back(ffn_in_grad * ffnin_scale, norm_middle, inv_middle)
    attnout_gain_grad = jnp.sum(middle_grad * norm_attn, axis=0)
    attn_raw_grad = rms_back(middle_grad * attnout_scale, norm_attn, inv_attn).astype(bf16)
    output_wgrad = contract_rows(attn_flat, attn_raw_grad)
    mix_grad = (
        contract_cols(attn_raw_grad, output_full)
        .astype(bf16)
        .reshape(local_rows, head_count, head_width)
    )
    prob_grad = jnp.einsum("qhd,kd->hqk", mix_grad, value_rows, preferred_element_type=f32)
    row_delta = jnp.sum(prob_grad * probs, axis=-1, keepdims=True)
    score_grad = (probs * (prob_grad - row_delta)).astype(bf16)
    value_grad_rows = jnp.einsum("hqk,qhd->kd", probs_low, mix_grad, preferred_element_type=f32)
    key_grad_rows = jnp.einsum("hqk,qhd->kd", score_grad, queries, preferred_element_type=f32)
    query_grad = jnp.einsum("hqk,kd->qhd", score_grad, key_rows, preferred_element_type=f32)
    key_value_rows = jnp.concatenate([key_grad_rows, value_grad_rows], axis=1)
    theirs = lax.dynamic_slice_in_dim(key_value_rows, local_rows - offset, local_rows)
    key_value_grad = mine(key_value_rows) + lax.ppermute(
        theirs.astype(bf16), "seq", other_half
    ).astype(f32)
    key_grad, value_grad = key_value_grad[:, :head_width], key_value_grad[:, head_width:]
    query_norm_grad = rotate(query_grad * scale, cos_table[:, None, :], -sin_table[:, None, :])
    query_gain_grad = jnp.sum(query_norm_grad * norm_query, axis=(0, 1))
    query_raw_low = (
        rms_back(query_norm_grad * query_scale, norm_query, inv_query)
        .astype(bf16)
        .reshape(local_rows, query_width)
    )
    key_norm_grad = rotate(key_grad, cos_table, -sin_table)
    key_gain_grad = jnp.sum(key_norm_grad * norm_key, axis=0)
    key_raw_low = rms_back(key_norm_grad * key_scale, norm_key, inv_key).astype(bf16)
    qkv_raw_low = jnp.concatenate([query_raw_low, key_raw_low, value_grad.astype(bf16)], axis=1)
    qkv_wgrad = contract_rows(normed, qkv_raw_low)
    normed_grad = contract_cols(qkv_raw_low, qkv_full)
    input_gain_grad = jnp.sum(normed_grad * norm_input, axis=0)
    scaled_grad = normed_grad * padded_input_scale
    inner = jnp.sum(scaled_grad * norm_input, axis=-1, keepdims=True) / width
    input_grad = middle_grad + take_back(inv_input * (scaled_grad - norm_input * inner), by_member)

    gain_grads = (
        query_gain_grad,
        key_gain_grad,
        attnout_gain_grad,
        ffnin_gain_grad,
        ffnout_gain_grad,
    )
    gain_rows = jnp.concatenate(
        [input_gain_grad.reshape(members, planes, padded)[:, :, :width_rows]]
        + [g.reshape(planes, members, -1).transpose(1, 0, 2) for g in gain_grads],
        axis=2,
    )
    gain_rows = jnp.pad(gain_rows, ((0, 0), (0, 0), (0, qkv_width - gain_rows.shape[2])))
    blocks = qkv_wgrad.reshape(members, planes, padded, qkv_width)
    row = lax.broadcasted_iota(jnp.int32, blocks.shape, 2)
    blocks = jnp.where(row == width_rows, gain_rows[:, :, None], blocks).astype(bf16)
    output_blocks = output_wgrad.astype(bf16).reshape(planes, members, mix_rows, -1)
    output_blocks = jnp.pad(
        output_blocks.transpose(1, 0, 2, 3),
        ((0, 0), (0, 0), (0, 0), (0, qkv_width - output_blocks.shape[3])),
    )
    share = owner_sum(jnp.concatenate([blocks, output_blocks], axis=2), 5)
    gate_up_sum = jnp.sum(
        gate_up_terms.reshape(planes, members, padded, 2 * unit_pad).astype(f32), axis=0
    )

    def unit_columns(total):
        total = total[:, :width_rows, :unit_count].reshape(
            members, width_rows, planes, hidden_rows
        )
        return total.transpose(1, 2, 0, 3).reshape(width_rows, planes * members * hidden_rows)

    gate_wgrad = unit_columns(gate_up_sum[:, :, :unit_pad])
    up_wgrad = unit_columns(gate_up_sum[:, :, unit_pad:])
    qkv_share, output_share = share[:padded], share[padded:, : output_weight.shape[1]]
    gain_shares, at = [], 0
    for count in gain_widths:
        gain_shares.append(qkv_share[width_rows, at : at + count])
        at += count
    return (
        result.astype(bf16)[None],
        input_grad[None],
        qkv_share[:width_rows, :query_width],
        qkv_share[:width_rows, query_width : query_width + head_width],
        qkv_share[:width_rows, query_width + head_width :],
        output_share,
        gate_wgrad,
        up_wgrad,
        down_wgrad,
        *gain_shares,
    )


def solution(mesh):
    dp, seq = mesh.shape["dp"], mesh.shape["seq"]
    split = Mesh(mesh.devices.reshape(dp // 4, 2, 2, seq), ALL)
    rows = P(("z", "x", "core"), "seq", None)
    matrix, vector = P(ALL, None), P(ALL)
    return jax.shard_map(
        body,
        mesh=split,
        in_specs=(rows, P(("z", "x", "core"), None), rows) + (matrix,) * 7 + (vector,) * 6,
        out_specs=(rows, rows) + (matrix,) * 7 + (vector,) * 6,
        check_vma=False,
    )
```

```python
import functools

import jax
import jax.numpy as jnp
from jax import lax
from jax.experimental import pallas as pl
from jax.experimental.pallas import tpu as pltpu
from jax.sharding import Mesh
from jax.sharding import PartitionSpec as P

epsilon = 1e-06
rope_base = 1000000.0
masked_score = -1e30


def inverse_rms(values):
    return lax.rsqrt(jnp.mean(values * values, axis=-1, keepdims=True) + epsilon)


def rms_back(grad_normed, normed, inverse):
    return inverse * (grad_normed - normed * jnp.mean(grad_normed * normed, axis=-1, keepdims=True))


def doc_positions(segments):
    length = segments.shape[0]
    smaller = segments[None, :] < segments[:, None]
    starts = jnp.sum(smaller.astype(jnp.int32), axis=1)
    return (jnp.arange(length, dtype=jnp.int32) - starts).astype(jnp.float32)


def rope_tables(positions, head_width):
    half_width = head_width // 2
    frequency = rope_base ** (-(2.0 / head_width) * jnp.arange(half_width, dtype=jnp.float32))
    angles = positions[..., None] * frequency
    return (jnp.cos(angles), jnp.sin(angles))


def rotate(values, cos_table, sin_table):
    half_width = values.shape[-1] // 2
    first_half = values[..., :half_width]
    second_half = values[..., half_width:]
    return jnp.concatenate(
        [
            first_half * cos_table - second_half * sin_table,
            second_half * cos_table + first_half * sin_table,
        ],
        axis=-1,
    )


def matmul(left, right):
    return jnp.dot(left, right, preferred_element_type=jnp.float32)


def contract_rows(left, right):
    return lax.dot_general(
        left, right, (((0,), (0,)), ((), ())), preferred_element_type=jnp.float32
    )


def contract_cols(left, right):
    return lax.dot_general(
        left, right, (((1,), (1,)), ((), ())), preferred_element_type=jnp.float32
    )


ALL = ("z", "x", "core", "seq")


def up_to(size, multiple):
    return (size + multiple - 1) // multiple * multiple


def place_columns(blocks, members, planes, rows, padded, by_member):
    source = lax.broadcasted_iota(jnp.int32, (blocks * rows, blocks * padded), 0)
    target = lax.broadcasted_iota(jnp.int32, (blocks * rows, blocks * padded), 1)
    block = source // rows
    if by_member:
        block = block % members * planes + block // members
    return (target == block * padded + source % rows).astype(jnp.bfloat16)


def take_back(padded_values, placing):
    high = lax.reduce_precision(padded_values, 8, 7)
    terms = jnp.concatenate([high, padded_values - high], axis=0).astype(jnp.bfloat16)
    both = contract_cols(terms, placing)
    rows = padded_values.shape[0]
    return both[:rows] + both[rows:]


PLANE = ("x", "core", "seq")

MESH_ID = pl.DeviceIdType.MESH
VMEM_BYTES = 48 * 2**20


def exchange(blocks, axes):
    return lax.all_to_all(blocks, axes, split_axis=0, concat_axis=0, tiled=True)


def busy(microseconds):
    return pl.CostEstimate(flops=0, bytes_accessed=microseconds * 3_000_000, transcendentals=0)


def plane_places():
    z, x, core, seq = (lax.axis_index(name) for name in ALL)
    sibling = (z, x, 1 - core, seq)
    along_x = (z, 1 - x, core, seq)
    along_y = (z, x, core, 1 - seq)

    def member(other_x, other_core, other_y):
        at_x = 1 - x if other_x else x
        at_core = 1 - core if other_core else core
        at_y = 1 - seq if other_y else seq
        return (at_x * 2 + at_core) * 2 + at_y

    return sibling, along_x, along_y, member


def greet(places):
    barrier = pltpu.get_barrier_semaphore()
    for place in places:
        pl.semaphore_signal(barrier, inc=1, device_id=place, device_id_type=MESH_ID)
    pl.semaphore_wait(barrier, len(places))


def sender(send_sems, recv_sems):
    def send(kind, source, target, place):
        copy = pltpu.make_async_remote_copy(
            src_ref=source,
            dst_ref=target,
            send_sem=send_sems.at[kind],
            recv_sem=recv_sems.at[kind],
            device_id=place,
            device_id_type=MESH_ID,
        )
        copy.start()
        return copy

    return send


def plane_spread(own_ref, out_ref, send_sems, recv_sems, local_sem, compute=lambda i: None):
    sibling, along_x, along_y, member = plane_places()
    half = own_ref.shape[0] // 2
    top, bottom = pl.ds(0, half), pl.ds(half, half)
    me = member(0, 0, 0)
    keep = pltpu.make_async_copy(own_ref, out_ref.at[me], local_sem)
    keep.start()
    send = sender(send_sems, recv_sems)

    def forward(kind, block, rows, place):
        return send(kind, out_ref.at[block, rows], out_ref.at[block, rows], place)

    own_x_top = send(1, own_ref.at[top], out_ref.at[me, top], along_x)
    own_y_bottom = send(3, own_ref.at[bottom], out_ref.at[me, bottom], along_y)
    own_sibling = send(0, own_ref, out_ref.at[me], sibling)
    own_x_bottom = send(2, own_ref.at[bottom], out_ref.at[me, bottom], along_x)
    own_y_top = send(4, own_ref.at[top], out_ref.at[me, top], along_y)
    x_block, y_block, diagonal = member(1, 0, 0), member(0, 0, 1), member(1, 0, 1)
    compute(0)
    own_x_top.wait_recv()
    diagonal_top = forward(5, x_block, top, along_y)
    x_top = forward(7, x_block, top, sibling)
    own_y_bottom.wait_recv()
    diagonal_bottom = forward(6, y_block, bottom, along_x)
    y_bottom = forward(9, y_block, bottom, sibling)
    own_sibling.wait_recv()
    compute(1)
    own_x_bottom.wait_recv()
    x_bottom = forward(8, x_block, bottom, sibling)
    own_y_top.wait_recv()
    y_top = forward(10, y_block, top, sibling)
    compute(2)
    diagonal_top.wait_recv()
    far_top = forward(11, diagonal, top, sibling)
    diagonal_bottom.wait_recv()
    far_bottom = forward(12, diagonal, bottom, sibling)
    compute(3)
    compute(4)
    for i, copies in ((5, (x_top, x_bottom)), (6, (y_bottom, y_top)), (7, (far_top, far_bottom))):
        for copy in copies:
            copy.wait_recv()
        compute(i)
    for copy in (
        own_x_top,
        own_y_bottom,
        own_sibling,
        own_x_bottom,
        own_y_top,
        diagonal_top,
        diagonal_bottom,
        x_top,
        y_bottom,
        x_bottom,
        y_top,
        far_top,
        far_bottom,
    ):
        copy.wait_send()
    keep.wait()


def gather_kernel(own_ref, out_ref, *sems):
    greet(plane_places()[:3])
    plane_spread(own_ref, out_ref, *sems)


def z_gather_kernel(planes, own_ref, out_ref, send_sems, recv_sems, own_sem):
    z, x, core, seq = (lax.axis_index(name) for name in ALL)
    others = [(lax.rem(z + k, planes), x, core, seq) for k in range(1, planes)]
    greet(others)
    keep = pltpu.make_async_copy(own_ref, out_ref.at[z], own_sem)
    keep.start()
    send = sender(send_sems, recv_sems)
    copies = [send(k, own_ref, out_ref.at[z], place) for k, place in enumerate(others)]
    for copy in copies:
        copy.wait_recv()
    for copy in copies:
        copy.wait_send()
    keep.wait()


GATHER_SEMS = [
    pltpu.SemaphoreType.DMA((13,)),
    pltpu.SemaphoreType.DMA((13,)),
    pltpu.SemaphoreType.DMA,
]


def z_gather(local, planes, collective_id):
    return pl.pallas_call(
        functools.partial(z_gather_kernel, planes),
        out_shape=jax.ShapeDtypeStruct((planes, *local.shape), local.dtype),
        in_specs=[pl.BlockSpec(memory_space=pltpu.VMEM)],
        out_specs=pl.BlockSpec(memory_space=pl.ANY),
        scratch_shapes=[
            pltpu.SemaphoreType.DMA((planes - 1,)),
            pltpu.SemaphoreType.DMA((planes - 1,)),
            pltpu.SemaphoreType.DMA,
        ],
        cost_estimate=busy(20),
        compiler_params=pltpu.CompilerParams(
            collective_id=collective_id, has_side_effects=True, vmem_limit_bytes=VMEM_BYTES
        ),
    )(local)


def plane_gather(local, collective_id):
    members = 8
    return pl.pallas_call(
        gather_kernel,
        out_shape=jax.ShapeDtypeStruct((members, *local.shape), local.dtype),
        in_specs=[pl.BlockSpec(memory_space=pl.ANY)],
        out_specs=pl.BlockSpec(memory_space=pl.ANY),
        scratch_shapes=GATHER_SEMS,
        cost_estimate=busy(25),
        compiler_params=pltpu.CompilerParams(
            collective_id=collective_id, has_side_effects=True, vmem_limit_bytes=VMEM_BYTES
        ),
    )(local)


def gather_rows(local, collective_id):
    rows, columns = local.shape
    out = plane_gather(local.reshape(rows // 16, 16, columns), collective_id)
    return out.reshape(-1, columns)


def add_rows(target, sources, start, count):
    def one(i, carry):
        total = sources[0][i].astype(jnp.float32)
        for source in sources[1:]:
            total = total + source[i].astype(jnp.float32)
        target[i] = total.astype(target.dtype)
        return carry

    lax.fori_loop(start, start + count, one, 0)


def plane_sum(
    part_ref, own_sum, near, sums, from_x, from_y, far_x, far_y, send_sems, recv_sems,
    work=lambda point: None,
):
    sibling, along_x, along_y, member = plane_places()
    rows = own_sum.shape[0]
    half = rows // 2
    top, bottom = pl.ds(0, half), pl.ds(half, half)
    send = sender(send_sems, recv_sems)
    chips = ((1, 1), (1, 0), (0, 1), (0, 0))
    mine = [part_ref.at[member(at_x, 0, at_y)] for at_x, at_y in chips]
    to_sibling = [
        send(k, part_ref.at[member(at_x, 1, at_y)], near.at[k], sibling)
        for k, (at_x, at_y) in enumerate(chips)
    ]
    work(0)
    to_sibling[0].wait_recv()
    add_rows(sums.at[0], (mine[0], near.at[0]), 0, rows)
    diagonal_x = send(4, sums.at[0, bottom], far_x.at[bottom], along_x)
    diagonal_y = send(5, sums.at[0, top], far_y.at[top], along_y)
    to_sibling[1].wait_recv()
    add_rows(sums.at[1], (mine[1], near.at[1]), half, half)
    direct_x = send(6, sums.at[1, bottom], from_x.at[bottom], along_x)
    to_sibling[2].wait_recv()
    add_rows(sums.at[2], (mine[2], near.at[2]), 0, half)
    direct_y = send(7, sums.at[2, top], from_y.at[top], along_y)
    to_sibling[3].wait_recv()
    work(1)
    diagonal_y.wait_recv()
    add_rows(sums.at[1], (mine[1], near.at[1], far_y), 0, half)
    joint_x = send(8, sums.at[1, top], from_x.at[top], along_x)
    diagonal_x.wait_recv()
    add_rows(sums.at[2], (mine[2], near.at[2], far_x), half, half)
    joint_y = send(9, sums.at[2, bottom], from_y.at[bottom], along_y)
    work(2)
    direct_x.wait_recv()
    direct_y.wait_recv()
    joint_x.wait_recv()
    joint_y.wait_recv()
    add_rows(own_sum, (mine[3], near.at[3], from_x, from_y), 0, rows)
    for copy in (*to_sibling, diagonal_x, diagonal_y, direct_x, direct_y, joint_x, joint_y):
        copy.wait_send()


def plane_sum_kernel(part_ref, out_ref, *scratch):
    sibling, along_x, along_y, _ = plane_places()
    greet((sibling, along_x, along_y))
    plane_sum(part_ref, out_ref, *scratch)


def plane_sum_scratch(shape, dtype):
    block = pltpu.VMEM(shape, dtype)
    return [
        pltpu.VMEM((4, *shape), dtype),
        pltpu.VMEM((3, *shape), dtype),
        block,
        block,
        block,
        block,
        pltpu.SemaphoreType.DMA((10,)),
        pltpu.SemaphoreType.DMA((10,)),
    ]


def plane_scatter_sum(partial, collective_id):
    members = 8
    rows, columns = partial.shape[0] // members, partial.shape[1]
    shape = (rows // 16, 16, columns)
    out = pl.pallas_call(
        plane_sum_kernel,
        out_shape=jax.ShapeDtypeStruct(shape, jnp.float32),
        in_specs=[pl.BlockSpec(memory_space=pltpu.VMEM)],
        out_specs=pl.BlockSpec(memory_space=pltpu.VMEM),
        scratch_shapes=plane_sum_scratch(shape, partial.dtype),
        cost_estimate=busy(25),
        compiler_params=pltpu.CompilerParams(
            collective_id=collective_id, has_side_effects=True, vmem_limit_bytes=VMEM_BYTES
        ),
    )(partial.reshape(members, *shape))
    return out.reshape(rows, columns)


gelu_inner = 0.7978845608028654
gelu_cubic = 0.044715


def pad_rows(target, source):
    rows = source.shape[0]
    target[pl.ds(0, rows)] = source[...]
    if target.shape[0] > rows:
        extra = target.shape[0] - rows
        target[pl.ds(rows, extra)] = jnp.zeros((extra, target.shape[1]), target.dtype)


def ffn_forward_kernel(in_ref, gate_up_ref, down_ref, part_ref, act_ref, to_gate, to_up, down, proj):
    units = act_ref.shape[1]

    @pl.when(pl.program_id(0) == 0)
    def _():
        pad_rows(down, down_ref)

    proj[...] = matmul(in_ref[...], gate_up_ref[...])
    step = 32

    def one(i, carry):
        rows = pl.ds(pl.multiple_of(i * step, step), step)
        gate, up = proj[rows, :units], proj[rows, units:]
        square = gate * gate
        bend = jnp.tanh(gelu_inner * gate * (1.0 + gelu_cubic * square))
        half = 0.5 * (1.0 + bend)
        value = gate * half
        slope = half + 0.5 * gate * (1.0 - bend * bend) * (
            gelu_inner * (1.0 + 3.0 * gelu_cubic * square)
        )
        to_gate[rows, :] = slope * up
        to_up[rows, :] = value
        act_ref[rows, :] = (value * up).astype(act_ref.dtype)
        return carry

    lax.fori_loop(0, in_ref.shape[0] // step, one, 0)
    part_ref[...] = matmul(act_ref[...], down[...]).astype(part_ref.dtype)


ROW_BLOCK = 256


def whole(array):
    return pl.BlockSpec(array.shape, lambda i: (0, 0), pipeline_mode=pl.Buffered(1))


def row_block(columns):
    return pl.BlockSpec((ROW_BLOCK, columns), lambda i: (i, 0))


def ffn_forward(rows_in, gate_up, down):
    rows, depth = rows_in.shape
    units, columns = gate_up.shape[1] // 2, down.shape[1]
    low = rows_in.dtype
    return pl.pallas_call(
        ffn_forward_kernel,
        grid=(rows // ROW_BLOCK,),
        in_specs=[row_block(depth), whole(gate_up), whole(down)],
        out_specs=[row_block(columns), row_block(units), row_block(units), row_block(units)],
        out_shape=[
            jax.ShapeDtypeStruct((rows, columns), low),
            jax.ShapeDtypeStruct((rows, units), low),
            jax.ShapeDtypeStruct((rows, units), jnp.float32),
            jax.ShapeDtypeStruct((rows, units), jnp.float32),
        ],
        scratch_shapes=[
            pltpu.VMEM((units, columns), low),
            pltpu.VMEM((ROW_BLOCK, 2 * units), jnp.float32),
        ],
        cost_estimate=busy(20),
        compiler_params=pltpu.CompilerParams(vmem_limit_bytes=VMEM_BYTES),
    )(rows_in, gate_up, down)


def gather_backward_kernel(
    own_ref, down_ref, gate_up_ref, to_gate_hbm, to_up_hbm, grad_ref, both_ref, part_ref,
    down, to_gate, to_up, load_sems, send_sems, recv_sems, local_sem,
):
    _, _, _, member = plane_places()
    units = down.shape[0]
    pieces, piece, columns = own_ref.shape
    rows = pieces * piece
    order = [
        member(*far)
        for far in (
            (0, 0, 0), (0, 1, 0), (1, 0, 0), (0, 0, 1), (1, 0, 1), (1, 1, 0), (0, 1, 1), (1, 1, 1),
        )
    ]

    def loads(i):
        at = pl.ds(pl.multiple_of(order[i] * rows, rows), rows)
        slot = i % 2
        return (
            pltpu.make_async_copy(to_gate_hbm.at[at], to_gate.at[slot], load_sems.at[0, slot]),
            pltpu.make_async_copy(to_up_hbm.at[at], to_up.at[slot], load_sems.at[1, slot]),
        )

    def compute(i):
        if i + 1 < len(order):
            for load in loads(i + 1):
                load.start()
        for load in loads(i):
            load.wait()
        block, slot = order[i], i % 2
        at = pl.ds(pl.multiple_of(block * rows, rows), rows)
        source = own_ref if i == 0 else grad_ref.at[block]
        act_grad = contract_cols(source[...].reshape(rows, columns), down[...])
        both_ref[at, :units] = (act_grad * to_gate[slot]).astype(both_ref.dtype)
        both_ref[at, units:] = (act_grad * to_up[slot]).astype(both_ref.dtype)
        part = contract_cols(both_ref[at, :], gate_up_ref[...]).astype(part_ref.dtype)
        part_ref[block] = part.reshape(pieces, piece, part.shape[1])

    for load in loads(0):
        load.start()
    pad_rows(down, down_ref)
    greet(plane_places()[:3])
    plane_spread(own_ref, grad_ref, send_sems, recv_sems, local_sem, compute)


def gather_backward(own, down, gate_up, to_gate, to_up, collective_id):
    rows, columns = own.shape
    members, piece = 8, 16
    depth, units = gate_up.shape[0], to_gate.shape[1]
    low = own.dtype
    vmem, anywhere = pl.BlockSpec(memory_space=pltpu.VMEM), pl.BlockSpec(memory_space=pl.ANY)
    grad, both, part = pl.pallas_call(
        gather_backward_kernel,
        out_shape=[
            jax.ShapeDtypeStruct((members, rows // piece, piece, columns), low),
            jax.ShapeDtypeStruct((members * rows, 2 * units), low),
            jax.ShapeDtypeStruct((members, rows // piece, piece, depth), low),
        ],
        in_specs=[vmem, vmem, vmem, anywhere, anywhere],
        out_specs=[vmem, vmem, vmem],
        scratch_shapes=[
            pltpu.VMEM((units, columns), low),
            pltpu.VMEM((2, rows, units), jnp.float32),
            pltpu.VMEM((2, rows, units), jnp.float32),
            pltpu.SemaphoreType.DMA((2, 2)),
            *GATHER_SEMS,
        ],
        cost_estimate=busy(35),
        compiler_params=pltpu.CompilerParams(
            collective_id=collective_id, has_side_effects=True, vmem_limit_bytes=VMEM_BYTES
        ),
    )(own.reshape(rows // piece, piece, columns), down, gate_up, to_gate, to_up)
    return grad.reshape(members * rows, columns), both, part


def sum_gradients_kernel(
    part_ref, in_hbm, both_hbm, act_hbm, grad_hbm, sum_ref, gate_up_ref, down_ref,
    rows_in, both, act, grad, load_sems, *scratch,
):
    loads = [
        pltpu.make_async_copy(source, target, load_sems.at[k])
        for k, (source, target) in enumerate(
            ((act_hbm, act), (grad_hbm, grad), (in_hbm, rows_in), (both_hbm, both))
        )
    ]
    for load in loads:
        load.start()
    down_step, step = down_ref.shape[1] // 3, 256

    def down_columns(i, carry):
        at = pl.ds(pl.multiple_of(i * down_step, 128), down_step)
        down_ref[:, at] = contract_rows(act[...], grad[:, at]).astype(down_ref.dtype)
        return carry

    def gate_up_columns(i, carry):
        at = pl.ds(pl.multiple_of(i * step, step), step)
        gate_up_ref[:, at] = contract_rows(rows_in[...], both[:, at]).astype(gate_up_ref.dtype)
        return carry

    blocks = gate_up_ref.shape[1] // step

    def work(point):
        if point == 0:
            loads[0].wait()
            loads[1].wait()
            lax.fori_loop(0, 3, down_columns, 0)
        if point == 1:
            loads[2].wait()
            loads[3].wait()
            lax.fori_loop(0, 2, gate_up_columns, 0)
        if point == 2:
            lax.fori_loop(2, blocks, gate_up_columns, 0)

    greet(plane_places()[:3])
    plane_sum(part_ref, sum_ref, *scratch, work=work)


def sum_gradients(part, rows_in, both, act, grad, collective_id):
    members, pieces, piece, depth = part.shape
    low = part.dtype
    vmem, anywhere = pl.BlockSpec(memory_space=pltpu.VMEM), pl.BlockSpec(memory_space=pl.ANY)
    total, gate_up, down = pl.pallas_call(
        sum_gradients_kernel,
        out_shape=[
            jax.ShapeDtypeStruct((pieces, piece, depth), jnp.float32),
            jax.ShapeDtypeStruct((depth, both.shape[1]), low),
            jax.ShapeDtypeStruct((act.shape[1], grad.shape[1]), low),
        ],
        in_specs=[vmem] + [anywhere] * 4,
        out_specs=[vmem, vmem, vmem],
        scratch_shapes=[
            pltpu.VMEM(rows_in.shape, low),
            pltpu.VMEM(both.shape, low),
            pltpu.VMEM(act.shape, low),
            pltpu.VMEM(grad.shape, low),
            pltpu.SemaphoreType.DMA((4,)),
            *plane_sum_scratch((pieces, piece, depth), low),
        ],
        cost_estimate=busy(35),
        compiler_params=pltpu.CompilerParams(
            collective_id=collective_id, has_side_effects=True, vmem_limit_bytes=60 * 2**20
        ),
    )(part, rows_in, both, act, grad)
    return total.reshape(pieces * piece, depth), gate_up, down


def owner_sum_kernel(planes, part_ref, out_ref, own_sum, leaving, arriving, z_send, z_recv, *scratch):
    sibling, along_x, along_y, _ = plane_places()
    z, x, core, seq = (lax.axis_index(name) for name in ALL)
    others = [(lax.rem(z + k, planes), x, core, seq) for k in range(1, planes)]
    greet((sibling, along_x, along_y, *others))
    plane_sum(part_ref, own_sum, *scratch)
    send = sender(z_send, z_recv)

    def narrow(i, carry):
        leaving[i] = own_sum[i].astype(leaving.dtype)
        return carry

    lax.fori_loop(0, planes, narrow, 0)
    copies = [
        send(k, leaving.at[place[0]], arriving.at[k], place) for k, place in enumerate(others)
    ]
    for copy in copies:
        copy.wait_recv()

    value = own_sum[z]
    for k in range(planes - 1):
        value = value + arriving[k].astype(jnp.float32)
    out_ref[...] = value
    for copy in copies:
        copy.wait_send()


def owner_sum(blocks, collective_id):
    members, planes, rows, columns = blocks.shape
    return pl.pallas_call(
        functools.partial(owner_sum_kernel, planes),
        out_shape=jax.ShapeDtypeStruct((rows, columns), jnp.float32),
        in_specs=[pl.BlockSpec(memory_space=pltpu.VMEM)],
        out_specs=pl.BlockSpec(memory_space=pltpu.VMEM),
        scratch_shapes=[
            pltpu.VMEM((planes, rows, columns), jnp.float32),
            pltpu.VMEM((planes, rows, columns), blocks.dtype),
            pltpu.VMEM((planes - 1, rows, columns), blocks.dtype),
            pltpu.SemaphoreType.DMA((planes - 1,)),
            pltpu.SemaphoreType.DMA((planes - 1,)),
            *plane_sum_scratch((planes, rows, columns), blocks.dtype),
        ],
        cost_estimate=busy(35),
        compiler_params=pltpu.CompilerParams(
            collective_id=collective_id, has_side_effects=True, vmem_limit_bytes=VMEM_BYTES
        ),
    )(blocks)


def body(
    tokens,
    segment_ids,
    cotangent,
    query_weight,
    key_weight,
    value_weight,
    output_weight,
    gate_weight,
    up_weight,
    down_weight,
    input_gain,
    query_gain,
    key_gain,
    attnout_gain,
    ffnin_gain,
    ffnout_gain,
):
    bf16, f32 = jnp.bfloat16, jnp.float32
    devices = lax.axis_size(ALL)
    members = lax.axis_size(PLANE)
    planes = lax.axis_size("z")
    seq_count = lax.axis_size("seq")
    width_rows = query_weight.shape[0]
    hidden_rows = down_weight.shape[0]
    head_width = key_weight.shape[1]
    query_width = query_weight.shape[1]
    head_count = query_width // head_width
    qkv_width = query_width + 2 * head_width
    mix_rows = output_weight.shape[0]
    padded = up_to(width_rows + 1, 8)
    width = devices * width_rows
    unit_count = planes * hidden_rows
    unit_pad = up_to(unit_count, 128)
    by_device = place_columns(devices, members, planes, width_rows, padded, False)
    by_member = place_columns(devices, members, planes, width_rows, padded, True)

    def column_blocks(weight):
        pieces = weight.reshape(width_rows, planes, members, hidden_rows)
        pieces = pieces.transpose(2, 0, 1, 3).reshape(members, width_rows, unit_count)
        return jnp.pad(
            pieces, ((0, 0), (0, padded - width_rows), (0, unit_pad - unit_count))
        )

    gate_up = jnp.concatenate([column_blocks(gate_weight), column_blocks(up_weight)], axis=2)
    gate_up = jnp.broadcast_to(gate_up[None], (planes,) + gate_up.shape)
    gate_up = gate_up.reshape((devices,) + gate_up.shape[2:])

    gains = (input_gain, query_gain, key_gain, attnout_gain, ffnin_gain, ffnout_gain)
    gain_row = jnp.concatenate(gains)
    gain_widths = [g.shape[0] for g in gains]
    gain_row = jnp.pad(gain_row, (0, qkv_width - gain_row.shape[0]))
    qkv_local = jnp.concatenate([query_weight, key_weight, value_weight], axis=1)
    packed = jnp.concatenate([qkv_local, gain_row[None]], axis=0)
    packed = jnp.pad(packed, ((0, padded - width_rows - 1), (0, 0)))
    output_wide = jnp.pad(output_weight, ((0, 0), (0, qkv_width - output_weight.shape[1])))
    packed = jnp.concatenate([packed, output_wide], axis=0)
    packed_all = z_gather(packed, planes, 0)
    gate_up, down_local, packed_all = lax.optimization_barrier(
        (gate_up, down_weight, packed_all)
    )
    packed_all = plane_gather(packed_all, 6)
    gate_up_full = exchange(gate_up, ALL).reshape(devices * padded, 2 * unit_pad)
    down_full = lax.all_gather(down_local, "z", axis=0, tiled=True)
    qkv_full = packed_all[:, :, :padded].reshape(devices * padded, qkv_width)
    output_full = packed_all[:, :, padded:, : output_weight.shape[1]].transpose(1, 0, 2, 3)
    output_full = output_full.reshape(devices * mix_rows, output_weight.shape[1])
    gain_rows = packed_all[:, :, width_rows, :].astype(f32)
    scales, at = [], 0
    for count in gain_widths:
        scales.append(gain_rows[:, :, at : at + count].transpose(1, 0, 2).reshape(-1))
        at += count
    padded_input_scale = jnp.pad(
        gain_rows[:, :, :width_rows], ((0, 0), (0, 0), (0, padded - width_rows))
    ).reshape(-1)
    _, query_scale, key_scale, attnout_scale, ffnin_scale, ffnout_scale = scales

    hidden = tokens[0].astype(f32)
    incoming = cotangent[0].astype(f32)
    local_rows = hidden.shape[0]
    full_length = local_rows * seq_count
    offset = lax.axis_index("seq") * local_rows
    segment_row = segment_ids[0]

    def mine(rows):
        return lax.dynamic_slice_in_dim(rows, offset, local_rows)

    my_segments = mine(segment_row)
    cos_full, sin_full = rope_tables(doc_positions(segment_row), head_width)
    cos_table, sin_table = mine(cos_full), mine(sin_full)
    scale = head_width ** (-0.5)

    other_half = [(0, 1), (1, 0)]
    first = lax.axis_index("seq") == 0
    other_tokens = lax.ppermute(tokens[0], "seq", other_half)
    row_tokens = jnp.concatenate(
        [
            jnp.where(first, tokens[0], other_tokens),
            jnp.where(first, other_tokens, tokens[0]),
        ]
    )
    row_hidden = matmul(row_tokens, by_member)
    row_inverse = lax.rsqrt(jnp.sum(row_hidden * row_hidden, axis=-1, keepdims=True) / width + epsilon)
    row_norm = row_hidden * row_inverse
    row_normed = (row_norm * padded_input_scale).astype(bf16)
    key_value_raw = matmul(row_normed, qkv_full[:, query_width:])
    row_key_raw = key_value_raw[:, :head_width]
    value_rows = key_value_raw[:, head_width:].astype(bf16)
    key_rows = rotate(
        row_key_raw * inverse_rms(row_key_raw) * key_scale, cos_full, sin_full
    ).astype(bf16)

    inv_input = mine(row_inverse)
    norm_input = mine(row_norm)
    normed = mine(row_normed)
    query_raw = matmul(normed, qkv_full[:, :query_width]).reshape(
        local_rows, head_count, head_width
    )
    inv_query = inverse_rms(query_raw)
    norm_query = query_raw * inv_query
    queries = (
        rotate(norm_query * query_scale, cos_table[:, None, :], sin_table[:, None, :]) * scale
    ).astype(bf16)
    key_raw = mine(row_key_raw)
    inv_key = inverse_rms(key_raw)
    norm_key = key_raw * inv_key

    query_places = offset + jnp.arange(local_rows, dtype=jnp.int32)
    key_places = jnp.arange(full_length, dtype=jnp.int32)
    allowed = (my_segments[:, None] == segment_row[None, :]) & (
        query_places[:, None] >= key_places[None, :]
    )
    raw_scores = jnp.einsum("qhd,kd->hqk", queries, key_rows, preferred_element_type=f32)
    scores = jnp.where(allowed[None], raw_scores, masked_score)
    peak = jnp.max(scores, axis=-1, keepdims=True)
    log_total = peak + jnp.log(jnp.sum(jnp.exp(scores - peak), axis=-1, keepdims=True))
    probs = jnp.exp(scores - log_total)
    probs_low = probs.astype(bf16)
    attn_mix = jnp.einsum("hqk,kd->qhd", probs_low, value_rows, preferred_element_type=f32)
    attn_flat = attn_mix.astype(bf16).reshape(local_rows, query_width)
    attn_raw = matmul(attn_flat, output_full)
    inv_attn = inverse_rms(attn_raw)
    norm_attn = attn_raw * inv_attn
    middle = hidden + norm_attn * attnout_scale
    inv_middle = inverse_rms(middle)
    norm_middle = middle * inv_middle
    ffn_in = (norm_middle * ffnin_scale).astype(bf16)

    plane_in = gather_rows(matmul(ffn_in, by_device).astype(bf16), 1)
    ffn_part, activated_low, to_gate, to_up = ffn_forward(plane_in, gate_up_full, down_full)
    ffn_raw = plane_scatter_sum(ffn_part, 2)
    inv_ffn = inverse_rms(ffn_raw)
    norm_ffn = ffn_raw * inv_ffn
    result = middle + norm_ffn * ffnout_scale
    ffnout_gain_grad = jnp.sum(incoming * norm_ffn, axis=0)
    ffn_raw_grad = rms_back(incoming * ffnout_scale, norm_ffn, inv_ffn).astype(bf16)

    plane_grad, gate_up_low, ffn_in_part = gather_backward(
        ffn_raw_grad, down_full, gate_up_full, to_gate, to_up, 3
    )
    ffn_in_grad, gate_up_blocks, down_blocks = sum_gradients(
        ffn_in_part, plane_in, gate_up_low, activated_low, plane_grad, 4
    )
    ffn_in_grad = take_back(ffn_in_grad, by_device)
    down_low = down_blocks[:unit_count].reshape(planes, hidden_rows, down_weight.shape[1])
    plane = lax.axis_index("z")
    down_wgrad = lax.dynamic_index_in_dim(down_low, plane, 0, keepdims=False).astype(f32)
    for k in range(1, planes):
        leaving = lax.dynamic_index_in_dim(down_low, lax.rem(plane + k, planes), 0, keepdims=False)
        shift = [(i, (i + k) % planes) for i in range(planes)]
        down_wgrad = down_wgrad + lax.ppermute(leaving, "z", shift).astype(f32)

    gate_up_terms = exchange(gate_up_blocks.reshape(devices, padded, 2 * unit_pad), ALL)
    ffnin_gain_grad = jnp.sum(ffn_in_grad * norm_middle, axis=0)
    middle_grad = incoming + rms_back(ffn_in_grad * ffnin_scale, norm_middle, inv_middle)
    attnout_gain_grad = jnp.sum(middle_grad * norm_attn, axis=0)
    attn_raw_grad = rms_back(middle_grad * attnout_scale, norm_attn, inv_attn).astype(bf16)
    output_wgrad = contract_rows(attn_flat, attn_raw_grad)
    mix_grad = (
        contract_cols(attn_raw_grad, output_full)
        .astype(bf16)
        .reshape(local_rows, head_count, head_width)
    )
    prob_grad = jnp.einsum("qhd,kd->hqk", mix_grad, value_rows, preferred_element_type=f32)
    row_delta = jnp.sum(prob_grad * probs, axis=-1, keepdims=True)
    score_grad = (probs * (prob_grad - row_delta)).astype(bf16)
    value_grad_rows = jnp.einsum("hqk,qhd->kd", probs_low, mix_grad, preferred_element_type=f32)
    key_grad_rows = jnp.einsum("hqk,qhd->kd", score_grad, queries, preferred_element_type=f32)
    query_grad = jnp.einsum("hqk,kd->qhd", score_grad, key_rows, preferred_element_type=f32)
    key_value_rows = jnp.concatenate([key_grad_rows, value_grad_rows], axis=1)
    theirs = lax.dynamic_slice_in_dim(key_value_rows, local_rows - offset, local_rows)
    key_value_grad = mine(key_value_rows) + lax.ppermute(
        theirs.astype(bf16), "seq", other_half
    ).astype(f32)
    key_grad, value_grad = key_value_grad[:, :head_width], key_value_grad[:, head_width:]
    query_norm_grad = rotate(query_grad * scale, cos_table[:, None, :], -sin_table[:, None, :])
    query_gain_grad = jnp.sum(query_norm_grad * norm_query, axis=(0, 1))
    query_raw_low = (
        rms_back(query_norm_grad * query_scale, norm_query, inv_query)
        .astype(bf16)
        .reshape(local_rows, query_width)
    )
    key_norm_grad = rotate(key_grad, cos_table, -sin_table)
    key_gain_grad = jnp.sum(key_norm_grad * norm_key, axis=0)
    key_raw_low = rms_back(key_norm_grad * key_scale, norm_key, inv_key).astype(bf16)
    qkv_raw_low = jnp.concatenate([query_raw_low, key_raw_low, value_grad.astype(bf16)], axis=1)
    qkv_wgrad = contract_rows(normed, qkv_raw_low)
    normed_grad = contract_cols(qkv_raw_low, qkv_full)
    input_gain_grad = jnp.sum(normed_grad * norm_input, axis=0)
    scaled_grad = normed_grad * padded_input_scale
    inner = jnp.sum(scaled_grad * norm_input, axis=-1, keepdims=True) / width
    input_grad = middle_grad + take_back(inv_input * (scaled_grad - norm_input * inner), by_member)

    gain_grads = (
        query_gain_grad,
        key_gain_grad,
        attnout_gain_grad,
        ffnin_gain_grad,
        ffnout_gain_grad,
    )
    gain_rows = jnp.concatenate(
        [input_gain_grad.reshape(members, planes, padded)[:, :, :width_rows]]
        + [g.reshape(planes, members, -1).transpose(1, 0, 2) for g in gain_grads],
        axis=2,
    )
    gain_rows = jnp.pad(gain_rows, ((0, 0), (0, 0), (0, qkv_width - gain_rows.shape[2])))
    blocks = qkv_wgrad.reshape(members, planes, padded, qkv_width)
    row = lax.broadcasted_iota(jnp.int32, blocks.shape, 2)
    blocks = jnp.where(row == width_rows, gain_rows[:, :, None], blocks).astype(bf16)
    output_blocks = output_wgrad.astype(bf16).reshape(planes, members, mix_rows, -1)
    output_blocks = jnp.pad(
        output_blocks.transpose(1, 0, 2, 3),
        ((0, 0), (0, 0), (0, 0), (0, qkv_width - output_blocks.shape[3])),
    )
    share = owner_sum(jnp.concatenate([blocks, output_blocks], axis=2), 5)
    gate_up_sum = jnp.sum(
        gate_up_terms.reshape(planes, members, padded, 2 * unit_pad).astype(f32), axis=0
    )

    def unit_columns(total):
        total = total[:, :width_rows, :unit_count].reshape(
            members, width_rows, planes, hidden_rows
        )
        return total.transpose(1, 2, 0, 3).reshape(width_rows, planes * members * hidden_rows)

    gate_wgrad = unit_columns(gate_up_sum[:, :, :unit_pad])
    up_wgrad = unit_columns(gate_up_sum[:, :, unit_pad:])
    qkv_share, output_share = share[:padded], share[padded:, : output_weight.shape[1]]
    gain_shares, at = [], 0
    for count in gain_widths:
        gain_shares.append(qkv_share[width_rows, at : at + count])
        at += count
    return (
        result.astype(bf16)[None],
        input_grad[None],
        qkv_share[:width_rows, :query_width],
        qkv_share[:width_rows, query_width : query_width + head_width],
        qkv_share[:width_rows, query_width + head_width :],
        output_share,
        gate_wgrad,
        up_wgrad,
        down_wgrad,
        *gain_shares,
    )


def solution(mesh):
    dp, seq = mesh.shape["dp"], mesh.shape["seq"]
    split = Mesh(mesh.devices.reshape(dp // 4, 2, 2, seq), ALL)
    rows = P(("z", "x", "core"), "seq", None)
    matrix, vector = P(ALL, None), P(ALL)
    return jax.shard_map(
        body,
        mesh=split,
        in_specs=(rows, P(("z", "x", "core"), None), rows) + (matrix,) * 7 + (vector,) * 6,
        out_specs=(rows, rows) + (matrix,) * 7 + (vector,) * 6,
        check_vma=False,
    )
```

```python
import functools

import jax
import jax.numpy as jnp
from jax import lax
from jax.experimental import pallas as pl
from jax.experimental.pallas import tpu as pltpu
from jax.sharding import Mesh
from jax.sharding import PartitionSpec as P

epsilon = 1e-06
rope_base = 1000000.0
masked_score = -1e30


def inverse_rms(values):
    return lax.rsqrt(jnp.mean(values * values, axis=-1, keepdims=True) + epsilon)


def rms_back(grad_normed, normed, inverse):
    return inverse * (grad_normed - normed * jnp.mean(grad_normed * normed, axis=-1, keepdims=True))


def doc_positions(segments):
    length = segments.shape[0]
    smaller = segments[None, :] < segments[:, None]
    starts = jnp.sum(smaller.astype(jnp.int32), axis=1)
    return (jnp.arange(length, dtype=jnp.int32) - starts).astype(jnp.float32)


def rope_tables(positions, head_width):
    half_width = head_width // 2
    frequency = rope_base ** (-(2.0 / head_width) * jnp.arange(half_width, dtype=jnp.float32))
    angles = positions[..., None] * frequency
    return (jnp.cos(angles), jnp.sin(angles))


def matmul(left, right):
    return jnp.dot(left, right, preferred_element_type=jnp.float32)


def contract_rows(left, right):
    return lax.dot_general(
        left, right, (((0,), (0,)), ((), ())), preferred_element_type=jnp.float32
    )


def contract_cols(left, right):
    return lax.dot_general(
        left, right, (((1,), (1,)), ((), ())), preferred_element_type=jnp.float32
    )


ALL = ("z", "x", "core", "seq")


def up_to(size, multiple):
    return (size + multiple - 1) // multiple * multiple


def place_columns(blocks, members, planes, rows, padded, by_member):
    source = lax.broadcasted_iota(jnp.int32, (blocks * rows, blocks * padded), 0)
    target = lax.broadcasted_iota(jnp.int32, (blocks * rows, blocks * padded), 1)
    block = source // rows
    if by_member:
        block = block % members * planes + block // members
    return (target == block * padded + source % rows).astype(jnp.bfloat16)


def take_back(padded_values, placing):
    high = lax.reduce_precision(padded_values, 8, 7)
    terms = jnp.concatenate([high, padded_values - high], axis=0).astype(jnp.bfloat16)
    both = contract_cols(terms, placing)
    rows = padded_values.shape[0]
    return both[:rows] + both[rows:]


PLANE = ("x", "core", "seq")

MESH_ID = pl.DeviceIdType.MESH
VMEM_BYTES = 48 * 2**20


def exchange(blocks, axes):
    return lax.all_to_all(blocks, axes, split_axis=0, concat_axis=0, tiled=True)


def busy(microseconds):
    return pl.CostEstimate(flops=0, bytes_accessed=microseconds * 3_000_000, transcendentals=0)


def plane_places():
    z, x, core, seq = (lax.axis_index(name) for name in ALL)
    sibling = (z, x, 1 - core, seq)
    along_x = (z, 1 - x, core, seq)
    along_y = (z, x, core, 1 - seq)

    def member(other_x, other_core, other_y):
        at_x = 1 - x if other_x else x
        at_core = 1 - core if other_core else core
        at_y = 1 - seq if other_y else seq
        return (at_x * 2 + at_core) * 2 + at_y

    return sibling, along_x, along_y, member


def greet(places):
    barrier = pltpu.get_barrier_semaphore()
    for place in places:
        pl.semaphore_signal(barrier, inc=1, device_id=place, device_id_type=MESH_ID)
    pl.semaphore_wait(barrier, len(places))


def sender(send_sems, recv_sems):
    def send(kind, source, target, place):
        copy = pltpu.make_async_remote_copy(
            src_ref=source,
            dst_ref=target,
            send_sem=send_sems.at[kind],
            recv_sem=recv_sems.at[kind],
            device_id=place,
            device_id_type=MESH_ID,
        )
        copy.start()
        return copy

    return send


def plane_spread(own_ref, out_ref, send_sems, recv_sems, local_sem, compute=lambda i: None):
    sibling, along_x, along_y, member = plane_places()
    half = own_ref.shape[0] // 2
    top, bottom = pl.ds(0, half), pl.ds(half, half)
    me = member(0, 0, 0)
    keep = pltpu.make_async_copy(own_ref, out_ref.at[me], local_sem)
    keep.start()
    send = sender(send_sems, recv_sems)

    def forward(kind, block, rows, place):
        return send(kind, out_ref.at[block, rows], out_ref.at[block, rows], place)

    own_x_top = send(1, own_ref.at[top], out_ref.at[me, top], along_x)
    own_y_bottom = send(3, own_ref.at[bottom], out_ref.at[me, bottom], along_y)
    own_sibling = send(0, own_ref, out_ref.at[me], sibling)
    own_x_bottom = send(2, own_ref.at[bottom], out_ref.at[me, bottom], along_x)
    own_y_top = send(4, own_ref.at[top], out_ref.at[me, top], along_y)
    x_block, y_block, diagonal = member(1, 0, 0), member(0, 0, 1), member(1, 0, 1)
    compute(0)
    own_x_top.wait_recv()
    diagonal_top = forward(5, x_block, top, along_y)
    x_top = forward(7, x_block, top, sibling)
    own_y_bottom.wait_recv()
    diagonal_bottom = forward(6, y_block, bottom, along_x)
    y_bottom = forward(9, y_block, bottom, sibling)
    own_sibling.wait_recv()
    compute(1)
    own_x_bottom.wait_recv()
    x_bottom = forward(8, x_block, bottom, sibling)
    own_y_top.wait_recv()
    y_top = forward(10, y_block, top, sibling)
    compute(2)
    diagonal_top.wait_recv()
    far_top = forward(11, diagonal, top, sibling)
    diagonal_bottom.wait_recv()
    far_bottom = forward(12, diagonal, bottom, sibling)
    compute(3)
    compute(4)
    for i, copies in ((5, (x_top, x_bottom)), (6, (y_bottom, y_top)), (7, (far_top, far_bottom))):
        for copy in copies:
            copy.wait_recv()
        compute(i)
    for copy in (
        own_x_top,
        own_y_bottom,
        own_sibling,
        own_x_bottom,
        own_y_top,
        diagonal_top,
        diagonal_bottom,
        x_top,
        y_bottom,
        x_bottom,
        y_top,
        far_top,
        far_bottom,
    ):
        copy.wait_send()
    keep.wait()


def gather_kernel(own_ref, out_ref, *sems):
    greet(plane_places()[:3])
    plane_spread(own_ref, out_ref, *sems)


def z_gather_kernel(planes, own_ref, out_ref, send_sems, recv_sems, own_sem):
    z, x, core, seq = (lax.axis_index(name) for name in ALL)
    others = [(lax.rem(z + k, planes), x, core, seq) for k in range(1, planes)]
    greet(others)
    keep = pltpu.make_async_copy(own_ref, out_ref.at[z], own_sem)
    keep.start()
    send = sender(send_sems, recv_sems)
    copies = [send(k, own_ref, out_ref.at[z], place) for k, place in enumerate(others)]
    for copy in copies:
        copy.wait_recv()
    for copy in copies:
        copy.wait_send()
    keep.wait()


GATHER_SEMS = [
    pltpu.SemaphoreType.DMA((13,)),
    pltpu.SemaphoreType.DMA((13,)),
    pltpu.SemaphoreType.DMA,
]


def z_gather(local, planes, collective_id):
    return pl.pallas_call(
        functools.partial(z_gather_kernel, planes),
        out_shape=jax.ShapeDtypeStruct((planes, *local.shape), local.dtype),
        in_specs=[pl.BlockSpec(memory_space=pltpu.VMEM)],
        out_specs=pl.BlockSpec(memory_space=pl.ANY),
        scratch_shapes=[
            pltpu.SemaphoreType.DMA((planes - 1,)),
            pltpu.SemaphoreType.DMA((planes - 1,)),
            pltpu.SemaphoreType.DMA,
        ],
        cost_estimate=busy(20),
        compiler_params=pltpu.CompilerParams(
            collective_id=collective_id, has_side_effects=True, vmem_limit_bytes=VMEM_BYTES
        ),
    )(local)


def plane_gather(local, collective_id):
    members = 8
    return pl.pallas_call(
        gather_kernel,
        out_shape=jax.ShapeDtypeStruct((members, *local.shape), local.dtype),
        in_specs=[pl.BlockSpec(memory_space=pl.ANY)],
        out_specs=pl.BlockSpec(memory_space=pl.ANY),
        scratch_shapes=GATHER_SEMS,
        cost_estimate=busy(25),
        compiler_params=pltpu.CompilerParams(
            collective_id=collective_id, has_side_effects=True, vmem_limit_bytes=VMEM_BYTES
        ),
    )(local)


def gather_rows(local, collective_id):
    rows, columns = local.shape
    out = plane_gather(local.reshape(rows // 16, 16, columns), collective_id)
    return out.reshape(-1, columns)


def add_rows(target, sources, start, count):
    def one(i, carry):
        total = sources[0][i].astype(jnp.float32)
        for source in sources[1:]:
            total = total + source[i].astype(jnp.float32)
        target[i] = total.astype(target.dtype)
        return carry

    lax.fori_loop(start, start + count, one, 0)


def plane_sum(
    part_ref, own_sum, near, sums, from_x, from_y, far_x, far_y, send_sems, recv_sems,
    work=lambda point: None,
):
    sibling, along_x, along_y, member = plane_places()
    rows = own_sum.shape[0]
    half = rows // 2
    top, bottom = pl.ds(0, half), pl.ds(half, half)
    send = sender(send_sems, recv_sems)
    chips = ((1, 1), (1, 0), (0, 1), (0, 0))
    mine = [part_ref.at[member(at_x, 0, at_y)] for at_x, at_y in chips]
    to_sibling = [
        send(k, part_ref.at[member(at_x, 1, at_y)], near.at[k], sibling)
        for k, (at_x, at_y) in enumerate(chips)
    ]
    work(0)
    to_sibling[0].wait_recv()
    add_rows(sums.at[0], (mine[0], near.at[0]), 0, rows)
    diagonal_x = send(4, sums.at[0, bottom], far_x.at[bottom], along_x)
    diagonal_y = send(5, sums.at[0, top], far_y.at[top], along_y)
    to_sibling[1].wait_recv()
    add_rows(sums.at[1], (mine[1], near.at[1]), half, half)
    direct_x = send(6, sums.at[1, bottom], from_x.at[bottom], along_x)
    to_sibling[2].wait_recv()
    add_rows(sums.at[2], (mine[2], near.at[2]), 0, half)
    direct_y = send(7, sums.at[2, top], from_y.at[top], along_y)
    to_sibling[3].wait_recv()
    work(1)
    diagonal_y.wait_recv()
    add_rows(sums.at[1], (mine[1], near.at[1], far_y), 0, half)
    joint_x = send(8, sums.at[1, top], from_x.at[top], along_x)
    diagonal_x.wait_recv()
    add_rows(sums.at[2], (mine[2], near.at[2], far_x), half, half)
    joint_y = send(9, sums.at[2, bottom], from_y.at[bottom], along_y)
    work(2)
    direct_x.wait_recv()
    direct_y.wait_recv()
    joint_x.wait_recv()
    joint_y.wait_recv()
    add_rows(own_sum, (mine[3], near.at[3], from_x, from_y), 0, rows)
    for copy in (*to_sibling, diagonal_x, diagonal_y, direct_x, direct_y, joint_x, joint_y):
        copy.wait_send()


def plane_sum_kernel(part_ref, out_ref, *scratch):
    sibling, along_x, along_y, _ = plane_places()
    greet((sibling, along_x, along_y))
    plane_sum(part_ref, out_ref, *scratch)


def plane_sum_scratch(shape, dtype):
    block = pltpu.VMEM(shape, dtype)
    return [
        pltpu.VMEM((4, *shape), dtype),
        pltpu.VMEM((3, *shape), dtype),
        block,
        block,
        block,
        block,
        pltpu.SemaphoreType.DMA((10,)),
        pltpu.SemaphoreType.DMA((10,)),
    ]


def plane_scatter_sum(partial, collective_id):
    members = 8
    rows, columns = partial.shape[0] // members, partial.shape[1]
    shape = (rows // 16, 16, columns)
    out = pl.pallas_call(
        plane_sum_kernel,
        out_shape=jax.ShapeDtypeStruct(shape, jnp.float32),
        in_specs=[pl.BlockSpec(memory_space=pltpu.VMEM)],
        out_specs=pl.BlockSpec(memory_space=pltpu.VMEM),
        scratch_shapes=plane_sum_scratch(shape, partial.dtype),
        cost_estimate=busy(25),
        compiler_params=pltpu.CompilerParams(
            collective_id=collective_id, has_side_effects=True, vmem_limit_bytes=VMEM_BYTES
        ),
    )(partial.reshape(members, *shape))
    return out.reshape(rows, columns)


gelu_inner = 0.7978845608028654
gelu_cubic = 0.044715


def pad_rows(target, source):
    rows = source.shape[0]
    target[pl.ds(0, rows)] = source[...]
    if target.shape[0] > rows:
        extra = target.shape[0] - rows
        target[pl.ds(rows, extra)] = jnp.zeros((extra, target.shape[1]), target.dtype)


def ffn_forward_kernel(in_ref, gate_up_ref, down_ref, part_ref, act_ref, to_gate, to_up, down, proj):
    units = act_ref.shape[1]

    @pl.when(pl.program_id(0) == 0)
    def _():
        pad_rows(down, down_ref)

    proj[...] = matmul(in_ref[...], gate_up_ref[...])
    step = 32

    def one(i, carry):
        rows = pl.ds(pl.multiple_of(i * step, step), step)
        gate, up = proj[rows, :units], proj[rows, units:]
        square = gate * gate
        bend = jnp.tanh(gelu_inner * gate * (1.0 + gelu_cubic * square))
        half = 0.5 * (1.0 + bend)
        value = gate * half
        slope = half + 0.5 * gate * (1.0 - bend * bend) * (
            gelu_inner * (1.0 + 3.0 * gelu_cubic * square)
        )
        to_gate[rows, :] = slope * up
        to_up[rows, :] = value
        act_ref[rows, :] = (value * up).astype(act_ref.dtype)
        return carry

    lax.fori_loop(0, in_ref.shape[0] // step, one, 0)
    part_ref[...] = matmul(act_ref[...], down[...]).astype(part_ref.dtype)


ROW_BLOCK = 256


def whole(array):
    return pl.BlockSpec(array.shape, lambda i: (0, 0), pipeline_mode=pl.Buffered(1))


def row_block(columns):
    return pl.BlockSpec((ROW_BLOCK, columns), lambda i: (i, 0))


def ffn_forward(rows_in, gate_up, down):
    rows, depth = rows_in.shape
    units, columns = gate_up.shape[1] // 2, down.shape[1]
    low = rows_in.dtype
    return pl.pallas_call(
        ffn_forward_kernel,
        grid=(rows // ROW_BLOCK,),
        in_specs=[row_block(depth), whole(gate_up), whole(down)],
        out_specs=[row_block(columns), row_block(units), row_block(units), row_block(units)],
        out_shape=[
            jax.ShapeDtypeStruct((rows, columns), low),
            jax.ShapeDtypeStruct((rows, units), low),
            jax.ShapeDtypeStruct((rows, units), jnp.float32),
            jax.ShapeDtypeStruct((rows, units), jnp.float32),
        ],
        scratch_shapes=[
            pltpu.VMEM((units, columns), low),
            pltpu.VMEM((ROW_BLOCK, 2 * units), jnp.float32),
        ],
        cost_estimate=busy(20),
        compiler_params=pltpu.CompilerParams(vmem_limit_bytes=VMEM_BYTES),
    )(rows_in, gate_up, down)


def gather_backward_kernel(
    own_ref, down_ref, gate_up_ref, to_gate_hbm, to_up_hbm, act_hbm, grad_ref, both_ref, part_ref,
    down_grad_ref, down, to_gate, to_up, act, act_sem, load_sems, send_sems, recv_sems, local_sem,
):
    _, _, _, member = plane_places()
    units = down.shape[0]
    pieces, piece, columns = own_ref.shape
    rows = pieces * piece
    order = [
        member(*far)
        for far in (
            (0, 0, 0), (0, 1, 0), (1, 0, 0), (0, 0, 1), (1, 0, 1), (1, 1, 0), (0, 1, 1), (1, 1, 1),
        )
    ]

    def loads(i):
        at = pl.ds(pl.multiple_of(order[i] * rows, rows), rows)
        slot = i % 2
        return (
            pltpu.make_async_copy(to_gate_hbm.at[at], to_gate.at[slot], load_sems.at[0, slot]),
            pltpu.make_async_copy(to_up_hbm.at[at], to_up.at[slot], load_sems.at[1, slot]),
        )

    def compute(i):
        if i + 1 < len(order):
            for load in loads(i + 1):
                load.start()
        for load in loads(i):
            load.wait()
        block, slot = order[i], i % 2
        at = pl.ds(pl.multiple_of(block * rows, rows), rows)
        source = own_ref if i == 0 else grad_ref.at[block]
        act_grad = contract_cols(source[...].reshape(rows, columns), down[...])
        both_ref[at, :units] = (act_grad * to_gate[slot]).astype(both_ref.dtype)
        both_ref[at, units:] = (act_grad * to_up[slot]).astype(both_ref.dtype)
        part = contract_cols(both_ref[at, :], gate_up_ref[...]).astype(part_ref.dtype)
        part_ref[block] = part.reshape(pieces, piece, part.shape[1])

    act_load = pltpu.make_async_copy(act_hbm, act, act_sem)
    act_load.start()
    for load in loads(0):
        load.start()
    pad_rows(down, down_ref)
    greet(plane_places()[:3])
    plane_spread(own_ref, grad_ref, send_sems, recv_sems, local_sem, compute)
    act_load.wait()
    grad = grad_ref[...].reshape(len(order) * rows, columns)
    down_grad = contract_rows(act[...], grad)
    down_grad_ref[...] = down_grad[: down_ref.shape[0]].astype(down_grad_ref.dtype)


def gather_backward(own, down, gate_up, to_gate, to_up, act, collective_id):
    rows, columns = own.shape
    members, piece = 8, 16
    depth, units = gate_up.shape[0], to_gate.shape[1]
    low = own.dtype
    vmem, anywhere = pl.BlockSpec(memory_space=pltpu.VMEM), pl.BlockSpec(memory_space=pl.ANY)
    grad, both, part, down_grad = pl.pallas_call(
        gather_backward_kernel,
        out_shape=[
            jax.ShapeDtypeStruct((members, rows // piece, piece, columns), low),
            jax.ShapeDtypeStruct((members * rows, 2 * units), low),
            jax.ShapeDtypeStruct((members, rows // piece, piece, depth), low),
            jax.ShapeDtypeStruct(down.shape, low),
        ],
        in_specs=[vmem, vmem, vmem, anywhere, anywhere, anywhere],
        out_specs=[vmem, vmem, vmem, vmem],
        scratch_shapes=[
            pltpu.VMEM((units, columns), low),
            pltpu.VMEM((2, rows, units), jnp.float32),
            pltpu.VMEM((2, rows, units), jnp.float32),
            pltpu.VMEM(act.shape, low),
            pltpu.SemaphoreType.DMA,
            pltpu.SemaphoreType.DMA((2, 2)),
            *GATHER_SEMS,
        ],
        cost_estimate=busy(35),
        compiler_params=pltpu.CompilerParams(
            collective_id=collective_id, has_side_effects=True, vmem_limit_bytes=VMEM_BYTES
        ),
    )(own.reshape(rows // piece, piece, columns), down, gate_up, to_gate, to_up, act)
    return both, part, down_grad


def sum_gradients_kernel(
    part_ref, down_ref, in_hbm, both_hbm, sum_ref, gate_up_ref, down_sum_ref,
    rows_in, both, arriving, load_sems, z_send, z_recv, *scratch,
):
    planes = down_ref.shape[0]
    z, x, core, seq = (lax.axis_index(name) for name in ALL)
    others = [(lax.rem(z + k, planes), x, core, seq) for k in range(1, planes)]
    loads = [
        pltpu.make_async_copy(source, target, load_sems.at[k])
        for k, (source, target) in enumerate(
            ((in_hbm, rows_in), (both_hbm, both))
        )
    ]
    for load in loads:
        load.start()
    step = 256

    def gate_up_columns(i, carry):
        at = pl.ds(pl.multiple_of(i * step, step), step)
        gate_up_ref[:, at] = contract_rows(rows_in[...], both[:, at]).astype(gate_up_ref.dtype)
        return carry

    blocks = gate_up_ref.shape[1] // step

    def work(point):
        if point == 0:
            for load in loads:
                load.wait()
            lax.fori_loop(0, 2, gate_up_columns, 0)
        if point == 1:
            lax.fori_loop(2, 3, gate_up_columns, 0)
        if point == 2:
            lax.fori_loop(3, blocks, gate_up_columns, 0)

    greet((*plane_places()[:3], *others))
    send = sender(z_send, z_recv)
    copies = [
        send(k, down_ref.at[place[0]], arriving.at[k], place) for k, place in enumerate(others)
    ]
    plane_sum(part_ref, sum_ref, *scratch, work=work)
    down_sum = down_ref[z].astype(jnp.float32)
    for k, copy in enumerate(copies):
        copy.wait_recv()
        down_sum = down_sum + arriving[k].astype(jnp.float32)
    down_sum_ref[...] = down_sum
    for copy in copies:
        copy.wait_send()


def sum_gradients(part, down, rows_in, both, collective_id):
    members, pieces, piece, depth = part.shape
    low = part.dtype
    vmem, anywhere = pl.BlockSpec(memory_space=pltpu.VMEM), pl.BlockSpec(memory_space=pl.ANY)
    total, gate_up, down_sum = pl.pallas_call(
        sum_gradients_kernel,
        out_shape=[
            jax.ShapeDtypeStruct((pieces, piece, depth), jnp.float32),
            jax.ShapeDtypeStruct((depth, both.shape[1]), low),
            jax.ShapeDtypeStruct(down.shape[1:], jnp.float32),
        ],
        in_specs=[vmem, vmem, anywhere, anywhere],
        out_specs=[vmem, vmem, vmem],
        scratch_shapes=[
            pltpu.VMEM(rows_in.shape, low),
            pltpu.VMEM(both.shape, low),
            pltpu.VMEM((down.shape[0] - 1, *down.shape[1:]), low),
            pltpu.SemaphoreType.DMA((2,)),
            pltpu.SemaphoreType.DMA((down.shape[0] - 1,)),
            pltpu.SemaphoreType.DMA((down.shape[0] - 1,)),
            *plane_sum_scratch((pieces, piece, depth), low),
        ],
        cost_estimate=busy(35),
        compiler_params=pltpu.CompilerParams(
            collective_id=collective_id, has_side_effects=True, vmem_limit_bytes=60 * 2**20
        ),
    )(part, down, rows_in, both)
    return total.reshape(pieces * piece, depth), gate_up, down_sum


def owner_sum_kernel(planes, part_ref, out_ref, own_sum, leaving, arriving, z_send, z_recv, *scratch):
    sibling, along_x, along_y, _ = plane_places()
    z, x, core, seq = (lax.axis_index(name) for name in ALL)
    others = [(lax.rem(z + k, planes), x, core, seq) for k in range(1, planes)]
    greet((sibling, along_x, along_y, *others))
    plane_sum(part_ref, own_sum, *scratch)
    send = sender(z_send, z_recv)

    def narrow(i, carry):
        leaving[i] = own_sum[i].astype(leaving.dtype)
        return carry

    lax.fori_loop(0, planes, narrow, 0)
    copies = [
        send(k, leaving.at[place[0]], arriving.at[k], place) for k, place in enumerate(others)
    ]
    for copy in copies:
        copy.wait_recv()

    value = own_sum[z]
    for k in range(planes - 1):
        value = value + arriving[k].astype(jnp.float32)
    out_ref[...] = value
    for copy in copies:
        copy.wait_send()


def owner_sum(blocks, collective_id):
    members, planes, rows, columns = blocks.shape
    return pl.pallas_call(
        functools.partial(owner_sum_kernel, planes),
        out_shape=jax.ShapeDtypeStruct((rows, columns), jnp.float32),
        in_specs=[pl.BlockSpec(memory_space=pltpu.VMEM)],
        out_specs=pl.BlockSpec(memory_space=pltpu.VMEM),
        scratch_shapes=[
            pltpu.VMEM((planes, rows, columns), jnp.float32),
            pltpu.VMEM((planes, rows, columns), blocks.dtype),
            pltpu.VMEM((planes - 1, rows, columns), blocks.dtype),
            pltpu.SemaphoreType.DMA((planes - 1,)),
            pltpu.SemaphoreType.DMA((planes - 1,)),
            *plane_sum_scratch((planes, rows, columns), blocks.dtype),
        ],
        cost_estimate=busy(35),
        compiler_params=pltpu.CompilerParams(
            collective_id=collective_id, has_side_effects=True, vmem_limit_bytes=VMEM_BYTES
        ),
    )(blocks)


def gain_places(blocks, planes, offset, count, per, by_member):
    lane = lax.broadcasted_iota(jnp.int32, (256, blocks * per), 0)
    column = lax.broadcasted_iota(jnp.int32, (256, blocks * per), 1)
    inner = column % per
    places = ((lane == offset + inner) & (inner < count)).astype(jnp.float32).astype(jnp.bfloat16)
    listed = lax.broadcasted_iota(jnp.int32, (blocks, blocks * per), 0)
    block = lax.broadcasted_iota(jnp.int32, (blocks, blocks * per), 1) // per
    members = blocks // planes
    if not by_member:
        block = block % members * planes + block // members
    return places, listed == block


def spread_gain(rows, planes, *where):
    places, chosen = gain_places(rows.shape[0], planes, *where)
    return jnp.sum(jnp.where(chosen, matmul(rows, places), 0.0), axis=0, keepdims=True)


def collect_gain(vector, blocks, planes, *where):
    places, chosen = gain_places(blocks, planes, *where)
    return contract_cols(jnp.where(chosen, vector, 0.0).astype(jnp.bfloat16), places)


def inverse_of(values, count):
    return lax.rsqrt(jnp.sum(values * values, axis=-1, keepdims=True) / count + epsilon)


def back_of(grad_normed, normed, inverse, count):
    inner = jnp.sum(grad_normed * normed, axis=-1, keepdims=True) / count
    return inverse * (grad_normed - normed * inner)


def turn(values, cos_table, sin_table):
    half = values.shape[1] // 2
    first, second = values[:, :half], values[:, half:]
    return first * cos_table - second * sin_table, second * cos_table + first * sin_table


def attention_forward_kernel(
    gain_at, width_rows, row_ref, hidden_ref, packed_ref, cos_ref, sin_ref, segment_column, segment_row, placing_ref,
    placed_ref, middle_ref, raw_ref, mix_ref, probs_ref, query_ref, key_ref, value_ref, query_raw_ref,
    key_raw_ref, qkv_ref, output_ref, input_scale, query_scale, key_scale, attnout_scale, ffnin_scale, ffnout_scale,
    gain_rows,
):
    bf16, f32 = jnp.bfloat16, jnp.float32
    members, planes, piece, _ = packed_ref.shape
    blocks = members * planes
    padded = qkv_ref.shape[0] // blocks
    mix_rows = piece - padded
    width = hidden_ref.shape[1]
    local_rows, full_rows = hidden_ref.shape[0], row_ref.shape[0]
    head = key_ref.shape[1]
    heads = query_ref.shape[1] // head
    offset = pl.multiple_of(lax.axis_index("seq") * local_rows, local_rows)
    mine = pl.ds(offset, local_rows)
    for i in range(blocks):
        member, plane = i // planes, i % planes
        block = packed_ref[member, plane]
        qkv_ref[padded * i : padded * (i + 1), :] = block[:padded]
        natural = mix_rows * (plane * members + member)
        output_ref[natural : natural + mix_rows, :] = block[padded:, :width]
        gain_rows[i : i + 1, :] = block[width_rows : width_rows + 1, :256].astype(f32)
    rows = gain_rows[...].astype(bf16)
    (at, count), *others = gain_at
    input_scale[...] = spread_gain(rows, planes, at, count, padded, True)
    targets = (query_scale, key_scale, attnout_scale, ffnin_scale, ffnout_scale)
    for target, (at, count) in zip(targets, others):
        target[...] = spread_gain(rows, planes, at, count, count, False)

    row = row_ref[...].astype(f32)
    normed = (row * inverse_of(row, width) * input_scale[...]).astype(bf16)
    key_value = matmul(normed, qkv_ref[:, heads * head :])
    key_raw = key_value[:, :head]
    value_ref[...] = key_value[:, head:].astype(bf16)
    half = head // 2
    turned = turn(key_raw * inverse_of(key_raw, head) * key_scale[...], cos_ref[...], sin_ref[...])
    key_ref[:, :half], key_ref[:, half:] = turned[0].astype(bf16), turned[1].astype(bf16)

    row = row_ref[mine, :].astype(f32)
    normed = (row * inverse_of(row, width) * input_scale[...]).astype(bf16)
    own = matmul(normed, qkv_ref[:, : (heads + 1) * head])
    query_raw_ref[...] = own[:, : heads * head]
    key_raw_ref[...] = own[:, heads * head :]
    cos_table, sin_table = cos_ref[mine, :], sin_ref[mine, :]
    places = offset + lax.broadcasted_iota(jnp.int32, (local_rows, full_rows), 0)
    earlier = places >= lax.broadcasted_iota(jnp.int32, (local_rows, full_rows), 1)
    allowed = (segment_column[...] == segment_row[...]) & earlier
    for h in range(heads):
        at = h * head
        query_raw = query_raw_ref[:, at : at + head]
        turned = turn(
            query_raw * inverse_of(query_raw, head) * query_scale[...], cos_table, sin_table
        )
        scale = head ** (-0.5)
        query_ref[:, at : at + half] = (turned[0] * scale).astype(bf16)
        query_ref[:, at + half : at + head] = (turned[1] * scale).astype(bf16)
        scores = contract_cols(query_ref[:, at : at + head], key_ref[...])
        scores = jnp.where(allowed, scores, masked_score)
        weights = jnp.exp(scores - jnp.max(scores, axis=-1, keepdims=True))
        probs = weights / jnp.sum(weights, axis=-1, keepdims=True)
        probs_ref[h] = probs
        mix_ref[:, at : at + head] = matmul(probs.astype(bf16), value_ref[...]).astype(bf16)
    attn_raw = matmul(mix_ref[...], output_ref[...])
    raw_ref[...] = attn_raw
    middle = hidden_ref[...].astype(f32) + attn_raw * inverse_of(attn_raw, width) * attnout_scale[...]
    middle_ref[...] = middle
    ffn_in = (middle * inverse_of(middle, width) * ffnin_scale[...]).astype(bf16)
    placed_ref[...] = matmul(ffn_in, placing_ref[...]).astype(bf16)


def attention_forward(
    row_padded, hidden, packed, cos_full, sin_full, segment_column, segment_row, placing, gain_at, width_rows, padded,
    head_width,
):
    bf16, f32 = jnp.bfloat16, jnp.float32
    members, planes, piece, qkv_width = packed.shape
    blocks = members * planes
    local_rows, width = hidden.shape
    query_width = qkv_width - 2 * head_width
    heads = query_width // head_width
    full_rows = row_padded.shape[0]
    depth = blocks * padded
    shape = jax.ShapeDtypeStruct
    vmem = pl.BlockSpec(memory_space=pltpu.VMEM)
    out_shape = [
        shape((local_rows, depth), bf16),
        shape((local_rows, width), f32),
        shape((local_rows, width), f32),
        shape((local_rows, query_width), bf16),
        shape((heads, local_rows, full_rows), f32),
        shape((local_rows, query_width), bf16),
        shape((full_rows, head_width), bf16),
        shape((full_rows, head_width), bf16),
        shape((local_rows, query_width), f32),
        shape((local_rows, head_width), f32),
        shape((depth, qkv_width), bf16),
        shape((query_width, width), bf16),
        shape((1, depth), f32),
        shape((1, head_width), f32),
        shape((1, head_width), f32),
        shape((1, width), f32),
        shape((1, width), f32),
        shape((1, width), f32),
    ]
    return pl.pallas_call(
        functools.partial(attention_forward_kernel, gain_at, width_rows),
        out_shape=out_shape,
        in_specs=[vmem] * 8,
        out_specs=[vmem] * len(out_shape),
        scratch_shapes=[pltpu.VMEM((blocks, 256), f32)],
        cost_estimate=busy(20),
        compiler_params=pltpu.CompilerParams(vmem_limit_bytes=60 * 2**20),
    )(row_padded, hidden, packed, cos_full, sin_full, segment_column, segment_row, placing)


def attention_backward_kernel(
    gain_at, width_rows, planes, grad_ref, incoming_ref, middle_ref, raw_ref, mix_ref, probs_ref, query_ref, key_ref,
    value_ref, query_raw_ref, key_raw_ref, row_ref, qkv_ref, output_ref, cos_ref, sin_ref, input_scale,
    query_scale, key_scale, attnout_scale, ffnin_scale, ffnout_grad, by_device, by_member,
    input_grad_ref, blocks_ref, key_value, query_grad, low_ref, leaving, arriving, send_sem, recv_sem,
):
    bf16, f32 = jnp.bfloat16, jnp.float32
    members = blocks_ref.shape[0]
    blocks = members * planes
    padded = qkv_ref.shape[0] // blocks
    mix_rows = blocks_ref.shape[2] - padded
    local_rows, width = incoming_ref.shape
    head = key_ref.shape[1]
    heads = query_ref.shape[1] // head
    half = head // 2
    seq = lax.axis_index("seq")
    mine = pl.ds(pl.multiple_of(seq * local_rows, local_rows), local_rows)
    theirs = pl.ds(pl.multiple_of((1 - seq) * local_rows, local_rows), local_rows)
    partner = plane_places()[2]
    greet((partner,))

    ffn_in_grad = take_back(grad_ref[...], by_device[...])
    middle = middle_ref[...]
    inverse = inverse_of(middle, width)
    normed = middle * inverse
    ffnin_grad = jnp.sum(ffn_in_grad * normed, axis=0, keepdims=True)
    middle_grad = incoming_ref[...].astype(f32) + back_of(
        ffn_in_grad * ffnin_scale[...], normed, inverse, width
    )
    input_grad_ref[...] = middle_grad
    raw = raw_ref[...]
    inverse = inverse_of(raw, width)
    normed = raw * inverse
    attnout_grad = jnp.sum(middle_grad * normed, axis=0, keepdims=True)
    raw_grad = back_of(middle_grad * attnout_scale[...], normed, inverse, width).astype(bf16)
    mix_grad = contract_cols(raw_grad, output_ref[...]).astype(bf16)
    for h in range(heads):
        at = h * head
        grad = mix_grad[:, at : at + head]
        probs = probs_ref[h]
        prob_grad = contract_cols(grad, value_ref[...])
        delta = jnp.sum(prob_grad * probs, axis=-1, keepdims=True)
        score_grad = (probs * (prob_grad - delta)).astype(bf16)
        to_keys = contract_rows(score_grad, query_ref[:, at : at + head])
        to_values = contract_rows(probs.astype(bf16), grad)
        if h == 0:
            key_value[:, :head], key_value[:, head:] = to_keys, to_values
        else:
            key_value[:, :head] += to_keys
            key_value[:, head:] += to_values
        query_grad[:, at : at + head] = matmul(score_grad, key_ref[...])
    leaving[...] = key_value[theirs, :].astype(bf16)
    copy = sender(send_sem, recv_sem)(0, leaving, arriving, partner)

    output_grad = contract_rows(mix_ref[...], raw_grad).astype(bf16)
    cos_table, sin_table = cos_ref[mine, :], sin_ref[mine, :]

    def head_back(grad, raw, scale_ref):
        turned = jnp.concatenate(turn(grad, cos_table, -sin_table), axis=1)
        inverse = inverse_of(raw, head)
        normed = raw * inverse
        gain = jnp.sum(turned * normed, axis=0, keepdims=True)
        return back_of(turned * scale_ref[...], normed, inverse, head).astype(bf16), gain

    query_gain = jnp.zeros((1, head), f32)
    for h in range(heads):
        at = h * head
        low, gain = head_back(
            query_grad[:, at : at + head] * head ** (-0.5),
            query_raw_ref[:, at : at + head],
            query_scale,
        )
        low_ref[:, at : at + head] = low
        query_gain = query_gain + gain
    copy.wait_recv()
    total = key_value[mine, :] + arriving[...].astype(f32)
    low, key_gain = head_back(total[:, :head], key_raw_ref[...], key_scale)
    low_ref[:, heads * head : (heads + 1) * head] = low
    low_ref[:, (heads + 1) * head :] = total[:, head:].astype(bf16)

    row = row_ref[mine, :].astype(f32)
    inverse = inverse_of(row, width)
    normed = row * inverse
    normed_grad = contract_cols(low_ref[...], qkv_ref[...])
    input_gain = jnp.sum(normed_grad * normed, axis=0, keepdims=True)
    input_grad_ref[...] += take_back(
        back_of(normed_grad * input_scale[...], normed, inverse, width), by_member[...]
    )
    (at, count), *others = gain_at
    gains = collect_gain(input_gain, blocks, planes, at, count, padded, True)
    vectors = (query_gain, key_gain, attnout_grad, ffnin_grad, ffnout_grad[...])
    for vector, (at, count) in zip(vectors, others):
        gains = gains + collect_gain(vector, blocks, planes, at, count, count, False)
    normed = (normed * input_scale[...]).astype(bf16)
    weights = contract_rows(normed, low_ref[...])
    row_of = lax.broadcasted_iota(jnp.int32, (padded, 256), 0)
    columns = blocks_ref.shape[3]
    for i in range(blocks):
        member, plane = i // planes, i % planes
        piece = weights[padded * i : padded * (i + 1)]
        first = jnp.where(row_of == width_rows, gains[i : i + 1], piece[:, :256])
        blocks_ref[member, plane, :padded, :256] = first.astype(bf16)
        blocks_ref[member, plane, :padded, 256:] = piece[:, 256:].astype(bf16)
        natural = mix_rows * (plane * members + member)
        blocks_ref[member, plane, padded:, :width] = output_grad[natural : natural + mix_rows]
        blocks_ref[member, plane, padded:, width:] = jnp.zeros((mix_rows, columns - width), bf16)
    copy.wait_send()


def attention_backward(arrays, gain_at, width_rows, planes, mix_rows, collective_id):
    bf16, f32 = jnp.bfloat16, jnp.float32
    grad, incoming, query, key, qkv = arrays[0], arrays[1], arrays[6], arrays[7], arrays[12]
    local_rows, width = incoming.shape
    members = 8
    padded = qkv.shape[0] // (members * planes)
    pair = pltpu.VMEM((local_rows, 2 * key.shape[1]), bf16)
    shape = jax.ShapeDtypeStruct
    vmem = pl.BlockSpec(memory_space=pltpu.VMEM)
    return pl.pallas_call(
        functools.partial(attention_backward_kernel, gain_at, width_rows, planes),
        out_shape=[
            shape((local_rows, width), f32),
            shape((members, planes, padded + mix_rows, qkv.shape[1]), bf16),
        ],
        in_specs=[vmem] * len(arrays),
        out_specs=[vmem] * 2,
        scratch_shapes=[
            pltpu.VMEM((key.shape[0], 2 * key.shape[1]), f32),
            pltpu.VMEM(query.shape, f32),
            pltpu.VMEM((local_rows, qkv.shape[1]), bf16),
            pair,
            pair,
            pltpu.SemaphoreType.DMA((1,)),
            pltpu.SemaphoreType.DMA((1,)),
        ],
        cost_estimate=busy(30),
        compiler_params=pltpu.CompilerParams(
            collective_id=collective_id, has_side_effects=True, vmem_limit_bytes=60 * 2**20
        ),
    )(*arrays)


def body(
    tokens,
    segment_ids,
    cotangent,
    query_weight,
    key_weight,
    value_weight,
    output_weight,
    gate_weight,
    up_weight,
    down_weight,
    input_gain,
    query_gain,
    key_gain,
    attnout_gain,
    ffnin_gain,
    ffnout_gain,
):
    bf16, f32 = jnp.bfloat16, jnp.float32
    devices = lax.axis_size(ALL)
    members = lax.axis_size(PLANE)
    planes = lax.axis_size("z")
    width_rows = query_weight.shape[0]
    hidden_rows = down_weight.shape[0]
    head_width = key_weight.shape[1]
    query_width = query_weight.shape[1]
    head_count = query_width // head_width
    qkv_width = query_width + 2 * head_width
    mix_rows = output_weight.shape[0]
    padded = up_to(width_rows + 1, 8)
    width = devices * width_rows
    unit_count = planes * hidden_rows
    unit_pad = up_to(unit_count, 128)
    by_device = place_columns(devices, members, planes, width_rows, padded, False)
    by_member = place_columns(devices, members, planes, width_rows, padded, True)

    def column_blocks(weight):
        pieces = weight.reshape(width_rows, planes, members, hidden_rows)
        pieces = pieces.transpose(2, 0, 1, 3).reshape(members, width_rows, unit_count)
        return jnp.pad(
            pieces, ((0, 0), (0, padded - width_rows), (0, unit_pad - unit_count))
        )

    gate_up = jnp.concatenate([column_blocks(gate_weight), column_blocks(up_weight)], axis=2)
    gate_up = jnp.broadcast_to(gate_up[None], (planes,) + gate_up.shape)
    gate_up = gate_up.reshape((devices,) + gate_up.shape[2:])

    gains = (input_gain, query_gain, key_gain, attnout_gain, ffnin_gain, ffnout_gain)
    gain_row = jnp.concatenate(gains)
    gain_widths = [g.shape[0] for g in gains]
    gain_row = jnp.pad(gain_row, (0, qkv_width - gain_row.shape[0]))
    qkv_local = jnp.concatenate([query_weight, key_weight, value_weight], axis=1)
    packed = jnp.concatenate([qkv_local, gain_row[None]], axis=0)
    packed = jnp.pad(packed, ((0, padded - width_rows - 1), (0, 0)))
    output_wide = jnp.pad(output_weight, ((0, 0), (0, qkv_width - output_weight.shape[1])))
    packed = jnp.concatenate([packed, output_wide], axis=0)
    packed_all = z_gather(packed, planes, 0)
    gate_up, down_local, packed_all = lax.optimization_barrier(
        (gate_up, down_weight, packed_all)
    )
    packed_all = plane_gather(packed_all, 6)
    gate_up_full = exchange(gate_up, ALL).reshape(devices * padded, 2 * unit_pad)
    down_full = lax.all_gather(down_local, "z", axis=0, tiled=True)
    incoming = cotangent[0].astype(f32)
    local_rows = tokens.shape[1]
    offset = lax.axis_index("seq") * local_rows
    segment_row = segment_ids[0]

    def mine(rows):
        return lax.dynamic_slice_in_dim(rows, offset, local_rows)

    cos_full, sin_full = rope_tables(doc_positions(segment_row), head_width)

    other_half = [(0, 1), (1, 0)]
    first = lax.axis_index("seq") == 0
    other_tokens = lax.ppermute(tokens[0], "seq", other_half)
    row_tokens = jnp.concatenate(
        [
            jnp.where(first, tokens[0], other_tokens),
            jnp.where(first, other_tokens, tokens[0]),
        ]
    )
    row_padded = matmul(row_tokens, by_member).astype(bf16)
    gain_at, at = [], 0
    for count in gain_widths:
        gain_at.append((at, count))
        at += count
    (
        ffn_in_placed,
        middle,
        attn_raw,
        attn_flat,
        probs,
        queries,
        key_rows,
        value_rows,
        query_raw,
        key_raw,
        qkv_full,
        output_full,
        *scales,
    ) = attention_forward(
        row_padded,
        tokens[0],
        packed_all,
        cos_full,
        sin_full,
        mine(segment_row)[:, None],
        segment_row[None],
        by_device,
        gain_at,
        width_rows,
        padded,
        head_width,
    )
    ffnout_scale = scales.pop()

    plane_in = gather_rows(ffn_in_placed, 1)
    ffn_part, activated_low, to_gate, to_up = ffn_forward(plane_in, gate_up_full, down_full)
    ffn_raw = plane_scatter_sum(ffn_part, 2)
    inv_ffn = inverse_rms(ffn_raw)
    norm_ffn = ffn_raw * inv_ffn
    result = middle + norm_ffn * ffnout_scale
    ffnout_gain_grad = jnp.sum(incoming * norm_ffn, axis=0)
    ffn_raw_grad = rms_back(incoming * ffnout_scale, norm_ffn, inv_ffn).astype(bf16)

    gate_up_low, ffn_in_part, down_blocks = gather_backward(
        ffn_raw_grad, down_full, gate_up_full, to_gate, to_up, activated_low, 3
    )
    down_blocks = down_blocks.reshape(planes, hidden_rows, down_weight.shape[1])
    ffn_in_grad, gate_up_blocks, down_wgrad = sum_gradients(
        ffn_in_part, down_blocks, plane_in, gate_up_low, 4
    )
    gate_up_terms = exchange(gate_up_blocks.reshape(devices, padded, 2 * unit_pad), ALL)
    input_grad, blocks = attention_backward(
        [
            ffn_in_grad,
            cotangent[0],
            middle,
            attn_raw,
            attn_flat,
            probs,
            queries,
            key_rows,
            value_rows,
            query_raw,
            key_raw,
            row_padded,
            qkv_full,
            output_full,
            cos_full,
            sin_full,
            *scales,
            ffnout_gain_grad[None],
            by_device,
            by_member,
        ],
        gain_at,
        width_rows,
        planes,
        mix_rows,
        7,
    )
    share = owner_sum(blocks, 5)
    gate_up_sum = jnp.sum(
        gate_up_terms.reshape(planes, members, padded, 2 * unit_pad).astype(f32), axis=0
    )

    def unit_columns(total):
        total = total[:, :width_rows, :unit_count].reshape(
            members, width_rows, planes, hidden_rows
        )
        return total.transpose(1, 2, 0, 3).reshape(width_rows, planes * members * hidden_rows)

    gate_wgrad = unit_columns(gate_up_sum[:, :, :unit_pad])
    up_wgrad = unit_columns(gate_up_sum[:, :, unit_pad:])
    qkv_share, output_share = share[:padded], share[padded:, : output_weight.shape[1]]
    gain_shares, at = [], 0
    for count in gain_widths:
        gain_shares.append(qkv_share[width_rows, at : at + count])
        at += count
    return (
        result.astype(bf16)[None],
        input_grad[None],
        qkv_share[:width_rows, :query_width],
        qkv_share[:width_rows, query_width : query_width + head_width],
        qkv_share[:width_rows, query_width + head_width :],
        output_share,
        gate_wgrad,
        up_wgrad,
        down_wgrad,
        *gain_shares,
    )


def solution(mesh):
    dp, seq = mesh.shape["dp"], mesh.shape["seq"]
    split = Mesh(mesh.devices.reshape(dp // 4, 2, 2, seq), ALL)
    rows = P(("z", "x", "core"), "seq", None)
    matrix, vector = P(ALL, None), P(ALL)
    return jax.shard_map(
        body,
        mesh=split,
        in_specs=(rows, P(("z", "x", "core"), None), rows) + (matrix,) * 7 + (vector,) * 6,
        out_specs=(rows, rows) + (matrix,) * 7 + (vector,) * 6,
        check_vma=False,
    )
```

```python
import functools

import jax
import jax.numpy as jnp
from jax import lax
from jax.experimental import pallas as pl
from jax.experimental.pallas import tpu as pltpu
from jax.sharding import Mesh
from jax.sharding import PartitionSpec as P

epsilon = 1e-06
rope_base = 1000000.0
masked_score = -1e30


def inverse_rms(values):
    return lax.rsqrt(jnp.mean(values * values, axis=-1, keepdims=True) + epsilon)


def rms_back(grad_normed, normed, inverse):
    return inverse * (grad_normed - normed * jnp.mean(grad_normed * normed, axis=-1, keepdims=True))


def doc_positions(segments):
    length = segments.shape[0]
    smaller = segments[None, :] < segments[:, None]
    starts = jnp.sum(smaller.astype(jnp.int32), axis=1)
    return (jnp.arange(length, dtype=jnp.int32) - starts).astype(jnp.float32)


def rope_tables(positions, head_width):
    half_width = head_width // 2
    frequency = rope_base ** (-(2.0 / head_width) * jnp.arange(half_width, dtype=jnp.float32))
    angles = positions[..., None] * frequency
    return (jnp.cos(angles), jnp.sin(angles))


def matmul(left, right):
    return jnp.dot(left, right, preferred_element_type=jnp.float32)


def contract_rows(left, right):
    return lax.dot_general(
        left, right, (((0,), (0,)), ((), ())), preferred_element_type=jnp.float32
    )


def contract_cols(left, right):
    return lax.dot_general(
        left, right, (((1,), (1,)), ((), ())), preferred_element_type=jnp.float32
    )


ALL = ("far", "z", "x", "core", "seq")
PLANES = ("far", "z")
CUBE = ("z", "x", "core", "seq")


def up_to(size, multiple):
    return (size + multiple - 1) // multiple * multiple


def place_columns(blocks, members, planes, rows, padded, by_member):
    source = lax.broadcasted_iota(jnp.int32, (blocks * rows, blocks * padded), 0)
    target = lax.broadcasted_iota(jnp.int32, (blocks * rows, blocks * padded), 1)
    block = source // rows
    if by_member:
        block = block % members * planes + block // members
    return (target == block * padded + source % rows).astype(jnp.bfloat16)


def take_back(padded_values, placing):
    high = lax.reduce_precision(padded_values, 8, 7)
    terms = jnp.concatenate([high, padded_values - high], axis=0).astype(jnp.bfloat16)
    both = contract_cols(terms, placing)
    rows = padded_values.shape[0]
    return both[:rows] + both[rows:]


PLANE = ("x", "core", "seq")

MESH_ID = pl.DeviceIdType.MESH
VMEM_BYTES = 48 * 2**20


def exchange(blocks, axes):
    return lax.all_to_all(blocks, axes, split_axis=0, concat_axis=0, tiled=True)


def busy(microseconds):
    return pl.CostEstimate(flops=0, bytes_accessed=microseconds * 3_000_000, transcendentals=0)


def shifted(flip_z, flip_x, flip_core, flip_y):
    far, *inner = (lax.axis_index(name) for name in ALL)
    flips = (flip_z, flip_x, flip_core, flip_y)
    return (far, *(1 - at if flip else at for at, flip in zip(inner, flips)))


def plane_places():
    def member(flip_x, flip_core, flip_y):
        _, _, x, core, seq = shifted(0, flip_x, flip_core, flip_y)
        return (x * 2 + core) * 2 + seq

    return shifted(0, 0, 1, 0), shifted(0, 1, 0, 0), shifted(0, 0, 0, 1), member


def cube_member(flip_z, flip_x, flip_y, flip_core):
    _, z, x, core, seq = shifted(flip_z, flip_x, flip_core, flip_y)
    return ((z * 2 + x) * 2 + core) * 2 + seq


def cube_places():
    return *plane_places()[:3], shifted(1, 0, 0, 0)


def other_planes(planes):
    far, z, x, core, seq = (lax.axis_index(name) for name in ALL)
    plane = far * 2 + z
    ring = [lax.rem(plane + k, planes) for k in range(1, planes)]
    return plane, [(at // 2, lax.rem(at, 2), x, core, seq) for at in ring], ring


def other_cubes(cubes):
    far, z, x, core, seq = (lax.axis_index(name) for name in ALL)
    return far, [(lax.rem(far + k, cubes), z, x, core, seq) for k in range(1, cubes)]


def greet(places):
    barrier = pltpu.get_barrier_semaphore()
    for place in places:
        pl.semaphore_signal(barrier, inc=1, device_id=place, device_id_type=MESH_ID)
    pl.semaphore_wait(barrier, len(places))


def sender(send_sems, recv_sems):
    def send(kind, source, target, place):
        copy = pltpu.make_async_remote_copy(
            src_ref=source,
            dst_ref=target,
            send_sem=send_sems.at[kind],
            recv_sem=recv_sems.at[kind],
            device_id=place,
            device_id_type=MESH_ID,
        )
        copy.start()
        return copy

    return send


def plane_spread(own_ref, out_ref, send_sems, recv_sems, local_sem):
    sibling, along_x, along_y, member = plane_places()
    half = own_ref.shape[0] // 2
    top, bottom = pl.ds(0, half), pl.ds(half, half)
    me = member(0, 0, 0)
    keep = pltpu.make_async_copy(own_ref, out_ref.at[me], local_sem)
    keep.start()
    send = sender(send_sems, recv_sems)

    def forward(kind, block, rows, place):
        return send(kind, out_ref.at[block, rows], out_ref.at[block, rows], place)

    own_x_top = send(1, own_ref.at[top], out_ref.at[me, top], along_x)
    own_y_bottom = send(3, own_ref.at[bottom], out_ref.at[me, bottom], along_y)
    own_sibling = send(0, own_ref, out_ref.at[me], sibling)
    own_x_bottom = send(2, own_ref.at[bottom], out_ref.at[me, bottom], along_x)
    own_y_top = send(4, own_ref.at[top], out_ref.at[me, top], along_y)
    x_block, y_block, diagonal = member(1, 0, 0), member(0, 0, 1), member(1, 0, 1)
    own_x_top.wait_recv()
    diagonal_top = forward(5, x_block, top, along_y)
    x_top = forward(7, x_block, top, sibling)
    own_y_bottom.wait_recv()
    diagonal_bottom = forward(6, y_block, bottom, along_x)
    y_bottom = forward(9, y_block, bottom, sibling)
    own_x_bottom.wait_recv()
    x_bottom = forward(8, x_block, bottom, sibling)
    own_y_top.wait_recv()
    y_top = forward(10, y_block, top, sibling)
    diagonal_top.wait_recv()
    far_top = forward(11, diagonal, top, sibling)
    diagonal_bottom.wait_recv()
    far_bottom = forward(12, diagonal, bottom, sibling)
    for copy in (own_sibling, x_top, y_bottom, x_bottom, y_top, far_top, far_bottom):
        copy.wait_recv()
    for copy in (
        own_x_top,
        own_y_bottom,
        own_sibling,
        own_x_bottom,
        own_y_top,
        diagonal_top,
        diagonal_bottom,
        x_top,
        y_bottom,
        x_bottom,
        y_top,
        far_top,
        far_bottom,
    ):
        copy.wait_send()
    keep.wait()


def cube_spread(own_ref, out_ref, send_sems, recv_sems, local_sem, compute=lambda i: None):
    sibling, along_x, along_y, along_z = cube_places()
    half = own_ref.shape[0] // 2
    top, bottom = pl.ds(0, half), pl.ds(half, half)
    me = cube_member(0, 0, 0, 0)
    keep = pltpu.make_async_copy(own_ref, out_ref.at[me], local_sem)
    keep.start()
    send = sender(send_sems, recv_sems)
    x_block, y_block, diagonal = (cube_member(0, *at, 0) for at in ((1, 0), (0, 1), (1, 1)))
    z_block, zx_block, zy_block, zd_block = (
        cube_member(1, *at, 0) for at in ((0, 0), (1, 0), (0, 1), (1, 1))
    )

    def half_on(kind, block, rows, place):
        return send(kind, out_ref.at[block, rows], out_ref.at[block, rows], place)

    def on(kind, block, place):
        return send(kind, out_ref.at[block], out_ref.at[block], place)

    own_x_top = send(1, own_ref.at[top], out_ref.at[me, top], along_x)
    own_y_bottom = send(3, own_ref.at[bottom], out_ref.at[me, bottom], along_y)
    own_z = send(13, own_ref, out_ref.at[me], along_z)
    own_sibling = send(0, own_ref, out_ref.at[me], sibling)
    own_x_bottom = send(2, own_ref.at[bottom], out_ref.at[me, bottom], along_x)
    own_y_top = send(4, own_ref.at[top], out_ref.at[me, top], along_y)
    compute(0)
    own_x_top.wait_recv()
    diagonal_top = half_on(5, x_block, top, along_y)
    x_top = half_on(7, x_block, top, sibling)
    own_y_bottom.wait_recv()
    diagonal_bottom = half_on(6, y_block, bottom, along_x)
    y_bottom = half_on(9, y_block, bottom, sibling)
    own_sibling.wait_recv()
    compute(1)
    own_z.wait_recv()
    z_to_x = on(14, z_block, along_x)
    z_to_y = on(15, z_block, along_y)
    z_near = on(16, z_block, sibling)
    own_x_bottom.wait_recv()
    x_bottom = half_on(8, x_block, bottom, sibling)
    own_y_top.wait_recv()
    y_top = half_on(10, y_block, top, sibling)
    compute(2)
    diagonal_top.wait_recv()
    far_top = half_on(11, diagonal, top, sibling)
    diagonal_bottom.wait_recv()
    far_bottom = half_on(12, diagonal, bottom, sibling)
    diagonal_z = on(17, diagonal, along_z)
    compute(3)
    compute(4)
    z_to_x.wait_recv()
    zx_near = on(18, zx_block, sibling)
    z_to_y.wait_recv()
    zy_near = on(19, zy_block, sibling)
    compute(5)
    compute(6)
    diagonal_z.wait_recv()
    zd_near = on(20, zd_block, sibling)
    compute(7)
    compute(8)
    last = (
        (x_top, x_bottom), (y_bottom, y_top), (far_top, far_bottom), (z_near,), (zx_near,), (zy_near,), (zd_near,),
    )
    for i, copies in enumerate(last):
        for copy in copies:
            copy.wait_recv()
        compute(9 + i)
    for copy in (
        own_x_top, own_y_bottom, own_z, own_sibling, own_x_bottom, own_y_top, diagonal_top, diagonal_bottom,
        z_to_x, z_to_y, diagonal_z,
    ):
        copy.wait_send()
    for copies in last:
        for copy in copies:
            copy.wait_send()
    keep.wait()


CUBE_ORDER = (
    (0, 0, 0, 0), (0, 0, 0, 1), (0, 1, 0, 0), (0, 0, 1, 0), (1, 0, 0, 0), (0, 1, 1, 0), (1, 1, 0, 0), (1, 0, 1, 0),
    (1, 1, 1, 0), (0, 1, 0, 1), (0, 0, 1, 1), (0, 1, 1, 1), (1, 0, 0, 1), (1, 1, 0, 1), (1, 0, 1, 1), (1, 1, 1, 1),
)


def cube_gather_kernel(own_ref, out_ref, *sems):
    greet(cube_places())
    cube_spread(own_ref, out_ref, *sems)


def weights_gather_kernel(cubes, own_ref, down_ref, out_ref, down_out, far_send, far_recv, own_sem, *sems):
    far, others = other_cubes(cubes)
    greet((*plane_places()[:3], *others))
    keep = pltpu.make_async_copy(down_ref, down_out.at[far], own_sem)
    keep.start()
    send = sender(far_send, far_recv)
    copies = [send(k, down_ref, down_out.at[far], place) for k, place in enumerate(others)]
    plane_spread(own_ref, out_ref, *sems)
    for copy in copies:
        copy.wait_recv()
    for copy in copies:
        copy.wait_send()
    keep.wait()


def z_gather_kernel(planes, own_ref, out_ref, send_sems, recv_sems, own_sem):
    plane, others, _ = other_planes(planes)
    greet(others)
    keep = pltpu.make_async_copy(own_ref, out_ref.at[plane], own_sem)
    keep.start()
    send = sender(send_sems, recv_sems)
    copies = [send(k, own_ref, out_ref.at[plane], place) for k, place in enumerate(others)]
    for copy in copies:
        copy.wait_recv()
    for copy in copies:
        copy.wait_send()
    keep.wait()


def gather_sems(count):
    return [
        pltpu.SemaphoreType.DMA((count,)),
        pltpu.SemaphoreType.DMA((count,)),
        pltpu.SemaphoreType.DMA,
    ]


def z_gather(local, planes, collective_id):
    return pl.pallas_call(
        functools.partial(z_gather_kernel, planes),
        out_shape=jax.ShapeDtypeStruct((planes, *local.shape), local.dtype),
        in_specs=[pl.BlockSpec(memory_space=pltpu.VMEM)],
        out_specs=pl.BlockSpec(memory_space=pl.ANY),
        scratch_shapes=[
            pltpu.SemaphoreType.DMA((planes - 1,)),
            pltpu.SemaphoreType.DMA((planes - 1,)),
            pltpu.SemaphoreType.DMA,
        ],
        cost_estimate=busy(20),
        compiler_params=pltpu.CompilerParams(
            collective_id=collective_id, has_side_effects=True, vmem_limit_bytes=VMEM_BYTES
        ),
    )(local)


def weights_gather(local, down, cubes, collective_id):
    members = 8
    anywhere = pl.BlockSpec(memory_space=pl.ANY)
    return pl.pallas_call(
        functools.partial(weights_gather_kernel, cubes),
        out_shape=[
            jax.ShapeDtypeStruct((members, *local.shape), local.dtype),
            jax.ShapeDtypeStruct((cubes, *down.shape), down.dtype),
        ],
        in_specs=[anywhere, anywhere],
        out_specs=[anywhere, anywhere],
        scratch_shapes=[
            pltpu.SemaphoreType.DMA((cubes - 1,)),
            pltpu.SemaphoreType.DMA((cubes - 1,)),
            pltpu.SemaphoreType.DMA,
            *gather_sems(13),
        ],
        cost_estimate=busy(30),
        compiler_params=pltpu.CompilerParams(
            collective_id=collective_id, has_side_effects=True, vmem_limit_bytes=VMEM_BYTES
        ),
    )(local, down)


def gather_rows(local, collective_id):
    rows, columns = local.shape
    members = 16
    out = pl.pallas_call(
        cube_gather_kernel,
        out_shape=jax.ShapeDtypeStruct((members, rows // 16, 16, columns), local.dtype),
        in_specs=[pl.BlockSpec(memory_space=pl.ANY)],
        out_specs=pl.BlockSpec(memory_space=pl.ANY),
        scratch_shapes=gather_sems(21),
        cost_estimate=busy(35),
        compiler_params=pltpu.CompilerParams(
            collective_id=collective_id, has_side_effects=True, vmem_limit_bytes=VMEM_BYTES
        ),
    )(local.reshape(rows // 16, 16, columns))
    return out.reshape(-1, columns)


def add_rows(target, sources, start, count):
    def one(i, carry):
        total = sources[0][i].astype(jnp.float32)
        for source in sources[1:]:
            total = total + source[i].astype(jnp.float32)
        target[i] = total.astype(target.dtype)
        return carry

    lax.fori_loop(start, start + count, one, 0)


def plane_sum(part_ref, own_sum, near, sums, from_x, from_y, far_x, far_y, send_sems, recv_sems):
    sibling, along_x, along_y, member = plane_places()
    rows = own_sum.shape[0]
    half = rows // 2
    top, bottom = pl.ds(0, half), pl.ds(half, half)
    send = sender(send_sems, recv_sems)
    chips = ((1, 1), (1, 0), (0, 1), (0, 0))
    mine = [part_ref.at[member(at_x, 0, at_y)] for at_x, at_y in chips]
    to_sibling = [
        send(k, part_ref.at[member(at_x, 1, at_y)], near.at[k], sibling)
        for k, (at_x, at_y) in enumerate(chips)
    ]
    to_sibling[0].wait_recv()
    add_rows(sums.at[0], (mine[0], near.at[0]), 0, rows)
    diagonal_x = send(4, sums.at[0, bottom], far_x.at[bottom], along_x)
    diagonal_y = send(5, sums.at[0, top], far_y.at[top], along_y)
    to_sibling[1].wait_recv()
    add_rows(sums.at[1], (mine[1], near.at[1]), half, half)
    direct_x = send(6, sums.at[1, bottom], from_x.at[bottom], along_x)
    to_sibling[2].wait_recv()
    add_rows(sums.at[2], (mine[2], near.at[2]), 0, half)
    direct_y = send(7, sums.at[2, top], from_y.at[top], along_y)
    to_sibling[3].wait_recv()
    diagonal_y.wait_recv()
    add_rows(sums.at[1], (mine[1], near.at[1], far_y), 0, half)
    joint_x = send(8, sums.at[1, top], from_x.at[top], along_x)
    diagonal_x.wait_recv()
    add_rows(sums.at[2], (mine[2], near.at[2], far_x), half, half)
    joint_y = send(9, sums.at[2, bottom], from_y.at[bottom], along_y)
    direct_x.wait_recv()
    direct_y.wait_recv()
    joint_x.wait_recv()
    joint_y.wait_recv()
    add_rows(own_sum, (mine[3], near.at[3], from_x, from_y), 0, rows)
    for copy in (*to_sibling, diagonal_x, diagonal_y, direct_x, direct_y, joint_x, joint_y):
        copy.wait_send()


def cube_sum(
    part_ref, own_sum, near, via_z, zx_in, zy_in, far_x, far_y, from_x, from_y, from_z, send_sems, recv_sems,
    work=lambda point: None,
):
    sibling, along_x, along_y, along_z = cube_places()
    pieces = own_sum.shape[0]
    half = pieces // 2
    top, bottom = pl.ds(0, half), pl.ds(half, half)
    send = sender(send_sems, recv_sems)
    chips = ((1, 1, 1), (1, 1, 0), (1, 0, 1), (0, 1, 0), (0, 0, 1), (0, 1, 1), (1, 0, 0), (0, 0, 0))
    z_diagonal, z_x, z_y, at_x, at_y, diagonal, at_z, here = range(8)
    mine = [part_ref.at[cube_member(*chip, 0)] for chip in chips]
    to_sibling = [
        send(k, part_ref.at[cube_member(*chip, 1)], near.at[k], sibling)
        for k, chip in enumerate(chips)
    ]

    def add(k, others=(), start=0, count=pieces):
        add_rows(near.at[k], (mine[k], near.at[k], *others), start, count)

    work(0)
    to_sibling[z_diagonal].wait_recv()
    add(z_diagonal)
    diagonal_z = send(8, near.at[z_diagonal], via_z, along_z)
    to_sibling[z_x].wait_recv()
    add(z_x)
    zx_out = send(9, near.at[z_x], zx_in, along_x)
    to_sibling[z_y].wait_recv()
    add(z_y)
    zy_out = send(10, near.at[z_y], zy_in, along_y)
    to_sibling[at_x].wait_recv()
    add(at_x, (), half, half)
    direct_x = send(13, near.at[at_x, bottom], from_x.at[bottom], along_x)
    to_sibling[at_y].wait_recv()
    add(at_y, (), 0, half)
    direct_y = send(14, near.at[at_y, top], from_y.at[top], along_y)
    to_sibling[diagonal].wait_recv()
    to_sibling[at_z].wait_recv()
    work(1)
    diagonal_z.wait_recv()
    add(diagonal, (via_z,))
    diagonal_x = send(11, near.at[diagonal, bottom], far_x.at[bottom], along_x)
    diagonal_y = send(12, near.at[diagonal, top], far_y.at[top], along_y)
    zx_out.wait_recv()
    zy_out.wait_recv()
    add(at_z, (zx_in, zy_in))
    joint_z = send(15, near.at[at_z], from_z, along_z)
    work(2)
    diagonal_y.wait_recv()
    add(at_x, (far_y,), 0, half)
    joint_x = send(16, near.at[at_x, top], from_x.at[top], along_x)
    diagonal_x.wait_recv()
    add(at_y, (far_x,), half, half)
    joint_y = send(17, near.at[at_y, bottom], from_y.at[bottom], along_y)
    to_sibling[here].wait_recv()
    work(3)
    for copy in (direct_x, direct_y, joint_z, joint_x, joint_y):
        copy.wait_recv()
    add_rows(own_sum, (mine[here], near.at[here], from_x, from_y, from_z), 0, pieces)
    for copy in (
        *to_sibling, diagonal_z, zx_out, zy_out, direct_x, direct_y, diagonal_x, diagonal_y, joint_z, joint_x, joint_y,
    ):
        copy.wait_send()


def cube_sum_kernel(part_ref, out_ref, *scratch):
    greet(cube_places())
    cube_sum(part_ref, out_ref, *scratch)


def cube_sum_scratch(shape, dtype):
    return [
        pltpu.VMEM((8, *shape), dtype),
        *[pltpu.VMEM(shape, dtype)] * 8,
        pltpu.SemaphoreType.DMA((18,)),
        pltpu.SemaphoreType.DMA((18,)),
    ]


def plane_sum_scratch(shape, dtype):
    block = pltpu.VMEM(shape, dtype)
    return [
        pltpu.VMEM((4, *shape), dtype),
        pltpu.VMEM((3, *shape), dtype),
        block,
        block,
        block,
        block,
        pltpu.SemaphoreType.DMA((10,)),
        pltpu.SemaphoreType.DMA((10,)),
    ]


def cube_scatter_sum(partial, collective_id):
    members = 16
    rows, columns = partial.shape[0] // members, partial.shape[1]
    shape = (rows // 16, 16, columns)
    out = pl.pallas_call(
        cube_sum_kernel,
        out_shape=jax.ShapeDtypeStruct(shape, jnp.float32),
        in_specs=[pl.BlockSpec(memory_space=pltpu.VMEM)],
        out_specs=pl.BlockSpec(memory_space=pltpu.VMEM),
        scratch_shapes=cube_sum_scratch(shape, partial.dtype),
        cost_estimate=busy(35),
        compiler_params=pltpu.CompilerParams(
            collective_id=collective_id, has_side_effects=True, vmem_limit_bytes=VMEM_BYTES
        ),
    )(partial.reshape(members, *shape))
    return out.reshape(rows, columns)


gelu_inner = 0.7978845608028654
gelu_cubic = 0.044715


def pad_rows(target, source):
    rows = source.shape[0]
    target[pl.ds(0, rows)] = source[...]
    if target.shape[0] > rows:
        extra = target.shape[0] - rows
        target[pl.ds(rows, extra)] = jnp.zeros((extra, target.shape[1]), target.dtype)


def ffn_forward_kernel(in_ref, gate_up_ref, down_ref, part_ref, act_ref, to_gate, to_up, down, proj):
    units = act_ref.shape[1]

    @pl.when(pl.program_id(0) == 0)
    def _():
        pad_rows(down, down_ref)

    proj[...] = matmul(in_ref[...], gate_up_ref[...])
    step = 32

    def one(i, carry):
        rows = pl.ds(pl.multiple_of(i * step, step), step)
        gate, up = proj[rows, :units], proj[rows, units:]
        square = gate * gate
        bend = jnp.tanh(gelu_inner * gate * (1.0 + gelu_cubic * square))
        half = 0.5 * (1.0 + bend)
        value = gate * half
        slope = half + 0.5 * gate * (1.0 - bend * bend) * (
            gelu_inner * (1.0 + 3.0 * gelu_cubic * square)
        )
        to_gate[rows, :] = slope * up
        to_up[rows, :] = value
        act_ref[rows, :] = (value * up).astype(act_ref.dtype)
        return carry

    lax.fori_loop(0, in_ref.shape[0] // step, one, 0)
    part_ref[...] = matmul(act_ref[...], down[...]).astype(part_ref.dtype)


ROW_BLOCK = 256


def whole(array):
    return pl.BlockSpec(array.shape, lambda i: (0, 0), pipeline_mode=pl.Buffered(1))


def row_block(columns):
    return pl.BlockSpec((ROW_BLOCK, columns), lambda i: (i, 0))


def ffn_forward(rows_in, gate_up, down):
    rows, depth = rows_in.shape
    units, columns = gate_up.shape[1] // 2, down.shape[1]
    low = rows_in.dtype
    return pl.pallas_call(
        ffn_forward_kernel,
        grid=(rows // ROW_BLOCK,),
        in_specs=[row_block(depth), whole(gate_up), whole(down)],
        out_specs=[row_block(columns), row_block(units), row_block(units), row_block(units)],
        out_shape=[
            jax.ShapeDtypeStruct((rows, columns), low),
            jax.ShapeDtypeStruct((rows, units), low),
            jax.ShapeDtypeStruct((rows, units), jnp.float32),
            jax.ShapeDtypeStruct((rows, units), jnp.float32),
        ],
        scratch_shapes=[
            pltpu.VMEM((units, columns), low),
            pltpu.VMEM((ROW_BLOCK, 2 * units), jnp.float32),
        ],
        cost_estimate=busy(20),
        compiler_params=pltpu.CompilerParams(vmem_limit_bytes=VMEM_BYTES),
    )(rows_in, gate_up, down)


def gather_backward_kernel(
    own_ref, down_ref, gate_up_ref, to_gate_hbm, to_up_hbm, act_hbm, grad_ref, both_ref, part_ref,
    down_grad_ref, down, to_gate, to_up, act, act_sem, load_sems, send_sems, recv_sems, local_sem,
):
    units = down.shape[0]
    pieces, piece, columns = own_ref.shape
    rows = pieces * piece
    order = [cube_member(*flips) for flips in CUBE_ORDER]

    def loads(i):
        at = pl.ds(pl.multiple_of(order[i] * rows, rows), rows)
        slot = i % 2
        return (
            pltpu.make_async_copy(to_gate_hbm.at[at], to_gate.at[slot], load_sems.at[0, slot]),
            pltpu.make_async_copy(to_up_hbm.at[at], to_up.at[slot], load_sems.at[1, slot]),
        )

    def compute(i):
        if i + 1 < len(order):
            for load in loads(i + 1):
                load.start()
        for load in loads(i):
            load.wait()
        block, slot = order[i], i % 2
        at = pl.ds(pl.multiple_of(block * rows, rows), rows)
        source = own_ref if i == 0 else grad_ref.at[block]
        act_grad = contract_cols(source[...].reshape(rows, columns), down[...])
        both_ref[at, :units] = (act_grad * to_gate[slot]).astype(both_ref.dtype)
        both_ref[at, units:] = (act_grad * to_up[slot]).astype(both_ref.dtype)
        part = contract_cols(both_ref[at, :], gate_up_ref[...]).astype(part_ref.dtype)
        part_ref[block] = part.reshape(pieces, piece, part.shape[1])

    act_load = pltpu.make_async_copy(act_hbm, act, act_sem)
    act_load.start()
    for load in loads(0):
        load.start()
    pad_rows(down, down_ref)
    greet(cube_places())
    cube_spread(own_ref, grad_ref, send_sems, recv_sems, local_sem, compute)
    act_load.wait()
    grad = grad_ref[...].reshape(len(order) * rows, columns)
    down_grad = contract_rows(act[...], grad)
    down_grad_ref[...] = down_grad[: down_ref.shape[0]].astype(down_grad_ref.dtype)


def gather_backward(own, down, gate_up, to_gate, to_up, act, collective_id):
    rows, columns = own.shape
    members, piece = 16, 16
    depth, units = gate_up.shape[0], to_gate.shape[1]
    low = own.dtype
    vmem, anywhere = pl.BlockSpec(memory_space=pltpu.VMEM), pl.BlockSpec(memory_space=pl.ANY)
    grad, both, part, down_grad = pl.pallas_call(
        gather_backward_kernel,
        out_shape=[
            jax.ShapeDtypeStruct((members, rows // piece, piece, columns), low),
            jax.ShapeDtypeStruct((members * rows, 2 * units), low),
            jax.ShapeDtypeStruct((members, rows // piece, piece, depth), low),
            jax.ShapeDtypeStruct(down.shape, low),
        ],
        in_specs=[vmem, vmem, vmem, anywhere, anywhere, anywhere],
        out_specs=[vmem, vmem, vmem, vmem],
        scratch_shapes=[
            pltpu.VMEM((units, columns), low),
            pltpu.VMEM((2, rows, units), jnp.float32),
            pltpu.VMEM((2, rows, units), jnp.float32),
            pltpu.VMEM(act.shape, low),
            pltpu.SemaphoreType.DMA,
            pltpu.SemaphoreType.DMA((2, 2)),
            *gather_sems(21),
        ],
        cost_estimate=busy(35),
        compiler_params=pltpu.CompilerParams(
            collective_id=collective_id, has_side_effects=True, vmem_limit_bytes=60 * 2**20
        ),
    )(own.reshape(rows // piece, piece, columns), down, gate_up, to_gate, to_up, act)
    return both, part, down_grad


def sum_gradients_kernel(
    part_ref, down_ref, in_hbm, both_hbm, sum_ref, gate_up_ref, down_sum_ref,
    columns_in, both, arriving, both_sem, in_sems, far_send, far_recv, *scratch,
):
    cubes = down_ref.shape[0]
    far, others = other_cubes(cubes)
    step = columns_in.shape[2]
    blocks = gate_up_ref.shape[0] // step

    def load(i):
        at = pl.ds(i * step, step)
        return pltpu.make_async_copy(in_hbm.at[:, at], columns_in.at[i % 2], in_sems.at[i % 2])

    both_load = pltpu.make_async_copy(both_hbm, both, both_sem)
    both_load.start()
    load(0).start()

    def rows_of(i):
        if i == 0:
            both_load.wait()
        if i + 1 < blocks:
            load(i + 1).start()
        load(i).wait()
        rows = contract_rows(columns_in[i % 2], both[...])
        gate_up_ref[pl.ds(i * step, step), :] = rows.astype(gate_up_ref.dtype)

    def work(point):
        spread = ((0,), (1,), (2, 3), tuple(range(4, blocks)))
        for i in spread[point]:
            rows_of(i)

    greet((*cube_places(), *others))
    send = sender(far_send, far_recv)
    copies = [
        send(k, down_ref.at[place[0]], arriving.at[k], place) for k, place in enumerate(others)
    ]
    cube_sum(part_ref, sum_ref, *scratch, work=work)
    down_sum = down_ref[far].astype(jnp.float32)
    for k, copy in enumerate(copies):
        copy.wait_recv()
        down_sum = down_sum + arriving[k].astype(jnp.float32)
    down_sum_ref[...] = down_sum
    for copy in copies:
        copy.wait_send()


def sum_gradients(part, down, rows_in, both, collective_id):
    members, pieces, piece, depth = part.shape
    low = part.dtype
    step = 256
    vmem, anywhere = pl.BlockSpec(memory_space=pltpu.VMEM), pl.BlockSpec(memory_space=pl.ANY)
    total, gate_up, down_sum = pl.pallas_call(
        sum_gradients_kernel,
        out_shape=[
            jax.ShapeDtypeStruct((pieces, piece, depth), jnp.float32),
            jax.ShapeDtypeStruct((depth, both.shape[1]), low),
            jax.ShapeDtypeStruct(down.shape[1:], jnp.float32),
        ],
        in_specs=[vmem, vmem, anywhere, anywhere],
        out_specs=[vmem, vmem, vmem],
        scratch_shapes=[
            pltpu.VMEM((2, rows_in.shape[0], step), low),
            pltpu.VMEM(both.shape, low),
            pltpu.VMEM((down.shape[0] - 1, *down.shape[1:]), low),
            pltpu.SemaphoreType.DMA,
            pltpu.SemaphoreType.DMA((2,)),
            pltpu.SemaphoreType.DMA((down.shape[0] - 1,)),
            pltpu.SemaphoreType.DMA((down.shape[0] - 1,)),
            *cube_sum_scratch((pieces, piece, depth), low),
        ],
        cost_estimate=busy(35),
        compiler_params=pltpu.CompilerParams(
            collective_id=collective_id, has_side_effects=True, vmem_limit_bytes=60 * 2**20
        ),
    )(part, down, rows_in, both)
    return total.reshape(pieces * piece, depth), gate_up, down_sum


def owner_sum_kernel(planes, part_ref, out_ref, own_sum, leaving, arriving, z_send, z_recv, *scratch):
    plane, others, ring = other_planes(planes)
    greet((*plane_places()[:3], *others))
    plane_sum(part_ref, own_sum, *scratch)
    send = sender(z_send, z_recv)

    def narrow(i, carry):
        leaving[i] = own_sum[i].astype(leaving.dtype)
        return carry

    lax.fori_loop(0, planes, narrow, 0)
    copies = [
        send(k, leaving.at[ring[k]], arriving.at[k], place) for k, place in enumerate(others)
    ]
    for copy in copies:
        copy.wait_recv()

    value = own_sum[plane]
    for k in range(planes - 1):
        value = value + arriving[k].astype(jnp.float32)
    out_ref[...] = value
    for copy in copies:
        copy.wait_send()


def owner_sum(blocks, collective_id):
    members, planes, rows, columns = blocks.shape
    return pl.pallas_call(
        functools.partial(owner_sum_kernel, planes),
        out_shape=jax.ShapeDtypeStruct((rows, columns), jnp.float32),
        in_specs=[pl.BlockSpec(memory_space=pltpu.VMEM)],
        out_specs=pl.BlockSpec(memory_space=pltpu.VMEM),
        scratch_shapes=[
            pltpu.VMEM((planes, rows, columns), jnp.float32),
            pltpu.VMEM((planes, rows, columns), blocks.dtype),
            pltpu.VMEM((planes - 1, rows, columns), blocks.dtype),
            pltpu.SemaphoreType.DMA((planes - 1,)),
            pltpu.SemaphoreType.DMA((planes - 1,)),
            *plane_sum_scratch((planes, rows, columns), blocks.dtype),
        ],
        cost_estimate=busy(35),
        compiler_params=pltpu.CompilerParams(
            collective_id=collective_id, has_side_effects=True, vmem_limit_bytes=VMEM_BYTES
        ),
    )(blocks)


def gain_places(blocks, planes, offset, count, per, by_member):
    lane = lax.broadcasted_iota(jnp.int32, (256, blocks * per), 0)
    column = lax.broadcasted_iota(jnp.int32, (256, blocks * per), 1)
    inner = column % per
    places = ((lane == offset + inner) & (inner < count)).astype(jnp.float32).astype(jnp.bfloat16)
    listed = lax.broadcasted_iota(jnp.int32, (blocks, blocks * per), 0)
    block = lax.broadcasted_iota(jnp.int32, (blocks, blocks * per), 1) // per
    members = blocks // planes
    if not by_member:
        block = block % members * planes + block // members
    return places, listed == block


def spread_gain(rows, planes, *where):
    places, chosen = gain_places(rows.shape[0], planes, *where)
    return jnp.sum(jnp.where(chosen, matmul(rows, places), 0.0), axis=0, keepdims=True)


def collect_gain(vector, blocks, planes, *where):
    places, chosen = gain_places(blocks, planes, *where)
    return contract_cols(jnp.where(chosen, vector, 0.0).astype(jnp.bfloat16), places)


def inverse_of(values, count):
    return lax.rsqrt(jnp.sum(values * values, axis=-1, keepdims=True) / count + epsilon)


def back_of(grad_normed, normed, inverse, count):
    inner = jnp.sum(grad_normed * normed, axis=-1, keepdims=True) / count
    return inverse * (grad_normed - normed * inner)


def turn(values, cos_table, sin_table):
    half = values.shape[1] // 2
    first, second = values[:, :half], values[:, half:]
    return first * cos_table - second * sin_table, second * cos_table + first * sin_table


def attention_forward_kernel(
    gain_at, width_rows, row_ref, hidden_ref, packed_ref, cos_ref, sin_ref, segment_column, segment_row, placing_ref,
    placed_ref, middle_ref, raw_ref, mix_ref, probs_ref, query_ref, key_ref, value_ref, query_raw_ref,
    key_raw_ref, qkv_ref, output_ref, input_scale, query_scale, key_scale, attnout_scale, ffnin_scale, ffnout_scale,
    gain_rows,
):
    bf16, f32 = jnp.bfloat16, jnp.float32
    members, planes, piece, _ = packed_ref.shape
    blocks = members * planes
    padded = qkv_ref.shape[0] // blocks
    mix_rows = piece - padded
    width = hidden_ref.shape[1]
    local_rows, full_rows = hidden_ref.shape[0], row_ref.shape[0]
    head = key_ref.shape[1]
    heads = query_ref.shape[1] // head
    offset = pl.multiple_of(lax.axis_index("seq") * local_rows, local_rows)
    mine = pl.ds(offset, local_rows)
    for i in range(blocks):
        member, plane = i // planes, i % planes
        block = packed_ref[member, plane]
        qkv_ref[padded * i : padded * (i + 1), :] = block[:padded]
        natural = mix_rows * (plane * members + member)
        output_ref[natural : natural + mix_rows, :] = block[padded:, :width]
        gain_rows[i : i + 1, :] = block[width_rows : width_rows + 1, :256].astype(f32)
    rows = gain_rows[...].astype(bf16)
    (at, count), *others = gain_at
    input_scale[...] = spread_gain(rows, planes, at, count, padded, True)
    targets = (query_scale, key_scale, attnout_scale, ffnin_scale, ffnout_scale)
    for target, (at, count) in zip(targets, others):
        target[...] = spread_gain(rows, planes, at, count, count, False)

    row = row_ref[...].astype(f32)
    normed = (row * inverse_of(row, width) * input_scale[...]).astype(bf16)
    key_value = matmul(normed, qkv_ref[:, heads * head :])
    key_raw = key_value[:, :head]
    value_ref[...] = key_value[:, head:].astype(bf16)
    half = head // 2
    turned = turn(key_raw * inverse_of(key_raw, head) * key_scale[...], cos_ref[...], sin_ref[...])
    key_ref[:, :half], key_ref[:, half:] = turned[0].astype(bf16), turned[1].astype(bf16)

    row = row_ref[mine, :].astype(f32)
    normed = (row * inverse_of(row, width) * input_scale[...]).astype(bf16)
    own = matmul(normed, qkv_ref[:, : (heads + 1) * head])
    query_raw_ref[...] = own[:, : heads * head]
    key_raw_ref[...] = own[:, heads * head :]
    cos_table, sin_table = cos_ref[mine, :], sin_ref[mine, :]
    places = offset + lax.broadcasted_iota(jnp.int32, (local_rows, full_rows), 0)
    earlier = places >= lax.broadcasted_iota(jnp.int32, (local_rows, full_rows), 1)
    allowed = (segment_column[...] == segment_row[...]) & earlier
    for h in range(heads):
        at = h * head
        query_raw = query_raw_ref[:, at : at + head]
        turned = turn(
            query_raw * inverse_of(query_raw, head) * query_scale[...], cos_table, sin_table
        )
        scale = head ** (-0.5)
        query_ref[:, at : at + half] = (turned[0] * scale).astype(bf16)
        query_ref[:, at + half : at + head] = (turned[1] * scale).astype(bf16)
        scores = contract_cols(query_ref[:, at : at + head], key_ref[...])
        scores = jnp.where(allowed, scores, masked_score)
        weights = jnp.exp(scores - jnp.max(scores, axis=-1, keepdims=True))
        probs = weights / jnp.sum(weights, axis=-1, keepdims=True)
        probs_ref[h] = probs
        mix_ref[:, at : at + head] = matmul(probs.astype(bf16), value_ref[...]).astype(bf16)
    attn_raw = matmul(mix_ref[...], output_ref[...])
    raw_ref[...] = attn_raw
    middle = hidden_ref[...].astype(f32) + attn_raw * inverse_of(attn_raw, width) * attnout_scale[...]
    middle_ref[...] = middle
    ffn_in = (middle * inverse_of(middle, width) * ffnin_scale[...]).astype(bf16)
    placed_ref[...] = matmul(ffn_in, placing_ref[...]).astype(bf16)


def attention_forward(
    row_padded, hidden, packed, cos_full, sin_full, segment_column, segment_row, placing, gain_at, width_rows, padded,
    head_width,
):
    bf16, f32 = jnp.bfloat16, jnp.float32
    members, planes, piece, qkv_width = packed.shape
    blocks = members * planes
    local_rows, width = hidden.shape
    query_width = qkv_width - 2 * head_width
    heads = query_width // head_width
    full_rows = row_padded.shape[0]
    depth = blocks * padded
    shape = jax.ShapeDtypeStruct
    vmem = pl.BlockSpec(memory_space=pltpu.VMEM)
    out_shape = [
        shape((local_rows, depth), bf16),
        shape((local_rows, width), f32),
        shape((local_rows, width), f32),
        shape((local_rows, query_width), bf16),
        shape((heads, local_rows, full_rows), f32),
        shape((local_rows, query_width), bf16),
        shape((full_rows, head_width), bf16),
        shape((full_rows, head_width), bf16),
        shape((local_rows, query_width), f32),
        shape((local_rows, head_width), f32),
        shape((depth, qkv_width), bf16),
        shape((query_width, width), bf16),
        shape((1, depth), f32),
        shape((1, head_width), f32),
        shape((1, head_width), f32),
        shape((1, width), f32),
        shape((1, width), f32),
        shape((1, width), f32),
    ]
    return pl.pallas_call(
        functools.partial(attention_forward_kernel, gain_at, width_rows),
        out_shape=out_shape,
        in_specs=[vmem] * 8,
        out_specs=[vmem] * len(out_shape),
        scratch_shapes=[pltpu.VMEM((blocks, 256), f32)],
        cost_estimate=busy(20),
        compiler_params=pltpu.CompilerParams(vmem_limit_bytes=60 * 2**20),
    )(row_padded, hidden, packed, cos_full, sin_full, segment_column, segment_row, placing)


def attention_backward_kernel(
    gain_at, width_rows, planes, grad_ref, incoming_ref, middle_ref, raw_ref, mix_ref, probs_ref, query_ref, key_ref,
    value_ref, query_raw_ref, key_raw_ref, row_ref, qkv_ref, output_ref, cos_ref, sin_ref, input_scale,
    query_scale, key_scale, attnout_scale, ffnin_scale, ffnout_grad, by_device, by_member,
    input_grad_ref, blocks_ref, key_value, query_grad, low_ref, leaving, arriving, send_sem, recv_sem,
):
    bf16, f32 = jnp.bfloat16, jnp.float32
    members = blocks_ref.shape[0]
    blocks = members * planes
    padded = qkv_ref.shape[0] // blocks
    mix_rows = blocks_ref.shape[2] - padded
    local_rows, width = incoming_ref.shape
    head = key_ref.shape[1]
    heads = query_ref.shape[1] // head
    half = head // 2
    seq = lax.axis_index("seq")
    mine = pl.ds(pl.multiple_of(seq * local_rows, local_rows), local_rows)
    theirs = pl.ds(pl.multiple_of((1 - seq) * local_rows, local_rows), local_rows)
    partner = plane_places()[2]
    greet((partner,))

    ffn_in_grad = take_back(grad_ref[...], by_device[...])
    middle = middle_ref[...]
    inverse = inverse_of(middle, width)
    normed = middle * inverse
    ffnin_grad = jnp.sum(ffn_in_grad * normed, axis=0, keepdims=True)
    middle_grad = incoming_ref[...].astype(f32) + back_of(
        ffn_in_grad * ffnin_scale[...], normed, inverse, width
    )
    input_grad_ref[...] = middle_grad
    raw = raw_ref[...]
    inverse = inverse_of(raw, width)
    normed = raw * inverse
    attnout_grad = jnp.sum(middle_grad * normed, axis=0, keepdims=True)
    raw_grad = back_of(middle_grad * attnout_scale[...], normed, inverse, width).astype(bf16)
    mix_grad = contract_cols(raw_grad, output_ref[...]).astype(bf16)
    for h in range(heads):
        at = h * head
        grad = mix_grad[:, at : at + head]
        probs = probs_ref[h]
        prob_grad = contract_cols(grad, value_ref[...])
        delta = jnp.sum(prob_grad * probs, axis=-1, keepdims=True)
        score_grad = (probs * (prob_grad - delta)).astype(bf16)
        to_keys = contract_rows(score_grad, query_ref[:, at : at + head])
        to_values = contract_rows(probs.astype(bf16), grad)
        if h == 0:
            key_value[:, :head], key_value[:, head:] = to_keys, to_values
        else:
            key_value[:, :head] += to_keys
            key_value[:, head:] += to_values
        query_grad[:, at : at + head] = matmul(score_grad, key_ref[...])
    leaving[...] = key_value[theirs, :].astype(bf16)
    copy = sender(send_sem, recv_sem)(0, leaving, arriving, partner)

    output_grad = contract_rows(mix_ref[...], raw_grad).astype(bf16)
    cos_table, sin_table = cos_ref[mine, :], sin_ref[mine, :]

    def head_back(grad, raw, scale_ref):
        turned = jnp.concatenate(turn(grad, cos_table, -sin_table), axis=1)
        inverse = inverse_of(raw, head)
        normed = raw * inverse
        gain = jnp.sum(turned * normed, axis=0, keepdims=True)
        return back_of(turned * scale_ref[...], normed, inverse, head).astype(bf16), gain

    query_gain = jnp.zeros((1, head), f32)
    for h in range(heads):
        at = h * head
        low, gain = head_back(
            query_grad[:, at : at + head] * head ** (-0.5),
            query_raw_ref[:, at : at + head],
            query_scale,
        )
        low_ref[:, at : at + head] = low
        query_gain = query_gain + gain
    copy.wait_recv()
    total = key_value[mine, :] + arriving[...].astype(f32)
    low, key_gain = head_back(total[:, :head], key_raw_ref[...], key_scale)
    low_ref[:, heads * head : (heads + 1) * head] = low
    low_ref[:, (heads + 1) * head :] = total[:, head:].astype(bf16)

    row = row_ref[mine, :].astype(f32)
    inverse = inverse_of(row, width)
    normed = row * inverse
    normed_grad = contract_cols(low_ref[...], qkv_ref[...])
    input_gain = jnp.sum(normed_grad * normed, axis=0, keepdims=True)
    input_grad_ref[...] += take_back(
        back_of(normed_grad * input_scale[...], normed, inverse, width), by_member[...]
    )
    (at, count), *others = gain_at
    gains = collect_gain(input_gain, blocks, planes, at, count, padded, True)
    vectors = (query_gain, key_gain, attnout_grad, ffnin_grad, ffnout_grad[...])
    for vector, (at, count) in zip(vectors, others):
        gains = gains + collect_gain(vector, blocks, planes, at, count, count, False)
    normed = (normed * input_scale[...]).astype(bf16)
    weights = contract_rows(normed, low_ref[...])
    row_of = lax.broadcasted_iota(jnp.int32, (padded, 256), 0)
    columns = blocks_ref.shape[3]
    for i in range(blocks):
        member, plane = i // planes, i % planes
        piece = weights[padded * i : padded * (i + 1)]
        first = jnp.where(row_of == width_rows, gains[i : i + 1], piece[:, :256])
        blocks_ref[member, plane, :padded, :256] = first.astype(bf16)
        blocks_ref[member, plane, :padded, 256:] = piece[:, 256:].astype(bf16)
        natural = mix_rows * (plane * members + member)
        blocks_ref[member, plane, padded:, :width] = output_grad[natural : natural + mix_rows]
        blocks_ref[member, plane, padded:, width:] = jnp.zeros((mix_rows, columns - width), bf16)
    copy.wait_send()


def attention_backward(arrays, gain_at, width_rows, planes, mix_rows, collective_id):
    bf16, f32 = jnp.bfloat16, jnp.float32
    grad, incoming, query, key, qkv = arrays[0], arrays[1], arrays[6], arrays[7], arrays[12]
    local_rows, width = incoming.shape
    members = 8
    padded = qkv.shape[0] // (members * planes)
    pair = pltpu.VMEM((local_rows, 2 * key.shape[1]), bf16)
    shape = jax.ShapeDtypeStruct
    vmem = pl.BlockSpec(memory_space=pltpu.VMEM)
    return pl.pallas_call(
        functools.partial(attention_backward_kernel, gain_at, width_rows, planes),
        out_shape=[
            shape((local_rows, width), f32),
            shape((members, planes, padded + mix_rows, qkv.shape[1]), bf16),
        ],
        in_specs=[vmem] * len(arrays),
        out_specs=[vmem] * 2,
        scratch_shapes=[
            pltpu.VMEM((key.shape[0], 2 * key.shape[1]), f32),
            pltpu.VMEM(query.shape, f32),
            pltpu.VMEM((local_rows, qkv.shape[1]), bf16),
            pair,
            pair,
            pltpu.SemaphoreType.DMA((1,)),
            pltpu.SemaphoreType.DMA((1,)),
        ],
        cost_estimate=busy(30),
        compiler_params=pltpu.CompilerParams(
            collective_id=collective_id, has_side_effects=True, vmem_limit_bytes=60 * 2**20
        ),
    )(*arrays)


def body(
    tokens,
    segment_ids,
    cotangent,
    query_weight,
    key_weight,
    value_weight,
    output_weight,
    gate_weight,
    up_weight,
    down_weight,
    input_gain,
    query_gain,
    key_gain,
    attnout_gain,
    ffnin_gain,
    ffnout_gain,
):
    bf16, f32 = jnp.bfloat16, jnp.float32
    devices = lax.axis_size(ALL)
    members = lax.axis_size(PLANE)
    planes = lax.axis_size(PLANES)
    cubes = lax.axis_size("far")
    group = lax.axis_size(CUBE)
    width_rows = query_weight.shape[0]
    hidden_rows = down_weight.shape[0]
    head_width = key_weight.shape[1]
    query_width = query_weight.shape[1]
    head_count = query_width // head_width
    qkv_width = query_width + 2 * head_width
    mix_rows = output_weight.shape[0]
    padded = up_to(width_rows + 1, 8)
    width = devices * width_rows
    unit_count = cubes * hidden_rows
    unit_pad = up_to(unit_count, 128)
    by_device = place_columns(devices, members, planes, width_rows, padded, False)
    by_member = place_columns(devices, members, planes, width_rows, padded, True)

    def column_blocks(weight):
        pieces = weight.reshape(width_rows, cubes, group, hidden_rows)
        pieces = pieces.transpose(2, 0, 1, 3).reshape(group, width_rows, unit_count)
        return jnp.pad(
            pieces, ((0, 0), (0, padded - width_rows), (0, unit_pad - unit_count))
        )

    gate_up = jnp.concatenate([column_blocks(gate_weight), column_blocks(up_weight)], axis=2)
    gate_up = jnp.broadcast_to(gate_up[None], (cubes,) + gate_up.shape)
    gate_up = gate_up.reshape((devices,) + gate_up.shape[2:])

    gains = (input_gain, query_gain, key_gain, attnout_gain, ffnin_gain, ffnout_gain)
    gain_row = jnp.concatenate(gains)
    gain_widths = [g.shape[0] for g in gains]
    gain_row = jnp.pad(gain_row, (0, qkv_width - gain_row.shape[0]))
    qkv_local = jnp.concatenate([query_weight, key_weight, value_weight], axis=1)
    packed = jnp.concatenate([qkv_local, gain_row[None]], axis=0)
    packed = jnp.pad(packed, ((0, padded - width_rows - 1), (0, 0)))
    output_wide = jnp.pad(output_weight, ((0, 0), (0, qkv_width - output_weight.shape[1])))
    packed = jnp.concatenate([packed, output_wide], axis=0)
    packed_all = z_gather(packed, planes, 0)
    packed_all, down_full = weights_gather(packed_all, down_weight, cubes, 6)
    down_full = down_full.reshape(unit_count, down_weight.shape[1])
    gate_up, packed_all = lax.optimization_barrier((gate_up, packed_all))
    gate_up_full = exchange(gate_up, ALL).reshape(devices * padded, 2 * unit_pad)
    incoming = cotangent[0].astype(f32)
    local_rows = tokens.shape[1]
    offset = lax.axis_index("seq") * local_rows
    segment_row = segment_ids[0]

    def mine(rows):
        return lax.dynamic_slice_in_dim(rows, offset, local_rows)

    cos_full, sin_full = rope_tables(doc_positions(segment_row), head_width)

    other_half = [(0, 1), (1, 0)]
    first = lax.axis_index("seq") == 0
    other_tokens = lax.ppermute(tokens[0], "seq", other_half)
    row_tokens = jnp.concatenate(
        [
            jnp.where(first, tokens[0], other_tokens),
            jnp.where(first, other_tokens, tokens[0]),
        ]
    )
    row_padded = matmul(row_tokens, by_member).astype(bf16)
    gain_at, at = [], 0
    for count in gain_widths:
        gain_at.append((at, count))
        at += count
    (
        ffn_in_placed,
        middle,
        attn_raw,
        attn_flat,
        probs,
        queries,
        key_rows,
        value_rows,
        query_raw,
        key_raw,
        qkv_full,
        output_full,
        *scales,
    ) = attention_forward(
        row_padded,
        tokens[0],
        packed_all,
        cos_full,
        sin_full,
        mine(segment_row)[:, None],
        segment_row[None],
        by_device,
        gain_at,
        width_rows,
        padded,
        head_width,
    )
    ffnout_scale = scales.pop()

    cube_in = gather_rows(ffn_in_placed, 1)
    ffn_part, activated_low, to_gate, to_up = ffn_forward(cube_in, gate_up_full, down_full)
    ffn_raw = cube_scatter_sum(ffn_part, 2)
    inv_ffn = inverse_rms(ffn_raw)
    norm_ffn = ffn_raw * inv_ffn
    result = middle + norm_ffn * ffnout_scale
    ffnout_gain_grad = jnp.sum(incoming * norm_ffn, axis=0)
    ffn_raw_grad = rms_back(incoming * ffnout_scale, norm_ffn, inv_ffn).astype(bf16)

    gate_up_low, ffn_in_part, down_blocks = gather_backward(
        ffn_raw_grad, down_full, gate_up_full, to_gate, to_up, activated_low, 3
    )
    down_blocks = down_blocks.reshape(cubes, hidden_rows, down_weight.shape[1])
    ffn_in_grad, gate_up_blocks, down_wgrad = sum_gradients(
        ffn_in_part, down_blocks, cube_in, gate_up_low, 4
    )
    gate_up_terms = exchange(gate_up_blocks.reshape(devices, padded, 2 * unit_pad), ALL)
    input_grad, blocks = attention_backward(
        [
            ffn_in_grad,
            cotangent[0],
            middle,
            attn_raw,
            attn_flat,
            probs,
            queries,
            key_rows,
            value_rows,
            query_raw,
            key_raw,
            row_padded,
            qkv_full,
            output_full,
            cos_full,
            sin_full,
            *scales,
            ffnout_gain_grad[None],
            by_device,
            by_member,
        ],
        gain_at,
        width_rows,
        planes,
        mix_rows,
        7,
    )
    share = owner_sum(blocks, 5)
    gate_up_sum = jnp.sum(
        gate_up_terms.reshape(cubes, group, padded, 2 * unit_pad).astype(f32), axis=0
    )

    def unit_columns(total):
        total = total[:, :width_rows, :unit_count].reshape(
            group, width_rows, cubes, hidden_rows
        )
        return total.transpose(1, 2, 0, 3).reshape(width_rows, cubes * group * hidden_rows)

    gate_wgrad = unit_columns(gate_up_sum[:, :, :unit_pad])
    up_wgrad = unit_columns(gate_up_sum[:, :, unit_pad:])
    qkv_share, output_share = share[:padded], share[padded:, : output_weight.shape[1]]
    gain_shares, at = [], 0
    for count in gain_widths:
        gain_shares.append(qkv_share[width_rows, at : at + count])
        at += count
    return (
        result.astype(bf16)[None],
        input_grad[None],
        qkv_share[:width_rows, :query_width],
        qkv_share[:width_rows, query_width : query_width + head_width],
        qkv_share[:width_rows, query_width + head_width :],
        output_share,
        gate_wgrad,
        up_wgrad,
        down_wgrad,
        *gain_shares,
    )


def solution(mesh):
    dp, seq = mesh.shape["dp"], mesh.shape["seq"]
    split = Mesh(mesh.devices.reshape(dp // 8, 2, 2, 2, seq), ALL)
    rows = P(("far", "z", "x", "core"), "seq", None)
    matrix, vector = P(ALL, None), P(ALL)
    return jax.shard_map(
        body,
        mesh=split,
        in_specs=(rows, P(("far", "z", "x", "core"), None), rows) + (matrix,) * 7 + (vector,) * 6,
        out_specs=(rows, rows) + (matrix,) * 7 + (vector,) * 6,
        check_vma=False,
    )
```

```python
import functools

import jax
import jax.numpy as jnp
from jax import lax
from jax.experimental import pallas as pl
from jax.experimental.pallas import tpu as pltpu
from jax.sharding import Mesh
from jax.sharding import PartitionSpec as P

epsilon = 1e-06
rope_base = 1000000.0
masked_score = -1e30


def inverse_rms(values):
    return lax.rsqrt(jnp.mean(values * values, axis=-1, keepdims=True) + epsilon)


def rms_back(grad_normed, normed, inverse):
    return inverse * (grad_normed - normed * jnp.mean(grad_normed * normed, axis=-1, keepdims=True))


def doc_positions(segments):
    length = segments.shape[0]
    smaller = segments[None, :] < segments[:, None]
    starts = jnp.sum(smaller.astype(jnp.int32), axis=1)
    return (jnp.arange(length, dtype=jnp.int32) - starts).astype(jnp.float32)


def rope_tables(positions, head_width):
    half_width = head_width // 2
    frequency = rope_base ** (-(2.0 / head_width) * jnp.arange(half_width, dtype=jnp.float32))
    angles = positions[..., None] * frequency
    return (jnp.cos(angles), jnp.sin(angles))


def matmul(left, right):
    return jnp.dot(left, right, preferred_element_type=jnp.float32)


def contract_rows(left, right):
    return lax.dot_general(
        left, right, (((0,), (0,)), ((), ())), preferred_element_type=jnp.float32
    )


def contract_cols(left, right):
    return lax.dot_general(
        left, right, (((1,), (1,)), ((), ())), preferred_element_type=jnp.float32
    )


ALL = ("far", "z", "x", "core", "seq")
PLANES = ("far", "z")
CUBE = ("z", "x", "core", "seq")


def up_to(size, multiple):
    return (size + multiple - 1) // multiple * multiple


def place_columns(blocks, members, planes, rows, padded, by_member):
    source = lax.broadcasted_iota(jnp.int32, (blocks * rows, blocks * padded), 0)
    target = lax.broadcasted_iota(jnp.int32, (blocks * rows, blocks * padded), 1)
    block = source // rows
    if by_member:
        block = block % members * planes + block // members
    return (target == block * padded + source % rows).astype(jnp.bfloat16)


def take_back(padded_values, placing):
    high = lax.reduce_precision(padded_values, 8, 7)
    terms = jnp.concatenate([high, padded_values - high], axis=0).astype(jnp.bfloat16)
    both = contract_cols(terms, placing)
    rows = padded_values.shape[0]
    return both[:rows] + both[rows:]


PLANE = ("x", "core", "seq")

MESH_ID = pl.DeviceIdType.MESH
VMEM_BYTES = 48 * 2**20


def exchange(blocks, axes):
    return lax.all_to_all(blocks, axes, split_axis=0, concat_axis=0, tiled=True)


def busy(microseconds):
    return pl.CostEstimate(flops=0, bytes_accessed=microseconds * 3_000_000, transcendentals=0)


def shifted(flip_z, flip_x, flip_core, flip_y):
    far, *inner = (lax.axis_index(name) for name in ALL)
    flips = (flip_z, flip_x, flip_core, flip_y)
    return (far, *(1 - at if flip else at for at, flip in zip(inner, flips)))


def plane_places():
    def member(flip_x, flip_core, flip_y):
        _, _, x, core, seq = shifted(0, flip_x, flip_core, flip_y)
        return (x * 2 + core) * 2 + seq

    return shifted(0, 0, 1, 0), shifted(0, 1, 0, 0), shifted(0, 0, 0, 1), member


def cube_member(flip_z, flip_x, flip_y, flip_core):
    _, z, x, core, seq = shifted(flip_z, flip_x, flip_core, flip_y)
    return ((z * 2 + x) * 2 + core) * 2 + seq


def cube_places():
    return *plane_places()[:3], shifted(1, 0, 0, 0)


def other_planes(planes):
    far, z, x, core, seq = (lax.axis_index(name) for name in ALL)
    plane = far * 2 + z
    ring = [lax.rem(plane + k, planes) for k in range(1, planes)]
    return plane, [(at // 2, lax.rem(at, 2), x, core, seq) for at in ring], ring


def other_cubes(cubes):
    far, z, x, core, seq = (lax.axis_index(name) for name in ALL)
    return far, [(lax.rem(far + k, cubes), z, x, core, seq) for k in range(1, cubes)]


def greet(places):
    barrier = pltpu.get_barrier_semaphore()
    for place in places:
        pl.semaphore_signal(barrier, inc=1, device_id=place, device_id_type=MESH_ID)
    pl.semaphore_wait(barrier, len(places))


def sender(send_sems, recv_sems):
    def send(kind, source, target, place):
        copy = pltpu.make_async_remote_copy(
            src_ref=source,
            dst_ref=target,
            send_sem=send_sems.at[kind],
            recv_sem=recv_sems.at[kind],
            device_id=place,
            device_id_type=MESH_ID,
        )
        copy.start()
        return copy

    return send


def plane_spread(own_ref, out_ref, send_sems, recv_sems, local_sem):
    sibling, along_x, along_y, member = plane_places()
    half = own_ref.shape[0] // 2
    top, bottom = pl.ds(0, half), pl.ds(half, half)
    me = member(0, 0, 0)
    keep = pltpu.make_async_copy(own_ref, out_ref.at[me], local_sem)
    keep.start()
    send = sender(send_sems, recv_sems)

    def forward(kind, block, rows, place):
        return send(kind, out_ref.at[block, rows], out_ref.at[block, rows], place)

    own_x_top = send(1, own_ref.at[top], out_ref.at[me, top], along_x)
    own_y_bottom = send(3, own_ref.at[bottom], out_ref.at[me, bottom], along_y)
    own_sibling = send(0, own_ref, out_ref.at[me], sibling)
    own_x_bottom = send(2, own_ref.at[bottom], out_ref.at[me, bottom], along_x)
    own_y_top = send(4, own_ref.at[top], out_ref.at[me, top], along_y)
    x_block, y_block, diagonal = member(1, 0, 0), member(0, 0, 1), member(1, 0, 1)
    own_x_top.wait_recv()
    diagonal_top = forward(5, x_block, top, along_y)
    x_top = forward(7, x_block, top, sibling)
    own_y_bottom.wait_recv()
    diagonal_bottom = forward(6, y_block, bottom, along_x)
    y_bottom = forward(9, y_block, bottom, sibling)
    own_x_bottom.wait_recv()
    x_bottom = forward(8, x_block, bottom, sibling)
    own_y_top.wait_recv()
    y_top = forward(10, y_block, top, sibling)
    diagonal_top.wait_recv()
    far_top = forward(11, diagonal, top, sibling)
    diagonal_bottom.wait_recv()
    far_bottom = forward(12, diagonal, bottom, sibling)
    for copy in (own_sibling, x_top, y_bottom, x_bottom, y_top, far_top, far_bottom):
        copy.wait_recv()
    for copy in (
        own_x_top,
        own_y_bottom,
        own_sibling,
        own_x_bottom,
        own_y_top,
        diagonal_top,
        diagonal_bottom,
        x_top,
        y_bottom,
        x_bottom,
        y_top,
        far_top,
        far_bottom,
    ):
        copy.wait_send()
    keep.wait()


def cube_spread(own_ref, out_ref, send_sems, recv_sems, local_sem, compute=lambda i: None):
    sibling, along_x, along_y, along_z = cube_places()
    half = own_ref.shape[0] // 2
    top, bottom = pl.ds(0, half), pl.ds(half, half)
    me = cube_member(0, 0, 0, 0)
    keep = pltpu.make_async_copy(own_ref, out_ref.at[me], local_sem)
    keep.start()
    send = sender(send_sems, recv_sems)
    x_block, y_block, diagonal = (cube_member(0, *at, 0) for at in ((1, 0), (0, 1), (1, 1)))
    z_block, zx_block, zy_block, zd_block = (
        cube_member(1, *at, 0) for at in ((0, 0), (1, 0), (0, 1), (1, 1))
    )

    def half_on(kind, block, rows, place):
        return send(kind, out_ref.at[block, rows], out_ref.at[block, rows], place)

    def on(kind, block, place):
        return send(kind, out_ref.at[block], out_ref.at[block], place)

    own_x_top = send(1, own_ref.at[top], out_ref.at[me, top], along_x)
    own_y_bottom = send(3, own_ref.at[bottom], out_ref.at[me, bottom], along_y)
    own_z = send(13, own_ref, out_ref.at[me], along_z)
    own_sibling = send(0, own_ref, out_ref.at[me], sibling)
    own_x_bottom = send(2, own_ref.at[bottom], out_ref.at[me, bottom], along_x)
    own_y_top = send(4, own_ref.at[top], out_ref.at[me, top], along_y)
    compute(0)
    own_x_top.wait_recv()
    diagonal_top = half_on(5, x_block, top, along_y)
    x_top = half_on(7, x_block, top, sibling)
    own_y_bottom.wait_recv()
    diagonal_bottom = half_on(6, y_block, bottom, along_x)
    y_bottom = half_on(9, y_block, bottom, sibling)
    own_sibling.wait_recv()
    compute(1)
    own_z.wait_recv()
    z_to_x = on(14, z_block, along_x)
    z_to_y = on(15, z_block, along_y)
    z_near = on(16, z_block, sibling)
    own_x_bottom.wait_recv()
    x_bottom = half_on(8, x_block, bottom, sibling)
    own_y_top.wait_recv()
    y_top = half_on(10, y_block, top, sibling)
    compute(2)
    diagonal_top.wait_recv()
    far_top = half_on(11, diagonal, top, sibling)
    diagonal_bottom.wait_recv()
    far_bottom = half_on(12, diagonal, bottom, sibling)
    diagonal_z = on(17, diagonal, along_z)
    compute(3)
    compute(4)
    z_to_x.wait_recv()
    zx_near = on(18, zx_block, sibling)
    z_to_y.wait_recv()
    zy_near = on(19, zy_block, sibling)
    compute(5)
    compute(6)
    diagonal_z.wait_recv()
    zd_near = on(20, zd_block, sibling)
    compute(7)
    compute(8)
    last = (
        (x_top, x_bottom), (y_bottom, y_top), (far_top, far_bottom), (z_near,), (zx_near,), (zy_near,), (zd_near,),
    )
    for i, copies in enumerate(last):
        for copy in copies:
            copy.wait_recv()
        compute(9 + i)
    for copy in (
        own_x_top, own_y_bottom, own_z, own_sibling, own_x_bottom, own_y_top, diagonal_top, diagonal_bottom,
        z_to_x, z_to_y, diagonal_z,
    ):
        copy.wait_send()
    for copies in last:
        for copy in copies:
            copy.wait_send()
    keep.wait()


CUBE_ORDER = (
    (0, 0, 0, 0), (0, 0, 0, 1), (0, 1, 0, 0), (0, 0, 1, 0), (1, 0, 0, 0), (0, 1, 1, 0), (1, 1, 0, 0), (1, 0, 1, 0),
    (1, 1, 1, 0), (0, 1, 0, 1), (0, 0, 1, 1), (0, 1, 1, 1), (1, 0, 0, 1), (1, 1, 0, 1), (1, 0, 1, 1), (1, 1, 1, 1),
)


def weights_gather_kernel(cubes, own_ref, down_ref, out_ref, down_out, far_send, far_recv, own_sem, *sems):
    far, others = other_cubes(cubes)
    greet((*plane_places()[:3], *others))
    keep = pltpu.make_async_copy(down_ref, down_out.at[far], own_sem)
    keep.start()
    send = sender(far_send, far_recv)
    copies = [send(k, down_ref, down_out.at[far], place) for k, place in enumerate(others)]
    plane_spread(own_ref, out_ref, *sems)
    for copy in copies:
        copy.wait_recv()
    for copy in copies:
        copy.wait_send()
    keep.wait()


def z_gather_kernel(planes, own_ref, out_ref, send_sems, recv_sems, own_sem):
    plane, others, _ = other_planes(planes)
    greet(others)
    keep = pltpu.make_async_copy(own_ref, out_ref.at[plane], own_sem)
    keep.start()
    send = sender(send_sems, recv_sems)
    copies = [send(k, own_ref, out_ref.at[plane], place) for k, place in enumerate(others)]
    for copy in copies:
        copy.wait_recv()
    for copy in copies:
        copy.wait_send()
    keep.wait()


def gather_sems(count):
    return [
        pltpu.SemaphoreType.DMA((count,)),
        pltpu.SemaphoreType.DMA((count,)),
        pltpu.SemaphoreType.DMA,
    ]


def z_gather(local, planes, collective_id):
    return pl.pallas_call(
        functools.partial(z_gather_kernel, planes),
        out_shape=jax.ShapeDtypeStruct((planes, *local.shape), local.dtype),
        in_specs=[pl.BlockSpec(memory_space=pltpu.VMEM)],
        out_specs=pl.BlockSpec(memory_space=pl.ANY),
        scratch_shapes=[
            pltpu.SemaphoreType.DMA((planes - 1,)),
            pltpu.SemaphoreType.DMA((planes - 1,)),
            pltpu.SemaphoreType.DMA,
        ],
        cost_estimate=busy(20),
        compiler_params=pltpu.CompilerParams(
            collective_id=collective_id, has_side_effects=True, vmem_limit_bytes=VMEM_BYTES
        ),
    )(local)


def weights_gather(local, down, cubes, collective_id):
    members = 8
    anywhere = pl.BlockSpec(memory_space=pl.ANY)
    return pl.pallas_call(
        functools.partial(weights_gather_kernel, cubes),
        out_shape=[
            jax.ShapeDtypeStruct((members, *local.shape), local.dtype),
            jax.ShapeDtypeStruct((cubes, *down.shape), down.dtype),
        ],
        in_specs=[anywhere, anywhere],
        out_specs=[anywhere, anywhere],
        scratch_shapes=[
            pltpu.SemaphoreType.DMA((cubes - 1,)),
            pltpu.SemaphoreType.DMA((cubes - 1,)),
            pltpu.SemaphoreType.DMA,
            *gather_sems(13),
        ],
        cost_estimate=busy(30),
        compiler_params=pltpu.CompilerParams(
            collective_id=collective_id, has_side_effects=True, vmem_limit_bytes=VMEM_BYTES
        ),
    )(local, down)


def add_rows(target, sources, start, count):
    def one(i, carry):
        total = sources[0][i].astype(jnp.float32)
        for source in sources[1:]:
            total = total + source[i].astype(jnp.float32)
        target[i] = total.astype(target.dtype)
        return carry

    lax.fori_loop(start, start + count, one, 0)


def plane_sum(part_ref, own_sum, near, sums, from_x, from_y, far_x, far_y, send_sems, recv_sems):
    sibling, along_x, along_y, member = plane_places()
    rows = own_sum.shape[0]
    half = rows // 2
    top, bottom = pl.ds(0, half), pl.ds(half, half)
    send = sender(send_sems, recv_sems)
    chips = ((1, 1), (1, 0), (0, 1), (0, 0))
    mine = [part_ref.at[member(at_x, 0, at_y)] for at_x, at_y in chips]
    to_sibling = [
        send(k, part_ref.at[member(at_x, 1, at_y)], near.at[k], sibling)
        for k, (at_x, at_y) in enumerate(chips)
    ]
    to_sibling[0].wait_recv()
    add_rows(sums.at[0], (mine[0], near.at[0]), 0, rows)
    diagonal_x = send(4, sums.at[0, bottom], far_x.at[bottom], along_x)
    diagonal_y = send(5, sums.at[0, top], far_y.at[top], along_y)
    to_sibling[1].wait_recv()
    add_rows(sums.at[1], (mine[1], near.at[1]), half, half)
    direct_x = send(6, sums.at[1, bottom], from_x.at[bottom], along_x)
    to_sibling[2].wait_recv()
    add_rows(sums.at[2], (mine[2], near.at[2]), 0, half)
    direct_y = send(7, sums.at[2, top], from_y.at[top], along_y)
    to_sibling[3].wait_recv()
    diagonal_y.wait_recv()
    add_rows(sums.at[1], (mine[1], near.at[1], far_y), 0, half)
    joint_x = send(8, sums.at[1, top], from_x.at[top], along_x)
    diagonal_x.wait_recv()
    add_rows(sums.at[2], (mine[2], near.at[2], far_x), half, half)
    joint_y = send(9, sums.at[2, bottom], from_y.at[bottom], along_y)
    direct_x.wait_recv()
    direct_y.wait_recv()
    joint_x.wait_recv()
    joint_y.wait_recv()
    add_rows(own_sum, (mine[3], near.at[3], from_x, from_y), 0, rows)
    for copy in (*to_sibling, diagonal_x, diagonal_y, direct_x, direct_y, joint_x, joint_y):
        copy.wait_send()


def cube_sum(
    part_hbm, own_sum, mine, near, via_z, zx_in, zy_in, far_x, far_y, from_x, from_y, from_z, load_sems, send_sems,
    recv_sems, work=lambda point: None,
):
    sibling, along_x, along_y, along_z = cube_places()
    pieces = own_sum.shape[0]
    half = pieces // 2
    top, bottom = pl.ds(0, half), pl.ds(half, half)
    send = sender(send_sems, recv_sems)
    chips = ((1, 1, 1), (1, 1, 0), (1, 0, 1), (0, 1, 0), (0, 0, 1), (0, 1, 1), (1, 0, 0), (0, 0, 0))
    z_diagonal, z_x, z_y, at_x, at_y, diagonal, at_z, here = range(8)
    to_sibling = [
        send(k, part_hbm.at[cube_member(*chip, 1)], near.at[k], sibling)
        for k, chip in enumerate(chips)
    ]
    loads = [
        pltpu.make_async_copy(part_hbm.at[cube_member(*chip, 0)], mine.at[k], load_sems.at[k])
        for k, chip in enumerate(chips)
    ]
    for load in loads:
        load.start()

    def both_in(k):
        to_sibling[k].wait_recv()
        loads[k].wait()

    def add(k, others=(), start=0, count=pieces):
        add_rows(near.at[k], (mine.at[k], near.at[k], *others), start, count)

    work(0)
    both_in(z_diagonal)
    add(z_diagonal)
    diagonal_z = send(8, near.at[z_diagonal], via_z, along_z)
    both_in(z_x)
    add(z_x)
    zx_out = send(9, near.at[z_x], zx_in, along_x)
    both_in(z_y)
    add(z_y)
    zy_out = send(10, near.at[z_y], zy_in, along_y)
    both_in(at_x)
    add(at_x, (), half, half)
    direct_x = send(13, near.at[at_x, bottom], from_x.at[bottom], along_x)
    both_in(at_y)
    add(at_y, (), 0, half)
    direct_y = send(14, near.at[at_y, top], from_y.at[top], along_y)
    both_in(diagonal)
    both_in(at_z)
    work(1)
    diagonal_z.wait_recv()
    add(diagonal, (via_z,))
    diagonal_x = send(11, near.at[diagonal, bottom], far_x.at[bottom], along_x)
    diagonal_y = send(12, near.at[diagonal, top], far_y.at[top], along_y)
    zx_out.wait_recv()
    zy_out.wait_recv()
    add(at_z, (zx_in, zy_in))
    joint_z = send(15, near.at[at_z], from_z, along_z)
    work(2)
    diagonal_y.wait_recv()
    add(at_x, (far_y,), 0, half)
    joint_x = send(16, near.at[at_x, top], from_x.at[top], along_x)
    diagonal_x.wait_recv()
    add(at_y, (far_x,), half, half)
    joint_y = send(17, near.at[at_y, bottom], from_y.at[bottom], along_y)
    both_in(here)
    work(3)
    for copy in (direct_x, direct_y, joint_z, joint_x, joint_y):
        copy.wait_recv()
    add_rows(own_sum, (mine.at[here], near.at[here], from_x, from_y, from_z), 0, pieces)
    for copy in (
        *to_sibling, diagonal_z, zx_out, zy_out, direct_x, direct_y, diagonal_x, diagonal_y, joint_z, joint_x, joint_y,
    ):
        copy.wait_send()


def cube_sum_kernel(part_ref, out_ref, *scratch):
    greet(cube_places())
    cube_sum(part_ref, out_ref, *scratch)


def cube_sum_scratch(shape, dtype):
    return [
        pltpu.VMEM((8, *shape), dtype),
        pltpu.VMEM((8, *shape), dtype),
        *[pltpu.VMEM(shape, dtype)] * 8,
        pltpu.SemaphoreType.DMA((8,)),
        pltpu.SemaphoreType.DMA((18,)),
        pltpu.SemaphoreType.DMA((18,)),
    ]


def plane_sum_scratch(shape, dtype):
    block = pltpu.VMEM(shape, dtype)
    return [
        pltpu.VMEM((4, *shape), dtype),
        pltpu.VMEM((3, *shape), dtype),
        block,
        block,
        block,
        block,
        pltpu.SemaphoreType.DMA((10,)),
        pltpu.SemaphoreType.DMA((10,)),
    ]


def cube_scatter_sum(partial, collective_id):
    shape = partial.shape[1:]
    out = pl.pallas_call(
        cube_sum_kernel,
        out_shape=jax.ShapeDtypeStruct(shape, jnp.float32),
        in_specs=[pl.BlockSpec(memory_space=pl.ANY)],
        out_specs=pl.BlockSpec(memory_space=pltpu.VMEM),
        scratch_shapes=cube_sum_scratch(shape, partial.dtype),
        cost_estimate=busy(35),
        compiler_params=pltpu.CompilerParams(
            collective_id=collective_id, has_side_effects=True, vmem_limit_bytes=VMEM_BYTES
        ),
    )(partial)
    return out.reshape(shape[0] * shape[1], shape[2])


gelu_inner = 0.7978845608028654
gelu_cubic = 0.044715


def pad_rows(target, source):
    rows = source.shape[0]
    target[pl.ds(0, rows)] = source[...]
    if target.shape[0] > rows:
        extra = target.shape[0] - rows
        target[pl.ds(rows, extra)] = jnp.zeros((extra, target.shape[1]), target.dtype)


def block_order(rows):
    order = [cube_member(*flips) for flips in CUBE_ORDER]
    return order, [pl.ds(pl.multiple_of(block * rows, rows), rows) for block in order]


def gather_forward_kernel(
    own_ref, gate_up_ref, down_ref, rows_hbm, part_hbm, act_hbm, to_gate_hbm, to_up_hbm,
    rows_in, down, proj, part, act, to_gate, to_up, put_sems, send_sems, recv_sems, local_sem,
):
    units = act.shape[2]
    pieces, piece, columns = own_ref.shape
    rows = pieces * piece
    order, places = block_order(rows)
    step = 32

    def puts(i):
        slot, block, at = i % 2, order[i], places[i]
        source = own_ref if i == 0 else rows_in.at[block]
        pairs = (
            (source, rows_hbm.at[block]),
            (part.at[slot], part_hbm.at[block]),
            (act.at[slot], act_hbm.at[at]),
            (to_gate.at[slot], to_gate_hbm.at[at]),
            (to_up.at[slot], to_up_hbm.at[at]),
        )
        return [
            pltpu.make_async_copy(*pair, put_sems.at[k, slot]) for k, pair in enumerate(pairs)
        ]

    def compute(i):
        if i >= 2:
            for put in puts(i - 2):
                put.wait()
        slot = i % 2
        source = own_ref if i == 0 else rows_in.at[order[i]]
        proj[...] = matmul(source[...].reshape(rows, columns), gate_up_ref[...])

        def one(j, carry):
            at = pl.ds(pl.multiple_of(j * step, step), step)
            gate, up = proj[at, :units], proj[at, units:]
            square = gate * gate
            bend = jnp.tanh(gelu_inner * gate * (1.0 + gelu_cubic * square))
            half = 0.5 * (1.0 + bend)
            value = gate * half
            slope = half + 0.5 * gate * (1.0 - bend * bend) * (
                gelu_inner * (1.0 + 3.0 * gelu_cubic * square)
            )
            to_gate[slot, at, :] = slope * up
            to_up[slot, at, :] = value
            act[slot, at, :] = (value * up).astype(act.dtype)
            return carry

        lax.fori_loop(0, rows // step, one, 0)
        result = matmul(act[slot], down[...]).astype(part.dtype)
        part[slot] = result.reshape(pieces, piece, result.shape[1])
        for put in puts(i):
            put.start()

    pad_rows(down, down_ref)
    greet(cube_places())
    cube_spread(own_ref, rows_in, send_sems, recv_sems, local_sem, compute)
    for i in (len(order) - 2, len(order) - 1):
        for put in puts(i):
            put.wait()


def gather_forward(own, gate_up, down, collective_id):
    rows, depth = own.shape
    members, piece = 16, 16
    pieces = rows // piece
    units, columns = gate_up.shape[1] // 2, down.shape[1]
    low, wide = own.dtype, jnp.float32
    shape = jax.ShapeDtypeStruct
    vmem, anywhere = pl.BlockSpec(memory_space=pltpu.VMEM), pl.BlockSpec(memory_space=pl.ANY)
    return pl.pallas_call(
        gather_forward_kernel,
        out_shape=[
            shape((members, pieces, piece, depth), low),
            shape((members, pieces, piece, columns), low),
            shape((members * rows, units), low),
            shape((members * rows, units), wide),
            shape((members * rows, units), wide),
        ],
        in_specs=[vmem, vmem, vmem],
        out_specs=[anywhere] * 5,
        scratch_shapes=[
            pltpu.VMEM((members, pieces, piece, depth), low),
            pltpu.VMEM((units, columns), low),
            pltpu.VMEM((rows, 2 * units), wide),
            pltpu.VMEM((2, pieces, piece, columns), low),
            pltpu.VMEM((2, rows, units), low),
            pltpu.VMEM((2, rows, units), wide),
            pltpu.VMEM((2, rows, units), wide),
            pltpu.SemaphoreType.DMA((5, 2)),
            *gather_sems(21),
        ],
        cost_estimate=busy(40),
        compiler_params=pltpu.CompilerParams(
            collective_id=collective_id, has_side_effects=True, vmem_limit_bytes=60 * 2**20
        ),
    )(own.reshape(pieces, piece, depth), gate_up, down)


def gather_backward_kernel(
    own_ref, down_ref, gate_up_ref, to_gate_hbm, to_up_hbm, act_hbm, both_hbm, part_hbm, down_grad_ref,
    grad, down, to_gate, to_up, act, both, part, act_sem, load_sems, put_sems, send_sems, recv_sems, local_sem,
):
    units = down.shape[0]
    pieces, piece, columns = own_ref.shape
    rows = pieces * piece
    order, places = block_order(rows)

    def loads(i):
        slot, at = i % 2, places[i]
        return (
            pltpu.make_async_copy(to_gate_hbm.at[at], to_gate.at[slot], load_sems.at[0, slot]),
            pltpu.make_async_copy(to_up_hbm.at[at], to_up.at[slot], load_sems.at[1, slot]),
        )

    def puts(i):
        slot = i % 2
        return (
            pltpu.make_async_copy(both.at[slot], both_hbm.at[places[i]], put_sems.at[0, slot]),
            pltpu.make_async_copy(part.at[slot], part_hbm.at[order[i]], put_sems.at[1, slot]),
        )

    def compute(i):
        if i + 1 < len(order):
            for load in loads(i + 1):
                load.start()
        for load in loads(i):
            load.wait()
        if i >= 2:
            for put in puts(i - 2):
                put.wait()
        slot = i % 2
        source = own_ref if i == 0 else grad.at[order[i]]
        act_grad = contract_cols(source[...].reshape(rows, columns), down[...])
        both[slot, :, :units] = (act_grad * to_gate[slot]).astype(both.dtype)
        both[slot, :, units:] = (act_grad * to_up[slot]).astype(both.dtype)
        result = contract_cols(both[slot], gate_up_ref[...]).astype(part.dtype)
        part[slot] = result.reshape(pieces, piece, result.shape[1])
        for put in puts(i):
            put.start()

    act_load = pltpu.make_async_copy(act_hbm, act, act_sem)
    act_load.start()
    for load in loads(0):
        load.start()
    pad_rows(down, down_ref)
    greet(cube_places())
    cube_spread(own_ref, grad, send_sems, recv_sems, local_sem, compute)
    act_load.wait()
    whole = grad[...].reshape(len(order) * rows, columns)
    down_grad = contract_rows(act[...], whole)
    down_grad_ref[...] = down_grad[: down_ref.shape[0]].astype(down_grad_ref.dtype)
    for i in (len(order) - 2, len(order) - 1):
        for put in puts(i):
            put.wait()


def gather_backward(own, down, gate_up, to_gate, to_up, act, collective_id):
    rows, columns = own.shape
    members, piece = 16, 16
    pieces = rows // piece
    depth, units = gate_up.shape[0], to_gate.shape[1]
    low, wide = own.dtype, jnp.float32
    shape = jax.ShapeDtypeStruct
    vmem, anywhere = pl.BlockSpec(memory_space=pltpu.VMEM), pl.BlockSpec(memory_space=pl.ANY)
    return pl.pallas_call(
        gather_backward_kernel,
        out_shape=[
            shape((members * rows, 2 * units), low),
            shape((members, pieces, piece, depth), low),
            shape(down.shape, low),
        ],
        in_specs=[vmem, vmem, vmem, anywhere, anywhere, anywhere],
        out_specs=[anywhere, anywhere, vmem],
        scratch_shapes=[
            pltpu.VMEM((members, pieces, piece, columns), low),
            pltpu.VMEM((units, columns), low),
            pltpu.VMEM((2, rows, units), wide),
            pltpu.VMEM((2, rows, units), wide),
            pltpu.VMEM(act.shape, low),
            pltpu.VMEM((2, rows, 2 * units), low),
            pltpu.VMEM((2, pieces, piece, depth), low),
            pltpu.SemaphoreType.DMA,
            pltpu.SemaphoreType.DMA((2, 2)),
            pltpu.SemaphoreType.DMA((2, 2)),
            *gather_sems(21),
        ],
        cost_estimate=busy(45),
        compiler_params=pltpu.CompilerParams(
            collective_id=collective_id, has_side_effects=True, vmem_limit_bytes=60 * 2**20
        ),
    )(own.reshape(pieces, piece, columns), down, gate_up, to_gate, to_up, act)


def sum_gradients_kernel(
    part_ref, down_ref, in_hbm, both_hbm, sum_ref, gate_up_ref, down_sum_ref,
    columns_in, both, arriving, both_sem, in_sems, far_send, far_recv, *scratch,
):
    cubes = down_ref.shape[0]
    far, others = other_cubes(cubes)
    step = columns_in.shape[2]
    blocks = gate_up_ref.shape[0] // step

    def load(i):
        at = pl.ds(i * step, step)
        return pltpu.make_async_copy(in_hbm.at[:, at], columns_in.at[i % 2], in_sems.at[i % 2])

    both_load = pltpu.make_async_copy(both_hbm, both, both_sem)
    both_load.start()
    load(0).start()

    def rows_of(i):
        if i == 0:
            both_load.wait()
        if i + 1 < blocks:
            load(i + 1).start()
        load(i).wait()
        rows = contract_rows(columns_in[i % 2], both[...])
        gate_up_ref[pl.ds(i * step, step), :] = rows.astype(gate_up_ref.dtype)

    def work(point):
        spread = ((), (0, 1), (2, 3), tuple(range(4, blocks)))
        for i in spread[point]:
            rows_of(i)

    greet((*cube_places(), *others))
    send = sender(far_send, far_recv)
    copies = [
        send(k, down_ref.at[place[0]], arriving.at[k], place) for k, place in enumerate(others)
    ]
    cube_sum(part_ref, sum_ref, *scratch, work=work)
    down_sum = down_ref[far].astype(jnp.float32)
    for k, copy in enumerate(copies):
        copy.wait_recv()
        down_sum = down_sum + arriving[k].astype(jnp.float32)
    down_sum_ref[...] = down_sum
    for copy in copies:
        copy.wait_send()


def sum_gradients(part, down, rows_in, both, collective_id):
    members, pieces, piece, depth = part.shape
    low = part.dtype
    step = 256
    vmem, anywhere = pl.BlockSpec(memory_space=pltpu.VMEM), pl.BlockSpec(memory_space=pl.ANY)
    total, gate_up, down_sum = pl.pallas_call(
        sum_gradients_kernel,
        out_shape=[
            jax.ShapeDtypeStruct((pieces, piece, depth), jnp.float32),
            jax.ShapeDtypeStruct((depth, both.shape[1]), low),
            jax.ShapeDtypeStruct(down.shape[1:], jnp.float32),
        ],
        in_specs=[anywhere, vmem, anywhere, anywhere],
        out_specs=[vmem, vmem, vmem],
        scratch_shapes=[
            pltpu.VMEM((2, rows_in.shape[0], step), low),
            pltpu.VMEM(both.shape, low),
            pltpu.VMEM((down.shape[0] - 1, *down.shape[1:]), low),
            pltpu.SemaphoreType.DMA,
            pltpu.SemaphoreType.DMA((2,)),
            pltpu.SemaphoreType.DMA((down.shape[0] - 1,)),
            pltpu.SemaphoreType.DMA((down.shape[0] - 1,)),
            *cube_sum_scratch((pieces, piece, depth), low),
        ],
        cost_estimate=busy(35),
        compiler_params=pltpu.CompilerParams(
            collective_id=collective_id, has_side_effects=True, vmem_limit_bytes=60 * 2**20
        ),
    )(part, down, rows_in, both)
    return total.reshape(pieces * piece, depth), gate_up, down_sum


def owner_sum_kernel(planes, part_ref, out_ref, own_sum, leaving, arriving, z_send, z_recv, *scratch):
    plane, others, ring = other_planes(planes)
    greet((*plane_places()[:3], *others))
    plane_sum(part_ref, own_sum, *scratch)
    send = sender(z_send, z_recv)

    def narrow(i, carry):
        leaving[i] = own_sum[i].astype(leaving.dtype)
        return carry

    lax.fori_loop(0, planes, narrow, 0)
    copies = [
        send(k, leaving.at[ring[k]], arriving.at[k], place) for k, place in enumerate(others)
    ]
    for copy in copies:
        copy.wait_recv()

    value = own_sum[plane]
    for k in range(planes - 1):
        value = value + arriving[k].astype(jnp.float32)
    out_ref[...] = value
    for copy in copies:
        copy.wait_send()


def owner_sum(blocks, collective_id):
    members, planes, rows, columns = blocks.shape
    return pl.pallas_call(
        functools.partial(owner_sum_kernel, planes),
        out_shape=jax.ShapeDtypeStruct((rows, columns), jnp.float32),
        in_specs=[pl.BlockSpec(memory_space=pltpu.VMEM)],
        out_specs=pl.BlockSpec(memory_space=pltpu.VMEM),
        scratch_shapes=[
            pltpu.VMEM((planes, rows, columns), jnp.float32),
            pltpu.VMEM((planes, rows, columns), blocks.dtype),
            pltpu.VMEM((planes - 1, rows, columns), blocks.dtype),
            pltpu.SemaphoreType.DMA((planes - 1,)),
            pltpu.SemaphoreType.DMA((planes - 1,)),
            *plane_sum_scratch((planes, rows, columns), blocks.dtype),
        ],
        cost_estimate=busy(35),
        compiler_params=pltpu.CompilerParams(
            collective_id=collective_id, has_side_effects=True, vmem_limit_bytes=VMEM_BYTES
        ),
    )(blocks)


def gain_places(blocks, planes, offset, count, per, by_member):
    lane = lax.broadcasted_iota(jnp.int32, (256, blocks * per), 0)
    column = lax.broadcasted_iota(jnp.int32, (256, blocks * per), 1)
    inner = column % per
    places = ((lane == offset + inner) & (inner < count)).astype(jnp.float32).astype(jnp.bfloat16)
    listed = lax.broadcasted_iota(jnp.int32, (blocks, blocks * per), 0)
    block = lax.broadcasted_iota(jnp.int32, (blocks, blocks * per), 1) // per
    members = blocks // planes
    if not by_member:
        block = block % members * planes + block // members
    return places, listed == block


def spread_gain(rows, planes, *where):
    places, chosen = gain_places(rows.shape[0], planes, *where)
    return jnp.sum(jnp.where(chosen, matmul(rows, places), 0.0), axis=0, keepdims=True)


def collect_gain(vector, blocks, planes, *where):
    places, chosen = gain_places(blocks, planes, *where)
    return contract_cols(jnp.where(chosen, vector, 0.0).astype(jnp.bfloat16), places)


def inverse_of(values, count):
    return lax.rsqrt(jnp.sum(values * values, axis=-1, keepdims=True) / count + epsilon)


def back_of(grad_normed, normed, inverse, count):
    inner = jnp.sum(grad_normed * normed, axis=-1, keepdims=True) / count
    return inverse * (grad_normed - normed * inner)


def turn(values, cos_table, sin_table):
    half = values.shape[1] // 2
    first, second = values[:, :half], values[:, half:]
    return first * cos_table - second * sin_table, second * cos_table + first * sin_table


def attention_forward_kernel(
    gain_at, width_rows, row_ref, hidden_ref, packed_ref, cos_ref, sin_ref, segment_column, segment_row, placing_ref,
    placed_ref, middle_ref, raw_ref, mix_ref, probs_ref, query_ref, key_ref, value_ref, query_raw_ref,
    key_raw_ref, qkv_ref, output_ref, input_scale, query_scale, key_scale, attnout_scale, ffnin_scale, ffnout_scale,
    gain_rows,
):
    bf16, f32 = jnp.bfloat16, jnp.float32
    members, planes, piece, _ = packed_ref.shape
    blocks = members * planes
    padded = qkv_ref.shape[0] // blocks
    mix_rows = piece - padded
    width = hidden_ref.shape[1]
    local_rows, full_rows = hidden_ref.shape[0], row_ref.shape[0]
    head = key_ref.shape[1]
    heads = query_ref.shape[1] // head
    offset = pl.multiple_of(lax.axis_index("seq") * local_rows, local_rows)
    mine = pl.ds(offset, local_rows)
    for i in range(blocks):
        member, plane = i // planes, i % planes
        block = packed_ref[member, plane]
        qkv_ref[padded * i : padded * (i + 1), :] = block[:padded]
        natural = mix_rows * (plane * members + member)
        output_ref[natural : natural + mix_rows, :] = block[padded:, :width]
        gain_rows[i : i + 1, :] = block[width_rows : width_rows + 1, :256].astype(f32)
    rows = gain_rows[...].astype(bf16)
    (at, count), *others = gain_at
    input_scale[...] = spread_gain(rows, planes, at, count, padded, True)
    targets = (query_scale, key_scale, attnout_scale, ffnin_scale, ffnout_scale)
    for target, (at, count) in zip(targets, others):
        target[...] = spread_gain(rows, planes, at, count, count, False)

    row = row_ref[...].astype(f32)
    normed = (row * inverse_of(row, width) * input_scale[...]).astype(bf16)
    key_value = matmul(normed, qkv_ref[:, heads * head :])
    key_raw = key_value[:, :head]
    value_ref[...] = key_value[:, head:].astype(bf16)
    half = head // 2
    turned = turn(key_raw * inverse_of(key_raw, head) * key_scale[...], cos_ref[...], sin_ref[...])
    key_ref[:, :half], key_ref[:, half:] = turned[0].astype(bf16), turned[1].astype(bf16)

    row = row_ref[mine, :].astype(f32)
    normed = (row * inverse_of(row, width) * input_scale[...]).astype(bf16)
    own = matmul(normed, qkv_ref[:, : (heads + 1) * head])
    query_raw_ref[...] = own[:, : heads * head]
    key_raw_ref[...] = own[:, heads * head :]
    cos_table, sin_table = cos_ref[mine, :], sin_ref[mine, :]
    places = offset + lax.broadcasted_iota(jnp.int32, (local_rows, full_rows), 0)
    earlier = places >= lax.broadcasted_iota(jnp.int32, (local_rows, full_rows), 1)
    allowed = (segment_column[...] == segment_row[...]) & earlier
    for h in range(heads):
        at = h * head
        query_raw = query_raw_ref[:, at : at + head]
        turned = turn(
            query_raw * inverse_of(query_raw, head) * query_scale[...], cos_table, sin_table
        )
        scale = head ** (-0.5)
        query_ref[:, at : at + half] = (turned[0] * scale).astype(bf16)
        query_ref[:, at + half : at + head] = (turned[1] * scale).astype(bf16)
        scores = contract_cols(query_ref[:, at : at + head], key_ref[...])
        scores = jnp.where(allowed, scores, masked_score)
        weights = jnp.exp(scores - jnp.max(scores, axis=-1, keepdims=True))
        probs = weights / jnp.sum(weights, axis=-1, keepdims=True)
        probs_ref[h] = probs
        mix_ref[:, at : at + head] = matmul(probs.astype(bf16), value_ref[...]).astype(bf16)
    attn_raw = matmul(mix_ref[...], output_ref[...])
    raw_ref[...] = attn_raw
    middle = hidden_ref[...].astype(f32) + attn_raw * inverse_of(attn_raw, width) * attnout_scale[...]
    middle_ref[...] = middle
    ffn_in = (middle * inverse_of(middle, width) * ffnin_scale[...]).astype(bf16)
    placed_ref[...] = matmul(ffn_in, placing_ref[...]).astype(bf16)


def attention_forward(
    row_padded, hidden, packed, cos_full, sin_full, segment_column, segment_row, placing, gain_at, width_rows, padded,
    head_width,
):
    bf16, f32 = jnp.bfloat16, jnp.float32
    members, planes, piece, qkv_width = packed.shape
    blocks = members * planes
    local_rows, width = hidden.shape
    query_width = qkv_width - 2 * head_width
    heads = query_width // head_width
    full_rows = row_padded.shape[0]
    depth = blocks * padded
    shape = jax.ShapeDtypeStruct
    vmem = pl.BlockSpec(memory_space=pltpu.VMEM)
    out_shape = [
        shape((local_rows, depth), bf16),
        shape((local_rows, width), f32),
        shape((local_rows, width), f32),
        shape((local_rows, query_width), bf16),
        shape((heads, local_rows, full_rows), f32),
        shape((local_rows, query_width), bf16),
        shape((full_rows, head_width), bf16),
        shape((full_rows, head_width), bf16),
        shape((local_rows, query_width), f32),
        shape((local_rows, head_width), f32),
        shape((depth, qkv_width), bf16),
        shape((query_width, width), bf16),
        shape((1, depth), f32),
        shape((1, head_width), f32),
        shape((1, head_width), f32),
        shape((1, width), f32),
        shape((1, width), f32),
        shape((1, width), f32),
    ]
    return pl.pallas_call(
        functools.partial(attention_forward_kernel, gain_at, width_rows),
        out_shape=out_shape,
        in_specs=[vmem] * 8,
        out_specs=[vmem] * len(out_shape),
        scratch_shapes=[pltpu.VMEM((blocks, 256), f32)],
        cost_estimate=busy(20),
        compiler_params=pltpu.CompilerParams(vmem_limit_bytes=60 * 2**20),
    )(row_padded, hidden, packed, cos_full, sin_full, segment_column, segment_row, placing)


def attention_backward_kernel(
    gain_at, width_rows, planes, grad_ref, incoming_ref, middle_ref, raw_ref, mix_ref, probs_ref, query_ref, key_ref,
    value_ref, query_raw_ref, key_raw_ref, row_ref, qkv_ref, output_ref, cos_ref, sin_ref, input_scale,
    query_scale, key_scale, attnout_scale, ffnin_scale, ffnout_grad, by_device, by_member,
    input_grad_ref, blocks_ref, key_value, query_grad, low_ref, leaving, arriving, send_sem, recv_sem,
):
    bf16, f32 = jnp.bfloat16, jnp.float32
    members = blocks_ref.shape[0]
    blocks = members * planes
    padded = qkv_ref.shape[0] // blocks
    mix_rows = blocks_ref.shape[2] - padded
    local_rows, width = incoming_ref.shape
    head = key_ref.shape[1]
    heads = query_ref.shape[1] // head
    half = head // 2
    seq = lax.axis_index("seq")
    mine = pl.ds(pl.multiple_of(seq * local_rows, local_rows), local_rows)
    theirs = pl.ds(pl.multiple_of((1 - seq) * local_rows, local_rows), local_rows)
    partner = plane_places()[2]
    greet((partner,))

    ffn_in_grad = take_back(grad_ref[...], by_device[...])
    middle = middle_ref[...]
    inverse = inverse_of(middle, width)
    normed = middle * inverse
    ffnin_grad = jnp.sum(ffn_in_grad * normed, axis=0, keepdims=True)
    middle_grad = incoming_ref[...].astype(f32) + back_of(
        ffn_in_grad * ffnin_scale[...], normed, inverse, width
    )
    input_grad_ref[...] = middle_grad
    raw = raw_ref[...]
    inverse = inverse_of(raw, width)
    normed = raw * inverse
    attnout_grad = jnp.sum(middle_grad * normed, axis=0, keepdims=True)
    raw_grad = back_of(middle_grad * attnout_scale[...], normed, inverse, width).astype(bf16)
    mix_grad = contract_cols(raw_grad, output_ref[...]).astype(bf16)
    for h in range(heads):
        at = h * head
        grad = mix_grad[:, at : at + head]
        probs = probs_ref[h]
        prob_grad = contract_cols(grad, value_ref[...])
        delta = jnp.sum(prob_grad * probs, axis=-1, keepdims=True)
        score_grad = (probs * (prob_grad - delta)).astype(bf16)
        to_keys = contract_rows(score_grad, query_ref[:, at : at + head])
        to_values = contract_rows(probs.astype(bf16), grad)
        if h == 0:
            key_value[:, :head], key_value[:, head:] = to_keys, to_values
        else:
            key_value[:, :head] += to_keys
            key_value[:, head:] += to_values
        query_grad[:, at : at + head] = matmul(score_grad, key_ref[...])
    leaving[...] = key_value[theirs, :].astype(bf16)
    copy = sender(send_sem, recv_sem)(0, leaving, arriving, partner)

    output_grad = contract_rows(mix_ref[...], raw_grad).astype(bf16)
    cos_table, sin_table = cos_ref[mine, :], sin_ref[mine, :]

    def head_back(grad, raw, scale_ref):
        turned = jnp.concatenate(turn(grad, cos_table, -sin_table), axis=1)
        inverse = inverse_of(raw, head)
        normed = raw * inverse
        gain = jnp.sum(turned * normed, axis=0, keepdims=True)
        return back_of(turned * scale_ref[...], normed, inverse, head).astype(bf16), gain

    query_gain = jnp.zeros((1, head), f32)
    for h in range(heads):
        at = h * head
        low, gain = head_back(
            query_grad[:, at : at + head] * head ** (-0.5),
            query_raw_ref[:, at : at + head],
            query_scale,
        )
        low_ref[:, at : at + head] = low
        query_gain = query_gain + gain
    copy.wait_recv()
    total = key_value[mine, :] + arriving[...].astype(f32)
    low, key_gain = head_back(total[:, :head], key_raw_ref[...], key_scale)
    low_ref[:, heads * head : (heads + 1) * head] = low
    low_ref[:, (heads + 1) * head :] = total[:, head:].astype(bf16)

    row = row_ref[mine, :].astype(f32)
    inverse = inverse_of(row, width)
    normed = row * inverse
    normed_grad = contract_cols(low_ref[...], qkv_ref[...])
    input_gain = jnp.sum(normed_grad * normed, axis=0, keepdims=True)
    input_grad_ref[...] += take_back(
        back_of(normed_grad * input_scale[...], normed, inverse, width), by_member[...]
    )
    (at, count), *others = gain_at
    gains = collect_gain(input_gain, blocks, planes, at, count, padded, True)
    vectors = (query_gain, key_gain, attnout_grad, ffnin_grad, ffnout_grad[...])
    for vector, (at, count) in zip(vectors, others):
        gains = gains + collect_gain(vector, blocks, planes, at, count, count, False)
    normed = (normed * input_scale[...]).astype(bf16)
    weights = contract_rows(normed, low_ref[...])
    row_of = lax.broadcasted_iota(jnp.int32, (padded, 256), 0)
    columns = blocks_ref.shape[3]
    for i in range(blocks):
        member, plane = i // planes, i % planes
        piece = weights[padded * i : padded * (i + 1)]
        first = jnp.where(row_of == width_rows, gains[i : i + 1], piece[:, :256])
        blocks_ref[member, plane, :padded, :256] = first.astype(bf16)
        blocks_ref[member, plane, :padded, 256:] = piece[:, 256:].astype(bf16)
        natural = mix_rows * (plane * members + member)
        blocks_ref[member, plane, padded:, :width] = output_grad[natural : natural + mix_rows]
        blocks_ref[member, plane, padded:, width:] = jnp.zeros((mix_rows, columns - width), bf16)
    copy.wait_send()


def attention_backward(arrays, gain_at, width_rows, planes, mix_rows, collective_id):
    bf16, f32 = jnp.bfloat16, jnp.float32
    grad, incoming, query, key, qkv = arrays[0], arrays[1], arrays[6], arrays[7], arrays[12]
    local_rows, width = incoming.shape
    members = 8
    padded = qkv.shape[0] // (members * planes)
    pair = pltpu.VMEM((local_rows, 2 * key.shape[1]), bf16)
    shape = jax.ShapeDtypeStruct
    vmem = pl.BlockSpec(memory_space=pltpu.VMEM)
    return pl.pallas_call(
        functools.partial(attention_backward_kernel, gain_at, width_rows, planes),
        out_shape=[
            shape((local_rows, width), f32),
            shape((members, planes, padded + mix_rows, qkv.shape[1]), bf16),
        ],
        in_specs=[vmem] * len(arrays),
        out_specs=[vmem] * 2,
        scratch_shapes=[
            pltpu.VMEM((key.shape[0], 2 * key.shape[1]), f32),
            pltpu.VMEM(query.shape, f32),
            pltpu.VMEM((local_rows, qkv.shape[1]), bf16),
            pair,
            pair,
            pltpu.SemaphoreType.DMA((1,)),
            pltpu.SemaphoreType.DMA((1,)),
        ],
        cost_estimate=busy(30),
        compiler_params=pltpu.CompilerParams(
            collective_id=collective_id, has_side_effects=True, vmem_limit_bytes=60 * 2**20
        ),
    )(*arrays)


def body(
    tokens,
    segment_ids,
    cotangent,
    query_weight,
    key_weight,
    value_weight,
    output_weight,
    gate_weight,
    up_weight,
    down_weight,
    input_gain,
    query_gain,
    key_gain,
    attnout_gain,
    ffnin_gain,
    ffnout_gain,
):
    bf16, f32 = jnp.bfloat16, jnp.float32
    devices = lax.axis_size(ALL)
    members = lax.axis_size(PLANE)
    planes = lax.axis_size(PLANES)
    cubes = lax.axis_size("far")
    group = lax.axis_size(CUBE)
    width_rows = query_weight.shape[0]
    hidden_rows = down_weight.shape[0]
    head_width = key_weight.shape[1]
    query_width = query_weight.shape[1]
    head_count = query_width // head_width
    qkv_width = query_width + 2 * head_width
    mix_rows = output_weight.shape[0]
    padded = up_to(width_rows + 1, 8)
    width = devices * width_rows
    unit_count = cubes * hidden_rows
    unit_pad = up_to(unit_count, 128)
    by_device = place_columns(devices, members, planes, width_rows, padded, False)
    by_member = place_columns(devices, members, planes, width_rows, padded, True)

    def column_blocks(weight):
        pieces = weight.reshape(width_rows, cubes, group, hidden_rows)
        pieces = pieces.transpose(2, 0, 1, 3).reshape(group, width_rows, unit_count)
        return jnp.pad(
            pieces, ((0, 0), (0, padded - width_rows), (0, unit_pad - unit_count))
        )

    gate_up = jnp.concatenate([column_blocks(gate_weight), column_blocks(up_weight)], axis=2)
    gate_up = jnp.broadcast_to(gate_up[None], (cubes,) + gate_up.shape)
    gate_up = gate_up.reshape((devices,) + gate_up.shape[2:])

    gains = (input_gain, query_gain, key_gain, attnout_gain, ffnin_gain, ffnout_gain)
    gain_row = jnp.concatenate(gains)
    gain_widths = [g.shape[0] for g in gains]
    gain_row = jnp.pad(gain_row, (0, qkv_width - gain_row.shape[0]))
    qkv_local = jnp.concatenate([query_weight, key_weight, value_weight], axis=1)
    packed = jnp.concatenate([qkv_local, gain_row[None]], axis=0)
    packed = jnp.pad(packed, ((0, padded - width_rows - 1), (0, 0)))
    output_wide = jnp.pad(output_weight, ((0, 0), (0, qkv_width - output_weight.shape[1])))
    packed = jnp.concatenate([packed, output_wide], axis=0)
    packed_all = z_gather(packed, planes, 0)
    gate_up, packed_all = lax.optimization_barrier((gate_up, packed_all))
    gate_up_full = exchange(gate_up, ALL).reshape(devices * padded, 2 * unit_pad)
    packed_all, down_full = weights_gather(packed_all, down_weight, cubes, 6)
    down_full = down_full.reshape(unit_count, down_weight.shape[1])
    incoming = cotangent[0].astype(f32)
    local_rows = tokens.shape[1]
    offset = lax.axis_index("seq") * local_rows
    segment_row = segment_ids[0]

    def mine(rows):
        return lax.dynamic_slice_in_dim(rows, offset, local_rows)

    cos_full, sin_full = rope_tables(doc_positions(segment_row), head_width)

    other_half = [(0, 1), (1, 0)]
    first = lax.axis_index("seq") == 0
    other_tokens = lax.ppermute(tokens[0], "seq", other_half)
    row_tokens = jnp.concatenate(
        [
            jnp.where(first, tokens[0], other_tokens),
            jnp.where(first, other_tokens, tokens[0]),
        ]
    )
    row_padded = matmul(row_tokens, by_member).astype(bf16)
    gain_at, at = [], 0
    for count in gain_widths:
        gain_at.append((at, count))
        at += count
    (
        ffn_in_placed,
        middle,
        attn_raw,
        attn_flat,
        probs,
        queries,
        key_rows,
        value_rows,
        query_raw,
        key_raw,
        qkv_full,
        output_full,
        *scales,
    ) = attention_forward(
        row_padded,
        tokens[0],
        packed_all,
        cos_full,
        sin_full,
        mine(segment_row)[:, None],
        segment_row[None],
        by_device,
        gain_at,
        width_rows,
        padded,
        head_width,
    )
    ffnout_scale = scales.pop()

    cube_in, ffn_part, activated_low, to_gate, to_up = gather_forward(
        ffn_in_placed, gate_up_full, down_full, 1
    )
    cube_in = cube_in.reshape(-1, cube_in.shape[-1])
    ffn_raw = cube_scatter_sum(ffn_part, 2)
    inv_ffn = inverse_rms(ffn_raw)
    norm_ffn = ffn_raw * inv_ffn
    result = middle + norm_ffn * ffnout_scale
    ffnout_gain_grad = jnp.sum(incoming * norm_ffn, axis=0)
    ffn_raw_grad = rms_back(incoming * ffnout_scale, norm_ffn, inv_ffn).astype(bf16)

    gate_up_low, ffn_in_part, down_blocks = gather_backward(
        ffn_raw_grad, down_full, gate_up_full, to_gate, to_up, activated_low, 3
    )
    down_blocks = down_blocks.reshape(cubes, hidden_rows, down_weight.shape[1])
    ffn_in_grad, gate_up_blocks, down_wgrad = sum_gradients(
        ffn_in_part, down_blocks, cube_in, gate_up_low, 4
    )
    gate_up_terms = exchange(gate_up_blocks.reshape(devices, padded, 2 * unit_pad), ALL)
    input_grad, blocks = attention_backward(
        [
            ffn_in_grad,
            cotangent[0],
            middle,
            attn_raw,
            attn_flat,
            probs,
            queries,
            key_rows,
            value_rows,
            query_raw,
            key_raw,
            row_padded,
            qkv_full,
            output_full,
            cos_full,
            sin_full,
            *scales,
            ffnout_gain_grad[None],
            by_device,
            by_member,
        ],
        gain_at,
        width_rows,
        planes,
        mix_rows,
        7,
    )
    share = owner_sum(blocks, 5)
    gate_up_sum = jnp.sum(
        gate_up_terms.reshape(cubes, group, padded, 2 * unit_pad).astype(f32), axis=0
    )

    def unit_columns(total):
        total = total[:, :width_rows, :unit_count].reshape(
            group, width_rows, cubes, hidden_rows
        )
        return total.transpose(1, 2, 0, 3).reshape(width_rows, cubes * group * hidden_rows)

    gate_wgrad = unit_columns(gate_up_sum[:, :, :unit_pad])
    up_wgrad = unit_columns(gate_up_sum[:, :, unit_pad:])
    qkv_share, output_share = share[:padded], share[padded:, : output_weight.shape[1]]
    gain_shares, at = [], 0
    for count in gain_widths:
        gain_shares.append(qkv_share[width_rows, at : at + count])
        at += count
    return (
        result.astype(bf16)[None],
        input_grad[None],
        qkv_share[:width_rows, :query_width],
        qkv_share[:width_rows, query_width : query_width + head_width],
        qkv_share[:width_rows, query_width + head_width :],
        output_share,
        gate_wgrad,
        up_wgrad,
        down_wgrad,
        *gain_shares,
    )


def solution(mesh):
    dp, seq = mesh.shape["dp"], mesh.shape["seq"]
    split = Mesh(mesh.devices.reshape(dp // 8, 2, 2, 2, seq), ALL)
    rows = P(("far", "z", "x", "core"), "seq", None)
    matrix, vector = P(ALL, None), P(ALL)
    return jax.shard_map(
        body,
        mesh=split,
        in_specs=(rows, P(("far", "z", "x", "core"), None), rows) + (matrix,) * 7 + (vector,) * 6,
        out_specs=(rows, rows) + (matrix,) * 7 + (vector,) * 6,
        check_vma=False,
    )
```

```python
import functools

import jax
import jax.numpy as jnp
from jax import lax
from jax.experimental import pallas as pl
from jax.experimental.pallas import tpu as pltpu
from jax.sharding import Mesh
from jax.sharding import PartitionSpec as P

epsilon = 1e-06
rope_base = 1000000.0
masked_score = -1e30


def inverse_rms(values):
    return lax.rsqrt(jnp.mean(values * values, axis=-1, keepdims=True) + epsilon)


def rms_back(grad_normed, normed, inverse):
    return inverse * (grad_normed - normed * jnp.mean(grad_normed * normed, axis=-1, keepdims=True))


def doc_positions(segments):
    length = segments.shape[0]
    smaller = segments[None, :] < segments[:, None]
    starts = jnp.sum(smaller.astype(jnp.int32), axis=1)
    return (jnp.arange(length, dtype=jnp.int32) - starts).astype(jnp.float32)


def rope_tables(positions, head_width):
    half_width = head_width // 2
    frequency = rope_base ** (-(2.0 / head_width) * jnp.arange(half_width, dtype=jnp.float32))
    angles = positions[..., None] * frequency
    return (jnp.cos(angles), jnp.sin(angles))


def matmul(left, right):
    return jnp.dot(left, right, preferred_element_type=jnp.float32)


def contract_rows(left, right):
    return lax.dot_general(
        left, right, (((0,), (0,)), ((), ())), preferred_element_type=jnp.float32
    )


def contract_cols(left, right):
    return lax.dot_general(
        left, right, (((1,), (1,)), ((), ())), preferred_element_type=jnp.float32
    )


ALL = ("far", "z", "x", "core", "seq")
PLANES = ("far", "z")
CUBE = ("z", "x", "core", "seq")


def up_to(size, multiple):
    return (size + multiple - 1) // multiple * multiple


def place_columns(blocks, members, planes, rows, padded, by_member):
    source = lax.broadcasted_iota(jnp.int32, (blocks * rows, blocks * padded), 0)
    target = lax.broadcasted_iota(jnp.int32, (blocks * rows, blocks * padded), 1)
    block = source // rows
    if by_member:
        block = block % members * planes + block // members
    return (target == block * padded + source % rows).astype(jnp.bfloat16)


def take_back(padded_values, placing):
    high = lax.reduce_precision(padded_values, 8, 7)
    terms = jnp.concatenate([high, padded_values - high], axis=0).astype(jnp.bfloat16)
    both = contract_cols(terms, placing)
    rows = padded_values.shape[0]
    return both[:rows] + both[rows:]


PLANE = ("x", "core", "seq")

MESH_ID = pl.DeviceIdType.MESH
VMEM_BYTES = 48 * 2**20


def exchange(blocks, axes):
    return lax.all_to_all(blocks, axes, split_axis=0, concat_axis=0, tiled=True)


def busy(microseconds):
    return pl.CostEstimate(flops=0, bytes_accessed=microseconds * 3_000_000, transcendentals=0)


def shifted(flip_z, flip_x, flip_core, flip_y):
    far, *inner = (lax.axis_index(name) for name in ALL)
    flips = (flip_z, flip_x, flip_core, flip_y)
    return (far, *(1 - at if flip else at for at, flip in zip(inner, flips)))


def plane_places():
    def member(flip_x, flip_core, flip_y):
        _, _, x, core, seq = shifted(0, flip_x, flip_core, flip_y)
        return (x * 2 + core) * 2 + seq

    return shifted(0, 0, 1, 0), shifted(0, 1, 0, 0), shifted(0, 0, 0, 1), member


def cube_member(flip_z, flip_x, flip_y, flip_core):
    _, z, x, core, seq = shifted(flip_z, flip_x, flip_core, flip_y)
    return ((z * 2 + x) * 2 + core) * 2 + seq


def cube_places():
    return *plane_places()[:3], shifted(1, 0, 0, 0)


def other_planes(planes):
    far, z, x, core, seq = (lax.axis_index(name) for name in ALL)
    plane = far * 2 + z
    ring = [lax.rem(plane + k, planes) for k in range(1, planes)]
    return plane, [(at // 2, lax.rem(at, 2), x, core, seq) for at in ring], ring


def other_cubes(cubes):
    far, z, x, core, seq = (lax.axis_index(name) for name in ALL)
    return far, [(lax.rem(far + k, cubes), z, x, core, seq) for k in range(1, cubes)]


def greet(places):
    barrier = pltpu.get_barrier_semaphore()
    for place in places:
        pl.semaphore_signal(barrier, inc=1, device_id=place, device_id_type=MESH_ID)
    pl.semaphore_wait(barrier, len(places))


def sender(send_sems, recv_sems):
    def send(kind, source, target, place):
        copy = pltpu.make_async_remote_copy(
            src_ref=source,
            dst_ref=target,
            send_sem=send_sems.at[kind],
            recv_sem=recv_sems.at[kind],
            device_id=place,
            device_id_type=MESH_ID,
        )
        copy.start()
        return copy

    return send


def plane_spread(own_ref, out_ref, send_sems, recv_sems, local_sem):
    sibling, along_x, along_y, member = plane_places()
    half = own_ref.shape[0] // 2
    top, bottom = pl.ds(0, half), pl.ds(half, half)
    me = member(0, 0, 0)
    keep = pltpu.make_async_copy(own_ref, out_ref.at[me], local_sem)
    keep.start()
    send = sender(send_sems, recv_sems)

    def forward(kind, block, rows, place):
        return send(kind, out_ref.at[block, rows], out_ref.at[block, rows], place)

    own_x_top = send(1, own_ref.at[top], out_ref.at[me, top], along_x)
    own_y_bottom = send(3, own_ref.at[bottom], out_ref.at[me, bottom], along_y)
    own_sibling = send(0, own_ref, out_ref.at[me], sibling)
    own_x_bottom = send(2, own_ref.at[bottom], out_ref.at[me, bottom], along_x)
    own_y_top = send(4, own_ref.at[top], out_ref.at[me, top], along_y)
    x_block, y_block, diagonal = member(1, 0, 0), member(0, 0, 1), member(1, 0, 1)
    own_x_top.wait_recv()
    diagonal_top = forward(5, x_block, top, along_y)
    x_top = forward(7, x_block, top, sibling)
    own_y_bottom.wait_recv()
    diagonal_bottom = forward(6, y_block, bottom, along_x)
    y_bottom = forward(9, y_block, bottom, sibling)
    own_x_bottom.wait_recv()
    x_bottom = forward(8, x_block, bottom, sibling)
    own_y_top.wait_recv()
    y_top = forward(10, y_block, top, sibling)
    diagonal_top.wait_recv()
    far_top = forward(11, diagonal, top, sibling)
    diagonal_bottom.wait_recv()
    far_bottom = forward(12, diagonal, bottom, sibling)
    for copy in (own_sibling, x_top, y_bottom, x_bottom, y_top, far_top, far_bottom):
        copy.wait_recv()
    for copy in (
        own_x_top,
        own_y_bottom,
        own_sibling,
        own_x_bottom,
        own_y_top,
        diagonal_top,
        diagonal_bottom,
        x_top,
        y_bottom,
        x_bottom,
        y_top,
        far_top,
        far_bottom,
    ):
        copy.wait_send()
    keep.wait()


def cube_spread(own_ref, out_ref, send_sems, recv_sems, local_sem, compute=lambda i: None):
    sibling, along_x, along_y, along_z = cube_places()
    half = own_ref.shape[0] // 2
    top, bottom = pl.ds(0, half), pl.ds(half, half)
    me = cube_member(0, 0, 0, 0)
    keep = pltpu.make_async_copy(own_ref, out_ref.at[me], local_sem)
    keep.start()
    send = sender(send_sems, recv_sems)
    x_block, y_block, diagonal = (cube_member(0, *at, 0) for at in ((1, 0), (0, 1), (1, 1)))
    z_block, zx_block, zy_block, zd_block = (
        cube_member(1, *at, 0) for at in ((0, 0), (1, 0), (0, 1), (1, 1))
    )

    def half_on(kind, block, rows, place):
        return send(kind, out_ref.at[block, rows], out_ref.at[block, rows], place)

    def on(kind, block, place):
        return send(kind, out_ref.at[block], out_ref.at[block], place)

    own_x_top = send(1, own_ref.at[top], out_ref.at[me, top], along_x)
    own_y_bottom = send(3, own_ref.at[bottom], out_ref.at[me, bottom], along_y)
    own_z = send(13, own_ref, out_ref.at[me], along_z)
    own_sibling = send(0, own_ref, out_ref.at[me], sibling)
    own_x_bottom = send(2, own_ref.at[bottom], out_ref.at[me, bottom], along_x)
    own_y_top = send(4, own_ref.at[top], out_ref.at[me, top], along_y)
    compute(0)
    own_x_top.wait_recv()
    diagonal_top = half_on(5, x_block, top, along_y)
    x_top = half_on(7, x_block, top, sibling)
    own_y_bottom.wait_recv()
    diagonal_bottom = half_on(6, y_block, bottom, along_x)
    y_bottom = half_on(9, y_block, bottom, sibling)
    own_sibling.wait_recv()
    compute(1)
    own_z.wait_recv()
    z_to_x = on(14, z_block, along_x)
    z_to_y = on(15, z_block, along_y)
    z_near = on(16, z_block, sibling)
    own_x_bottom.wait_recv()
    x_bottom = half_on(8, x_block, bottom, sibling)
    own_y_top.wait_recv()
    y_top = half_on(10, y_block, top, sibling)
    compute(2)
    diagonal_top.wait_recv()
    far_top = half_on(11, diagonal, top, sibling)
    diagonal_bottom.wait_recv()
    far_bottom = half_on(12, diagonal, bottom, sibling)
    diagonal_z = on(17, diagonal, along_z)
    compute(3)
    compute(4)
    z_to_x.wait_recv()
    zx_near = on(18, zx_block, sibling)
    z_to_y.wait_recv()
    zy_near = on(19, zy_block, sibling)
    compute(5)
    compute(6)
    diagonal_z.wait_recv()
    zd_near = on(20, zd_block, sibling)
    compute(7)
    compute(8)
    last = (
        (x_top, x_bottom), (y_bottom, y_top), (far_top, far_bottom), (z_near,), (zx_near,), (zy_near,), (zd_near,),
    )
    for i, copies in enumerate(last):
        for copy in copies:
            copy.wait_recv()
        compute(9 + i)
    for copy in (
        own_x_top, own_y_bottom, own_z, own_sibling, own_x_bottom, own_y_top, diagonal_top, diagonal_bottom,
        z_to_x, z_to_y, diagonal_z,
    ):
        copy.wait_send()
    for copies in last:
        for copy in copies:
            copy.wait_send()
    keep.wait()


CUBE_ORDER = (
    (0, 0, 0, 0), (0, 0, 0, 1), (0, 1, 0, 0), (0, 0, 1, 0), (1, 0, 0, 0), (0, 1, 1, 0), (1, 1, 0, 0), (1, 0, 1, 0),
    (1, 1, 1, 0), (0, 1, 0, 1), (0, 0, 1, 1), (0, 1, 1, 1), (1, 0, 0, 1), (1, 1, 0, 1), (1, 0, 1, 1), (1, 1, 1, 1),
)


def cube_gather_kernel(own_ref, out_ref, *sems):
    greet(cube_places())
    cube_spread(own_ref, out_ref, *sems)


def plane_gather_kernel(own_ref, out_ref, *sems):
    greet(plane_places()[:3])
    plane_spread(own_ref, out_ref, *sems)


def z_gather_kernel(planes, own_ref, out_ref, send_sems, recv_sems, own_sem):
    plane, others, _ = other_planes(planes)
    greet(others)
    keep = pltpu.make_async_copy(own_ref, out_ref.at[plane], own_sem)
    keep.start()
    send = sender(send_sems, recv_sems)
    copies = [send(k, own_ref, out_ref.at[plane], place) for k, place in enumerate(others)]
    for copy in copies:
        copy.wait_recv()
    for copy in copies:
        copy.wait_send()
    keep.wait()


def gather_sems(count):
    return [
        pltpu.SemaphoreType.DMA((count,)),
        pltpu.SemaphoreType.DMA((count,)),
        pltpu.SemaphoreType.DMA,
    ]


def z_gather(local, planes, collective_id):
    return pl.pallas_call(
        functools.partial(z_gather_kernel, planes),
        out_shape=jax.ShapeDtypeStruct((planes, *local.shape), local.dtype),
        in_specs=[pl.BlockSpec(memory_space=pltpu.VMEM)],
        out_specs=pl.BlockSpec(memory_space=pl.ANY),
        scratch_shapes=[
            pltpu.SemaphoreType.DMA((planes - 1,)),
            pltpu.SemaphoreType.DMA((planes - 1,)),
            pltpu.SemaphoreType.DMA,
        ],
        cost_estimate=busy(20),
        compiler_params=pltpu.CompilerParams(
            collective_id=collective_id, has_side_effects=True, vmem_limit_bytes=VMEM_BYTES
        ),
    )(local)


def plane_gather(local, collective_id):
    members = 8
    return pl.pallas_call(
        plane_gather_kernel,
        out_shape=jax.ShapeDtypeStruct((members, *local.shape), local.dtype),
        in_specs=[pl.BlockSpec(memory_space=pl.ANY)],
        out_specs=pl.BlockSpec(memory_space=pl.ANY),
        scratch_shapes=gather_sems(13),
        cost_estimate=busy(30),
        compiler_params=pltpu.CompilerParams(
            collective_id=collective_id, has_side_effects=True, vmem_limit_bytes=VMEM_BYTES
        ),
    )(local)


def gather_rows(local, collective_id):
    rows, columns = local.shape
    members = 16
    out = pl.pallas_call(
        cube_gather_kernel,
        out_shape=jax.ShapeDtypeStruct((members, rows // 16, 16, columns), local.dtype),
        in_specs=[pl.BlockSpec(memory_space=pl.ANY)],
        out_specs=pl.BlockSpec(memory_space=pl.ANY),
        scratch_shapes=gather_sems(21),
        cost_estimate=busy(35),
        compiler_params=pltpu.CompilerParams(
            collective_id=collective_id, has_side_effects=True, vmem_limit_bytes=VMEM_BYTES
        ),
    )(local.reshape(rows // 16, 16, columns))
    return out.reshape(-1, columns)


def add_rows(target, sources, start, count):
    def one(i, carry):
        total = sources[0][i].astype(jnp.float32)
        for source in sources[1:]:
            total = total + source[i].astype(jnp.float32)
        target[i] = total.astype(target.dtype)
        return carry

    lax.fori_loop(start, start + count, one, 0)


def plane_sum(part_ref, own_sum, near, sums, from_x, from_y, far_x, far_y, send_sems, recv_sems):
    sibling, along_x, along_y, member = plane_places()
    rows = own_sum.shape[0]
    half = rows // 2
    top, bottom = pl.ds(0, half), pl.ds(half, half)
    send = sender(send_sems, recv_sems)
    chips = ((1, 1), (1, 0), (0, 1), (0, 0))
    mine = [part_ref.at[member(at_x, 0, at_y)] for at_x, at_y in chips]
    to_sibling = [
        send(k, part_ref.at[member(at_x, 1, at_y)], near.at[k], sibling)
        for k, (at_x, at_y) in enumerate(chips)
    ]
    to_sibling[0].wait_recv()
    add_rows(sums.at[0], (mine[0], near.at[0]), 0, rows)
    diagonal_x = send(4, sums.at[0, bottom], far_x.at[bottom], along_x)
    diagonal_y = send(5, sums.at[0, top], far_y.at[top], along_y)
    to_sibling[1].wait_recv()
    add_rows(sums.at[1], (mine[1], near.at[1]), half, half)
    direct_x = send(6, sums.at[1, bottom], from_x.at[bottom], along_x)
    to_sibling[2].wait_recv()
    add_rows(sums.at[2], (mine[2], near.at[2]), 0, half)
    direct_y = send(7, sums.at[2, top], from_y.at[top], along_y)
    to_sibling[3].wait_recv()
    diagonal_y.wait_recv()
    add_rows(sums.at[1], (mine[1], near.at[1], far_y), 0, half)
    joint_x = send(8, sums.at[1, top], from_x.at[top], along_x)
    diagonal_x.wait_recv()
    add_rows(sums.at[2], (mine[2], near.at[2], far_x), half, half)
    joint_y = send(9, sums.at[2, bottom], from_y.at[bottom], along_y)
    direct_x.wait_recv()
    direct_y.wait_recv()
    joint_x.wait_recv()
    joint_y.wait_recv()
    add_rows(own_sum, (mine[3], near.at[3], from_x, from_y), 0, rows)
    for copy in (*to_sibling, diagonal_x, diagonal_y, direct_x, direct_y, joint_x, joint_y):
        copy.wait_send()


def cube_sum(
    part_hbm, own_sum, mine, near, via_z, zx_in, zy_in, far_x, far_y, from_x, from_y, from_z, load_sems, send_sems,
    recv_sems, work=lambda point: None,
):
    sibling, along_x, along_y, along_z = cube_places()
    pieces = own_sum.shape[0]
    half = pieces // 2
    top, bottom = pl.ds(0, half), pl.ds(half, half)
    send = sender(send_sems, recv_sems)
    chips = ((1, 1, 1), (1, 1, 0), (1, 0, 1), (0, 1, 0), (0, 0, 1), (0, 1, 1), (1, 0, 0), (0, 0, 0))
    z_diagonal, z_x, z_y, at_x, at_y, diagonal, at_z, here = range(8)
    to_sibling = [
        send(k, part_hbm.at[cube_member(*chip, 1)], near.at[k], sibling)
        for k, chip in enumerate(chips)
    ]
    loads = [
        pltpu.make_async_copy(part_hbm.at[cube_member(*chip, 0)], mine.at[k], load_sems.at[k])
        for k, chip in enumerate(chips)
    ]
    for load in loads:
        load.start()

    def both_in(k):
        to_sibling[k].wait_recv()
        loads[k].wait()

    def add(k, others=(), start=0, count=pieces):
        add_rows(near.at[k], (mine.at[k], near.at[k], *others), start, count)

    work(0)
    both_in(z_diagonal)
    add(z_diagonal)
    diagonal_z = send(8, near.at[z_diagonal], via_z, along_z)
    both_in(z_x)
    add(z_x)
    zx_out = send(9, near.at[z_x], zx_in, along_x)
    both_in(z_y)
    add(z_y)
    zy_out = send(10, near.at[z_y], zy_in, along_y)
    both_in(at_x)
    add(at_x, (), half, half)
    direct_x = send(13, near.at[at_x, bottom], from_x.at[bottom], along_x)
    both_in(at_y)
    add(at_y, (), 0, half)
    direct_y = send(14, near.at[at_y, top], from_y.at[top], along_y)
    both_in(diagonal)
    both_in(at_z)
    work(1)
    diagonal_z.wait_recv()
    add(diagonal, (via_z,))
    diagonal_x = send(11, near.at[diagonal, bottom], far_x.at[bottom], along_x)
    diagonal_y = send(12, near.at[diagonal, top], far_y.at[top], along_y)
    zx_out.wait_recv()
    zy_out.wait_recv()
    add(at_z, (zx_in, zy_in))
    joint_z = send(15, near.at[at_z], from_z, along_z)
    work(2)
    diagonal_y.wait_recv()
    add(at_x, (far_y,), 0, half)
    joint_x = send(16, near.at[at_x, top], from_x.at[top], along_x)
    diagonal_x.wait_recv()
    add(at_y, (far_x,), half, half)
    joint_y = send(17, near.at[at_y, bottom], from_y.at[bottom], along_y)
    both_in(here)
    work(3)
    for copy in (direct_x, direct_y, joint_z, joint_x, joint_y):
        copy.wait_recv()
    add_rows(own_sum, (mine.at[here], near.at[here], from_x, from_y, from_z), 0, pieces)
    for copy in (
        *to_sibling, diagonal_z, zx_out, zy_out, direct_x, direct_y, diagonal_x, diagonal_y, joint_z, joint_x, joint_y,
    ):
        copy.wait_send()


def cube_sum_kernel(part_ref, out_ref, *scratch):
    greet(cube_places())
    cube_sum(part_ref, out_ref, *scratch)


def cube_sum_scratch(shape, dtype):
    return [
        pltpu.VMEM((8, *shape), dtype),
        pltpu.VMEM((8, *shape), dtype),
        *[pltpu.VMEM(shape, dtype)] * 8,
        pltpu.SemaphoreType.DMA((8,)),
        pltpu.SemaphoreType.DMA((18,)),
        pltpu.SemaphoreType.DMA((18,)),
    ]


def plane_sum_scratch(shape, dtype):
    block = pltpu.VMEM(shape, dtype)
    return [
        pltpu.VMEM((4, *shape), dtype),
        pltpu.VMEM((3, *shape), dtype),
        block,
        block,
        block,
        block,
        pltpu.SemaphoreType.DMA((10,)),
        pltpu.SemaphoreType.DMA((10,)),
    ]


def cube_scatter_sum(partial, collective_id):
    shape = partial.shape[1:]
    out = pl.pallas_call(
        cube_sum_kernel,
        out_shape=jax.ShapeDtypeStruct(shape, jnp.float32),
        in_specs=[pl.BlockSpec(memory_space=pl.ANY)],
        out_specs=pl.BlockSpec(memory_space=pltpu.VMEM),
        scratch_shapes=cube_sum_scratch(shape, partial.dtype),
        cost_estimate=busy(35),
        compiler_params=pltpu.CompilerParams(
            collective_id=collective_id, has_side_effects=True, vmem_limit_bytes=VMEM_BYTES
        ),
    )(partial)
    return out.reshape(shape[0] * shape[1], shape[2])


gelu_inner = 0.7978845608028654
gelu_cubic = 0.044715


def pad_rows(target, source):
    rows = source.shape[0]
    target[pl.ds(0, rows)] = source[...]
    if target.shape[0] > rows:
        extra = target.shape[0] - rows
        target[pl.ds(rows, extra)] = jnp.zeros((extra, target.shape[1]), target.dtype)


def ffn_forward_kernel(in_ref, gate_up_ref, down_ref, part_ref, act_ref, to_gate, to_up, down, proj):
    units = act_ref.shape[1]

    @pl.when(pl.program_id(0) == 0)
    def _():
        pad_rows(down, down_ref)

    proj[...] = matmul(in_ref[...], gate_up_ref[...])
    step = 32

    def one(i, carry):
        rows = pl.ds(pl.multiple_of(i * step, step), step)
        gate, up = proj[rows, :units], proj[rows, units:]
        square = gate * gate
        bend = jnp.tanh(gelu_inner * gate * (1.0 + gelu_cubic * square))
        half = 0.5 * (1.0 + bend)
        value = gate * half
        slope = half + 0.5 * gate * (1.0 - bend * bend) * (
            gelu_inner * (1.0 + 3.0 * gelu_cubic * square)
        )
        to_gate[rows, :] = slope * up
        to_up[rows, :] = value
        act_ref[rows, :] = (value * up).astype(act_ref.dtype)
        return carry

    lax.fori_loop(0, in_ref.shape[0] // step, one, 0)
    part_ref[...] = matmul(act_ref[...], down[...]).astype(part_ref.dtype)


ROW_BLOCK = 256


def whole(array):
    return pl.BlockSpec(array.shape, lambda i: (0, 0), pipeline_mode=pl.Buffered(1))


def row_block(columns):
    return pl.BlockSpec((ROW_BLOCK, columns), lambda i: (i, 0))


def ffn_forward(rows_in, gate_up, down):
    rows, depth = rows_in.shape
    units, columns = gate_up.shape[1] // 2, down.shape[1]
    low = rows_in.dtype
    return pl.pallas_call(
        ffn_forward_kernel,
        grid=(rows // ROW_BLOCK,),
        in_specs=[row_block(depth), whole(gate_up), whole(down)],
        out_specs=[row_block(columns), row_block(units), row_block(units), row_block(units)],
        out_shape=[
            jax.ShapeDtypeStruct((rows, columns), low),
            jax.ShapeDtypeStruct((rows, units), low),
            jax.ShapeDtypeStruct((rows, units), jnp.float32),
            jax.ShapeDtypeStruct((rows, units), jnp.float32),
        ],
        scratch_shapes=[
            pltpu.VMEM((units, columns), low),
            pltpu.VMEM((ROW_BLOCK, 2 * units), jnp.float32),
        ],
        cost_estimate=busy(20),
        compiler_params=pltpu.CompilerParams(vmem_limit_bytes=VMEM_BYTES),
    )(rows_in, gate_up, down)


def block_order(rows):
    order = [cube_member(*flips) for flips in CUBE_ORDER]
    return order, [pl.ds(pl.multiple_of(block * rows, rows), rows) for block in order]


def gather_backward_kernel(
    own_ref, down_ref, gate_up_ref, to_gate_hbm, to_up_hbm, act_hbm, both_hbm, part_hbm, down_grad_ref,
    grad, down, to_gate, to_up, act, both, part, act_sem, load_sems, put_sems, send_sems, recv_sems, local_sem,
):
    units = down.shape[0]
    pieces, piece, columns = own_ref.shape
    rows = pieces * piece
    order, places = block_order(rows)

    def loads(i):
        slot, at = i % 2, places[i]
        return (
            pltpu.make_async_copy(to_gate_hbm.at[at], to_gate.at[slot], load_sems.at[0, slot]),
            pltpu.make_async_copy(to_up_hbm.at[at], to_up.at[slot], load_sems.at[1, slot]),
        )

    def puts(i):
        slot = i % 2
        return (
            pltpu.make_async_copy(both.at[slot], both_hbm.at[places[i]], put_sems.at[0, slot]),
            pltpu.make_async_copy(part.at[slot], part_hbm.at[order[i]], put_sems.at[1, slot]),
        )

    def compute(i):
        if i + 1 < len(order):
            for load in loads(i + 1):
                load.start()
        for load in loads(i):
            load.wait()
        if i >= 2:
            for put in puts(i - 2):
                put.wait()
        slot = i % 2
        source = own_ref if i == 0 else grad.at[order[i]]
        act_grad = contract_cols(source[...].reshape(rows, columns), down[...])
        both[slot, :, :units] = (act_grad * to_gate[slot]).astype(both.dtype)
        both[slot, :, units:] = (act_grad * to_up[slot]).astype(both.dtype)
        result = contract_cols(both[slot], gate_up_ref[...]).astype(part.dtype)
        part[slot] = result.reshape(pieces, piece, result.shape[1])
        for put in puts(i):
            put.start()

    act_load = pltpu.make_async_copy(act_hbm, act, act_sem)
    act_load.start()
    for load in loads(0):
        load.start()
    pad_rows(down, down_ref)
    greet(cube_places())
    cube_spread(own_ref, grad, send_sems, recv_sems, local_sem, compute)
    act_load.wait()
    whole = grad[...].reshape(len(order) * rows, columns)
    down_grad = contract_rows(act[...], whole)
    down_grad_ref[...] = down_grad[: down_ref.shape[0]].astype(down_grad_ref.dtype)
    for i in (len(order) - 2, len(order) - 1):
        for put in puts(i):
            put.wait()


def gather_backward(own, down, gate_up, to_gate, to_up, act, collective_id):
    rows, columns = own.shape
    members, piece = 16, 16
    pieces = rows // piece
    depth, units = gate_up.shape[0], to_gate.shape[1]
    low, wide = own.dtype, jnp.float32
    shape = jax.ShapeDtypeStruct
    vmem, anywhere = pl.BlockSpec(memory_space=pltpu.VMEM), pl.BlockSpec(memory_space=pl.ANY)
    return pl.pallas_call(
        gather_backward_kernel,
        out_shape=[
            shape((members * rows, 2 * units), low),
            shape((members, pieces, piece, depth), low),
            shape(down.shape, low),
        ],
        in_specs=[vmem, vmem, vmem, anywhere, anywhere, anywhere],
        out_specs=[anywhere, anywhere, vmem],
        scratch_shapes=[
            pltpu.VMEM((members, pieces, piece, columns), low),
            pltpu.VMEM((units, columns), low),
            pltpu.VMEM((2, rows, units), wide),
            pltpu.VMEM((2, rows, units), wide),
            pltpu.VMEM(act.shape, low),
            pltpu.VMEM((2, rows, 2 * units), low),
            pltpu.VMEM((2, pieces, piece, depth), low),
            pltpu.SemaphoreType.DMA,
            pltpu.SemaphoreType.DMA((2, 2)),
            pltpu.SemaphoreType.DMA((2, 2)),
            *gather_sems(21),
        ],
        cost_estimate=busy(45),
        compiler_params=pltpu.CompilerParams(
            collective_id=collective_id, has_side_effects=True, vmem_limit_bytes=60 * 2**20
        ),
    )(own.reshape(pieces, piece, columns), down, gate_up, to_gate, to_up, act)


def sum_gradients_kernel(
    part_ref, down_ref, in_hbm, both_hbm, sum_ref, gate_up_ref, down_sum_ref,
    columns_in, both, arriving, both_sem, in_sems, far_send, far_recv, *scratch,
):
    cubes = down_ref.shape[0]
    far, others = other_cubes(cubes)
    step = columns_in.shape[2]
    blocks = gate_up_ref.shape[0] // step

    def load(i):
        at = pl.ds(i * step, step)
        return pltpu.make_async_copy(in_hbm.at[:, at], columns_in.at[i % 2], in_sems.at[i % 2])

    both_load = pltpu.make_async_copy(both_hbm, both, both_sem)
    both_load.start()
    load(0).start()

    def rows_of(i):
        if i == 0:
            both_load.wait()
        if i + 1 < blocks:
            load(i + 1).start()
        load(i).wait()
        rows = contract_rows(columns_in[i % 2], both[...])
        gate_up_ref[pl.ds(i * step, step), :] = rows.astype(gate_up_ref.dtype)

    def work(point):
        spread = ((), (0, 1), (2, 3), tuple(range(4, blocks)))
        for i in spread[point]:
            rows_of(i)

    greet((*cube_places(), *others))
    send = sender(far_send, far_recv)
    copies = [
        send(k, down_ref.at[place[0]], arriving.at[k], place) for k, place in enumerate(others)
    ]
    cube_sum(part_ref, sum_ref, *scratch, work=work)
    down_sum = down_ref[far].astype(jnp.float32)
    for k, copy in enumerate(copies):
        copy.wait_recv()
        down_sum = down_sum + arriving[k].astype(jnp.float32)
    down_sum_ref[...] = down_sum
    for copy in copies:
        copy.wait_send()


def sum_gradients(part, down, rows_in, both, collective_id):
    members, pieces, piece, depth = part.shape
    low = part.dtype
    step = 256
    vmem, anywhere = pl.BlockSpec(memory_space=pltpu.VMEM), pl.BlockSpec(memory_space=pl.ANY)
    total, gate_up, down_sum = pl.pallas_call(
        sum_gradients_kernel,
        out_shape=[
            jax.ShapeDtypeStruct((pieces, piece, depth), jnp.float32),
            jax.ShapeDtypeStruct((depth, both.shape[1]), low),
            jax.ShapeDtypeStruct(down.shape[1:], jnp.float32),
        ],
        in_specs=[anywhere, vmem, anywhere, anywhere],
        out_specs=[vmem, vmem, vmem],
        scratch_shapes=[
            pltpu.VMEM((2, rows_in.shape[0], step), low),
            pltpu.VMEM(both.shape, low),
            pltpu.VMEM((down.shape[0] - 1, *down.shape[1:]), low),
            pltpu.SemaphoreType.DMA,
            pltpu.SemaphoreType.DMA((2,)),
            pltpu.SemaphoreType.DMA((down.shape[0] - 1,)),
            pltpu.SemaphoreType.DMA((down.shape[0] - 1,)),
            *cube_sum_scratch((pieces, piece, depth), low),
        ],
        cost_estimate=busy(35),
        compiler_params=pltpu.CompilerParams(
            collective_id=collective_id, has_side_effects=True, vmem_limit_bytes=60 * 2**20
        ),
    )(part, down, rows_in, both)
    return total.reshape(pieces * piece, depth), gate_up, down_sum


def owner_sum_kernel(planes, part_ref, out_ref, own_sum, leaving, arriving, z_send, z_recv, *scratch):
    plane, others, ring = other_planes(planes)
    greet((*plane_places()[:3], *others))
    plane_sum(part_ref, own_sum, *scratch)
    send = sender(z_send, z_recv)

    def narrow(i, carry):
        leaving[i] = own_sum[i].astype(leaving.dtype)
        return carry

    lax.fori_loop(0, planes, narrow, 0)
    copies = [
        send(k, leaving.at[ring[k]], arriving.at[k], place) for k, place in enumerate(others)
    ]
    for copy in copies:
        copy.wait_recv()

    value = own_sum[plane]
    for k in range(planes - 1):
        value = value + arriving[k].astype(jnp.float32)
    out_ref[...] = value
    for copy in copies:
        copy.wait_send()


def owner_sum(blocks, collective_id):
    members, planes, rows, columns = blocks.shape
    return pl.pallas_call(
        functools.partial(owner_sum_kernel, planes),
        out_shape=jax.ShapeDtypeStruct((rows, columns), jnp.float32),
        in_specs=[pl.BlockSpec(memory_space=pltpu.VMEM)],
        out_specs=pl.BlockSpec(memory_space=pltpu.VMEM),
        scratch_shapes=[
            pltpu.VMEM((planes, rows, columns), jnp.float32),
            pltpu.VMEM((planes, rows, columns), blocks.dtype),
            pltpu.VMEM((planes - 1, rows, columns), blocks.dtype),
            pltpu.SemaphoreType.DMA((planes - 1,)),
            pltpu.SemaphoreType.DMA((planes - 1,)),
            *plane_sum_scratch((planes, rows, columns), blocks.dtype),
        ],
        cost_estimate=busy(35),
        compiler_params=pltpu.CompilerParams(
            collective_id=collective_id, has_side_effects=True, vmem_limit_bytes=VMEM_BYTES
        ),
    )(blocks)


GAIN_SLOT = 128


def gain_places(blocks, planes, count, per, by_member):
    lane = lax.broadcasted_iota(jnp.int32, (GAIN_SLOT, blocks * per), 0)
    inner = lax.broadcasted_iota(jnp.int32, (GAIN_SLOT, blocks * per), 1) % per
    places = ((lane == inner) & (inner < count)).astype(jnp.float32).astype(jnp.bfloat16)
    listed = lax.broadcasted_iota(jnp.int32, (blocks, blocks * per), 0)
    block = lax.broadcasted_iota(jnp.int32, (blocks, blocks * per), 1) // per
    members = blocks // planes
    if not by_member:
        block = block % members * planes + block // members
    return places, listed == block


def spread_gain(rows, planes, *where):
    places, chosen = gain_places(rows.shape[0], planes, *where)
    return jnp.sum(jnp.where(chosen, matmul(rows, places), 0.0), axis=0, keepdims=True)


def collect_gain(vector, blocks, planes, *where):
    places, chosen = gain_places(blocks, planes, *where)
    return contract_cols(jnp.where(chosen, vector, 0.0).astype(jnp.bfloat16), places)


def inverse_of(values, count):
    return lax.rsqrt(jnp.sum(values * values, axis=-1, keepdims=True) / count + epsilon)


def back_of(grad_normed, normed, inverse, count):
    inner = jnp.sum(grad_normed * normed, axis=-1, keepdims=True) / count
    return inverse * (grad_normed - normed * inner)


def turn(values, cos_table, sin_table):
    half = values.shape[1] // 2
    first, second = values[:, :half], values[:, half:]
    return first * cos_table - second * sin_table, second * cos_table + first * sin_table


def attention_forward_kernel(
    gain_widths, width_rows, row_ref, hidden_ref, packed_ref, cos_ref, sin_ref, segment_column, segment_row, placing_ref,
    placed_ref, middle_ref, raw_ref, mix_ref, probs_ref, query_ref, key_ref, value_ref, query_raw_ref,
    key_raw_ref, qkv_ref, output_ref, input_scale, query_scale, key_scale, attnout_scale, ffnin_scale, ffnout_scale,
    gain_rows,
):
    bf16, f32 = jnp.bfloat16, jnp.float32
    members, planes, piece, _ = packed_ref.shape
    blocks = members * planes
    padded = qkv_ref.shape[0] // blocks
    mix_rows = piece - padded
    width = hidden_ref.shape[1]
    local_rows, full_rows = hidden_ref.shape[0], row_ref.shape[0]
    head = key_ref.shape[1]
    heads = query_ref.shape[1] // head
    offset = pl.multiple_of(lax.axis_index("seq") * local_rows, local_rows)
    mine = pl.ds(offset, local_rows)
    for i in range(blocks):
        member, plane = i // planes, i % planes
        block = packed_ref[member, plane]
        qkv_ref[padded * i : padded * (i + 1), :] = block[:padded]
        natural = mix_rows * (plane * members + member)
        output_ref[natural : natural + mix_rows, :] = block[padded:, :width]
        gain_rows[i : i + 1, :] = block[width_rows : width_rows + 1, : gain_rows.shape[1]].astype(f32)
    targets = (input_scale, query_scale, key_scale, attnout_scale, ffnin_scale, ffnout_scale)
    for k, (target, count) in enumerate(zip(targets, gain_widths)):
        rows = gain_rows[:, k * GAIN_SLOT : (k + 1) * GAIN_SLOT].astype(bf16)
        target[...] = spread_gain(rows, planes, count, count if k else padded, k == 0)

    row = row_ref[...].astype(f32)
    normed = (row * inverse_of(row, width) * input_scale[...]).astype(bf16)
    key_value = matmul(normed, qkv_ref[:, heads * head :])
    key_raw = key_value[:, :head]
    value_ref[...] = key_value[:, head:].astype(bf16)
    half = head // 2
    turned = turn(key_raw * inverse_of(key_raw, head) * key_scale[...], cos_ref[...], sin_ref[...])
    key_ref[:, :half], key_ref[:, half:] = turned[0].astype(bf16), turned[1].astype(bf16)

    row = row_ref[mine, :].astype(f32)
    normed = (row * inverse_of(row, width) * input_scale[...]).astype(bf16)
    own = matmul(normed, qkv_ref[:, : (heads + 1) * head])
    query_raw_ref[...] = own[:, : heads * head]
    key_raw_ref[...] = own[:, heads * head :]
    cos_table, sin_table = cos_ref[mine, :], sin_ref[mine, :]
    places = offset + lax.broadcasted_iota(jnp.int32, (local_rows, full_rows), 0)
    earlier = places >= lax.broadcasted_iota(jnp.int32, (local_rows, full_rows), 1)
    allowed = (segment_column[...] == segment_row[...]) & earlier
    for h in range(heads):
        at = h * head
        query_raw = query_raw_ref[:, at : at + head]
        turned = turn(
            query_raw * inverse_of(query_raw, head) * query_scale[...], cos_table, sin_table
        )
        scale = head ** (-0.5)
        query_ref[:, at : at + half] = (turned[0] * scale).astype(bf16)
        query_ref[:, at + half : at + head] = (turned[1] * scale).astype(bf16)
        scores = contract_cols(query_ref[:, at : at + head], key_ref[...])
        scores = jnp.where(allowed, scores, masked_score)
        weights = jnp.exp(scores - jnp.max(scores, axis=-1, keepdims=True))
        probs = weights / jnp.sum(weights, axis=-1, keepdims=True)
        probs_ref[h] = probs
        mix_ref[:, at : at + head] = matmul(probs.astype(bf16), value_ref[...]).astype(bf16)
    attn_raw = matmul(mix_ref[...], output_ref[...])
    raw_ref[...] = attn_raw
    middle = hidden_ref[...].astype(f32) + attn_raw * inverse_of(attn_raw, width) * attnout_scale[...]
    middle_ref[...] = middle
    ffn_in = (middle * inverse_of(middle, width) * ffnin_scale[...]).astype(bf16)
    placed_ref[...] = matmul(ffn_in, placing_ref[...]).astype(bf16)


def attention_forward(
    row_padded, hidden, packed, cos_full, sin_full, segment_column, segment_row, placing, gain_widths, width_rows, padded,
    head_width,
):
    bf16, f32 = jnp.bfloat16, jnp.float32
    members, planes, piece, qkv_width = packed.shape
    blocks = members * planes
    local_rows, width = hidden.shape
    query_width = qkv_width - 2 * head_width
    heads = query_width // head_width
    full_rows = row_padded.shape[0]
    depth = blocks * padded
    shape = jax.ShapeDtypeStruct
    vmem = pl.BlockSpec(memory_space=pltpu.VMEM)
    out_shape = [
        shape((local_rows, depth), bf16),
        shape((local_rows, width), f32),
        shape((local_rows, width), f32),
        shape((local_rows, query_width), bf16),
        shape((heads, local_rows, full_rows), f32),
        shape((local_rows, query_width), bf16),
        shape((full_rows, head_width), bf16),
        shape((full_rows, head_width), bf16),
        shape((local_rows, query_width), f32),
        shape((local_rows, head_width), f32),
        shape((depth, qkv_width), bf16),
        shape((query_width, width), bf16),
        shape((1, depth), f32),
        shape((1, head_width), f32),
        shape((1, head_width), f32),
        shape((1, width), f32),
        shape((1, width), f32),
        shape((1, width), f32),
    ]
    return pl.pallas_call(
        functools.partial(attention_forward_kernel, gain_widths, width_rows),
        out_shape=out_shape,
        in_specs=[vmem] * 8,
        out_specs=[vmem] * len(out_shape),
        scratch_shapes=[pltpu.VMEM((blocks, len(gain_widths) * GAIN_SLOT), f32)],
        cost_estimate=busy(20),
        compiler_params=pltpu.CompilerParams(vmem_limit_bytes=60 * 2**20),
    )(row_padded, hidden, packed, cos_full, sin_full, segment_column, segment_row, placing)


def attention_backward_kernel(
    gain_widths, width_rows, planes, grad_ref, incoming_ref, middle_ref, raw_ref, mix_ref, probs_ref, query_ref, key_ref,
    value_ref, query_raw_ref, key_raw_ref, row_ref, qkv_ref, output_ref, cos_ref, sin_ref, input_scale,
    query_scale, key_scale, attnout_scale, ffnin_scale, ffnout_grad, by_device, by_member,
    input_grad_ref, blocks_ref, key_value, query_grad, low_ref, leaving, arriving, send_sem, recv_sem,
):
    bf16, f32 = jnp.bfloat16, jnp.float32
    members = blocks_ref.shape[0]
    blocks = members * planes
    padded = qkv_ref.shape[0] // blocks
    mix_rows = blocks_ref.shape[2] - padded
    local_rows, width = incoming_ref.shape
    head = key_ref.shape[1]
    heads = query_ref.shape[1] // head
    half = head // 2
    seq = lax.axis_index("seq")
    mine = pl.ds(pl.multiple_of(seq * local_rows, local_rows), local_rows)
    theirs = pl.ds(pl.multiple_of((1 - seq) * local_rows, local_rows), local_rows)
    partner = plane_places()[2]
    greet((partner,))

    ffn_in_grad = take_back(grad_ref[...], by_device[...])
    middle = middle_ref[...]
    inverse = inverse_of(middle, width)
    normed = middle * inverse
    ffnin_grad = jnp.sum(ffn_in_grad * normed, axis=0, keepdims=True)
    middle_grad = incoming_ref[...].astype(f32) + back_of(
        ffn_in_grad * ffnin_scale[...], normed, inverse, width
    )
    input_grad_ref[...] = middle_grad
    raw = raw_ref[...]
    inverse = inverse_of(raw, width)
    normed = raw * inverse
    attnout_grad = jnp.sum(middle_grad * normed, axis=0, keepdims=True)
    raw_grad = back_of(middle_grad * attnout_scale[...], normed, inverse, width).astype(bf16)
    mix_grad = contract_cols(raw_grad, output_ref[...]).astype(bf16)
    for h in range(heads):
        at = h * head
        grad = mix_grad[:, at : at + head]
        probs = probs_ref[h]
        prob_grad = contract_cols(grad, value_ref[...])
        delta = jnp.sum(prob_grad * probs, axis=-1, keepdims=True)
        score_grad = (probs * (prob_grad - delta)).astype(bf16)
        to_keys = contract_rows(score_grad, query_ref[:, at : at + head])
        to_values = contract_rows(probs.astype(bf16), grad)
        if h == 0:
            key_value[:, :head], key_value[:, head:] = to_keys, to_values
        else:
            key_value[:, :head] += to_keys
            key_value[:, head:] += to_values
        query_grad[:, at : at + head] = matmul(score_grad, key_ref[...])
    leaving[...] = key_value[theirs, :].astype(bf16)
    copy = sender(send_sem, recv_sem)(0, leaving, arriving, partner)

    output_grad = contract_rows(mix_ref[...], raw_grad).astype(bf16)
    cos_table, sin_table = cos_ref[mine, :], sin_ref[mine, :]

    def head_back(grad, raw, scale_ref):
        turned = jnp.concatenate(turn(grad, cos_table, -sin_table), axis=1)
        inverse = inverse_of(raw, head)
        normed = raw * inverse
        gain = jnp.sum(turned * normed, axis=0, keepdims=True)
        return back_of(turned * scale_ref[...], normed, inverse, head).astype(bf16), gain

    query_gain = jnp.zeros((1, head), f32)
    for h in range(heads):
        at = h * head
        low, gain = head_back(
            query_grad[:, at : at + head] * head ** (-0.5),
            query_raw_ref[:, at : at + head],
            query_scale,
        )
        low_ref[:, at : at + head] = low
        query_gain = query_gain + gain
    copy.wait_recv()
    total = key_value[mine, :] + arriving[...].astype(f32)
    low, key_gain = head_back(total[:, :head], key_raw_ref[...], key_scale)
    low_ref[:, heads * head : (heads + 1) * head] = low
    low_ref[:, (heads + 1) * head :] = total[:, head:].astype(bf16)

    row = row_ref[mine, :].astype(f32)
    inverse = inverse_of(row, width)
    normed = row * inverse
    normed_grad = contract_cols(low_ref[...], qkv_ref[...])
    input_gain = jnp.sum(normed_grad * normed, axis=0, keepdims=True)
    input_grad_ref[...] += take_back(
        back_of(normed_grad * input_scale[...], normed, inverse, width), by_member[...]
    )
    vectors = (input_gain, query_gain, key_gain, attnout_grad, ffnin_grad, ffnout_grad[...])
    gains = jnp.concatenate(
        [
            collect_gain(vector, blocks, planes, count, count if k else padded, k == 0)
            for k, (vector, count) in enumerate(zip(vectors, gain_widths))
        ],
        axis=1,
    )
    lanes = gains.shape[1]
    normed = (normed * input_scale[...]).astype(bf16)
    weights = contract_rows(normed, low_ref[...])
    row_of = lax.broadcasted_iota(jnp.int32, (padded, lanes), 0)
    columns = blocks_ref.shape[3]
    for i in range(blocks):
        member, plane = i // planes, i % planes
        piece = weights[padded * i : padded * (i + 1)]
        first = jnp.where(row_of == width_rows, gains[i : i + 1], piece[:, :lanes])
        blocks_ref[member, plane, :padded, :lanes] = first.astype(bf16)
        blocks_ref[member, plane, :padded, lanes:] = piece[:, lanes:].astype(bf16)
        natural = mix_rows * (plane * members + member)
        blocks_ref[member, plane, padded:, :width] = output_grad[natural : natural + mix_rows]
        blocks_ref[member, plane, padded:, width:] = jnp.zeros((mix_rows, columns - width), bf16)
    copy.wait_send()


def attention_backward(arrays, gain_widths, width_rows, planes, mix_rows, collective_id):
    bf16, f32 = jnp.bfloat16, jnp.float32
    grad, incoming, query, key, qkv = arrays[0], arrays[1], arrays[6], arrays[7], arrays[12]
    local_rows, width = incoming.shape
    members = 8
    padded = qkv.shape[0] // (members * planes)
    pair = pltpu.VMEM((local_rows, 2 * key.shape[1]), bf16)
    shape = jax.ShapeDtypeStruct
    vmem = pl.BlockSpec(memory_space=pltpu.VMEM)
    return pl.pallas_call(
        functools.partial(attention_backward_kernel, gain_widths, width_rows, planes),
        out_shape=[
            shape((local_rows, width), f32),
            shape((members, planes, padded + mix_rows, qkv.shape[1]), bf16),
        ],
        in_specs=[vmem] * len(arrays),
        out_specs=[vmem] * 2,
        scratch_shapes=[
            pltpu.VMEM((key.shape[0], 2 * key.shape[1]), f32),
            pltpu.VMEM(query.shape, f32),
            pltpu.VMEM((local_rows, qkv.shape[1]), bf16),
            pair,
            pair,
            pltpu.SemaphoreType.DMA((1,)),
            pltpu.SemaphoreType.DMA((1,)),
        ],
        cost_estimate=busy(30),
        compiler_params=pltpu.CompilerParams(
            collective_id=collective_id, has_side_effects=True, vmem_limit_bytes=60 * 2**20
        ),
    )(*arrays)


def body(
    tokens,
    segment_ids,
    cotangent,
    query_weight,
    key_weight,
    value_weight,
    output_weight,
    gate_weight,
    up_weight,
    down_weight,
    input_gain,
    query_gain,
    key_gain,
    attnout_gain,
    ffnin_gain,
    ffnout_gain,
):
    bf16, f32 = jnp.bfloat16, jnp.float32
    devices = lax.axis_size(ALL)
    members = lax.axis_size(PLANE)
    planes = lax.axis_size(PLANES)
    cubes = lax.axis_size("far")
    group = lax.axis_size(CUBE)
    width_rows = query_weight.shape[0]
    hidden_rows = down_weight.shape[0]
    head_width = key_weight.shape[1]
    query_width = query_weight.shape[1]
    head_count = query_width // head_width
    qkv_width = query_width + 2 * head_width
    mix_rows = output_weight.shape[0]
    padded = up_to(width_rows + 1, 8)
    width = devices * width_rows
    unit_count = cubes * hidden_rows
    unit_pad = up_to(unit_count, 128)
    by_device = place_columns(devices, members, planes, width_rows, padded, False)
    by_member = place_columns(devices, members, planes, width_rows, padded, True)

    def column_blocks(weight):
        pieces = weight.reshape(width_rows, cubes, group, hidden_rows)
        pieces = pieces.transpose(2, 0, 1, 3).reshape(group, width_rows, unit_count)
        return jnp.pad(
            pieces, ((0, 0), (0, padded - width_rows), (0, unit_pad - unit_count))
        )

    gate_up = jnp.concatenate([column_blocks(gate_weight), column_blocks(up_weight)], axis=2)
    gate_up = jnp.broadcast_to(gate_up[None], (cubes,) + gate_up.shape)
    gate_up = gate_up.reshape((devices,) + gate_up.shape[2:])

    gains = (input_gain, query_gain, key_gain, attnout_gain, ffnin_gain, ffnout_gain)
    gain_widths = [g.shape[0] for g in gains]
    gain_row = jnp.concatenate(
        [jnp.pad(g[None], ((0, 0), (0, GAIN_SLOT - g.shape[0]))) for g in gains], axis=1
    )
    gain_row = jnp.pad(gain_row, ((0, 0), (0, qkv_width - gain_row.shape[1])))
    qkv_local = jnp.concatenate([query_weight, key_weight, value_weight], axis=1)
    packed = jnp.concatenate([qkv_local, gain_row], axis=0)
    packed = jnp.pad(packed, ((0, padded - width_rows - 1), (0, 0)))
    output_wide = jnp.pad(output_weight, ((0, 0), (0, qkv_width - output_weight.shape[1])))
    packed = jnp.concatenate([packed, output_wide], axis=0)
    packed_all = z_gather(packed, planes, 0)
    far = lax.axis_index("far")
    down_terms = [down_weight]
    for k in range(1, cubes):
        shift = [(i, (i + k) % cubes) for i in range(cubes)]
        down_terms.append(lax.ppermute(down_weight, "far", shift))
    packed_all, *down_terms = lax.optimization_barrier((packed_all, *down_terms))
    packed_all = plane_gather(packed_all, 6)
    gate_up, packed_all = lax.optimization_barrier((gate_up, packed_all))
    gate_up_full = exchange(gate_up, ALL).reshape(devices * padded, 2 * unit_pad)
    down_full = jnp.zeros((cubes, *down_weight.shape), bf16)
    for k, term in enumerate(down_terms):
        at = lax.rem(far - k + cubes, cubes)
        down_full = lax.dynamic_update_index_in_dim(down_full, term, at, 0)
    down_full = down_full.reshape(unit_count, down_weight.shape[1])
    incoming = cotangent[0].astype(f32)
    local_rows = tokens.shape[1]
    offset = lax.axis_index("seq") * local_rows
    segment_row = segment_ids[0]

    def mine(rows):
        return lax.dynamic_slice_in_dim(rows, offset, local_rows)

    cos_full, sin_full = rope_tables(doc_positions(segment_row), head_width)

    other_half = [(0, 1), (1, 0)]
    first = lax.axis_index("seq") == 0
    other_tokens = lax.ppermute(tokens[0], "seq", other_half)
    row_tokens = jnp.concatenate(
        [
            jnp.where(first, tokens[0], other_tokens),
            jnp.where(first, other_tokens, tokens[0]),
        ]
    )
    row_padded = matmul(row_tokens, by_member).astype(bf16)
    (
        ffn_in_placed,
        middle,
        attn_raw,
        attn_flat,
        probs,
        queries,
        key_rows,
        value_rows,
        query_raw,
        key_raw,
        qkv_full,
        output_full,
        *scales,
    ) = attention_forward(
        row_padded,
        tokens[0],
        packed_all,
        cos_full,
        sin_full,
        mine(segment_row)[:, None],
        segment_row[None],
        by_device,
        gain_widths,
        width_rows,
        padded,
        head_width,
    )
    ffnout_scale = scales.pop()

    cube_in = gather_rows(ffn_in_placed, 1)
    ffn_part, activated_low, to_gate, to_up = ffn_forward(cube_in, gate_up_full, down_full)
    ffn_part = ffn_part.reshape(group, local_rows // 16, 16, ffn_part.shape[1])
    ffn_raw = cube_scatter_sum(ffn_part, 2)
    inv_ffn = inverse_rms(ffn_raw)
    norm_ffn = ffn_raw * inv_ffn
    result = middle + norm_ffn * ffnout_scale
    ffnout_gain_grad = jnp.sum(incoming * norm_ffn, axis=0)
    ffn_raw_grad = rms_back(incoming * ffnout_scale, norm_ffn, inv_ffn).astype(bf16)

    gate_up_low, ffn_in_part, down_blocks = gather_backward(
        ffn_raw_grad, down_full, gate_up_full, to_gate, to_up, activated_low, 3
    )
    down_blocks = down_blocks.reshape(cubes, hidden_rows, down_weight.shape[1])
    ffn_in_grad, gate_up_blocks, down_wgrad = sum_gradients(
        ffn_in_part, down_blocks, cube_in, gate_up_low, 4
    )
    gate_up_terms = exchange(gate_up_blocks.reshape(devices, padded, 2 * unit_pad), ALL)
    input_grad, blocks = attention_backward(
        [
            ffn_in_grad,
            cotangent[0],
            middle,
            attn_raw,
            attn_flat,
            probs,
            queries,
            key_rows,
            value_rows,
            query_raw,
            key_raw,
            row_padded,
            qkv_full,
            output_full,
            cos_full,
            sin_full,
            *scales,
            ffnout_gain_grad[None],
            by_device,
            by_member,
        ],
        gain_widths,
        width_rows,
        planes,
        mix_rows,
        7,
    )
    share = owner_sum(blocks, 5)
    gate_up_sum = jnp.sum(
        gate_up_terms.reshape(cubes, group, padded, 2 * unit_pad).astype(f32), axis=0
    )

    def unit_columns(total):
        total = total[:, :width_rows, :unit_count].reshape(
            group, width_rows, cubes, hidden_rows
        )
        return total.transpose(1, 2, 0, 3).reshape(width_rows, cubes * group * hidden_rows)

    gate_wgrad = unit_columns(gate_up_sum[:, :, :unit_pad])
    up_wgrad = unit_columns(gate_up_sum[:, :, unit_pad:])
    qkv_share, output_share = share[:padded], share[padded:, : output_weight.shape[1]]
    gain_shares = [
        qkv_share[width_rows, k * GAIN_SLOT : k * GAIN_SLOT + count]
        for k, count in enumerate(gain_widths)
    ]
    return (
        result.astype(bf16)[None],
        input_grad[None],
        qkv_share[:width_rows, :query_width],
        qkv_share[:width_rows, query_width : query_width + head_width],
        qkv_share[:width_rows, query_width + head_width :],
        output_share,
        gate_wgrad,
        up_wgrad,
        down_wgrad,
        *gain_shares,
    )


def solution(mesh):
    dp, seq = mesh.shape["dp"], mesh.shape["seq"]
    split = Mesh(mesh.devices.reshape(dp // 8, 2, 2, 2, seq), ALL)
    rows = P(("far", "z", "x", "core"), "seq", None)
    matrix, vector = P(ALL, None), P(ALL)
    return jax.shard_map(
        body,
        mesh=split,
        in_specs=(rows, P(("far", "z", "x", "core"), None), rows) + (matrix,) * 7 + (vector,) * 6,
        out_specs=(rows, rows) + (matrix,) * 7 + (vector,) * 6,
        check_vma=False,
    )
```

```python
import functools

import jax
import jax.numpy as jnp
import numpy as np
from jax import lax
from jax.experimental import pallas as pl
from jax.experimental.pallas import tpu as pltpu
from jax.sharding import Mesh
from jax.sharding import PartitionSpec as P

epsilon = 1e-06
rope_base = 1000000.0
masked_score = -1e30


def inverse_rms(values):
    return lax.rsqrt(jnp.mean(values * values, axis=-1, keepdims=True) + epsilon)


def rms_back(grad_normed, normed, inverse):
    return inverse * (grad_normed - normed * jnp.mean(grad_normed * normed, axis=-1, keepdims=True))


def doc_positions(segments):
    length = segments.shape[0]
    smaller = segments[None, :] < segments[:, None]
    starts = jnp.sum(smaller.astype(jnp.int32), axis=1)
    return (jnp.arange(length, dtype=jnp.int32) - starts).astype(jnp.float32)


def rope_tables(positions, head_width):
    half_width = head_width // 2
    frequency = rope_base ** (-(2.0 / head_width) * jnp.arange(half_width, dtype=jnp.float32))
    angles = positions[..., None] * frequency
    return (jnp.cos(angles), jnp.sin(angles))


def matmul(left, right):
    return jnp.dot(left, right, preferred_element_type=jnp.float32)


def contract_rows(left, right):
    return lax.dot_general(
        left, right, (((0,), (0,)), ((), ())), preferred_element_type=jnp.float32
    )


def contract_cols(left, right):
    return lax.dot_general(
        left, right, (((1,), (1,)), ((), ())), preferred_element_type=jnp.float32
    )


ALL = ("far", "z", "x", "core", "seq")
PLANES = ("far", "z")
CUBE = ("z", "x", "core", "seq")


def up_to(size, multiple):
    return (size + multiple - 1) // multiple * multiple


def place_columns(blocks, members, planes, rows, padded, by_member):
    source = np.arange(blocks * rows)
    block, inner = source // rows, source % rows
    if by_member:
        block = block % members * planes + block // members
    placing = np.zeros((blocks * rows, blocks * padded), np.float32)
    placing[source, block * padded + inner] = 1.0
    return jnp.asarray(placing.astype(jnp.bfloat16))


def take_back(padded_values, placing):
    high = lax.reduce_precision(padded_values, 8, 7)
    terms = jnp.concatenate([high, padded_values - high], axis=0).astype(jnp.bfloat16)
    both = contract_cols(terms, placing)
    rows = padded_values.shape[0]
    return both[:rows] + both[rows:]


PLANE = ("x", "core", "seq")

MESH_ID = pl.DeviceIdType.MESH
VMEM_BYTES = 48 * 2**20


def exchange(blocks, axes):
    return lax.all_to_all(blocks, axes, split_axis=0, concat_axis=0, tiled=True)


def busy(microseconds):
    return pl.CostEstimate(flops=0, bytes_accessed=microseconds * 3_000_000, transcendentals=0)


def shifted(flip_z, flip_x, flip_core, flip_y):
    far, *inner = (lax.axis_index(name) for name in ALL)
    flips = (flip_z, flip_x, flip_core, flip_y)
    return (far, *(1 - at if flip else at for at, flip in zip(inner, flips)))


def plane_places():
    def member(flip_x, flip_core, flip_y):
        _, _, x, core, seq = shifted(0, flip_x, flip_core, flip_y)
        return (x * 2 + core) * 2 + seq

    return shifted(0, 0, 1, 0), shifted(0, 1, 0, 0), shifted(0, 0, 0, 1), member


def cube_member(flip_z, flip_x, flip_y, flip_core):
    _, z, x, core, seq = shifted(flip_z, flip_x, flip_core, flip_y)
    return ((z * 2 + x) * 2 + core) * 2 + seq


def cube_places():
    return *plane_places()[:3], shifted(1, 0, 0, 0)


def other_planes(planes):
    far, z, x, core, seq = (lax.axis_index(name) for name in ALL)
    plane = far * 2 + z
    ring = [lax.rem(plane + k, planes) for k in range(1, planes)]
    return plane, [(at // 2, lax.rem(at, 2), x, core, seq) for at in ring], ring


def other_cubes(cubes):
    far, z, x, core, seq = (lax.axis_index(name) for name in ALL)
    return far, [(lax.rem(far + k, cubes), z, x, core, seq) for k in range(1, cubes)]


def greet(places):
    barrier = pltpu.get_barrier_semaphore()
    for place in places:
        pl.semaphore_signal(barrier, inc=1, device_id=place, device_id_type=MESH_ID)
    pl.semaphore_wait(barrier, len(places))


def sender(send_sems, recv_sems):
    def send(kind, source, target, place):
        copy = pltpu.make_async_remote_copy(
            src_ref=source,
            dst_ref=target,
            send_sem=send_sems.at[kind],
            recv_sem=recv_sems.at[kind],
            device_id=place,
            device_id_type=MESH_ID,
        )
        copy.start()
        return copy

    return send


def plane_spread(own_ref, out_ref, send_sems, recv_sems, local_sem):
    sibling, along_x, along_y, member = plane_places()
    half = own_ref.shape[0] // 2
    top, bottom = pl.ds(0, half), pl.ds(half, half)
    me = member(0, 0, 0)
    keep = pltpu.make_async_copy(own_ref, out_ref.at[me], local_sem)
    keep.start()
    send = sender(send_sems, recv_sems)

    def forward(kind, block, rows, place):
        return send(kind, out_ref.at[block, rows], out_ref.at[block, rows], place)

    own_x_top = send(1, own_ref.at[top], out_ref.at[me, top], along_x)
    own_y_bottom = send(3, own_ref.at[bottom], out_ref.at[me, bottom], along_y)
    own_sibling = send(0, own_ref, out_ref.at[me], sibling)
    own_x_bottom = send(2, own_ref.at[bottom], out_ref.at[me, bottom], along_x)
    own_y_top = send(4, own_ref.at[top], out_ref.at[me, top], along_y)
    x_block, y_block, diagonal = member(1, 0, 0), member(0, 0, 1), member(1, 0, 1)
    own_x_top.wait_recv()
    diagonal_top = forward(5, x_block, top, along_y)
    x_top = forward(7, x_block, top, sibling)
    own_y_bottom.wait_recv()
    diagonal_bottom = forward(6, y_block, bottom, along_x)
    y_bottom = forward(9, y_block, bottom, sibling)
    own_x_bottom.wait_recv()
    x_bottom = forward(8, x_block, bottom, sibling)
    own_y_top.wait_recv()
    y_top = forward(10, y_block, top, sibling)
    diagonal_top.wait_recv()
    far_top = forward(11, diagonal, top, sibling)
    diagonal_bottom.wait_recv()
    far_bottom = forward(12, diagonal, bottom, sibling)
    for copy in (own_sibling, x_top, y_bottom, x_bottom, y_top, far_top, far_bottom):
        copy.wait_recv()
    for copy in (
        own_x_top,
        own_y_bottom,
        own_sibling,
        own_x_bottom,
        own_y_top,
        diagonal_top,
        diagonal_bottom,
        x_top,
        y_bottom,
        x_bottom,
        y_top,
        far_top,
        far_bottom,
    ):
        copy.wait_send()
    keep.wait()


def cube_spread(own_ref, out_ref, send_sems, recv_sems, local_sem, compute=lambda i: None):
    sibling, along_x, along_y, along_z = cube_places()
    half = own_ref.shape[0] // 2
    top, bottom = pl.ds(0, half), pl.ds(half, half)
    me = cube_member(0, 0, 0, 0)
    keep = pltpu.make_async_copy(own_ref, out_ref.at[me], local_sem)
    keep.start()
    send = sender(send_sems, recv_sems)
    x_block, y_block, diagonal = (cube_member(0, *at, 0) for at in ((1, 0), (0, 1), (1, 1)))
    z_block, zx_block, zy_block, zd_block = (
        cube_member(1, *at, 0) for at in ((0, 0), (1, 0), (0, 1), (1, 1))
    )

    def half_on(kind, block, rows, place):
        return send(kind, out_ref.at[block, rows], out_ref.at[block, rows], place)

    def on(kind, block, place):
        return send(kind, out_ref.at[block], out_ref.at[block], place)

    own_x_top = send(1, own_ref.at[top], out_ref.at[me, top], along_x)
    own_y_bottom = send(3, own_ref.at[bottom], out_ref.at[me, bottom], along_y)
    own_z = send(13, own_ref, out_ref.at[me], along_z)
    own_sibling = send(0, own_ref, out_ref.at[me], sibling)
    own_x_bottom = send(2, own_ref.at[bottom], out_ref.at[me, bottom], along_x)
    own_y_top = send(4, own_ref.at[top], out_ref.at[me, top], along_y)
    compute(0)
    own_x_top.wait_recv()
    diagonal_top = half_on(5, x_block, top, along_y)
    x_top = half_on(7, x_block, top, sibling)
    own_y_bottom.wait_recv()
    diagonal_bottom = half_on(6, y_block, bottom, along_x)
    y_bottom = half_on(9, y_block, bottom, sibling)
    own_sibling.wait_recv()
    compute(1)
    own_z.wait_recv()
    z_to_x = on(14, z_block, along_x)
    z_to_y = on(15, z_block, along_y)
    z_near = on(16, z_block, sibling)
    own_x_bottom.wait_recv()
    x_bottom = half_on(8, x_block, bottom, sibling)
    own_y_top.wait_recv()
    y_top = half_on(10, y_block, top, sibling)
    compute(2)
    diagonal_top.wait_recv()
    far_top = half_on(11, diagonal, top, sibling)
    diagonal_bottom.wait_recv()
    far_bottom = half_on(12, diagonal, bottom, sibling)
    diagonal_z = on(17, diagonal, along_z)
    compute(3)
    compute(4)
    z_to_x.wait_recv()
    zx_near = on(18, zx_block, sibling)
    z_to_y.wait_recv()
    zy_near = on(19, zy_block, sibling)
    compute(5)
    compute(6)
    diagonal_z.wait_recv()
    zd_near = on(20, zd_block, sibling)
    compute(7)
    compute(8)
    last = (
        (x_top, x_bottom), (y_bottom, y_top), (far_top, far_bottom), (z_near,), (zx_near,), (zy_near,), (zd_near,),
    )
    for i, copies in enumerate(last):
        for copy in copies:
            copy.wait_recv()
        compute(9 + i)
    for copy in (
        own_x_top, own_y_bottom, own_z, own_sibling, own_x_bottom, own_y_top, diagonal_top, diagonal_bottom,
        z_to_x, z_to_y, diagonal_z,
    ):
        copy.wait_send()
    for copies in last:
        for copy in copies:
            copy.wait_send()
    keep.wait()


CUBE_ORDER = (
    (0, 0, 0, 0), (0, 0, 0, 1), (0, 1, 0, 0), (0, 0, 1, 0), (1, 0, 0, 0), (0, 1, 1, 0), (1, 1, 0, 0), (1, 0, 1, 0),
    (1, 1, 1, 0), (0, 1, 0, 1), (0, 0, 1, 1), (0, 1, 1, 1), (1, 0, 0, 1), (1, 1, 0, 1), (1, 0, 1, 1), (1, 1, 1, 1),
)


def cube_gather_kernel(own_ref, out_ref, *sems):
    greet(cube_places())
    cube_spread(own_ref, out_ref, *sems)


def weights_gather_kernel(cubes, own_ref, down_ref, out_ref, down_out, far_send, far_recv, own_sem, *sems):
    far, others = other_cubes(cubes)
    greet((*plane_places()[:3], *others))
    keep = pltpu.make_async_copy(down_ref, down_out.at[far], own_sem)
    keep.start()
    send = sender(far_send, far_recv)
    copies = [send(k, down_ref, down_out.at[far], place) for k, place in enumerate(others)]
    plane_spread(own_ref, out_ref, *sems)
    for copy in copies:
        copy.wait_recv()
    for copy in copies:
        copy.wait_send()
    keep.wait()


def z_gather_kernel(planes, own_ref, out_ref, send_sems, recv_sems, own_sem):
    plane, others, _ = other_planes(planes)
    greet(others)
    keep = pltpu.make_async_copy(own_ref, out_ref.at[plane], own_sem)
    keep.start()
    send = sender(send_sems, recv_sems)
    copies = [send(k, own_ref, out_ref.at[plane], place) for k, place in enumerate(others)]
    for copy in copies:
        copy.wait_recv()
    for copy in copies:
        copy.wait_send()
    keep.wait()


def gather_sems(count):
    return [
        pltpu.SemaphoreType.DMA((count,)),
        pltpu.SemaphoreType.DMA((count,)),
        pltpu.SemaphoreType.DMA,
    ]


def z_gather(local, planes, collective_id):
    return pl.pallas_call(
        functools.partial(z_gather_kernel, planes),
        out_shape=jax.ShapeDtypeStruct((planes, *local.shape), local.dtype),
        in_specs=[pl.BlockSpec(memory_space=pltpu.VMEM)],
        out_specs=pl.BlockSpec(memory_space=pl.ANY),
        scratch_shapes=[
            pltpu.SemaphoreType.DMA((planes - 1,)),
            pltpu.SemaphoreType.DMA((planes - 1,)),
            pltpu.SemaphoreType.DMA,
        ],
        cost_estimate=busy(20),
        compiler_params=pltpu.CompilerParams(
            collective_id=collective_id, has_side_effects=True, vmem_limit_bytes=VMEM_BYTES
        ),
    )(local)


def weights_gather(local, down, cubes, collective_id):
    members = 8
    anywhere = pl.BlockSpec(memory_space=pl.ANY)
    return pl.pallas_call(
        functools.partial(weights_gather_kernel, cubes),
        out_shape=[
            jax.ShapeDtypeStruct((members, *local.shape), local.dtype),
            jax.ShapeDtypeStruct((cubes, *down.shape), down.dtype),
        ],
        in_specs=[anywhere, anywhere],
        out_specs=[anywhere, anywhere],
        scratch_shapes=[
            pltpu.SemaphoreType.DMA((cubes - 1,)),
            pltpu.SemaphoreType.DMA((cubes - 1,)),
            pltpu.SemaphoreType.DMA,
            *gather_sems(13),
        ],
        cost_estimate=busy(30),
        compiler_params=pltpu.CompilerParams(
            collective_id=collective_id, has_side_effects=True, vmem_limit_bytes=VMEM_BYTES
        ),
    )(local, down)


def gather_rows(local, collective_id):
    rows, columns = local.shape
    members = 16
    out = pl.pallas_call(
        cube_gather_kernel,
        out_shape=jax.ShapeDtypeStruct((members, rows // 16, 16, columns), local.dtype),
        in_specs=[pl.BlockSpec(memory_space=pl.ANY)],
        out_specs=pl.BlockSpec(memory_space=pl.ANY),
        scratch_shapes=gather_sems(21),
        cost_estimate=busy(35),
        compiler_params=pltpu.CompilerParams(
            collective_id=collective_id, has_side_effects=True, vmem_limit_bytes=VMEM_BYTES
        ),
    )(local.reshape(rows // 16, 16, columns))
    return out.reshape(-1, columns)


def add_rows(target, sources, start, count):
    def one(i, carry):
        total = sources[0][i].astype(jnp.float32)
        for source in sources[1:]:
            total = total + source[i].astype(jnp.float32)
        target[i] = total.astype(target.dtype)
        return carry

    lax.fori_loop(start, start + count, one, 0)


def plane_sum(part_ref, own_sum, near, sums, from_x, from_y, far_x, far_y, send_sems, recv_sems):
    sibling, along_x, along_y, member = plane_places()
    rows = own_sum.shape[0]
    half = rows // 2
    top, bottom = pl.ds(0, half), pl.ds(half, half)
    send = sender(send_sems, recv_sems)
    chips = ((1, 1), (1, 0), (0, 1), (0, 0))
    mine = [part_ref.at[member(at_x, 0, at_y)] for at_x, at_y in chips]
    to_sibling = [
        send(k, part_ref.at[member(at_x, 1, at_y)], near.at[k], sibling)
        for k, (at_x, at_y) in enumerate(chips)
    ]
    to_sibling[0].wait_recv()
    add_rows(sums.at[0], (mine[0], near.at[0]), 0, rows)
    diagonal_x = send(4, sums.at[0, bottom], far_x.at[bottom], along_x)
    diagonal_y = send(5, sums.at[0, top], far_y.at[top], along_y)
    to_sibling[1].wait_recv()
    add_rows(sums.at[1], (mine[1], near.at[1]), half, half)
    direct_x = send(6, sums.at[1, bottom], from_x.at[bottom], along_x)
    to_sibling[2].wait_recv()
    add_rows(sums.at[2], (mine[2], near.at[2]), 0, half)
    direct_y = send(7, sums.at[2, top], from_y.at[top], along_y)
    to_sibling[3].wait_recv()
    diagonal_y.wait_recv()
    add_rows(sums.at[1], (mine[1], near.at[1], far_y), 0, half)
    joint_x = send(8, sums.at[1, top], from_x.at[top], along_x)
    diagonal_x.wait_recv()
    add_rows(sums.at[2], (mine[2], near.at[2], far_x), half, half)
    joint_y = send(9, sums.at[2, bottom], from_y.at[bottom], along_y)
    direct_x.wait_recv()
    direct_y.wait_recv()
    joint_x.wait_recv()
    joint_y.wait_recv()
    add_rows(own_sum, (mine[3], near.at[3], from_x, from_y), 0, rows)
    for copy in (*to_sibling, diagonal_x, diagonal_y, direct_x, direct_y, joint_x, joint_y):
        copy.wait_send()


def cube_sum(
    part_hbm, own_sum, mine, near, via_z, zx_in, zy_in, far_x, far_y, from_x, from_y, from_z, load_sems, send_sems,
    recv_sems, work=lambda point: None,
):
    sibling, along_x, along_y, along_z = cube_places()
    pieces = own_sum.shape[0]
    half = pieces // 2
    top, bottom = pl.ds(0, half), pl.ds(half, half)
    send = sender(send_sems, recv_sems)
    chips = ((1, 1, 1), (1, 1, 0), (1, 0, 1), (0, 1, 0), (0, 0, 1), (0, 1, 1), (1, 0, 0), (0, 0, 0))
    z_diagonal, z_x, z_y, at_x, at_y, diagonal, at_z, here = range(8)
    to_sibling = [
        send(k, part_hbm.at[cube_member(*chip, 1)], near.at[k], sibling)
        for k, chip in enumerate(chips)
    ]
    loads = [
        pltpu.make_async_copy(part_hbm.at[cube_member(*chip, 0)], mine.at[k], load_sems.at[k])
        for k, chip in enumerate(chips)
    ]
    for load in loads:
        load.start()

    def both_in(k):
        to_sibling[k].wait_recv()
        loads[k].wait()

    def add(k, others=(), start=0, count=pieces):
        add_rows(near.at[k], (mine.at[k], near.at[k], *others), start, count)

    work(0)
    both_in(z_diagonal)
    add(z_diagonal)
    diagonal_z = send(8, near.at[z_diagonal], via_z, along_z)
    both_in(z_x)
    add(z_x)
    zx_out = send(9, near.at[z_x], zx_in, along_x)
    both_in(z_y)
    add(z_y)
    zy_out = send(10, near.at[z_y], zy_in, along_y)
    both_in(at_x)
    add(at_x, (), half, half)
    direct_x = send(13, near.at[at_x, bottom], from_x.at[bottom], along_x)
    both_in(at_y)
    add(at_y, (), 0, half)
    direct_y = send(14, near.at[at_y, top], from_y.at[top], along_y)
    both_in(diagonal)
    both_in(at_z)
    work(1)
    diagonal_z.wait_recv()
    add(diagonal, (via_z,))
    diagonal_x = send(11, near.at[diagonal, bottom], far_x.at[bottom], along_x)
    diagonal_y = send(12, near.at[diagonal, top], far_y.at[top], along_y)
    zx_out.wait_recv()
    zy_out.wait_recv()
    add(at_z, (zx_in, zy_in))
    joint_z = send(15, near.at[at_z], from_z, along_z)
    work(2)
    diagonal_y.wait_recv()
    add(at_x, (far_y,), 0, half)
    joint_x = send(16, near.at[at_x, top], from_x.at[top], along_x)
    diagonal_x.wait_recv()
    add(at_y, (far_x,), half, half)
    joint_y = send(17, near.at[at_y, bottom], from_y.at[bottom], along_y)
    both_in(here)
    work(3)
    for copy in (direct_x, direct_y, joint_z, joint_x, joint_y):
        copy.wait_recv()
    add_rows(own_sum, (mine.at[here], near.at[here], from_x, from_y, from_z), 0, pieces)
    for copy in (
        *to_sibling, diagonal_z, zx_out, zy_out, direct_x, direct_y, diagonal_x, diagonal_y, joint_z, joint_x, joint_y,
    ):
        copy.wait_send()


def cube_sum_kernel(part_ref, out_ref, *scratch):
    greet(cube_places())
    cube_sum(part_ref, out_ref, *scratch)


def cube_sum_scratch(shape, dtype):
    return [
        pltpu.VMEM((8, *shape), dtype),
        pltpu.VMEM((8, *shape), dtype),
        *[pltpu.VMEM(shape, dtype)] * 8,
        pltpu.SemaphoreType.DMA((8,)),
        pltpu.SemaphoreType.DMA((18,)),
        pltpu.SemaphoreType.DMA((18,)),
    ]


def plane_sum_scratch(shape, dtype):
    block = pltpu.VMEM(shape, dtype)
    return [
        pltpu.VMEM((4, *shape), dtype),
        pltpu.VMEM((3, *shape), dtype),
        block,
        block,
        block,
        block,
        pltpu.SemaphoreType.DMA((10,)),
        pltpu.SemaphoreType.DMA((10,)),
    ]


def cube_scatter_sum(partial, collective_id):
    shape = partial.shape[1:]
    out = pl.pallas_call(
        cube_sum_kernel,
        out_shape=jax.ShapeDtypeStruct(shape, jnp.float32),
        in_specs=[pl.BlockSpec(memory_space=pl.ANY)],
        out_specs=pl.BlockSpec(memory_space=pltpu.VMEM),
        scratch_shapes=cube_sum_scratch(shape, partial.dtype),
        cost_estimate=busy(35),
        compiler_params=pltpu.CompilerParams(
            collective_id=collective_id, has_side_effects=True, vmem_limit_bytes=VMEM_BYTES
        ),
    )(partial)
    return out.reshape(shape[0] * shape[1], shape[2])


gelu_inner = 0.7978845608028654
gelu_cubic = 0.044715


def pad_rows(target, source):
    rows = source.shape[0]
    target[pl.ds(0, rows)] = source[...]
    if target.shape[0] > rows:
        extra = target.shape[0] - rows
        target[pl.ds(rows, extra)] = jnp.zeros((extra, target.shape[1]), target.dtype)


def ffn_forward_kernel(in_ref, gate_up_ref, down_ref, part_ref, act_ref, to_gate, to_up, down, proj):
    units = act_ref.shape[1]

    @pl.when(pl.program_id(0) == 0)
    def _():
        pad_rows(down, down_ref)

    step = 64
    half_rows = in_ref.shape[0] // 2

    def mid(base):
        for i in range(half_rows // step):
            rows = pl.ds(base + i * step, step)
            gate, up = proj[rows, :units], proj[rows, units:]
            square = gate * gate
            bend = jnp.tanh(gelu_inner * gate * (1.0 + gelu_cubic * square))
            half = 0.5 * (1.0 + bend)
            value = gate * half
            slope = half + 0.5 * gate * (1.0 - bend * bend) * (
                gelu_inner * (1.0 + 3.0 * gelu_cubic * square)
            )
            to_gate[rows, :] = slope * up
            to_up[rows, :] = value
            act_ref[rows, :] = (value * up).astype(act_ref.dtype)

    first, second = pl.ds(0, half_rows), pl.ds(half_rows, half_rows)
    proj[first, :] = matmul(in_ref[first, :], gate_up_ref[...])
    proj[second, :] = matmul(in_ref[second, :], gate_up_ref[...])
    mid(0)
    part_ref[first, :] = matmul(act_ref[first, :], down[...]).astype(part_ref.dtype)
    mid(half_rows)
    part_ref[second, :] = matmul(act_ref[second, :], down[...]).astype(part_ref.dtype)


ROW_BLOCK = 512


def whole(array):
    return pl.BlockSpec(array.shape, lambda i: (0, 0), pipeline_mode=pl.Buffered(1))


def row_block(columns):
    return pl.BlockSpec((ROW_BLOCK, columns), lambda i: (i, 0))


def ffn_forward(rows_in, gate_up, down):
    rows, depth = rows_in.shape
    units, columns = gate_up.shape[1] // 2, down.shape[1]
    low = rows_in.dtype
    return pl.pallas_call(
        ffn_forward_kernel,
        grid=(rows // ROW_BLOCK,),
        in_specs=[row_block(depth), whole(gate_up), whole(down)],
        out_specs=[row_block(columns), row_block(units), row_block(units), row_block(units)],
        out_shape=[
            jax.ShapeDtypeStruct((rows, columns), low),
            jax.ShapeDtypeStruct((rows, units), low),
            jax.ShapeDtypeStruct((rows, units), jnp.float32),
            jax.ShapeDtypeStruct((rows, units), jnp.float32),
        ],
        scratch_shapes=[
            pltpu.VMEM((units, columns), low),
            pltpu.VMEM((ROW_BLOCK, 2 * units), jnp.float32),
        ],
        cost_estimate=busy(20),
        compiler_params=pltpu.CompilerParams(vmem_limit_bytes=VMEM_BYTES),
    )(rows_in, gate_up, down)


def block_order(rows):
    order = [cube_member(*flips) for flips in CUBE_ORDER]
    return order, [pl.ds(pl.multiple_of(block * rows, rows), rows) for block in order]


def gather_backward_kernel(
    own_ref, down_ref, gate_up_ref, to_gate_hbm, to_up_hbm, act_hbm, both_hbm, part_hbm, down_grad_ref,
    grad, down, to_gate, to_up, act, both, part, act_sem, load_sems, put_sems, send_sems, recv_sems, local_sem,
):
    units = down.shape[0]
    pieces, piece, columns = own_ref.shape
    rows = pieces * piece
    order, places = block_order(rows)

    def loads(i):
        slot, at = i % 2, places[i]
        return (
            pltpu.make_async_copy(to_gate_hbm.at[at], to_gate.at[slot], load_sems.at[0, slot]),
            pltpu.make_async_copy(to_up_hbm.at[at], to_up.at[slot], load_sems.at[1, slot]),
        )

    def puts(i):
        slot = i % 2
        return (
            pltpu.make_async_copy(both.at[slot], both_hbm.at[places[i]], put_sems.at[0, slot]),
            pltpu.make_async_copy(part.at[slot], part_hbm.at[order[i]], put_sems.at[1, slot]),
        )

    def compute(i):
        if i + 1 < len(order):
            for load in loads(i + 1):
                load.start()
        for load in loads(i):
            load.wait()
        if i >= 2:
            for put in puts(i - 2):
                put.wait()
        slot = i % 2
        source = own_ref if i == 0 else grad.at[order[i]]
        act_grad = contract_cols(source[...].reshape(rows, columns), down[...])
        both[slot, :, :units] = (act_grad * to_gate[slot]).astype(both.dtype)
        both[slot, :, units:] = (act_grad * to_up[slot]).astype(both.dtype)
        result = contract_cols(both[slot], gate_up_ref[...]).astype(part.dtype)
        part[slot] = result.reshape(pieces, piece, result.shape[1])
        for put in puts(i):
            put.start()

    act_load = pltpu.make_async_copy(act_hbm, act, act_sem)
    act_load.start()
    for load in loads(0):
        load.start()
    pad_rows(down, down_ref)
    greet(cube_places())
    cube_spread(own_ref, grad, send_sems, recv_sems, local_sem, compute)
    act_load.wait()
    whole = grad[...].reshape(len(order) * rows, columns)
    down_grad = contract_rows(act[...], whole)
    down_grad_ref[...] = down_grad[: down_ref.shape[0]].astype(down_grad_ref.dtype)
    for i in (len(order) - 2, len(order) - 1):
        for put in puts(i):
            put.wait()


def gather_backward(own, down, gate_up, to_gate, to_up, act, collective_id):
    rows, columns = own.shape
    members, piece = 16, 16
    pieces = rows // piece
    depth, units = gate_up.shape[0], to_gate.shape[1]
    low, wide = own.dtype, jnp.float32
    shape = jax.ShapeDtypeStruct
    vmem, anywhere = pl.BlockSpec(memory_space=pltpu.VMEM), pl.BlockSpec(memory_space=pl.ANY)
    return pl.pallas_call(
        gather_backward_kernel,
        out_shape=[
            shape((members * rows, 2 * units), low),
            shape((members, pieces, piece, depth), low),
            shape(down.shape, low),
        ],
        in_specs=[vmem, vmem, vmem, anywhere, anywhere, anywhere],
        out_specs=[anywhere, anywhere, vmem],
        scratch_shapes=[
            pltpu.VMEM((members, pieces, piece, columns), low),
            pltpu.VMEM((units, columns), low),
            pltpu.VMEM((2, rows, units), wide),
            pltpu.VMEM((2, rows, units), wide),
            pltpu.VMEM(act.shape, low),
            pltpu.VMEM((2, rows, 2 * units), low),
            pltpu.VMEM((2, pieces, piece, depth), low),
            pltpu.SemaphoreType.DMA,
            pltpu.SemaphoreType.DMA((2, 2)),
            pltpu.SemaphoreType.DMA((2, 2)),
            *gather_sems(21),
        ],
        cost_estimate=busy(45),
        compiler_params=pltpu.CompilerParams(
            collective_id=collective_id, has_side_effects=True, vmem_limit_bytes=60 * 2**20
        ),
    )(own.reshape(pieces, piece, columns), down, gate_up, to_gate, to_up, act)


def sum_gradients_kernel(
    part_ref, down_ref, in_hbm, both_hbm, sum_ref, gate_up_ref, down_sum_ref,
    columns_in, both, arriving, both_sem, in_sems, far_send, far_recv, *scratch,
):
    cubes = down_ref.shape[0]
    far, others = other_cubes(cubes)
    step = columns_in.shape[2]
    blocks = gate_up_ref.shape[0] // step

    def load(i):
        at = pl.ds(i * step, step)
        return pltpu.make_async_copy(in_hbm.at[:, at], columns_in.at[i % 2], in_sems.at[i % 2])

    both_load = pltpu.make_async_copy(both_hbm, both, both_sem)
    both_load.start()
    load(0).start()

    def rows_of(i):
        if i == 0:
            both_load.wait()
        if i + 1 < blocks:
            load(i + 1).start()
        load(i).wait()
        rows = contract_rows(columns_in[i % 2], both[...])
        gate_up_ref[pl.ds(i * step, step), :] = rows.astype(gate_up_ref.dtype)

    def work(point):
        spread = ((), (0, 1), (2, 3), tuple(range(4, blocks)))
        for i in spread[point]:
            rows_of(i)

    greet((*cube_places(), *others))
    send = sender(far_send, far_recv)
    copies = [
        send(k, down_ref.at[place[0]], arriving.at[k], place) for k, place in enumerate(others)
    ]
    cube_sum(part_ref, sum_ref, *scratch, work=work)
    down_sum = down_ref[far].astype(jnp.float32)
    for k, copy in enumerate(copies):
        copy.wait_recv()
        down_sum = down_sum + arriving[k].astype(jnp.float32)
    down_sum_ref[...] = down_sum
    for copy in copies:
        copy.wait_send()


def sum_gradients(part, down, rows_in, both, collective_id):
    members, pieces, piece, depth = part.shape
    low = part.dtype
    step = 256
    vmem, anywhere = pl.BlockSpec(memory_space=pltpu.VMEM), pl.BlockSpec(memory_space=pl.ANY)
    total, gate_up, down_sum = pl.pallas_call(
        sum_gradients_kernel,
        out_shape=[
            jax.ShapeDtypeStruct((pieces, piece, depth), jnp.float32),
            jax.ShapeDtypeStruct((depth, both.shape[1]), low),
            jax.ShapeDtypeStruct(down.shape[1:], jnp.float32),
        ],
        in_specs=[anywhere, vmem, anywhere, anywhere],
        out_specs=[vmem, vmem, vmem],
        scratch_shapes=[
            pltpu.VMEM((2, rows_in.shape[0], step), low),
            pltpu.VMEM(both.shape, low),
            pltpu.VMEM((down.shape[0] - 1, *down.shape[1:]), low),
            pltpu.SemaphoreType.DMA,
            pltpu.SemaphoreType.DMA((2,)),
            pltpu.SemaphoreType.DMA((down.shape[0] - 1,)),
            pltpu.SemaphoreType.DMA((down.shape[0] - 1,)),
            *cube_sum_scratch((pieces, piece, depth), low),
        ],
        cost_estimate=busy(35),
        compiler_params=pltpu.CompilerParams(
            collective_id=collective_id, has_side_effects=True, vmem_limit_bytes=60 * 2**20
        ),
    )(part, down, rows_in, both)
    return total.reshape(pieces * piece, depth), gate_up, down_sum


def unit_sum_kernel(terms_ref, gate_ref, up_ref):
    cubes, group, _, lanes = terms_ref.shape
    rows, hidden = gate_ref.shape
    units, half = hidden // (cubes * group), lanes // 2
    for member in range(group):
        total = terms_ref[0, member].astype(jnp.float32)
        for cube in range(1, cubes):
            total = total + terms_ref[cube, member].astype(jnp.float32)
        for cube in range(cubes):
            at = (cube * group + member) * units
            gate_ref[:, at : at + units] = total[:rows, cube * units : (cube + 1) * units]
            up_ref[:, at : at + units] = total[
                :rows, half + cube * units : half + (cube + 1) * units
            ]


def unit_sum(terms, rows, hidden):
    vmem = pl.BlockSpec(memory_space=pltpu.VMEM)
    return pl.pallas_call(
        unit_sum_kernel,
        out_shape=[jax.ShapeDtypeStruct((rows, hidden), jnp.float32)] * 2,
        in_specs=[vmem],
        out_specs=[vmem, vmem],
        cost_estimate=busy(5),
        compiler_params=pltpu.CompilerParams(vmem_limit_bytes=VMEM_BYTES),
    )(terms)


def owner_sum_kernel(planes, part_ref, out_ref, own_sum, leaving, arriving, z_send, z_recv, *scratch):
    plane, others, ring = other_planes(planes)
    greet((*plane_places()[:3], *others))
    plane_sum(part_ref, own_sum, *scratch)
    send = sender(z_send, z_recv)

    def narrow(i, carry):
        leaving[i] = own_sum[i].astype(leaving.dtype)
        return carry

    lax.fori_loop(0, planes, narrow, 0)
    copies = [
        send(k, leaving.at[ring[k]], arriving.at[k], place) for k, place in enumerate(others)
    ]
    for copy in copies:
        copy.wait_recv()

    value = own_sum[plane]
    for k in range(planes - 1):
        value = value + arriving[k].astype(jnp.float32)
    out_ref[...] = value
    for copy in copies:
        copy.wait_send()


def owner_sum(blocks, collective_id):
    members, planes, rows, columns = blocks.shape
    return pl.pallas_call(
        functools.partial(owner_sum_kernel, planes),
        out_shape=jax.ShapeDtypeStruct((rows, columns), jnp.float32),
        in_specs=[pl.BlockSpec(memory_space=pltpu.VMEM)],
        out_specs=pl.BlockSpec(memory_space=pltpu.VMEM),
        scratch_shapes=[
            pltpu.VMEM((planes, rows, columns), jnp.float32),
            pltpu.VMEM((planes, rows, columns), blocks.dtype),
            pltpu.VMEM((planes - 1, rows, columns), blocks.dtype),
            pltpu.SemaphoreType.DMA((planes - 1,)),
            pltpu.SemaphoreType.DMA((planes - 1,)),
            *plane_sum_scratch((planes, rows, columns), blocks.dtype),
        ],
        cost_estimate=busy(35),
        compiler_params=pltpu.CompilerParams(
            collective_id=collective_id, has_side_effects=True, vmem_limit_bytes=VMEM_BYTES
        ),
    )(blocks)


GAIN_SLOT = 128
TILE_ROWS, TILE_LANES = 8, 128


def packed_strips(rows, width, columns):
    across, into = width // TILE_LANES, columns // TILE_LANES
    strips, tile, tiles = [], 0, rows // TILE_ROWS * across
    while tile < tiles:
        run = min(across - tile % across, into - tile % into)
        strips.append(
            (
                tile // across * TILE_ROWS,
                tile % across * TILE_LANES,
                tile // into * TILE_ROWS,
                tile % into * TILE_LANES,
                run * TILE_LANES,
            )
        )
        tile += run
    return strips, up_to(tiles, into) // into * TILE_ROWS


def pack_tiles(array, columns):
    strips, rows = packed_strips(*array.shape, columns)
    lines = []
    for row in range(0, rows, TILE_ROWS):
        parts = [
            array[r : r + TILE_ROWS, c : c + n] for r, c, to, _, n in strips if to == row
        ]
        line = jnp.concatenate(parts, axis=1)
        lines.append(jnp.pad(line, ((0, 0), (0, columns - line.shape[1]))))
    return jnp.concatenate(lines, axis=0)


def unpack_tiles(array, rows, width):
    strips, _ = packed_strips(rows, width, array.shape[1])
    lines = []
    for row in range(0, rows, TILE_ROWS):
        parts = [
            array[to : to + TILE_ROWS, at : at + n] for r, _, to, at, n in strips if r == row
        ]
        lines.append(jnp.concatenate(parts, axis=1))
    return jnp.concatenate(lines, axis=0)


def gain_places(blocks, planes, count, per, by_member):
    lane = lax.broadcasted_iota(jnp.int32, (GAIN_SLOT, blocks * per), 0)
    inner = lax.broadcasted_iota(jnp.int32, (GAIN_SLOT, blocks * per), 1) % per
    places = ((lane == inner) & (inner < count)).astype(jnp.float32).astype(jnp.bfloat16)
    listed = lax.broadcasted_iota(jnp.int32, (blocks, blocks * per), 0)
    block = lax.broadcasted_iota(jnp.int32, (blocks, blocks * per), 1) // per
    members = blocks // planes
    if not by_member:
        block = block % members * planes + block // members
    return places, listed == block


def spread_gain(rows, planes, *where):
    places, chosen = gain_places(rows.shape[0], planes, *where)
    return jnp.sum(jnp.where(chosen, matmul(rows, places), 0.0), axis=0, keepdims=True)


def collect_gain(vector, blocks, planes, *where):
    places, chosen = gain_places(blocks, planes, *where)
    return contract_cols(jnp.where(chosen, vector, 0.0).astype(jnp.bfloat16), places)


def inverse_of(values, count):
    return lax.rsqrt(jnp.sum(values * values, axis=-1, keepdims=True) / count + epsilon)


def back_of(grad_normed, normed, inverse, count):
    inner = jnp.sum(grad_normed * normed, axis=-1, keepdims=True) / count
    return inverse * (grad_normed - normed * inner)


def turn(values, cos_table, sin_table):
    half = values.shape[1] // 2
    first, second = values[:, :half], values[:, half:]
    return first * cos_table - second * sin_table, second * cos_table + first * sin_table


def attention_forward_kernel(
    gain_widths, width_rows, row_ref, hidden_ref, packed_ref, cos_ref, sin_ref, segment_column, segment_row, placing_ref,
    placed_ref, middle_ref, raw_ref, mix_ref, probs_ref, query_ref, key_ref, value_ref, query_raw_ref,
    key_raw_ref, qkv_ref, output_ref, input_scale, query_scale, key_scale, attnout_scale, ffnin_scale, ffnout_scale,
    gain_rows,
):
    bf16, f32 = jnp.bfloat16, jnp.float32
    members, planes, piece, _ = packed_ref.shape
    blocks = members * planes
    padded = qkv_ref.shape[0] // blocks
    width = hidden_ref.shape[1]
    mix_rows = output_ref.shape[0] // blocks
    strips, _ = packed_strips(mix_rows, width, packed_ref.shape[3])
    local_rows, full_rows = hidden_ref.shape[0], row_ref.shape[0]
    head = key_ref.shape[1]
    heads = query_ref.shape[1] // head
    offset = pl.multiple_of(lax.axis_index("seq") * local_rows, local_rows)
    mine = pl.ds(offset, local_rows)
    for i in range(blocks):
        member, plane = i // planes, i % planes
        block = packed_ref[member, plane]
        qkv_ref[padded * i : padded * (i + 1), :] = block[:padded]
        natural = mix_rows * (plane * members + member)
        for r, c, to, at, n in strips:
            tiles = block[padded + to : padded + to + TILE_ROWS, at : at + n]
            output_ref[natural + r : natural + r + TILE_ROWS, c : c + n] = tiles
        gain_rows[i : i + 1, :] = block[width_rows : width_rows + 1, : gain_rows.shape[1]].astype(f32)
    targets = (input_scale, query_scale, key_scale, attnout_scale, ffnin_scale, ffnout_scale)
    for k, (target, count) in enumerate(zip(targets, gain_widths)):
        rows = gain_rows[:, k * GAIN_SLOT : (k + 1) * GAIN_SLOT].astype(bf16)
        target[...] = spread_gain(rows, planes, count, count if k else padded, k == 0)

    row = row_ref[...].astype(f32)
    normed = (row * inverse_of(row, width) * input_scale[...]).astype(bf16)
    key_value = matmul(normed, qkv_ref[:, heads * head :])
    key_raw = key_value[:, :head]
    value_ref[...] = key_value[:, head:].astype(bf16)
    half = head // 2
    turned = turn(key_raw * inverse_of(key_raw, head) * key_scale[...], cos_ref[...], sin_ref[...])
    key_ref[:, :half], key_ref[:, half:] = turned[0].astype(bf16), turned[1].astype(bf16)

    row = row_ref[mine, :].astype(f32)
    normed = (row * inverse_of(row, width) * input_scale[...]).astype(bf16)
    own = matmul(normed, qkv_ref[:, : (heads + 1) * head])
    query_raw_ref[...] = own[:, : heads * head]
    key_raw_ref[...] = own[:, heads * head :]
    cos_table, sin_table = cos_ref[mine, :], sin_ref[mine, :]
    places = offset + lax.broadcasted_iota(jnp.int32, (local_rows, full_rows), 0)
    earlier = places >= lax.broadcasted_iota(jnp.int32, (local_rows, full_rows), 1)
    allowed = (segment_column[...] == segment_row[...]) & earlier
    for h in range(heads):
        at = h * head
        query_raw = query_raw_ref[:, at : at + head]
        turned = turn(
            query_raw * inverse_of(query_raw, head) * query_scale[...], cos_table, sin_table
        )
        scale = head ** (-0.5)
        query_ref[:, at : at + half] = (turned[0] * scale).astype(bf16)
        query_ref[:, at + half : at + head] = (turned[1] * scale).astype(bf16)
        scores = contract_cols(query_ref[:, at : at + head], key_ref[...])
        scores = jnp.where(allowed, scores, masked_score)
        weights = jnp.exp(scores - jnp.max(scores, axis=-1, keepdims=True))
        probs = weights / jnp.sum(weights, axis=-1, keepdims=True)
        probs_ref[h] = probs
        mix_ref[:, at : at + head] = matmul(probs.astype(bf16), value_ref[...]).astype(bf16)
    attn_raw = matmul(mix_ref[...], output_ref[...])
    raw_ref[...] = attn_raw
    middle = hidden_ref[...].astype(f32) + attn_raw * inverse_of(attn_raw, width) * attnout_scale[...]
    middle_ref[...] = middle
    ffn_in = (middle * inverse_of(middle, width) * ffnin_scale[...]).astype(bf16)
    placed_ref[...] = matmul(ffn_in, placing_ref[...]).astype(bf16)


def attention_forward(
    row_padded, hidden, packed, cos_full, sin_full, segment_column, segment_row, placing, gain_widths, width_rows, padded,
    head_width,
):
    bf16, f32 = jnp.bfloat16, jnp.float32
    members, planes, piece, qkv_width = packed.shape
    blocks = members * planes
    local_rows, width = hidden.shape
    query_width = qkv_width - 2 * head_width
    heads = query_width // head_width
    full_rows = row_padded.shape[0]
    depth = blocks * padded
    shape = jax.ShapeDtypeStruct
    vmem = pl.BlockSpec(memory_space=pltpu.VMEM)
    out_shape = [
        shape((local_rows, depth), bf16),
        shape((local_rows, width), f32),
        shape((local_rows, width), f32),
        shape((local_rows, query_width), bf16),
        shape((heads, local_rows, full_rows), f32),
        shape((local_rows, query_width), bf16),
        shape((full_rows, head_width), bf16),
        shape((full_rows, head_width), bf16),
        shape((local_rows, query_width), f32),
        shape((local_rows, head_width), f32),
        shape((depth, qkv_width), bf16),
        shape((query_width, width), bf16),
        shape((1, depth), f32),
        shape((1, head_width), f32),
        shape((1, head_width), f32),
        shape((1, width), f32),
        shape((1, width), f32),
        shape((1, width), f32),
    ]
    return pl.pallas_call(
        functools.partial(attention_forward_kernel, gain_widths, width_rows),
        out_shape=out_shape,
        in_specs=[vmem] * 8,
        out_specs=[vmem] * len(out_shape),
        scratch_shapes=[pltpu.VMEM((blocks, len(gain_widths) * GAIN_SLOT), f32)],
        cost_estimate=busy(20),
        compiler_params=pltpu.CompilerParams(vmem_limit_bytes=60 * 2**20),
    )(row_padded, hidden, packed, cos_full, sin_full, segment_column, segment_row, placing)


def attention_backward_kernel(
    gain_widths, width_rows, planes, grad_ref, incoming_ref, middle_ref, raw_ref, mix_ref, probs_ref, query_ref, key_ref,
    value_ref, query_raw_ref, key_raw_ref, row_ref, qkv_ref, output_ref, cos_ref, sin_ref, input_scale,
    query_scale, key_scale, attnout_scale, ffnin_scale, ffnout_grad, by_device, by_member,
    input_grad_ref, blocks_ref, key_value, query_grad, low_ref, leaving, arriving, send_sem, recv_sem,
):
    bf16, f32 = jnp.bfloat16, jnp.float32
    members = blocks_ref.shape[0]
    blocks = members * planes
    padded = qkv_ref.shape[0] // blocks
    mix_rows = output_ref.shape[0] // blocks
    local_rows, width = incoming_ref.shape
    strips, _ = packed_strips(mix_rows, width, blocks_ref.shape[3])
    head = key_ref.shape[1]
    heads = query_ref.shape[1] // head
    half = head // 2
    seq = lax.axis_index("seq")
    mine = pl.ds(pl.multiple_of(seq * local_rows, local_rows), local_rows)
    theirs = pl.ds(pl.multiple_of((1 - seq) * local_rows, local_rows), local_rows)
    partner = plane_places()[2]
    greet((partner,))

    ffn_in_grad = take_back(grad_ref[...], by_device[...])
    middle = middle_ref[...]
    inverse = inverse_of(middle, width)
    normed = middle * inverse
    ffnin_grad = jnp.sum(ffn_in_grad * normed, axis=0, keepdims=True)
    middle_grad = incoming_ref[...].astype(f32) + back_of(
        ffn_in_grad * ffnin_scale[...], normed, inverse, width
    )
    input_grad_ref[...] = middle_grad
    raw = raw_ref[...]
    inverse = inverse_of(raw, width)
    normed = raw * inverse
    attnout_grad = jnp.sum(middle_grad * normed, axis=0, keepdims=True)
    raw_grad = back_of(middle_grad * attnout_scale[...], normed, inverse, width).astype(bf16)
    mix_grad = contract_cols(raw_grad, output_ref[...]).astype(bf16)
    for h in range(heads):
        at = h * head
        grad = mix_grad[:, at : at + head]
        probs = probs_ref[h]
        prob_grad = contract_cols(grad, value_ref[...])
        delta = jnp.sum(prob_grad * probs, axis=-1, keepdims=True)
        score_grad = (probs * (prob_grad - delta)).astype(bf16)
        to_keys = contract_rows(score_grad, query_ref[:, at : at + head])
        to_values = contract_rows(probs.astype(bf16), grad)
        if h == 0:
            key_value[:, :head], key_value[:, head:] = to_keys, to_values
        else:
            key_value[:, :head] += to_keys
            key_value[:, head:] += to_values
        query_grad[:, at : at + head] = matmul(score_grad, key_ref[...])
    leaving[...] = key_value[theirs, :].astype(bf16)
    copy = sender(send_sem, recv_sem)(0, leaving, arriving, partner)

    output_grad = contract_rows(mix_ref[...], raw_grad).astype(bf16)
    cos_table, sin_table = cos_ref[mine, :], sin_ref[mine, :]

    def head_back(grad, raw, scale_ref):
        turned = jnp.concatenate(turn(grad, cos_table, -sin_table), axis=1)
        inverse = inverse_of(raw, head)
        normed = raw * inverse
        gain = jnp.sum(turned * normed, axis=0, keepdims=True)
        return back_of(turned * scale_ref[...], normed, inverse, head).astype(bf16), gain

    query_gain = jnp.zeros((1, head), f32)
    for h in range(heads):
        at = h * head
        low, gain = head_back(
            query_grad[:, at : at + head] * head ** (-0.5),
            query_raw_ref[:, at : at + head],
            query_scale,
        )
        low_ref[:, at : at + head] = low
        query_gain = query_gain + gain
    copy.wait_recv()
    total = key_value[mine, :] + arriving[...].astype(f32)
    low, key_gain = head_back(total[:, :head], key_raw_ref[...], key_scale)
    low_ref[:, heads * head : (heads + 1) * head] = low
    low_ref[:, (heads + 1) * head :] = total[:, head:].astype(bf16)

    row = row_ref[mine, :].astype(f32)
    inverse = inverse_of(row, width)
    normed = row * inverse
    normed_grad = contract_cols(low_ref[...], qkv_ref[...])
    input_gain = jnp.sum(normed_grad * normed, axis=0, keepdims=True)
    input_grad_ref[...] += take_back(
        back_of(normed_grad * input_scale[...], normed, inverse, width), by_member[...]
    )
    vectors = (input_gain, query_gain, key_gain, attnout_grad, ffnin_grad, ffnout_grad[...])
    gains = jnp.concatenate(
        [
            collect_gain(vector, blocks, planes, count, count if k else padded, k == 0)
            for k, (vector, count) in enumerate(zip(vectors, gain_widths))
        ],
        axis=1,
    )
    lanes = gains.shape[1]
    normed = (normed * input_scale[...]).astype(bf16)
    weights = contract_rows(normed, low_ref[...])
    row_of = lax.broadcasted_iota(jnp.int32, (padded, lanes), 0)
    columns = blocks_ref.shape[3]
    for i in range(blocks):
        member, plane = i // planes, i % planes
        piece = weights[padded * i : padded * (i + 1)]
        first = jnp.where(row_of == width_rows, gains[i : i + 1], piece[:, :lanes])
        blocks_ref[member, plane, :padded, :lanes] = first.astype(bf16)
        blocks_ref[member, plane, :padded, lanes:] = piece[:, lanes:].astype(bf16)
        natural = mix_rows * (plane * members + member)
        for r, c, to, at, n in strips:
            tiles = output_grad[natural + r : natural + r + TILE_ROWS, c : c + n]
            blocks_ref[member, plane, padded + to : padded + to + TILE_ROWS, at : at + n] = tiles
        _, _, to, at, n = strips[-1]
        if at + n < columns:
            rest = jnp.zeros((TILE_ROWS, columns - at - n), bf16)
            blocks_ref[member, plane, padded + to : padded + to + TILE_ROWS, at + n :] = rest
    copy.wait_send()


def attention_backward(arrays, gain_widths, width_rows, planes, mix_rows, collective_id):
    bf16, f32 = jnp.bfloat16, jnp.float32
    grad, incoming, query, key, qkv = arrays[0], arrays[1], arrays[6], arrays[7], arrays[12]
    local_rows, width = incoming.shape
    members = 8
    padded = qkv.shape[0] // (members * planes)
    _, packed_rows = packed_strips(mix_rows, width, qkv.shape[1])
    pair = pltpu.VMEM((local_rows, 2 * key.shape[1]), bf16)
    shape = jax.ShapeDtypeStruct
    vmem = pl.BlockSpec(memory_space=pltpu.VMEM)
    return pl.pallas_call(
        functools.partial(attention_backward_kernel, gain_widths, width_rows, planes),
        out_shape=[
            shape((local_rows, width), f32),
            shape((members, planes, padded + packed_rows, qkv.shape[1]), bf16),
        ],
        in_specs=[vmem] * len(arrays),
        out_specs=[vmem] * 2,
        scratch_shapes=[
            pltpu.VMEM((key.shape[0], 2 * key.shape[1]), f32),
            pltpu.VMEM(query.shape, f32),
            pltpu.VMEM((local_rows, qkv.shape[1]), bf16),
            pair,
            pair,
            pltpu.SemaphoreType.DMA((1,)),
            pltpu.SemaphoreType.DMA((1,)),
        ],
        cost_estimate=busy(30),
        compiler_params=pltpu.CompilerParams(
            collective_id=collective_id, has_side_effects=True, vmem_limit_bytes=60 * 2**20
        ),
    )(*arrays)


def body(
    tokens,
    segment_ids,
    cotangent,
    query_weight,
    key_weight,
    value_weight,
    output_weight,
    gate_weight,
    up_weight,
    down_weight,
    input_gain,
    query_gain,
    key_gain,
    attnout_gain,
    ffnin_gain,
    ffnout_gain,
):
    bf16, f32 = jnp.bfloat16, jnp.float32
    devices = lax.axis_size(ALL)
    members = lax.axis_size(PLANE)
    planes = lax.axis_size(PLANES)
    cubes = lax.axis_size("far")
    group = lax.axis_size(CUBE)
    width_rows = query_weight.shape[0]
    hidden_rows = down_weight.shape[0]
    head_width = key_weight.shape[1]
    query_width = query_weight.shape[1]
    head_count = query_width // head_width
    qkv_width = query_width + 2 * head_width
    mix_rows = output_weight.shape[0]
    padded = up_to(width_rows + 1, 8)
    width = devices * width_rows
    unit_count = cubes * hidden_rows
    unit_pad = up_to(unit_count, 128)
    by_device = place_columns(devices, members, planes, width_rows, padded, False)
    by_member = place_columns(devices, members, planes, width_rows, padded, True)

    def column_blocks(weight):
        pieces = weight.reshape(width_rows, cubes, group, hidden_rows)
        pieces = pieces.transpose(2, 0, 1, 3).reshape(group, width_rows, unit_count)
        return jnp.pad(
            pieces, ((0, 0), (0, padded - width_rows), (0, unit_pad - unit_count))
        )

    gate_up = jnp.concatenate([column_blocks(gate_weight), column_blocks(up_weight)], axis=2)
    gate_up = jnp.broadcast_to(gate_up[None], (cubes,) + gate_up.shape)
    gate_up = gate_up.reshape((devices,) + gate_up.shape[2:])

    gains = (input_gain, query_gain, key_gain, attnout_gain, ffnin_gain, ffnout_gain)
    gain_widths = [g.shape[0] for g in gains]
    gain_row = jnp.concatenate(
        [jnp.pad(g[None], ((0, 0), (0, GAIN_SLOT - g.shape[0]))) for g in gains], axis=1
    )
    gain_row = jnp.pad(gain_row, ((0, 0), (0, qkv_width - gain_row.shape[1])))
    qkv_local = jnp.concatenate([query_weight, key_weight, value_weight], axis=1)
    packed = jnp.concatenate([qkv_local, gain_row], axis=0)
    packed = jnp.pad(packed, ((0, padded - width_rows - 1), (0, 0)))
    packed = jnp.concatenate([packed, pack_tiles(output_weight, qkv_width)], axis=0)
    packed_all = z_gather(packed, planes, 0)
    other_tokens = lax.ppermute(tokens[0], "seq", [(0, 1), (1, 0)])
    packed_all, other_tokens = lax.optimization_barrier((packed_all, other_tokens))
    packed_all, down_full = weights_gather(packed_all, down_weight, cubes, 6)
    down_full = down_full.reshape(unit_count, down_weight.shape[1])
    gate_up, packed_all = lax.optimization_barrier((gate_up, packed_all))
    gate_up_full = exchange(gate_up, ALL).reshape(devices * padded, 2 * unit_pad)
    incoming = cotangent[0].astype(f32)
    local_rows = tokens.shape[1]
    offset = lax.axis_index("seq") * local_rows
    segment_row = segment_ids[0]

    def mine(rows):
        return lax.dynamic_slice_in_dim(rows, offset, local_rows)

    cos_full, sin_full = rope_tables(doc_positions(segment_row), head_width)

    first = lax.axis_index("seq") == 0
    row_tokens = jnp.concatenate(
        [
            jnp.where(first, tokens[0], other_tokens),
            jnp.where(first, other_tokens, tokens[0]),
        ]
    )
    row_padded = matmul(row_tokens, by_member).astype(bf16)
    (
        ffn_in_placed,
        middle,
        attn_raw,
        attn_flat,
        probs,
        queries,
        key_rows,
        value_rows,
        query_raw,
        key_raw,
        qkv_full,
        output_full,
        *scales,
    ) = attention_forward(
        row_padded,
        tokens[0],
        packed_all,
        cos_full,
        sin_full,
        mine(segment_row)[:, None],
        segment_row[None],
        by_device,
        gain_widths,
        width_rows,
        padded,
        head_width,
    )
    ffnout_scale = scales.pop()

    cube_in = gather_rows(ffn_in_placed, 1)
    ffn_part, activated_low, to_gate, to_up = ffn_forward(cube_in, gate_up_full, down_full)
    ffn_part = ffn_part.reshape(group, local_rows // 16, 16, ffn_part.shape[1])
    ffn_raw = cube_scatter_sum(ffn_part, 2)
    inv_ffn = inverse_rms(ffn_raw)
    norm_ffn = ffn_raw * inv_ffn
    result = middle + norm_ffn * ffnout_scale
    ffnout_gain_grad = jnp.sum(incoming * norm_ffn, axis=0)
    ffn_raw_grad = rms_back(incoming * ffnout_scale, norm_ffn, inv_ffn).astype(bf16)

    gate_up_low, ffn_in_part, down_blocks = gather_backward(
        ffn_raw_grad, down_full, gate_up_full, to_gate, to_up, activated_low, 3
    )
    down_blocks = down_blocks.reshape(cubes, hidden_rows, down_weight.shape[1])
    ffn_in_grad, gate_up_blocks, down_wgrad = sum_gradients(
        ffn_in_part, down_blocks, cube_in, gate_up_low, 4
    )
    gate_up_terms = exchange(gate_up_blocks.reshape(devices, padded, 2 * unit_pad), ALL)
    input_grad, blocks = attention_backward(
        [
            ffn_in_grad,
            cotangent[0],
            middle,
            attn_raw,
            attn_flat,
            probs,
            queries,
            key_rows,
            value_rows,
            query_raw,
            key_raw,
            row_padded,
            qkv_full,
            output_full,
            cos_full,
            sin_full,
            *scales,
            ffnout_gain_grad[None],
            by_device,
            by_member,
        ],
        gain_widths,
        width_rows,
        planes,
        mix_rows,
        7,
    )
    share = owner_sum(blocks, 5)
    gate_wgrad, up_wgrad = unit_sum(
        gate_up_terms.reshape(cubes, group, padded, 2 * unit_pad), width_rows, gate_weight.shape[1]
    )
    qkv_share, output_share = share[:padded], unpack_tiles(share[padded:], *output_weight.shape)
    gain_shares = [
        qkv_share[width_rows, k * GAIN_SLOT : k * GAIN_SLOT + count]
        for k, count in enumerate(gain_widths)
    ]
    return (
        result.astype(bf16)[None],
        input_grad[None],
        qkv_share[:width_rows, :query_width],
        qkv_share[:width_rows, query_width : query_width + head_width],
        qkv_share[:width_rows, query_width + head_width :],
        output_share,
        gate_wgrad,
        up_wgrad,
        down_wgrad,
        *gain_shares,
    )


def solution(mesh):
    dp, seq = mesh.shape["dp"], mesh.shape["seq"]
    split = Mesh(mesh.devices.reshape(dp // 8, 2, 2, 2, seq), ALL)
    rows = P(("far", "z", "x", "core"), "seq", None)
    matrix, vector = P(ALL, None), P(ALL)
    return jax.shard_map(
        body,
        mesh=split,
        in_specs=(rows, P(("far", "z", "x", "core"), None), rows) + (matrix,) * 7 + (vector,) * 6,
        out_specs=(rows, rows) + (matrix,) * 7 + (vector,) * 6,
        check_vma=False,
    )
```

```python
import functools

import jax
import jax.numpy as jnp
import numpy as np
from jax import lax
from jax.experimental import pallas as pl
from jax.experimental.pallas import tpu as pltpu
from jax.sharding import Mesh
from jax.sharding import PartitionSpec as P

epsilon = 1e-06
rope_base = 1000000.0
masked_score = -1e30


def inverse_rms(values):
    return lax.rsqrt(jnp.mean(values * values, axis=-1, keepdims=True) + epsilon)


def rms_back(grad_normed, normed, inverse):
    return inverse * (grad_normed - normed * jnp.mean(grad_normed * normed, axis=-1, keepdims=True))


def doc_positions(segments):
    length = segments.shape[0]
    smaller = segments[None, :] < segments[:, None]
    starts = jnp.sum(smaller.astype(jnp.int32), axis=1)
    return (jnp.arange(length, dtype=jnp.int32) - starts).astype(jnp.float32)


def rope_tables(positions, head_width):
    half_width = head_width // 2
    frequency = rope_base ** (-(2.0 / head_width) * jnp.arange(half_width, dtype=jnp.float32))
    angles = positions[..., None] * frequency
    return (jnp.cos(angles), jnp.sin(angles))


def matmul(left, right):
    return jnp.dot(left, right, preferred_element_type=jnp.float32)


def contract_rows(left, right):
    return lax.dot_general(
        left, right, (((0,), (0,)), ((), ())), preferred_element_type=jnp.float32
    )


def contract_cols(left, right):
    return lax.dot_general(
        left, right, (((1,), (1,)), ((), ())), preferred_element_type=jnp.float32
    )


ALL = ("far", "z", "x", "core", "seq")
PLANES = ("far", "z")
CUBE = ("z", "x", "core", "seq")


def up_to(size, multiple):
    return (size + multiple - 1) // multiple * multiple


def place_columns(blocks, rows, padded):
    source = np.arange(blocks * rows)
    block, inner = source // rows, source % rows
    placing = np.zeros((blocks * rows, blocks * padded), np.float32)
    placing[source, block * padded + inner] = 1.0
    return jnp.asarray(placing.astype(jnp.bfloat16))


def take_back(padded_values, placing):
    high = lax.reduce_precision(padded_values, 8, 7)
    terms = jnp.concatenate([high, padded_values - high], axis=0).astype(jnp.bfloat16)
    both = contract_cols(terms, placing)
    rows = padded_values.shape[0]
    return both[:rows] + both[rows:]


PLANE = ("x", "core", "seq")

MESH_ID = pl.DeviceIdType.MESH
VMEM_BYTES = 48 * 2**20


def exchange(blocks, axes):
    return lax.all_to_all(blocks, axes, split_axis=0, concat_axis=0, tiled=True)


def busy(microseconds):
    return pl.CostEstimate(flops=0, bytes_accessed=microseconds * 3_000_000, transcendentals=0)


def shifted(flip_z, flip_x, flip_core, flip_y):
    far, *inner = (lax.axis_index(name) for name in ALL)
    flips = (flip_z, flip_x, flip_core, flip_y)
    return (far, *(1 - at if flip else at for at, flip in zip(inner, flips)))


def plane_places():
    def member(flip_x, flip_core, flip_y):
        _, _, x, core, seq = shifted(0, flip_x, flip_core, flip_y)
        return (x * 2 + core) * 2 + seq

    return shifted(0, 0, 1, 0), shifted(0, 1, 0, 0), shifted(0, 0, 0, 1), member


def cube_member(flip_z, flip_x, flip_y, flip_core):
    _, z, x, core, seq = shifted(flip_z, flip_x, flip_core, flip_y)
    return ((z * 2 + x) * 2 + core) * 2 + seq


def cube_places():
    return *plane_places()[:3], shifted(1, 0, 0, 0)


def other_planes(planes):
    far, z, x, core, seq = (lax.axis_index(name) for name in ALL)
    plane = far * 2 + z
    ring = [lax.rem(plane + k, planes) for k in range(1, planes)]
    return plane, [(at // 2, lax.rem(at, 2), x, core, seq) for at in ring], ring


def other_cubes(cubes):
    far, z, x, core, seq = (lax.axis_index(name) for name in ALL)
    return far, [(lax.rem(far + k, cubes), z, x, core, seq) for k in range(1, cubes)]


def greet(places):
    barrier = pltpu.get_barrier_semaphore()
    for place in places:
        pl.semaphore_signal(barrier, inc=1, device_id=place, device_id_type=MESH_ID)
    pl.semaphore_wait(barrier, len(places))


def sender(send_sems, recv_sems):
    def send(kind, source, target, place):
        copy = pltpu.make_async_remote_copy(
            src_ref=source,
            dst_ref=target,
            send_sem=send_sems.at[kind],
            recv_sem=recv_sems.at[kind],
            device_id=place,
            device_id_type=MESH_ID,
        )
        copy.start()
        return copy

    return send


def plane_spread(own_ref, out_ref, send_sems, recv_sems, local_sem, meanwhile=lambda: None):
    sibling, along_x, along_y, member = plane_places()
    half = own_ref.shape[0] // 2
    top, bottom = pl.ds(0, half), pl.ds(half, half)
    me = member(0, 0, 0)
    keep = pltpu.make_async_copy(own_ref, out_ref.at[me], local_sem)
    keep.start()
    send = sender(send_sems, recv_sems)

    def forward(kind, block, rows, place):
        return send(kind, out_ref.at[block, rows], out_ref.at[block, rows], place)

    own_x_top = send(1, own_ref.at[top], out_ref.at[me, top], along_x)
    own_y_bottom = send(3, own_ref.at[bottom], out_ref.at[me, bottom], along_y)
    own_sibling = send(0, own_ref, out_ref.at[me], sibling)
    own_x_bottom = send(2, own_ref.at[bottom], out_ref.at[me, bottom], along_x)
    own_y_top = send(4, own_ref.at[top], out_ref.at[me, top], along_y)
    x_block, y_block, diagonal = member(1, 0, 0), member(0, 0, 1), member(1, 0, 1)
    meanwhile()
    own_x_top.wait_recv()
    diagonal_top = forward(5, x_block, top, along_y)
    x_top = forward(7, x_block, top, sibling)
    own_y_bottom.wait_recv()
    diagonal_bottom = forward(6, y_block, bottom, along_x)
    y_bottom = forward(9, y_block, bottom, sibling)
    own_x_bottom.wait_recv()
    x_bottom = forward(8, x_block, bottom, sibling)
    own_y_top.wait_recv()
    y_top = forward(10, y_block, top, sibling)
    diagonal_top.wait_recv()
    far_top = forward(11, diagonal, top, sibling)
    diagonal_bottom.wait_recv()
    far_bottom = forward(12, diagonal, bottom, sibling)
    for copy in (own_sibling, x_top, y_bottom, x_bottom, y_top, far_top, far_bottom):
        copy.wait_recv()
    for copy in (
        own_x_top,
        own_y_bottom,
        own_sibling,
        own_x_bottom,
        own_y_top,
        diagonal_top,
        diagonal_bottom,
        x_top,
        y_bottom,
        x_bottom,
        y_top,
        far_top,
        far_bottom,
    ):
        copy.wait_send()
    keep.wait()


def cube_spread(own_ref, out_ref, send_sems, recv_sems, local_sem, compute=lambda i: None):
    sibling, along_x, along_y, along_z = cube_places()
    half = own_ref.shape[0] // 2
    top, bottom = pl.ds(0, half), pl.ds(half, half)
    me = cube_member(0, 0, 0, 0)
    keep = pltpu.make_async_copy(own_ref, out_ref.at[me], local_sem)
    keep.start()
    send = sender(send_sems, recv_sems)
    x_block, y_block, diagonal = (cube_member(0, *at, 0) for at in ((1, 0), (0, 1), (1, 1)))
    z_block, zx_block, zy_block, zd_block = (
        cube_member(1, *at, 0) for at in ((0, 0), (1, 0), (0, 1), (1, 1))
    )

    def half_on(kind, block, rows, place):
        return send(kind, out_ref.at[block, rows], out_ref.at[block, rows], place)

    def on(kind, block, place):
        return send(kind, out_ref.at[block], out_ref.at[block], place)

    own_x_top = send(1, own_ref.at[top], out_ref.at[me, top], along_x)
    own_y_bottom = send(3, own_ref.at[bottom], out_ref.at[me, bottom], along_y)
    own_z = send(13, own_ref, out_ref.at[me], along_z)
    own_sibling = send(0, own_ref, out_ref.at[me], sibling)
    own_x_bottom = send(2, own_ref.at[bottom], out_ref.at[me, bottom], along_x)
    own_y_top = send(4, own_ref.at[top], out_ref.at[me, top], along_y)
    compute(0)
    own_x_top.wait_recv()
    diagonal_top = half_on(5, x_block, top, along_y)
    x_top = half_on(7, x_block, top, sibling)
    own_y_bottom.wait_recv()
    diagonal_bottom = half_on(6, y_block, bottom, along_x)
    y_bottom = half_on(9, y_block, bottom, sibling)
    own_sibling.wait_recv()
    compute(1)
    own_z.wait_recv()
    z_to_x = on(14, z_block, along_x)
    z_to_y = on(15, z_block, along_y)
    z_near = on(16, z_block, sibling)
    own_x_bottom.wait_recv()
    x_bottom = half_on(8, x_block, bottom, sibling)
    own_y_top.wait_recv()
    y_top = half_on(10, y_block, top, sibling)
    compute(2)
    diagonal_top.wait_recv()
    far_top = half_on(11, diagonal, top, sibling)
    diagonal_bottom.wait_recv()
    far_bottom = half_on(12, diagonal, bottom, sibling)
    diagonal_z = on(17, diagonal, along_z)
    compute(3)
    compute(4)
    z_to_x.wait_recv()
    zx_near = on(18, zx_block, sibling)
    z_to_y.wait_recv()
    zy_near = on(19, zy_block, sibling)
    compute(5)
    compute(6)
    diagonal_z.wait_recv()
    zd_near = on(20, zd_block, sibling)
    compute(7)
    compute(8)
    last = (
        (x_top, x_bottom), (y_bottom, y_top), (far_top, far_bottom), (z_near,), (zx_near,), (zy_near,), (zd_near,),
    )
    for i, copies in enumerate(last):
        for copy in copies:
            copy.wait_recv()
        compute(9 + i)
    for copy in (
        own_x_top, own_y_bottom, own_z, own_sibling, own_x_bottom, own_y_top, diagonal_top, diagonal_bottom,
        z_to_x, z_to_y, diagonal_z,
    ):
        copy.wait_send()
    for copies in last:
        for copy in copies:
            copy.wait_send()
    keep.wait()


CUBE_ORDER = (
    (0, 0, 0, 0), (0, 0, 0, 1), (0, 1, 0, 0), (0, 0, 1, 0), (1, 0, 0, 0), (0, 1, 1, 0), (1, 1, 0, 0), (1, 0, 1, 0),
    (1, 1, 1, 0), (0, 1, 0, 1), (0, 0, 1, 1), (0, 1, 1, 1), (1, 0, 0, 1), (1, 1, 0, 1), (1, 0, 1, 1), (1, 1, 1, 1),
)


def cube_gather_kernel(own_ref, out_ref, *sems):
    greet(cube_places())
    cube_spread(own_ref, out_ref, *sems)


def weights_gather_kernel(
    cubes, own_ref, down_ref, gate_ref, up_ref, out_ref, down_out, blocks_ref, far_send, far_recv, own_sem, *sems
):
    _, group, padded, lanes = blocks_ref.shape
    rows, hidden = gate_ref.shape
    units, half = hidden // (cubes * group), lanes // 2

    def cut_blocks():
        spare = jnp.zeros((rows, half - cubes * units), blocks_ref.dtype)
        below = jnp.zeros((padded - rows, lanes), blocks_ref.dtype)
        for member in range(group):
            for base, ref in ((0, gate_ref), (half, up_ref)):
                pieces = [
                    ref[:, (cube * group + member) * units : (cube * group + member + 1) * units]
                    for cube in range(cubes)
                ]
                piece = jnp.concatenate(pieces + [spare], axis=1)
                for cube in range(cubes):
                    blocks_ref[cube, member, :rows, base : base + half] = piece
            for cube in range(cubes):
                blocks_ref[cube, member, rows:, :] = below

    far, others = other_cubes(cubes)
    greet((*plane_places()[:3], *others))
    keep = pltpu.make_async_copy(down_ref, down_out.at[far], own_sem)
    keep.start()
    send = sender(far_send, far_recv)
    copies = [send(k, down_ref, down_out.at[far], place) for k, place in enumerate(others)]
    plane_spread(own_ref, out_ref, *sems, meanwhile=cut_blocks)
    for copy in copies:
        copy.wait_recv()
    for copy in copies:
        copy.wait_send()
    keep.wait()


def z_gather_kernel(
    planes, padded, query_ref, key_ref, value_ref, output_ref, *refs,
):
    *gains, out_ref, own, send_sems, recv_sems, own_sem = refs
    rows, columns = query_ref.shape[0], own.shape[1]
    plane, others, _ = other_planes(planes)
    at = 0
    for ref in (query_ref, key_ref, value_ref):
        own[:rows, at : at + ref.shape[1]] = ref[...]
        at += ref.shape[1]
    slots = [
        jnp.concatenate(
            [ref[...].astype(jnp.float32), jnp.zeros((1, GAIN_SLOT - ref.shape[1]), jnp.float32)],
            axis=1,
        )
        for ref in gains
    ]
    slots.append(jnp.zeros((1, columns - len(slots) * GAIN_SLOT), jnp.float32))
    line = jnp.concatenate(slots, axis=1)
    spare = jnp.zeros((padded - rows - 1, columns), jnp.float32)
    own[rows:padded, :] = jnp.concatenate([line, spare], axis=0).astype(own.dtype)
    strips, _ = packed_strips(*output_ref.shape, columns)
    for r, c, to, at, n in strips:
        tiles = output_ref[r : r + TILE_ROWS, c : c + n]
        own[padded + to : padded + to + TILE_ROWS, at : at + n] = tiles
    _, _, to, at, n = strips[-1]
    if at + n < columns:
        rest = jnp.zeros((TILE_ROWS, columns - at - n), own.dtype)
        own[padded + to : padded + to + TILE_ROWS, at + n :] = rest
    greet(others)
    keep = pltpu.make_async_copy(own, out_ref.at[plane], own_sem)
    keep.start()
    send = sender(send_sems, recv_sems)
    copies = [send(k, own, out_ref.at[plane], place) for k, place in enumerate(others)]
    for copy in copies:
        copy.wait_recv()
    for copy in copies:
        copy.wait_send()
    keep.wait()


def gather_sems(count):
    return [
        pltpu.SemaphoreType.DMA((count,)),
        pltpu.SemaphoreType.DMA((count,)),
        pltpu.SemaphoreType.DMA,
    ]


def z_gather(query, key, value, output, gains, planes, padded, collective_id):
    columns = query.shape[1] + key.shape[1] + value.shape[1]
    shape = (padded + packed_strips(*output.shape, columns)[1], columns)
    arrays = [query, key, value, output, *(gain[None] for gain in gains)]
    return pl.pallas_call(
        functools.partial(z_gather_kernel, planes, padded),
        out_shape=jax.ShapeDtypeStruct((planes, *shape), query.dtype),
        in_specs=[pl.BlockSpec(memory_space=pltpu.VMEM)] * len(arrays),
        out_specs=pl.BlockSpec(memory_space=pl.ANY),
        scratch_shapes=[
            pltpu.VMEM(shape, query.dtype),
            pltpu.SemaphoreType.DMA((planes - 1,)),
            pltpu.SemaphoreType.DMA((planes - 1,)),
            pltpu.SemaphoreType.DMA,
        ],
        cost_estimate=busy(20),
        compiler_params=pltpu.CompilerParams(
            collective_id=collective_id, has_side_effects=True, vmem_limit_bytes=VMEM_BYTES
        ),
    )(*arrays)


def weights_gather(local, down, gate, up, block, cubes, collective_id):
    members = 8
    vmem, anywhere = pl.BlockSpec(memory_space=pltpu.VMEM), pl.BlockSpec(memory_space=pl.ANY)
    return pl.pallas_call(
        functools.partial(weights_gather_kernel, cubes),
        out_shape=[
            jax.ShapeDtypeStruct((members, *local.shape), local.dtype),
            jax.ShapeDtypeStruct((cubes, *down.shape), down.dtype),
            jax.ShapeDtypeStruct((cubes, *block), gate.dtype),
        ],
        in_specs=[anywhere, anywhere, vmem, vmem],
        out_specs=[anywhere, anywhere, vmem],
        scratch_shapes=[
            pltpu.SemaphoreType.DMA((cubes - 1,)),
            pltpu.SemaphoreType.DMA((cubes - 1,)),
            pltpu.SemaphoreType.DMA,
            *gather_sems(13),
        ],
        cost_estimate=busy(30),
        compiler_params=pltpu.CompilerParams(
            collective_id=collective_id, has_side_effects=True, vmem_limit_bytes=VMEM_BYTES
        ),
    )(local, down, gate, up)


def gather_rows(local, collective_id):
    rows, columns = local.shape
    members = 16
    out = pl.pallas_call(
        cube_gather_kernel,
        out_shape=jax.ShapeDtypeStruct((members, rows // 16, 16, columns), local.dtype),
        in_specs=[pl.BlockSpec(memory_space=pl.ANY)],
        out_specs=pl.BlockSpec(memory_space=pl.ANY),
        scratch_shapes=gather_sems(21),
        cost_estimate=busy(35),
        compiler_params=pltpu.CompilerParams(
            collective_id=collective_id, has_side_effects=True, vmem_limit_bytes=VMEM_BYTES
        ),
    )(local.reshape(rows // 16, 16, columns))
    return out.reshape(-1, columns)


def add_rows(target, sources, start, count):
    def one(i, carry):
        total = sources[0][i].astype(jnp.float32)
        for source in sources[1:]:
            total = total + source[i].astype(jnp.float32)
        target[i] = total.astype(target.dtype)
        return carry

    lax.fori_loop(start, start + count, one, 0)


def plane_sum(part_ref, own_sum, near, sums, from_x, from_y, far_x, far_y, send_sems, recv_sems):
    sibling, along_x, along_y, member = plane_places()
    rows = own_sum.shape[0]
    half = rows // 2
    top, bottom = pl.ds(0, half), pl.ds(half, half)
    send = sender(send_sems, recv_sems)
    chips = ((1, 1), (1, 0), (0, 1), (0, 0))
    mine = [part_ref.at[member(at_x, 0, at_y)] for at_x, at_y in chips]
    to_sibling = [
        send(k, part_ref.at[member(at_x, 1, at_y)], near.at[k], sibling)
        for k, (at_x, at_y) in enumerate(chips)
    ]
    to_sibling[0].wait_recv()
    add_rows(sums.at[0], (mine[0], near.at[0]), 0, rows)
    diagonal_x = send(4, sums.at[0, bottom], far_x.at[bottom], along_x)
    diagonal_y = send(5, sums.at[0, top], far_y.at[top], along_y)
    to_sibling[1].wait_recv()
    add_rows(sums.at[1], (mine[1], near.at[1]), half, half)
    direct_x = send(6, sums.at[1, bottom], from_x.at[bottom], along_x)
    to_sibling[2].wait_recv()
    add_rows(sums.at[2], (mine[2], near.at[2]), 0, half)
    direct_y = send(7, sums.at[2, top], from_y.at[top], along_y)
    to_sibling[3].wait_recv()
    diagonal_y.wait_recv()
    add_rows(sums.at[1], (mine[1], near.at[1], far_y), 0, half)
    joint_x = send(8, sums.at[1, top], from_x.at[top], along_x)
    diagonal_x.wait_recv()
    add_rows(sums.at[2], (mine[2], near.at[2], far_x), half, half)
    joint_y = send(9, sums.at[2, bottom], from_y.at[bottom], along_y)
    direct_x.wait_recv()
    direct_y.wait_recv()
    joint_x.wait_recv()
    joint_y.wait_recv()
    add_rows(own_sum, (mine[3], near.at[3], from_x, from_y), 0, rows)
    for copy in (*to_sibling, diagonal_x, diagonal_y, direct_x, direct_y, joint_x, joint_y):
        copy.wait_send()


def cube_sum(
    part_hbm, own_sum, mine, near, via_z, zx_in, zy_in, far_x, far_y, from_x, from_y, from_z, load_sems, send_sems,
    recv_sems, work=lambda point: None,
):
    sibling, along_x, along_y, along_z = cube_places()
    pieces = own_sum.shape[0]
    half = pieces // 2
    top, bottom = pl.ds(0, half), pl.ds(half, half)
    send = sender(send_sems, recv_sems)
    chips = ((1, 1, 1), (1, 1, 0), (1, 0, 1), (0, 1, 0), (0, 0, 1), (0, 1, 1), (1, 0, 0), (0, 0, 0))
    z_diagonal, z_x, z_y, at_x, at_y, diagonal, at_z, here = range(8)
    to_sibling = [
        send(k, part_hbm.at[cube_member(*chip, 1)], near.at[k], sibling)
        for k, chip in enumerate(chips)
    ]
    loads = [
        pltpu.make_async_copy(part_hbm.at[cube_member(*chip, 0)], mine.at[k], load_sems.at[k])
        for k, chip in enumerate(chips)
    ]
    for load in loads:
        load.start()

    def both_in(k):
        to_sibling[k].wait_recv()
        loads[k].wait()

    def add(k, others=(), start=0, count=pieces):
        add_rows(near.at[k], (mine.at[k], near.at[k], *others), start, count)

    work(0)
    both_in(z_diagonal)
    add(z_diagonal)
    diagonal_z = send(8, near.at[z_diagonal], via_z, along_z)
    both_in(z_x)
    add(z_x)
    zx_out = send(9, near.at[z_x], zx_in, along_x)
    both_in(z_y)
    add(z_y)
    zy_out = send(10, near.at[z_y], zy_in, along_y)
    both_in(at_x)
    add(at_x, (), half, half)
    direct_x = send(13, near.at[at_x, bottom], from_x.at[bottom], along_x)
    both_in(at_y)
    add(at_y, (), 0, half)
    direct_y = send(14, near.at[at_y, top], from_y.at[top], along_y)
    both_in(diagonal)
    both_in(at_z)
    work(1)
    diagonal_z.wait_recv()
    add(diagonal, (via_z,))
    diagonal_x = send(11, near.at[diagonal, bottom], far_x.at[bottom], along_x)
    diagonal_y = send(12, near.at[diagonal, top], far_y.at[top], along_y)
    zx_out.wait_recv()
    zy_out.wait_recv()
    add(at_z, (zx_in, zy_in))
    joint_z = send(15, near.at[at_z], from_z, along_z)
    work(2)
    diagonal_y.wait_recv()
    add(at_x, (far_y,), 0, half)
    joint_x = send(16, near.at[at_x, top], from_x.at[top], along_x)
    diagonal_x.wait_recv()
    add(at_y, (far_x,), half, half)
    joint_y = send(17, near.at[at_y, bottom], from_y.at[bottom], along_y)
    both_in(here)
    work(3)
    for copy in (direct_x, direct_y, joint_z, joint_x, joint_y):
        copy.wait_recv()
    add_rows(own_sum, (mine.at[here], near.at[here], from_x, from_y, from_z), 0, pieces)
    for copy in (
        *to_sibling, diagonal_z, zx_out, zy_out, direct_x, direct_y, diagonal_x, diagonal_y, joint_z, joint_x, joint_y,
    ):
        copy.wait_send()


def cube_sum_kernel(part_ref, out_ref, *scratch):
    greet(cube_places())
    cube_sum(part_ref, out_ref, *scratch)


def cube_sum_scratch(shape, dtype):
    return [
        pltpu.VMEM((8, *shape), dtype),
        pltpu.VMEM((8, *shape), dtype),
        *[pltpu.VMEM(shape, dtype)] * 8,
        pltpu.SemaphoreType.DMA((8,)),
        pltpu.SemaphoreType.DMA((18,)),
        pltpu.SemaphoreType.DMA((18,)),
    ]


def plane_sum_scratch(shape, dtype):
    block = pltpu.VMEM(shape, dtype)
    return [
        pltpu.VMEM((4, *shape), dtype),
        pltpu.VMEM((3, *shape), dtype),
        block,
        block,
        block,
        block,
        pltpu.SemaphoreType.DMA((10,)),
        pltpu.SemaphoreType.DMA((10,)),
    ]


def cube_scatter_sum(partial, collective_id):
    shape = partial.shape[1:]
    out = pl.pallas_call(
        cube_sum_kernel,
        out_shape=jax.ShapeDtypeStruct(shape, jnp.float32),
        in_specs=[pl.BlockSpec(memory_space=pl.ANY)],
        out_specs=pl.BlockSpec(memory_space=pltpu.VMEM),
        scratch_shapes=cube_sum_scratch(shape, partial.dtype),
        cost_estimate=busy(35),
        compiler_params=pltpu.CompilerParams(
            collective_id=collective_id, has_side_effects=True, vmem_limit_bytes=VMEM_BYTES
        ),
    )(partial)
    return out.reshape(shape[0] * shape[1], shape[2])


gelu_inner = 0.7978845608028654
gelu_cubic = 0.044715


def pad_rows(target, source):
    rows = source.shape[0]
    target[pl.ds(0, rows)] = source[...]
    if target.shape[0] > rows:
        extra = target.shape[0] - rows
        target[pl.ds(rows, extra)] = jnp.zeros((extra, target.shape[1]), target.dtype)


def ffn_forward_kernel(in_ref, gate_up_ref, down_ref, part_ref, act_ref, to_gate, to_up, down, proj):
    units = act_ref.shape[1]

    @pl.when(pl.program_id(0) == 0)
    def _():
        pad_rows(down, down_ref)

    step = 64
    half_rows = in_ref.shape[0] // 2

    def mid(base):
        for i in range(half_rows // step):
            rows = pl.ds(base + i * step, step)
            gate, up = proj[rows, :units], proj[rows, units:]
            square = gate * gate
            bend = jnp.tanh(gelu_inner * gate * (1.0 + gelu_cubic * square))
            half = 0.5 * (1.0 + bend)
            value = gate * half
            slope = half + 0.5 * gate * (1.0 - bend * bend) * (
                gelu_inner * (1.0 + 3.0 * gelu_cubic * square)
            )
            to_gate[rows, :] = slope * up
            to_up[rows, :] = value
            act_ref[rows, :] = (value * up).astype(act_ref.dtype)

    first, second = pl.ds(0, half_rows), pl.ds(half_rows, half_rows)
    proj[first, :] = matmul(in_ref[first, :], gate_up_ref[...])
    proj[second, :] = matmul(in_ref[second, :], gate_up_ref[...])
    mid(0)
    part_ref[first, :] = matmul(act_ref[first, :], down[...]).astype(part_ref.dtype)
    mid(half_rows)
    part_ref[second, :] = matmul(act_ref[second, :], down[...]).astype(part_ref.dtype)


ROW_BLOCK = 512


def whole(array):
    return pl.BlockSpec(array.shape, lambda i: (0, 0), pipeline_mode=pl.Buffered(1))


def row_block(columns):
    return pl.BlockSpec((ROW_BLOCK, columns), lambda i: (i, 0))


def ffn_forward(rows_in, gate_up, down):
    rows, depth = rows_in.shape
    units, columns = gate_up.shape[1] // 2, down.shape[1]
    low = rows_in.dtype
    return pl.pallas_call(
        ffn_forward_kernel,
        grid=(rows // ROW_BLOCK,),
        in_specs=[row_block(depth), whole(gate_up), whole(down)],
        out_specs=[row_block(columns), row_block(units), row_block(units), row_block(units)],
        out_shape=[
            jax.ShapeDtypeStruct((rows, columns), low),
            jax.ShapeDtypeStruct((rows, units), low),
            jax.ShapeDtypeStruct((rows, units), jnp.float32),
            jax.ShapeDtypeStruct((rows, units), jnp.float32),
        ],
        scratch_shapes=[
            pltpu.VMEM((units, columns), low),
            pltpu.VMEM((ROW_BLOCK, 2 * units), jnp.float32),
        ],
        cost_estimate=busy(20),
        compiler_params=pltpu.CompilerParams(vmem_limit_bytes=VMEM_BYTES),
    )(rows_in, gate_up, down)


def block_order(rows):
    order = [cube_member(*flips) for flips in CUBE_ORDER]
    return order, [pl.ds(pl.multiple_of(block * rows, rows), rows) for block in order]


def gather_backward_kernel(
    own_ref, down_ref, gate_up_ref, to_gate_hbm, to_up_hbm, act_hbm, both_hbm, part_hbm, down_grad_ref,
    grad, down, to_gate, to_up, act, both, part, act_sem, load_sems, put_sems, send_sems, recv_sems, local_sem,
):
    units = down.shape[0]
    pieces, piece, columns = own_ref.shape
    rows = pieces * piece
    order, places = block_order(rows)

    def loads(i):
        slot, at = i % 2, places[i]
        return (
            pltpu.make_async_copy(to_gate_hbm.at[at], to_gate.at[slot], load_sems.at[0, slot]),
            pltpu.make_async_copy(to_up_hbm.at[at], to_up.at[slot], load_sems.at[1, slot]),
        )

    def puts(i):
        slot = i % 2
        return (
            pltpu.make_async_copy(both.at[slot], both_hbm.at[places[i]], put_sems.at[0, slot]),
            pltpu.make_async_copy(part.at[slot], part_hbm.at[order[i]], put_sems.at[1, slot]),
        )

    def compute(i):
        if i + 1 < len(order):
            for load in loads(i + 1):
                load.start()
        for load in loads(i):
            load.wait()
        if i >= 2:
            for put in puts(i - 2):
                put.wait()
        slot = i % 2
        source = own_ref if i == 0 else grad.at[order[i]]
        act_grad = contract_cols(source[...].reshape(rows, columns), down[...])
        both[slot, :, :units] = (act_grad * to_gate[slot]).astype(both.dtype)
        both[slot, :, units:] = (act_grad * to_up[slot]).astype(both.dtype)
        result = contract_cols(both[slot], gate_up_ref[...]).astype(part.dtype)
        part[slot] = result.reshape(pieces, piece, result.shape[1])
        for put in puts(i):
            put.start()

    act_load = pltpu.make_async_copy(act_hbm, act, act_sem)
    act_load.start()
    for load in loads(0):
        load.start()
    pad_rows(down, down_ref)
    greet(cube_places())
    cube_spread(own_ref, grad, send_sems, recv_sems, local_sem, compute)
    act_load.wait()
    whole = grad[...].reshape(len(order) * rows, columns)
    down_grad = contract_rows(act[...], whole)
    down_grad_ref[...] = down_grad[: down_ref.shape[0]].astype(down_grad_ref.dtype)
    for i in (len(order) - 2, len(order) - 1):
        for put in puts(i):
            put.wait()


def gather_backward(own, down, gate_up, to_gate, to_up, act, collective_id):
    rows, columns = own.shape
    members, piece = 16, 16
    pieces = rows // piece
    depth, units = gate_up.shape[0], to_gate.shape[1]
    low, wide = own.dtype, jnp.float32
    shape = jax.ShapeDtypeStruct
    vmem, anywhere = pl.BlockSpec(memory_space=pltpu.VMEM), pl.BlockSpec(memory_space=pl.ANY)
    return pl.pallas_call(
        gather_backward_kernel,
        out_shape=[
            shape((members * rows, 2 * units), low),
            shape((members, pieces, piece, depth), low),
            shape(down.shape, low),
        ],
        in_specs=[vmem, vmem, vmem, anywhere, anywhere, anywhere],
        out_specs=[anywhere, anywhere, vmem],
        scratch_shapes=[
            pltpu.VMEM((members, pieces, piece, columns), low),
            pltpu.VMEM((units, columns), low),
            pltpu.VMEM((2, rows, units), wide),
            pltpu.VMEM((2, rows, units), wide),
            pltpu.VMEM(act.shape, low),
            pltpu.VMEM((2, rows, 2 * units), low),
            pltpu.VMEM((2, pieces, piece, depth), low),
            pltpu.SemaphoreType.DMA,
            pltpu.SemaphoreType.DMA((2, 2)),
            pltpu.SemaphoreType.DMA((2, 2)),
            *gather_sems(21),
        ],
        cost_estimate=busy(45),
        compiler_params=pltpu.CompilerParams(
            collective_id=collective_id, has_side_effects=True, vmem_limit_bytes=60 * 2**20
        ),
    )(own.reshape(pieces, piece, columns), down, gate_up, to_gate, to_up, act)


def sum_gradients_kernel(
    part_ref, down_ref, in_hbm, both_hbm, sum_ref, gate_up_ref, down_sum_ref,
    columns_in, both, arriving, both_sem, in_sems, far_send, far_recv, *scratch,
):
    cubes = down_ref.shape[0]
    far, others = other_cubes(cubes)
    step = columns_in.shape[2]
    blocks = gate_up_ref.shape[0] // step

    def load(i):
        at = pl.ds(i * step, step)
        return pltpu.make_async_copy(in_hbm.at[:, at], columns_in.at[i % 2], in_sems.at[i % 2])

    both_load = pltpu.make_async_copy(both_hbm, both, both_sem)
    both_load.start()
    load(0).start()

    def rows_of(i):
        if i == 0:
            both_load.wait()
        if i + 1 < blocks:
            load(i + 1).start()
        load(i).wait()
        rows = contract_rows(columns_in[i % 2], both[...])
        gate_up_ref[pl.ds(i * step, step), :] = rows.astype(gate_up_ref.dtype)

    def work(point):
        spread = ((), (0, 1), (2, 3), tuple(range(4, blocks)))
        for i in spread[point]:
            rows_of(i)

    greet((*cube_places(), *others))
    send = sender(far_send, far_recv)
    copies = [
        send(k, down_ref.at[place[0]], arriving.at[k], place) for k, place in enumerate(others)
    ]
    cube_sum(part_ref, sum_ref, *scratch, work=work)
    down_sum = down_ref[far].astype(jnp.float32)
    for k, copy in enumerate(copies):
        copy.wait_recv()
        down_sum = down_sum + arriving[k].astype(jnp.float32)
    down_sum_ref[...] = down_sum
    for copy in copies:
        copy.wait_send()


def sum_gradients(part, down, rows_in, both, collective_id):
    members, pieces, piece, depth = part.shape
    low = part.dtype
    step = 256
    vmem, anywhere = pl.BlockSpec(memory_space=pltpu.VMEM), pl.BlockSpec(memory_space=pl.ANY)
    total, gate_up, down_sum = pl.pallas_call(
        sum_gradients_kernel,
        out_shape=[
            jax.ShapeDtypeStruct((pieces, piece, depth), jnp.float32),
            jax.ShapeDtypeStruct((depth, both.shape[1]), low),
            jax.ShapeDtypeStruct(down.shape[1:], jnp.float32),
        ],
        in_specs=[anywhere, vmem, anywhere, anywhere],
        out_specs=[vmem, vmem, vmem],
        scratch_shapes=[
            pltpu.VMEM((2, rows_in.shape[0], step), low),
            pltpu.VMEM(both.shape, low),
            pltpu.VMEM((down.shape[0] - 1, *down.shape[1:]), low),
            pltpu.SemaphoreType.DMA,
            pltpu.SemaphoreType.DMA((2,)),
            pltpu.SemaphoreType.DMA((down.shape[0] - 1,)),
            pltpu.SemaphoreType.DMA((down.shape[0] - 1,)),
            *cube_sum_scratch((pieces, piece, depth), low),
        ],
        cost_estimate=busy(35),
        compiler_params=pltpu.CompilerParams(
            collective_id=collective_id, has_side_effects=True, vmem_limit_bytes=60 * 2**20
        ),
    )(part, down, rows_in, both)
    return total.reshape(pieces * piece, depth), gate_up, down_sum


def unit_sum_kernel(terms_ref, gate_ref, up_ref):
    cubes, group, _, lanes = terms_ref.shape
    rows, hidden = gate_ref.shape
    units, half = hidden // (cubes * group), lanes // 2
    for member in range(group):
        total = terms_ref[0, member].astype(jnp.float32)
        for cube in range(1, cubes):
            total = total + terms_ref[cube, member].astype(jnp.float32)
        for cube in range(cubes):
            at = (cube * group + member) * units
            gate_ref[:, at : at + units] = total[:rows, cube * units : (cube + 1) * units]
            up_ref[:, at : at + units] = total[
                :rows, half + cube * units : half + (cube + 1) * units
            ]


def unit_sum(terms, rows, hidden):
    vmem = pl.BlockSpec(memory_space=pltpu.VMEM)
    return pl.pallas_call(
        unit_sum_kernel,
        out_shape=[jax.ShapeDtypeStruct((rows, hidden), jnp.float32)] * 2,
        in_specs=[vmem],
        out_specs=[vmem, vmem],
        cost_estimate=busy(5),
        compiler_params=pltpu.CompilerParams(vmem_limit_bytes=VMEM_BYTES),
    )(terms)


def owner_sum_kernel(planes, part_ref, out_ref, own_sum, leaving, arriving, z_send, z_recv, *scratch):
    plane, others, ring = other_planes(planes)
    greet((*plane_places()[:3], *others))
    plane_sum(part_ref, own_sum, *scratch)
    send = sender(z_send, z_recv)

    def narrow(i, carry):
        leaving[i] = own_sum[i].astype(leaving.dtype)
        return carry

    lax.fori_loop(0, planes, narrow, 0)
    copies = [
        send(k, leaving.at[ring[k]], arriving.at[k], place) for k, place in enumerate(others)
    ]
    for copy in copies:
        copy.wait_recv()

    value = own_sum[plane]
    for k in range(planes - 1):
        value = value + arriving[k].astype(jnp.float32)
    out_ref[...] = value
    for copy in copies:
        copy.wait_send()


def owner_sum(blocks, collective_id):
    members, planes, rows, columns = blocks.shape
    return pl.pallas_call(
        functools.partial(owner_sum_kernel, planes),
        out_shape=jax.ShapeDtypeStruct((rows, columns), jnp.float32),
        in_specs=[pl.BlockSpec(memory_space=pltpu.VMEM)],
        out_specs=pl.BlockSpec(memory_space=pltpu.VMEM),
        scratch_shapes=[
            pltpu.VMEM((planes, rows, columns), jnp.float32),
            pltpu.VMEM((planes, rows, columns), blocks.dtype),
            pltpu.VMEM((planes - 1, rows, columns), blocks.dtype),
            pltpu.SemaphoreType.DMA((planes - 1,)),
            pltpu.SemaphoreType.DMA((planes - 1,)),
            *plane_sum_scratch((planes, rows, columns), blocks.dtype),
        ],
        cost_estimate=busy(35),
        compiler_params=pltpu.CompilerParams(
            collective_id=collective_id, has_side_effects=True, vmem_limit_bytes=VMEM_BYTES
        ),
    )(blocks)


GAIN_SLOT = 128
TILE_ROWS, TILE_LANES = 8, 128


def packed_strips(rows, width, columns):
    across, into = width // TILE_LANES, columns // TILE_LANES
    strips, tile, tiles = [], 0, rows // TILE_ROWS * across
    while tile < tiles:
        run = min(across - tile % across, into - tile % into)
        strips.append(
            (
                tile // across * TILE_ROWS,
                tile % across * TILE_LANES,
                tile // into * TILE_ROWS,
                tile % into * TILE_LANES,
                run * TILE_LANES,
            )
        )
        tile += run
    return strips, up_to(tiles, into) // into * TILE_ROWS


def unpack_tiles(array, rows, width):
    strips, _ = packed_strips(rows, width, array.shape[1])
    lines = []
    for row in range(0, rows, TILE_ROWS):
        parts = [
            array[to : to + TILE_ROWS, at : at + n] for r, _, to, at, n in strips if r == row
        ]
        lines.append(jnp.concatenate(parts, axis=1))
    return jnp.concatenate(lines, axis=0)


def gain_places(blocks, planes, count):
    lane = lax.broadcasted_iota(jnp.int32, (GAIN_SLOT, blocks * count), 0)
    inner = lax.broadcasted_iota(jnp.int32, (GAIN_SLOT, blocks * count), 1) % count
    places = (lane == inner).astype(jnp.float32).astype(jnp.bfloat16)
    listed = lax.broadcasted_iota(jnp.int32, (blocks, blocks * count), 0)
    block = lax.broadcasted_iota(jnp.int32, (blocks, blocks * count), 1) // count
    members = blocks // planes
    block = block % members * planes + block // members
    return places, listed == block


def spread_gain(rows, planes, count):
    places, chosen = gain_places(rows.shape[0], planes, count)
    return jnp.sum(jnp.where(chosen, matmul(rows, places), 0.0), axis=0, keepdims=True)


def collect_gain(vector, blocks, planes, count):
    places, chosen = gain_places(blocks, planes, count)
    return contract_cols(jnp.where(chosen, vector, 0.0).astype(jnp.bfloat16), places)


def inverse_of(values, count):
    return lax.rsqrt(jnp.sum(values * values, axis=-1, keepdims=True) / count + epsilon)


def back_of(grad_normed, normed, inverse, count):
    inner = jnp.sum(grad_normed * normed, axis=-1, keepdims=True) / count
    return inverse * (grad_normed - normed * inner)


def turn(values, cos_table, sin_table):
    half = values.shape[1] // 2
    first, second = values[:, :half], values[:, half:]
    return first * cos_table - second * sin_table, second * cos_table + first * sin_table


def attention_forward_kernel(
    gain_widths, width_rows, padded, row_ref, hidden_ref, packed_ref, cos_ref, sin_ref, segment_column, segment_row, placing_ref,
    placed_ref, middle_ref, raw_ref, mix_ref, probs_ref, query_ref, key_ref, value_ref, query_raw_ref,
    key_raw_ref, qkv_ref, output_ref, input_scale, query_scale, key_scale, attnout_scale, ffnin_scale, ffnout_scale,
    gain_rows,
):
    bf16, f32 = jnp.bfloat16, jnp.float32
    members, planes, piece, _ = packed_ref.shape
    blocks = members * planes
    width = hidden_ref.shape[1]
    mix_rows = output_ref.shape[0] // blocks
    strips, _ = packed_strips(mix_rows, width, packed_ref.shape[3])
    local_rows, full_rows = hidden_ref.shape[0], row_ref.shape[0]
    head = key_ref.shape[1]
    heads = query_ref.shape[1] // head
    offset = pl.multiple_of(lax.axis_index("seq") * local_rows, local_rows)
    mine = pl.ds(offset, local_rows)
    for i in range(blocks):
        member, plane = i // planes, i % planes
        block = packed_ref[member, plane]
        natural = width_rows * (plane * members + member)
        qkv_ref[natural : natural + width_rows, :] = block[:width_rows]
        natural = mix_rows * (plane * members + member)
        for r, c, to, at, n in strips:
            tiles = block[padded + to : padded + to + TILE_ROWS, at : at + n]
            output_ref[natural + r : natural + r + TILE_ROWS, c : c + n] = tiles
        gain_rows[i : i + 1, :] = block[width_rows : width_rows + 1, : gain_rows.shape[1]].astype(f32)
    targets = (input_scale, query_scale, key_scale, attnout_scale, ffnin_scale, ffnout_scale)
    for k, (target, count) in enumerate(zip(targets, gain_widths)):
        rows = gain_rows[:, k * GAIN_SLOT : (k + 1) * GAIN_SLOT].astype(bf16)
        target[...] = spread_gain(rows, planes, count)

    row = row_ref[...].astype(f32)
    normed = (row * inverse_of(row, width) * input_scale[...]).astype(bf16)
    key_value = matmul(normed, qkv_ref[:, heads * head :])
    key_raw = key_value[:, :head]
    value_ref[...] = key_value[:, head:].astype(bf16)
    half = head // 2
    turned = turn(key_raw * inverse_of(key_raw, head) * key_scale[...], cos_ref[...], sin_ref[...])
    key_ref[:, :half], key_ref[:, half:] = turned[0].astype(bf16), turned[1].astype(bf16)

    row = row_ref[mine, :].astype(f32)
    normed = (row * inverse_of(row, width) * input_scale[...]).astype(bf16)
    own = matmul(normed, qkv_ref[:, : (heads + 1) * head])
    query_raw_ref[...] = own[:, : heads * head]
    key_raw_ref[...] = own[:, heads * head :]
    cos_table, sin_table = cos_ref[mine, :], sin_ref[mine, :]
    places = offset + lax.broadcasted_iota(jnp.int32, (local_rows, full_rows), 0)
    earlier = places >= lax.broadcasted_iota(jnp.int32, (local_rows, full_rows), 1)
    allowed = (segment_column[...] == segment_row[...]) & earlier
    for h in range(heads):
        at = h * head
        query_raw = query_raw_ref[:, at : at + head]
        turned = turn(
            query_raw * inverse_of(query_raw, head) * query_scale[...], cos_table, sin_table
        )
        scale = head ** (-0.5)
        query_ref[:, at : at + half] = (turned[0] * scale).astype(bf16)
        query_ref[:, at + half : at + head] = (turned[1] * scale).astype(bf16)
        scores = contract_cols(query_ref[:, at : at + head], key_ref[...])
        scores = jnp.where(allowed, scores, masked_score)
        weights = jnp.exp(scores - jnp.max(scores, axis=-1, keepdims=True))
        probs = weights / jnp.sum(weights, axis=-1, keepdims=True)
        probs_ref[h] = probs
        mix_ref[:, at : at + head] = matmul(probs.astype(bf16), value_ref[...]).astype(bf16)
    attn_raw = matmul(mix_ref[...], output_ref[...])
    raw_ref[...] = attn_raw
    middle = hidden_ref[...].astype(f32) + attn_raw * inverse_of(attn_raw, width) * attnout_scale[...]
    middle_ref[...] = middle
    ffn_in = (middle * inverse_of(middle, width) * ffnin_scale[...]).astype(bf16)
    placed_ref[...] = matmul(ffn_in, placing_ref[...]).astype(bf16)


def attention_forward(
    row_tokens, hidden, packed, cos_full, sin_full, segment_column, segment_row, placing, gain_widths, width_rows, padded,
    head_width,
):
    bf16, f32 = jnp.bfloat16, jnp.float32
    members, planes, piece, qkv_width = packed.shape
    blocks = members * planes
    local_rows, width = hidden.shape
    query_width = qkv_width - 2 * head_width
    heads = query_width // head_width
    full_rows = row_tokens.shape[0]
    depth = blocks * padded
    shape = jax.ShapeDtypeStruct
    vmem = pl.BlockSpec(memory_space=pltpu.VMEM)
    out_shape = [
        shape((local_rows, depth), bf16),
        shape((local_rows, width), f32),
        shape((local_rows, width), f32),
        shape((local_rows, query_width), bf16),
        shape((heads, local_rows, full_rows), f32),
        shape((local_rows, query_width), bf16),
        shape((full_rows, head_width), bf16),
        shape((full_rows, head_width), bf16),
        shape((local_rows, query_width), f32),
        shape((local_rows, head_width), f32),
        shape((width, qkv_width), bf16),
        shape((query_width, width), bf16),
        shape((1, width), f32),
        shape((1, head_width), f32),
        shape((1, head_width), f32),
        shape((1, width), f32),
        shape((1, width), f32),
        shape((1, width), f32),
    ]
    return pl.pallas_call(
        functools.partial(attention_forward_kernel, gain_widths, width_rows, padded),
        out_shape=out_shape,
        in_specs=[vmem] * 8,
        out_specs=[vmem] * len(out_shape),
        scratch_shapes=[pltpu.VMEM((blocks, len(gain_widths) * GAIN_SLOT), f32)],
        cost_estimate=busy(20),
        compiler_params=pltpu.CompilerParams(vmem_limit_bytes=60 * 2**20),
    )(row_tokens, hidden, packed, cos_full, sin_full, segment_column, segment_row, placing)


def attention_backward_kernel(
    gain_widths, width_rows, planes, padded, grad_ref, incoming_ref, middle_ref, raw_ref, mix_ref, probs_ref, query_ref, key_ref,
    value_ref, query_raw_ref, key_raw_ref, row_ref, qkv_ref, output_ref, cos_ref, sin_ref, input_scale,
    query_scale, key_scale, attnout_scale, ffnin_scale, ffnout_grad, by_device,
    input_grad_ref, blocks_ref, key_value, query_grad, low_ref, leaving, arriving, send_sem, recv_sem,
):
    bf16, f32 = jnp.bfloat16, jnp.float32
    members = blocks_ref.shape[0]
    blocks = members * planes
    mix_rows = output_ref.shape[0] // blocks
    local_rows, width = incoming_ref.shape
    strips, _ = packed_strips(mix_rows, width, blocks_ref.shape[3])
    head = key_ref.shape[1]
    heads = query_ref.shape[1] // head
    half = head // 2
    seq = lax.axis_index("seq")
    mine = pl.ds(pl.multiple_of(seq * local_rows, local_rows), local_rows)
    theirs = pl.ds(pl.multiple_of((1 - seq) * local_rows, local_rows), local_rows)
    partner = plane_places()[2]
    greet((partner,))

    ffn_in_grad = take_back(grad_ref[...], by_device[...])
    middle = middle_ref[...]
    inverse = inverse_of(middle, width)
    normed = middle * inverse
    ffnin_grad = jnp.sum(ffn_in_grad * normed, axis=0, keepdims=True)
    middle_grad = incoming_ref[...].astype(f32) + back_of(
        ffn_in_grad * ffnin_scale[...], normed, inverse, width
    )
    input_grad_ref[...] = middle_grad
    raw = raw_ref[...]
    inverse = inverse_of(raw, width)
    normed = raw * inverse
    attnout_grad = jnp.sum(middle_grad * normed, axis=0, keepdims=True)
    raw_grad = back_of(middle_grad * attnout_scale[...], normed, inverse, width).astype(bf16)
    mix_grad = contract_cols(raw_grad, output_ref[...]).astype(bf16)
    for h in range(heads):
        at = h * head
        grad = mix_grad[:, at : at + head]
        probs = probs_ref[h]
        prob_grad = contract_cols(grad, value_ref[...])
        delta = jnp.sum(prob_grad * probs, axis=-1, keepdims=True)
        score_grad = (probs * (prob_grad - delta)).astype(bf16)
        to_keys = contract_rows(score_grad, query_ref[:, at : at + head])
        to_values = contract_rows(probs.astype(bf16), grad)
        if h == 0:
            key_value[:, :head], key_value[:, head:] = to_keys, to_values
        else:
            key_value[:, :head] += to_keys
            key_value[:, head:] += to_values
        query_grad[:, at : at + head] = matmul(score_grad, key_ref[...])
    leaving[...] = key_value[theirs, :].astype(bf16)
    copy = sender(send_sem, recv_sem)(0, leaving, arriving, partner)

    output_grad = contract_rows(mix_ref[...], raw_grad).astype(bf16)
    cos_table, sin_table = cos_ref[mine, :], sin_ref[mine, :]

    def head_back(grad, raw, scale_ref):
        turned = jnp.concatenate(turn(grad, cos_table, -sin_table), axis=1)
        inverse = inverse_of(raw, head)
        normed = raw * inverse
        gain = jnp.sum(turned * normed, axis=0, keepdims=True)
        return back_of(turned * scale_ref[...], normed, inverse, head).astype(bf16), gain

    query_gain = jnp.zeros((1, head), f32)
    for h in range(heads):
        at = h * head
        low, gain = head_back(
            query_grad[:, at : at + head] * head ** (-0.5),
            query_raw_ref[:, at : at + head],
            query_scale,
        )
        low_ref[:, at : at + head] = low
        query_gain = query_gain + gain
    copy.wait_recv()
    total = key_value[mine, :] + arriving[...].astype(f32)
    low, key_gain = head_back(total[:, :head], key_raw_ref[...], key_scale)
    low_ref[:, heads * head : (heads + 1) * head] = low
    low_ref[:, (heads + 1) * head :] = total[:, head:].astype(bf16)

    row = row_ref[mine, :].astype(f32)
    inverse = inverse_of(row, width)
    normed = row * inverse
    normed_grad = contract_cols(low_ref[...], qkv_ref[...])
    input_gain = jnp.sum(normed_grad * normed, axis=0, keepdims=True)
    input_grad_ref[...] += back_of(normed_grad * input_scale[...], normed, inverse, width)
    vectors = (input_gain, query_gain, key_gain, attnout_grad, ffnin_grad, ffnout_grad[...])
    gains = jnp.concatenate(
        [
            collect_gain(vector, blocks, planes, count)
            for vector, count in zip(vectors, gain_widths)
        ],
        axis=1,
    )
    columns = blocks_ref.shape[3]
    gains = jnp.concatenate([gains, jnp.zeros((blocks, columns - gains.shape[1]), f32)], axis=1)
    spare = jnp.zeros((padded - width_rows - 1, columns), f32)
    normed = (normed * input_scale[...]).astype(bf16)
    weights = contract_rows(normed, low_ref[...])
    for i in range(blocks):
        member, plane = i // planes, i % planes
        natural = width_rows * (plane * members + member)
        piece = weights[natural : natural + width_rows]
        block = jnp.concatenate([piece, gains[i : i + 1], spare], axis=0)
        blocks_ref[member, plane, :padded, :] = block.astype(bf16)
        natural = mix_rows * (plane * members + member)
        for r, c, to, at, n in strips:
            tiles = output_grad[natural + r : natural + r + TILE_ROWS, c : c + n]
            blocks_ref[member, plane, padded + to : padded + to + TILE_ROWS, at : at + n] = tiles
        _, _, to, at, n = strips[-1]
        if at + n < columns:
            rest = jnp.zeros((TILE_ROWS, columns - at - n), bf16)
            blocks_ref[member, plane, padded + to : padded + to + TILE_ROWS, at + n :] = rest
    copy.wait_send()


def attention_backward(arrays, gain_widths, width_rows, planes, padded, mix_rows, collective_id):
    bf16, f32 = jnp.bfloat16, jnp.float32
    grad, incoming, query, key, qkv = arrays[0], arrays[1], arrays[6], arrays[7], arrays[12]
    local_rows, width = incoming.shape
    members = 8
    _, packed_rows = packed_strips(mix_rows, width, qkv.shape[1])
    pair = pltpu.VMEM((local_rows, 2 * key.shape[1]), bf16)
    shape = jax.ShapeDtypeStruct
    vmem = pl.BlockSpec(memory_space=pltpu.VMEM)
    return pl.pallas_call(
        functools.partial(attention_backward_kernel, gain_widths, width_rows, planes, padded),
        out_shape=[
            shape((local_rows, width), f32),
            shape((members, planes, padded + packed_rows, qkv.shape[1]), bf16),
        ],
        in_specs=[vmem] * len(arrays),
        out_specs=[vmem] * 2,
        scratch_shapes=[
            pltpu.VMEM((key.shape[0], 2 * key.shape[1]), f32),
            pltpu.VMEM(query.shape, f32),
            pltpu.VMEM((local_rows, qkv.shape[1]), bf16),
            pair,
            pair,
            pltpu.SemaphoreType.DMA((1,)),
            pltpu.SemaphoreType.DMA((1,)),
        ],
        cost_estimate=busy(30),
        compiler_params=pltpu.CompilerParams(
            collective_id=collective_id, has_side_effects=True, vmem_limit_bytes=60 * 2**20
        ),
    )(*arrays)


def body(
    tokens,
    segment_ids,
    cotangent,
    query_weight,
    key_weight,
    value_weight,
    output_weight,
    gate_weight,
    up_weight,
    down_weight,
    input_gain,
    query_gain,
    key_gain,
    attnout_gain,
    ffnin_gain,
    ffnout_gain,
):
    bf16, f32 = jnp.bfloat16, jnp.float32
    devices = lax.axis_size(ALL)
    members = lax.axis_size(PLANE)
    planes = lax.axis_size(PLANES)
    cubes = lax.axis_size("far")
    group = lax.axis_size(CUBE)
    width_rows = query_weight.shape[0]
    hidden_rows = down_weight.shape[0]
    head_width = key_weight.shape[1]
    query_width = query_weight.shape[1]
    head_count = query_width // head_width
    qkv_width = query_width + 2 * head_width
    mix_rows = output_weight.shape[0]
    padded = up_to(width_rows + 1, 8)
    width = devices * width_rows
    unit_count = cubes * hidden_rows
    unit_pad = up_to(unit_count, 128)
    by_device = place_columns(devices, width_rows, padded)

    gains = (input_gain, query_gain, key_gain, attnout_gain, ffnin_gain, ffnout_gain)
    gain_widths = [g.shape[0] for g in gains]
    packed_all = z_gather(
        query_weight, key_weight, value_weight, output_weight, gains, planes, padded, 0
    )
    other_tokens = lax.ppermute(tokens[0], "seq", [(0, 1), (1, 0)])
    packed_all, other_tokens = lax.optimization_barrier((packed_all, other_tokens))
    packed_all, down_full, gate_up = weights_gather(
        packed_all, down_weight, gate_weight, up_weight, (group, padded, 2 * unit_pad), cubes, 6
    )
    down_full = down_full.reshape(unit_count, down_weight.shape[1])
    gate_up, packed_all = lax.optimization_barrier((gate_up, packed_all))
    gate_up = gate_up.reshape(devices, padded, 2 * unit_pad)
    gate_up_full = exchange(gate_up, ALL).reshape(devices * padded, 2 * unit_pad)
    incoming = cotangent[0].astype(f32)
    local_rows = tokens.shape[1]
    offset = lax.axis_index("seq") * local_rows
    segment_row = segment_ids[0]

    def mine(rows):
        return lax.dynamic_slice_in_dim(rows, offset, local_rows)

    cos_full, sin_full = rope_tables(doc_positions(segment_row), head_width)

    first = lax.axis_index("seq") == 0
    row_tokens = jnp.concatenate(
        [
            jnp.where(first, tokens[0], other_tokens),
            jnp.where(first, other_tokens, tokens[0]),
        ]
    )
    (
        ffn_in_placed,
        middle,
        attn_raw,
        attn_flat,
        probs,
        queries,
        key_rows,
        value_rows,
        query_raw,
        key_raw,
        qkv_full,
        output_full,
        *scales,
    ) = attention_forward(
        row_tokens,
        tokens[0],
        packed_all,
        cos_full,
        sin_full,
        mine(segment_row)[:, None],
        segment_row[None],
        by_device,
        gain_widths,
        width_rows,
        padded,
        head_width,
    )
    ffnout_scale = scales.pop()

    cube_in = gather_rows(ffn_in_placed, 1)
    ffn_part, activated_low, to_gate, to_up = ffn_forward(cube_in, gate_up_full, down_full)
    ffn_part = ffn_part.reshape(group, local_rows // 16, 16, ffn_part.shape[1])
    ffn_raw = cube_scatter_sum(ffn_part, 2)
    inv_ffn = inverse_rms(ffn_raw)
    norm_ffn = ffn_raw * inv_ffn
    result = middle + norm_ffn * ffnout_scale
    ffnout_gain_grad = jnp.sum(incoming * norm_ffn, axis=0)
    ffn_raw_grad = rms_back(incoming * ffnout_scale, norm_ffn, inv_ffn).astype(bf16)

    gate_up_low, ffn_in_part, down_blocks = gather_backward(
        ffn_raw_grad, down_full, gate_up_full, to_gate, to_up, activated_low, 3
    )
    down_blocks = down_blocks.reshape(cubes, hidden_rows, down_weight.shape[1])
    ffn_in_grad, gate_up_blocks, down_wgrad = sum_gradients(
        ffn_in_part, down_blocks, cube_in, gate_up_low, 4
    )
    gate_up_terms = exchange(gate_up_blocks.reshape(devices, padded, 2 * unit_pad), ALL)
    input_grad, blocks = attention_backward(
        [
            ffn_in_grad,
            cotangent[0],
            middle,
            attn_raw,
            attn_flat,
            probs,
            queries,
            key_rows,
            value_rows,
            query_raw,
            key_raw,
            row_tokens,
            qkv_full,
            output_full,
            cos_full,
            sin_full,
            *scales,
            ffnout_gain_grad[None],
            by_device,
        ],
        gain_widths,
        width_rows,
        planes,
        padded,
        mix_rows,
        7,
    )
    share = owner_sum(blocks, 5)
    gate_wgrad, up_wgrad = unit_sum(
        gate_up_terms.reshape(cubes, group, padded, 2 * unit_pad), width_rows, gate_weight.shape[1]
    )
    qkv_share, output_share = share[:padded], unpack_tiles(share[padded:], *output_weight.shape)
    gain_shares = [
        qkv_share[width_rows, k * GAIN_SLOT : k * GAIN_SLOT + count]
        for k, count in enumerate(gain_widths)
    ]
    return (
        result.astype(bf16)[None],
        input_grad[None],
        qkv_share[:width_rows, :query_width],
        qkv_share[:width_rows, query_width : query_width + head_width],
        qkv_share[:width_rows, query_width + head_width :],
        output_share,
        gate_wgrad,
        up_wgrad,
        down_wgrad,
        *gain_shares,
    )


def solution(mesh):
    dp, seq = mesh.shape["dp"], mesh.shape["seq"]
    split = Mesh(mesh.devices.reshape(dp // 8, 2, 2, 2, seq), ALL)
    rows = P(("far", "z", "x", "core"), "seq", None)
    matrix, vector = P(ALL, None), P(ALL)
    return jax.shard_map(
        body,
        mesh=split,
        in_specs=(rows, P(("far", "z", "x", "core"), None), rows) + (matrix,) * 7 + (vector,) * 6,
        out_specs=(rows, rows) + (matrix,) * 7 + (vector,) * 6,
        check_vma=False,
    )
```

```python
import functools

import jax
import jax.numpy as jnp
import numpy as np
from jax import lax
from jax.experimental import pallas as pl
from jax.experimental.pallas import tpu as pltpu
from jax.sharding import Mesh
from jax.sharding import PartitionSpec as P

epsilon = 1e-06
rope_base = 1000000.0
masked_score = -1e30


def inverse_rms(values):
    return lax.rsqrt(jnp.mean(values * values, axis=-1, keepdims=True) + epsilon)


def rms_back(grad_normed, normed, inverse):
    return inverse * (grad_normed - normed * jnp.mean(grad_normed * normed, axis=-1, keepdims=True))


def doc_positions(segments):
    length = segments.shape[0]
    smaller = segments[None, :] < segments[:, None]
    starts = jnp.sum(smaller.astype(jnp.int32), axis=1)
    return (jnp.arange(length, dtype=jnp.int32) - starts).astype(jnp.float32)


def rope_tables(positions, head_width):
    half_width = head_width // 2
    frequency = rope_base ** (-(2.0 / head_width) * jnp.arange(half_width, dtype=jnp.float32))
    angles = positions[..., None] * frequency
    return (jnp.cos(angles), jnp.sin(angles))


def matmul(left, right):
    return jnp.dot(left, right, preferred_element_type=jnp.float32)


def contract_rows(left, right):
    return lax.dot_general(
        left, right, (((0,), (0,)), ((), ())), preferred_element_type=jnp.float32
    )


def contract_cols(left, right):
    return lax.dot_general(
        left, right, (((1,), (1,)), ((), ())), preferred_element_type=jnp.float32
    )


ALL = ("far", "z", "x", "core", "seq")
PLANES = ("far", "z")
CUBE = ("z", "x", "core", "seq")


def up_to(size, multiple):
    return (size + multiple - 1) // multiple * multiple


def place_columns(blocks, rows, padded):
    source = np.arange(blocks * rows)
    block, inner = source // rows, source % rows
    placing = np.zeros((blocks * rows, blocks * padded), np.float32)
    placing[source, block * padded + inner] = 1.0
    return jnp.asarray(placing.astype(jnp.bfloat16))


def take_back(padded_values, placing):
    high = lax.reduce_precision(padded_values, 8, 7)
    terms = jnp.concatenate([high, padded_values - high], axis=0).astype(jnp.bfloat16)
    both = contract_cols(terms, placing)
    rows = padded_values.shape[0]
    return both[:rows] + both[rows:]


PLANE = ("x", "core", "seq")

MESH_ID = pl.DeviceIdType.MESH
VMEM_BYTES = 48 * 2**20


def exchange(blocks, axes):
    return lax.all_to_all(blocks, axes, split_axis=0, concat_axis=0, tiled=True)


def busy(microseconds):
    return pl.CostEstimate(flops=0, bytes_accessed=microseconds * 3_000_000, transcendentals=0)


def shifted(flip_z, flip_x, flip_core, flip_y):
    far, *inner = (lax.axis_index(name) for name in ALL)
    flips = (flip_z, flip_x, flip_core, flip_y)
    return (far, *(1 - at if flip else at for at, flip in zip(inner, flips)))


def plane_places():
    def member(flip_x, flip_core, flip_y):
        _, _, x, core, seq = shifted(0, flip_x, flip_core, flip_y)
        return (x * 2 + core) * 2 + seq

    return shifted(0, 0, 1, 0), shifted(0, 1, 0, 0), shifted(0, 0, 0, 1), member


def cube_member(flip_z, flip_x, flip_y, flip_core):
    _, z, x, core, seq = shifted(flip_z, flip_x, flip_core, flip_y)
    return ((z * 2 + x) * 2 + core) * 2 + seq


def cube_places():
    return *plane_places()[:3], shifted(1, 0, 0, 0)


def other_planes(planes):
    far, z, x, core, seq = (lax.axis_index(name) for name in ALL)
    plane = far * 2 + z
    ring = [lax.rem(plane + k, planes) for k in range(1, planes)]
    return plane, [(at // 2, lax.rem(at, 2), x, core, seq) for at in ring], ring


def other_cubes(cubes):
    far, z, x, core, seq = (lax.axis_index(name) for name in ALL)
    return far, [(lax.rem(far + k, cubes), z, x, core, seq) for k in range(1, cubes)]


def greet(places):
    barrier = pltpu.get_barrier_semaphore()
    for place in places:
        pl.semaphore_signal(barrier, inc=1, device_id=place, device_id_type=MESH_ID)
    pl.semaphore_wait(barrier, len(places))


def sender(send_sems, recv_sems):
    def send(kind, source, target, place):
        copy = pltpu.make_async_remote_copy(
            src_ref=source,
            dst_ref=target,
            send_sem=send_sems.at[kind],
            recv_sem=recv_sems.at[kind],
            device_id=place,
            device_id_type=MESH_ID,
        )
        copy.start()
        return copy

    return send


def plane_spread(own_ref, out_ref, send_sems, recv_sems, local_sem, meanwhile=lambda: None):
    sibling, along_x, along_y, member = plane_places()
    half = own_ref.shape[0] // 2
    top, bottom = pl.ds(0, half), pl.ds(half, half)
    me = member(0, 0, 0)
    keep = pltpu.make_async_copy(own_ref, out_ref.at[me], local_sem)
    keep.start()
    send = sender(send_sems, recv_sems)

    def forward(kind, block, rows, place):
        return send(kind, out_ref.at[block, rows], out_ref.at[block, rows], place)

    own_x_top = send(1, own_ref.at[top], out_ref.at[me, top], along_x)
    own_y_bottom = send(3, own_ref.at[bottom], out_ref.at[me, bottom], along_y)
    own_sibling = send(0, own_ref, out_ref.at[me], sibling)
    own_x_bottom = send(2, own_ref.at[bottom], out_ref.at[me, bottom], along_x)
    own_y_top = send(4, own_ref.at[top], out_ref.at[me, top], along_y)
    x_block, y_block, diagonal = member(1, 0, 0), member(0, 0, 1), member(1, 0, 1)
    meanwhile()
    own_x_top.wait_recv()
    diagonal_top = forward(5, x_block, top, along_y)
    x_top = forward(7, x_block, top, sibling)
    own_y_bottom.wait_recv()
    diagonal_bottom = forward(6, y_block, bottom, along_x)
    y_bottom = forward(9, y_block, bottom, sibling)
    own_x_bottom.wait_recv()
    x_bottom = forward(8, x_block, bottom, sibling)
    own_y_top.wait_recv()
    y_top = forward(10, y_block, top, sibling)
    diagonal_top.wait_recv()
    far_top = forward(11, diagonal, top, sibling)
    diagonal_bottom.wait_recv()
    far_bottom = forward(12, diagonal, bottom, sibling)
    for copy in (own_sibling, x_top, y_bottom, x_bottom, y_top, far_top, far_bottom):
        copy.wait_recv()
    for copy in (
        own_x_top,
        own_y_bottom,
        own_sibling,
        own_x_bottom,
        own_y_top,
        diagonal_top,
        diagonal_bottom,
        x_top,
        y_bottom,
        x_bottom,
        y_top,
        far_top,
        far_bottom,
    ):
        copy.wait_send()
    keep.wait()


def cube_spread(own_ref, out_ref, send_sems, recv_sems, local_sem, compute=lambda i: None):
    sibling, along_x, along_y, along_z = cube_places()
    half = own_ref.shape[0] // 2
    top, bottom = pl.ds(0, half), pl.ds(half, half)
    me = cube_member(0, 0, 0, 0)
    keep = pltpu.make_async_copy(own_ref, out_ref.at[me], local_sem)
    keep.start()
    send = sender(send_sems, recv_sems)
    x_block, y_block, diagonal = (cube_member(0, *at, 0) for at in ((1, 0), (0, 1), (1, 1)))
    z_block, zx_block, zy_block, zd_block = (
        cube_member(1, *at, 0) for at in ((0, 0), (1, 0), (0, 1), (1, 1))
    )

    def half_on(kind, block, rows, place):
        return send(kind, out_ref.at[block, rows], out_ref.at[block, rows], place)

    def on(kind, block, place):
        return send(kind, out_ref.at[block], out_ref.at[block], place)

    own_x_top = send(1, own_ref.at[top], out_ref.at[me, top], along_x)
    own_y_bottom = send(3, own_ref.at[bottom], out_ref.at[me, bottom], along_y)
    own_z = send(13, own_ref, out_ref.at[me], along_z)
    own_sibling = send(0, own_ref, out_ref.at[me], sibling)
    own_x_bottom = send(2, own_ref.at[bottom], out_ref.at[me, bottom], along_x)
    own_y_top = send(4, own_ref.at[top], out_ref.at[me, top], along_y)
    compute(0)
    own_x_top.wait_recv()
    diagonal_top = half_on(5, x_block, top, along_y)
    x_top = half_on(7, x_block, top, sibling)
    own_y_bottom.wait_recv()
    diagonal_bottom = half_on(6, y_block, bottom, along_x)
    y_bottom = half_on(9, y_block, bottom, sibling)
    own_sibling.wait_recv()
    compute(1)
    own_z.wait_recv()
    z_to_x = on(14, z_block, along_x)
    z_to_y = on(15, z_block, along_y)
    z_near = on(16, z_block, sibling)
    own_x_bottom.wait_recv()
    x_bottom = half_on(8, x_block, bottom, sibling)
    own_y_top.wait_recv()
    y_top = half_on(10, y_block, top, sibling)
    compute(2)
    diagonal_top.wait_recv()
    far_top = half_on(11, diagonal, top, sibling)
    diagonal_bottom.wait_recv()
    far_bottom = half_on(12, diagonal, bottom, sibling)
    diagonal_z = on(17, diagonal, along_z)
    compute(3)
    compute(4)
    z_to_x.wait_recv()
    zx_near = on(18, zx_block, sibling)
    z_to_y.wait_recv()
    zy_near = on(19, zy_block, sibling)
    compute(5)
    compute(6)
    diagonal_z.wait_recv()
    zd_near = on(20, zd_block, sibling)
    compute(7)
    compute(8)
    last = (
        (x_top, x_bottom), (y_bottom, y_top), (far_top, far_bottom), (z_near,), (zx_near,), (zy_near,), (zd_near,),
    )
    for i, copies in enumerate(last):
        for copy in copies:
            copy.wait_recv()
        compute(9 + i)
    for copy in (
        own_x_top, own_y_bottom, own_z, own_sibling, own_x_bottom, own_y_top, diagonal_top, diagonal_bottom,
        z_to_x, z_to_y, diagonal_z,
    ):
        copy.wait_send()
    for copies in last:
        for copy in copies:
            copy.wait_send()
    keep.wait()


CUBE_ORDER = (
    (0, 0, 0, 0), (0, 0, 0, 1), (0, 1, 0, 0), (0, 0, 1, 0), (1, 0, 0, 0), (0, 1, 1, 0), (1, 1, 0, 0), (1, 0, 1, 0),
    (1, 1, 1, 0), (0, 1, 0, 1), (0, 0, 1, 1), (0, 1, 1, 1), (1, 0, 0, 1), (1, 1, 0, 1), (1, 0, 1, 1), (1, 1, 1, 1),
)


def cube_gather_kernel(own_ref, out_ref, *sems):
    greet(cube_places())
    cube_spread(own_ref, out_ref, *sems)


def weights_gather_kernel(
    cubes, own_ref, down_ref, gate_hbm, up_hbm, out_ref, down_out, blocks_hbm, gate_ref, up_ref, blocks, load_sems,
    put_sems, far_send, far_recv, own_sem, *sems
):
    group, padded, lanes = blocks.shape
    rows, hidden = gate_ref.shape
    units, half = hidden // (cubes * group), lanes // 2

    loads = [
        pltpu.make_async_copy(gate_hbm, gate_ref, load_sems.at[0]),
        pltpu.make_async_copy(up_hbm, up_ref, load_sems.at[1]),
    ]
    puts = [
        pltpu.make_async_copy(blocks, blocks_hbm.at[cube], put_sems.at[cube])
        for cube in range(cubes)
    ]

    def cut_blocks():
        for load in loads:
            load.wait()
        spare = jnp.zeros((rows, half - cubes * units), blocks.dtype)
        below = jnp.zeros((padded - rows, lanes), blocks.dtype)
        for member in range(group):
            for base, ref in ((0, gate_ref), (half, up_ref)):
                pieces = [
                    ref[:, (cube * group + member) * units : (cube * group + member + 1) * units]
                    for cube in range(cubes)
                ]
                piece = jnp.concatenate(pieces + [spare], axis=1)
                blocks[member, :rows, base : base + half] = piece
            blocks[member, rows:, :] = below
        for put in puts:
            put.start()

    for load in loads:
        load.start()
    far, others = other_cubes(cubes)
    greet((*plane_places()[:3], *others))
    keep = pltpu.make_async_copy(down_ref, down_out.at[far], own_sem)
    keep.start()
    send = sender(far_send, far_recv)
    copies = [send(k, down_ref, down_out.at[far], place) for k, place in enumerate(others)]
    plane_spread(own_ref, out_ref, *sems, meanwhile=cut_blocks)
    for put in puts:
        put.wait()
    for copy in copies:
        copy.wait_recv()
    for copy in copies:
        copy.wait_send()
    keep.wait()


def z_gather_kernel(planes, padded, count, *refs):
    sources, out_ref, held = refs[:count], refs[count], refs[count + 1 : 2 * count + 1]
    own, load_sems, send_sems, recv_sems, own_sem = refs[2 * count + 1 :]
    loads = [
        pltpu.make_async_copy(source, target, load_sems.at[k])
        for k, (source, target) in enumerate(zip(sources, held))
    ]
    for load in loads:
        load.start()
    for load in loads:
        load.wait()
    query_ref, key_ref, value_ref, output_ref, *gains = held
    rows, columns = query_ref.shape[0], own.shape[1]
    plane, others, _ = other_planes(planes)
    at = 0
    for ref in (query_ref, key_ref, value_ref):
        own[:rows, at : at + ref.shape[1]] = ref[...]
        at += ref.shape[1]
    slots = [
        jnp.concatenate(
            [ref[...].astype(jnp.float32), jnp.zeros((1, GAIN_SLOT - ref.shape[1]), jnp.float32)],
            axis=1,
        )
        for ref in gains
    ]
    slots.append(jnp.zeros((1, columns - len(slots) * GAIN_SLOT), jnp.float32))
    line = jnp.concatenate(slots, axis=1)
    spare = jnp.zeros((padded - rows - 1, columns), jnp.float32)
    own[rows:padded, :] = jnp.concatenate([line, spare], axis=0).astype(own.dtype)
    strips, _ = packed_strips(*output_ref.shape, columns)
    for r, c, to, at, n in strips:
        tiles = output_ref[r : r + TILE_ROWS, c : c + n]
        own[padded + to : padded + to + TILE_ROWS, at : at + n] = tiles
    _, _, to, at, n = strips[-1]
    if at + n < columns:
        rest = jnp.zeros((TILE_ROWS, columns - at - n), own.dtype)
        own[padded + to : padded + to + TILE_ROWS, at + n :] = rest
    greet(others)
    keep = pltpu.make_async_copy(own, out_ref.at[plane], own_sem)
    keep.start()
    send = sender(send_sems, recv_sems)
    copies = [send(k, own, out_ref.at[plane], place) for k, place in enumerate(others)]
    for copy in copies:
        copy.wait_recv()
    for copy in copies:
        copy.wait_send()
    keep.wait()


def gather_sems(count):
    return [
        pltpu.SemaphoreType.DMA((count,)),
        pltpu.SemaphoreType.DMA((count,)),
        pltpu.SemaphoreType.DMA,
    ]


def z_gather(query, key, value, output, gains, planes, padded, collective_id):
    columns = query.shape[1] + key.shape[1] + value.shape[1]
    shape = (padded + packed_strips(*output.shape, columns)[1], columns)
    arrays = [query, key, value, output, *(gain[None] for gain in gains)]
    return pl.pallas_call(
        functools.partial(z_gather_kernel, planes, padded, len(arrays)),
        out_shape=jax.ShapeDtypeStruct((planes, *shape), query.dtype),
        in_specs=[pl.BlockSpec(memory_space=pltpu.HBM)] * len(arrays),
        out_specs=pl.BlockSpec(memory_space=pl.ANY),
        scratch_shapes=[
            *[pltpu.VMEM(array.shape, array.dtype) for array in arrays],
            pltpu.VMEM(shape, query.dtype),
            pltpu.SemaphoreType.DMA((len(arrays),)),
            pltpu.SemaphoreType.DMA((planes - 1,)),
            pltpu.SemaphoreType.DMA((planes - 1,)),
            pltpu.SemaphoreType.DMA,
        ],
        cost_estimate=busy(20),
        compiler_params=pltpu.CompilerParams(
            collective_id=collective_id, has_side_effects=True, vmem_limit_bytes=60 * 2**20
        ),
    )(*arrays)


def weights_gather(local, down, gate, up, block, cubes, collective_id):
    members = 8
    hbm, anywhere = pl.BlockSpec(memory_space=pltpu.HBM), pl.BlockSpec(memory_space=pl.ANY)
    return pl.pallas_call(
        functools.partial(weights_gather_kernel, cubes),
        out_shape=[
            jax.ShapeDtypeStruct((members, *local.shape), local.dtype),
            jax.ShapeDtypeStruct((cubes, *down.shape), down.dtype),
            jax.ShapeDtypeStruct((cubes, *block), gate.dtype),
        ],
        in_specs=[anywhere, hbm, hbm, hbm],
        out_specs=[anywhere, hbm, hbm],
        scratch_shapes=[
            pltpu.VMEM(gate.shape, gate.dtype),
            pltpu.VMEM(up.shape, up.dtype),
            pltpu.VMEM(block, gate.dtype),
            pltpu.SemaphoreType.DMA((2,)),
            pltpu.SemaphoreType.DMA((cubes,)),
            pltpu.SemaphoreType.DMA((cubes - 1,)),
            pltpu.SemaphoreType.DMA((cubes - 1,)),
            pltpu.SemaphoreType.DMA,
            *gather_sems(13),
        ],
        cost_estimate=busy(30),
        compiler_params=pltpu.CompilerParams(
            collective_id=collective_id, has_side_effects=True, vmem_limit_bytes=60 * 2**20
        ),
    )(local, down, gate, up)


def gather_rows(local, collective_id):
    rows, columns = local.shape
    members = 16
    out = pl.pallas_call(
        cube_gather_kernel,
        out_shape=jax.ShapeDtypeStruct((members, rows // 16, 16, columns), local.dtype),
        in_specs=[pl.BlockSpec(memory_space=pl.ANY)],
        out_specs=pl.BlockSpec(memory_space=pl.ANY),
        scratch_shapes=gather_sems(21),
        cost_estimate=busy(35),
        compiler_params=pltpu.CompilerParams(
            collective_id=collective_id, has_side_effects=True, vmem_limit_bytes=VMEM_BYTES
        ),
    )(local.reshape(rows // 16, 16, columns))
    return out.reshape(-1, columns)


def add_rows(target, sources, start, count):
    def one(i, carry):
        total = sources[0][i].astype(jnp.float32)
        for source in sources[1:]:
            total = total + source[i].astype(jnp.float32)
        target[i] = total.astype(target.dtype)
        return carry

    lax.fori_loop(start, start + count, one, 0)


def plane_sum(part_ref, own_sum, near, sums, from_x, from_y, far_x, far_y, send_sems, recv_sems):
    sibling, along_x, along_y, member = plane_places()
    rows = own_sum.shape[0]
    half = rows // 2
    top, bottom = pl.ds(0, half), pl.ds(half, half)
    send = sender(send_sems, recv_sems)
    chips = ((1, 1), (1, 0), (0, 1), (0, 0))
    mine = [part_ref.at[member(at_x, 0, at_y)] for at_x, at_y in chips]
    to_sibling = [
        send(k, part_ref.at[member(at_x, 1, at_y)], near.at[k], sibling)
        for k, (at_x, at_y) in enumerate(chips)
    ]
    to_sibling[0].wait_recv()
    add_rows(sums.at[0], (mine[0], near.at[0]), 0, rows)
    diagonal_x = send(4, sums.at[0, bottom], far_x.at[bottom], along_x)
    diagonal_y = send(5, sums.at[0, top], far_y.at[top], along_y)
    to_sibling[1].wait_recv()
    add_rows(sums.at[1], (mine[1], near.at[1]), half, half)
    direct_x = send(6, sums.at[1, bottom], from_x.at[bottom], along_x)
    to_sibling[2].wait_recv()
    add_rows(sums.at[2], (mine[2], near.at[2]), 0, half)
    direct_y = send(7, sums.at[2, top], from_y.at[top], along_y)
    to_sibling[3].wait_recv()
    diagonal_y.wait_recv()
    add_rows(sums.at[1], (mine[1], near.at[1], far_y), 0, half)
    joint_x = send(8, sums.at[1, top], from_x.at[top], along_x)
    diagonal_x.wait_recv()
    add_rows(sums.at[2], (mine[2], near.at[2], far_x), half, half)
    joint_y = send(9, sums.at[2, bottom], from_y.at[bottom], along_y)
    direct_x.wait_recv()
    direct_y.wait_recv()
    joint_x.wait_recv()
    joint_y.wait_recv()
    add_rows(own_sum, (mine[3], near.at[3], from_x, from_y), 0, rows)
    for copy in (*to_sibling, diagonal_x, diagonal_y, direct_x, direct_y, joint_x, joint_y):
        copy.wait_send()


def cube_sum(
    part_hbm, own_sum, mine, near, via_z, zx_in, zy_in, far_x, far_y, from_x, from_y, from_z, load_sems, send_sems,
    recv_sems, work=lambda point: None,
):
    sibling, along_x, along_y, along_z = cube_places()
    pieces = own_sum.shape[0]
    half = pieces // 2
    top, bottom = pl.ds(0, half), pl.ds(half, half)
    send = sender(send_sems, recv_sems)
    chips = ((1, 1, 1), (1, 1, 0), (1, 0, 1), (0, 1, 0), (0, 0, 1), (0, 1, 1), (1, 0, 0), (0, 0, 0))
    z_diagonal, z_x, z_y, at_x, at_y, diagonal, at_z, here = range(8)
    to_sibling = [
        send(k, part_hbm.at[cube_member(*chip, 1)], near.at[k], sibling)
        for k, chip in enumerate(chips)
    ]
    loads = [
        pltpu.make_async_copy(part_hbm.at[cube_member(*chip, 0)], mine.at[k], load_sems.at[k])
        for k, chip in enumerate(chips)
    ]
    for load in loads:
        load.start()

    def both_in(k):
        to_sibling[k].wait_recv()
        loads[k].wait()

    def add(k, others=(), start=0, count=pieces):
        add_rows(near.at[k], (mine.at[k], near.at[k], *others), start, count)

    work(0)
    both_in(z_diagonal)
    add(z_diagonal)
    diagonal_z = send(8, near.at[z_diagonal], via_z, along_z)
    both_in(z_x)
    add(z_x)
    zx_out = send(9, near.at[z_x], zx_in, along_x)
    both_in(z_y)
    add(z_y)
    zy_out = send(10, near.at[z_y], zy_in, along_y)
    both_in(at_x)
    add(at_x, (), half, half)
    direct_x = send(13, near.at[at_x, bottom], from_x.at[bottom], along_x)
    both_in(at_y)
    add(at_y, (), 0, half)
    direct_y = send(14, near.at[at_y, top], from_y.at[top], along_y)
    both_in(diagonal)
    both_in(at_z)
    work(1)
    diagonal_z.wait_recv()
    add(diagonal, (via_z,))
    diagonal_x = send(11, near.at[diagonal, bottom], far_x.at[bottom], along_x)
    diagonal_y = send(12, near.at[diagonal, top], far_y.at[top], along_y)
    zx_out.wait_recv()
    zy_out.wait_recv()
    add(at_z, (zx_in, zy_in))
    joint_z = send(15, near.at[at_z], from_z, along_z)
    work(2)
    diagonal_y.wait_recv()
    add(at_x, (far_y,), 0, half)
    joint_x = send(16, near.at[at_x, top], from_x.at[top], along_x)
    diagonal_x.wait_recv()
    add(at_y, (far_x,), half, half)
    joint_y = send(17, near.at[at_y, bottom], from_y.at[bottom], along_y)
    both_in(here)
    work(3)
    for copy in (direct_x, direct_y, joint_z, joint_x, joint_y):
        copy.wait_recv()
    add_rows(own_sum, (mine.at[here], near.at[here], from_x, from_y, from_z), 0, pieces)
    for copy in (
        *to_sibling, diagonal_z, zx_out, zy_out, direct_x, direct_y, diagonal_x, diagonal_y, joint_z, joint_x, joint_y,
    ):
        copy.wait_send()


def cube_sum_kernel(part_ref, out_ref, *scratch):
    greet(cube_places())
    cube_sum(part_ref, out_ref, *scratch)


def cube_sum_scratch(shape, dtype):
    return [
        pltpu.VMEM((8, *shape), dtype),
        pltpu.VMEM((8, *shape), dtype),
        *[pltpu.VMEM(shape, dtype)] * 8,
        pltpu.SemaphoreType.DMA((8,)),
        pltpu.SemaphoreType.DMA((18,)),
        pltpu.SemaphoreType.DMA((18,)),
    ]


def plane_sum_scratch(shape, dtype):
    block = pltpu.VMEM(shape, dtype)
    return [
        pltpu.VMEM((4, *shape), dtype),
        pltpu.VMEM((3, *shape), dtype),
        block,
        block,
        block,
        block,
        pltpu.SemaphoreType.DMA((10,)),
        pltpu.SemaphoreType.DMA((10,)),
    ]


def cube_scatter_sum(partial, collective_id):
    shape = partial.shape[1:]
    out = pl.pallas_call(
        cube_sum_kernel,
        out_shape=jax.ShapeDtypeStruct(shape, jnp.float32),
        in_specs=[pl.BlockSpec(memory_space=pl.ANY)],
        out_specs=pl.BlockSpec(memory_space=pltpu.VMEM),
        scratch_shapes=cube_sum_scratch(shape, partial.dtype),
        cost_estimate=busy(35),
        compiler_params=pltpu.CompilerParams(
            collective_id=collective_id, has_side_effects=True, vmem_limit_bytes=VMEM_BYTES
        ),
    )(partial)
    return out.reshape(shape[0] * shape[1], shape[2])


gelu_inner = 0.7978845608028654
gelu_cubic = 0.044715


def pad_rows(target, source):
    rows = source.shape[0]
    target[pl.ds(0, rows)] = source[...]
    if target.shape[0] > rows:
        extra = target.shape[0] - rows
        target[pl.ds(rows, extra)] = jnp.zeros((extra, target.shape[1]), target.dtype)


def ffn_forward_kernel(in_ref, gate_up_ref, down_ref, part_ref, act_ref, to_gate, to_up, down, proj):
    units = act_ref.shape[1]

    @pl.when(pl.program_id(0) == 0)
    def _():
        pad_rows(down, down_ref)

    step = 64
    half_rows = in_ref.shape[0] // 2

    def mid(base):
        for i in range(half_rows // step):
            rows = pl.ds(base + i * step, step)
            gate, up = proj[rows, :units], proj[rows, units:]
            square = gate * gate
            bend = jnp.tanh(gelu_inner * gate * (1.0 + gelu_cubic * square))
            half = 0.5 * (1.0 + bend)
            value = gate * half
            slope = half + 0.5 * gate * (1.0 - bend * bend) * (
                gelu_inner * (1.0 + 3.0 * gelu_cubic * square)
            )
            to_gate[rows, :] = slope * up
            to_up[rows, :] = value
            act_ref[rows, :] = (value * up).astype(act_ref.dtype)

    first, second = pl.ds(0, half_rows), pl.ds(half_rows, half_rows)
    proj[first, :] = matmul(in_ref[first, :], gate_up_ref[...])
    proj[second, :] = matmul(in_ref[second, :], gate_up_ref[...])
    mid(0)
    part_ref[first, :] = matmul(act_ref[first, :], down[...]).astype(part_ref.dtype)
    mid(half_rows)
    part_ref[second, :] = matmul(act_ref[second, :], down[...]).astype(part_ref.dtype)


ROW_BLOCK = 512


def whole(array):
    return pl.BlockSpec(array.shape, lambda i: (0, 0), pipeline_mode=pl.Buffered(1))


def row_block(columns):
    return pl.BlockSpec((ROW_BLOCK, columns), lambda i: (i, 0))


def ffn_forward(rows_in, gate_up, down):
    rows, depth = rows_in.shape
    units, columns = gate_up.shape[1] // 2, down.shape[1]
    low = rows_in.dtype
    return pl.pallas_call(
        ffn_forward_kernel,
        grid=(rows // ROW_BLOCK,),
        in_specs=[row_block(depth), whole(gate_up), whole(down)],
        out_specs=[row_block(columns), row_block(units), row_block(units), row_block(units)],
        out_shape=[
            jax.ShapeDtypeStruct((rows, columns), low),
            jax.ShapeDtypeStruct((rows, units), low),
            jax.ShapeDtypeStruct((rows, units), jnp.float32),
            jax.ShapeDtypeStruct((rows, units), jnp.float32),
        ],
        scratch_shapes=[
            pltpu.VMEM((units, columns), low),
            pltpu.VMEM((ROW_BLOCK, 2 * units), jnp.float32),
        ],
        cost_estimate=busy(20),
        compiler_params=pltpu.CompilerParams(vmem_limit_bytes=VMEM_BYTES),
    )(rows_in, gate_up, down)


def block_order(rows):
    order = [cube_member(*flips) for flips in CUBE_ORDER]
    return order, [pl.ds(pl.multiple_of(block * rows, rows), rows) for block in order]


def gather_backward_kernel(
    own_ref, down_ref, gate_up_ref, to_gate_hbm, to_up_hbm, act_hbm, both_hbm, part_hbm, down_grad_ref,
    grad, down, to_gate, to_up, act, both, part, act_sem, load_sems, put_sems, send_sems, recv_sems, local_sem,
):
    units = down.shape[0]
    pieces, piece, columns = own_ref.shape
    rows = pieces * piece
    order, places = block_order(rows)

    def loads(i):
        slot, at = i % 2, places[i]
        return (
            pltpu.make_async_copy(to_gate_hbm.at[at], to_gate.at[slot], load_sems.at[0, slot]),
            pltpu.make_async_copy(to_up_hbm.at[at], to_up.at[slot], load_sems.at[1, slot]),
        )

    def puts(i):
        slot = i % 2
        return (
            pltpu.make_async_copy(both.at[slot], both_hbm.at[places[i]], put_sems.at[0, slot]),
            pltpu.make_async_copy(part.at[slot], part_hbm.at[order[i]], put_sems.at[1, slot]),
        )

    def compute(i):
        if i + 1 < len(order):
            for load in loads(i + 1):
                load.start()
        for load in loads(i):
            load.wait()
        if i >= 2:
            for put in puts(i - 2):
                put.wait()
        slot = i % 2
        source = own_ref if i == 0 else grad.at[order[i]]
        act_grad = contract_cols(source[...].reshape(rows, columns), down[...])
        both[slot, :, :units] = (act_grad * to_gate[slot]).astype(both.dtype)
        both[slot, :, units:] = (act_grad * to_up[slot]).astype(both.dtype)
        result = contract_cols(both[slot], gate_up_ref[...]).astype(part.dtype)
        part[slot] = result.reshape(pieces, piece, result.shape[1])
        for put in puts(i):
            put.start()

    act_load = pltpu.make_async_copy(act_hbm, act, act_sem)
    act_load.start()
    for load in loads(0):
        load.start()
    pad_rows(down, down_ref)
    greet(cube_places())
    cube_spread(own_ref, grad, send_sems, recv_sems, local_sem, compute)
    act_load.wait()
    whole = grad[...].reshape(len(order) * rows, columns)
    down_grad = contract_rows(act[...], whole)
    down_grad_ref[...] = down_grad[: down_ref.shape[0]].astype(down_grad_ref.dtype)
    for i in (len(order) - 2, len(order) - 1):
        for put in puts(i):
            put.wait()


def gather_backward(own, down, gate_up, to_gate, to_up, act, collective_id):
    rows, columns = own.shape
    members, piece = 16, 16
    pieces = rows // piece
    depth, units = gate_up.shape[0], to_gate.shape[1]
    low, wide = own.dtype, jnp.float32
    shape = jax.ShapeDtypeStruct
    vmem, anywhere = pl.BlockSpec(memory_space=pltpu.VMEM), pl.BlockSpec(memory_space=pl.ANY)
    return pl.pallas_call(
        gather_backward_kernel,
        out_shape=[
            shape((members * rows, 2 * units), low),
            shape((members, pieces, piece, depth), low),
            shape(down.shape, low),
        ],
        in_specs=[vmem, vmem, vmem, anywhere, anywhere, anywhere],
        out_specs=[anywhere, anywhere, vmem],
        scratch_shapes=[
            pltpu.VMEM((members, pieces, piece, columns), low),
            pltpu.VMEM((units, columns), low),
            pltpu.VMEM((2, rows, units), wide),
            pltpu.VMEM((2, rows, units), wide),
            pltpu.VMEM(act.shape, low),
            pltpu.VMEM((2, rows, 2 * units), low),
            pltpu.VMEM((2, pieces, piece, depth), low),
            pltpu.SemaphoreType.DMA,
            pltpu.SemaphoreType.DMA((2, 2)),
            pltpu.SemaphoreType.DMA((2, 2)),
            *gather_sems(21),
        ],
        cost_estimate=busy(45),
        compiler_params=pltpu.CompilerParams(
            collective_id=collective_id, has_side_effects=True, vmem_limit_bytes=60 * 2**20
        ),
    )(own.reshape(pieces, piece, columns), down, gate_up, to_gate, to_up, act)


def sum_gradients_kernel(
    part_ref, down_ref, in_hbm, both_hbm, sum_ref, gate_up_ref, down_sum_ref,
    columns_in, both, arriving, both_sem, in_sems, far_send, far_recv, *scratch,
):
    cubes = down_ref.shape[0]
    far, others = other_cubes(cubes)
    step = columns_in.shape[2]
    blocks = gate_up_ref.shape[0] // step

    def load(i):
        at = pl.ds(i * step, step)
        return pltpu.make_async_copy(in_hbm.at[:, at], columns_in.at[i % 2], in_sems.at[i % 2])

    both_load = pltpu.make_async_copy(both_hbm, both, both_sem)
    both_load.start()
    load(0).start()

    def rows_of(i):
        if i == 0:
            both_load.wait()
        if i + 1 < blocks:
            load(i + 1).start()
        load(i).wait()
        rows = contract_rows(columns_in[i % 2], both[...])
        gate_up_ref[pl.ds(i * step, step), :] = rows.astype(gate_up_ref.dtype)

    def work(point):
        spread = ((), (0, 1), (2, 3), tuple(range(4, blocks)))
        for i in spread[point]:
            rows_of(i)

    greet((*cube_places(), *others))
    send = sender(far_send, far_recv)
    copies = [
        send(k, down_ref.at[place[0]], arriving.at[k], place) for k, place in enumerate(others)
    ]
    cube_sum(part_ref, sum_ref, *scratch, work=work)
    down_sum = down_ref[far].astype(jnp.float32)
    for k, copy in enumerate(copies):
        copy.wait_recv()
        down_sum = down_sum + arriving[k].astype(jnp.float32)
    down_sum_ref[...] = down_sum
    for copy in copies:
        copy.wait_send()


def sum_gradients(part, down, rows_in, both, collective_id):
    members, pieces, piece, depth = part.shape
    low = part.dtype
    step = 256
    vmem, anywhere = pl.BlockSpec(memory_space=pltpu.VMEM), pl.BlockSpec(memory_space=pl.ANY)
    total, gate_up, down_sum = pl.pallas_call(
        sum_gradients_kernel,
        out_shape=[
            jax.ShapeDtypeStruct((pieces, piece, depth), jnp.float32),
            jax.ShapeDtypeStruct((depth, both.shape[1]), low),
            jax.ShapeDtypeStruct(down.shape[1:], jnp.float32),
        ],
        in_specs=[anywhere, vmem, anywhere, anywhere],
        out_specs=[vmem, vmem, vmem],
        scratch_shapes=[
            pltpu.VMEM((2, rows_in.shape[0], step), low),
            pltpu.VMEM(both.shape, low),
            pltpu.VMEM((down.shape[0] - 1, *down.shape[1:]), low),
            pltpu.SemaphoreType.DMA,
            pltpu.SemaphoreType.DMA((2,)),
            pltpu.SemaphoreType.DMA((down.shape[0] - 1,)),
            pltpu.SemaphoreType.DMA((down.shape[0] - 1,)),
            *cube_sum_scratch((pieces, piece, depth), low),
        ],
        cost_estimate=busy(35),
        compiler_params=pltpu.CompilerParams(
            collective_id=collective_id, has_side_effects=True, vmem_limit_bytes=60 * 2**20
        ),
    )(part, down, rows_in, both)
    return total.reshape(pieces * piece, depth), gate_up, down_sum


def unit_sum_kernel(terms_ref, gate_ref, up_ref):
    cubes, group, _, lanes = terms_ref.shape
    rows, hidden = gate_ref.shape
    units, half = hidden // (cubes * group), lanes // 2
    for member in range(group):
        total = terms_ref[0, member].astype(jnp.float32)
        for cube in range(1, cubes):
            total = total + terms_ref[cube, member].astype(jnp.float32)
        for cube in range(cubes):
            at = (cube * group + member) * units
            gate_ref[:, at : at + units] = total[:rows, cube * units : (cube + 1) * units]
            up_ref[:, at : at + units] = total[
                :rows, half + cube * units : half + (cube + 1) * units
            ]


def unit_sum(terms, rows, hidden):
    vmem = pl.BlockSpec(memory_space=pltpu.VMEM)
    return pl.pallas_call(
        unit_sum_kernel,
        out_shape=[jax.ShapeDtypeStruct((rows, hidden), jnp.float32)] * 2,
        in_specs=[vmem],
        out_specs=[vmem, vmem],
        cost_estimate=busy(5),
        compiler_params=pltpu.CompilerParams(vmem_limit_bytes=VMEM_BYTES),
    )(terms)


def owner_sum_kernel(planes, part_ref, out_ref, own_sum, leaving, arriving, z_send, z_recv, *scratch):
    plane, others, ring = other_planes(planes)
    greet((*plane_places()[:3], *others))
    plane_sum(part_ref, own_sum, *scratch)
    send = sender(z_send, z_recv)

    def narrow(i, carry):
        leaving[i] = own_sum[i].astype(leaving.dtype)
        return carry

    lax.fori_loop(0, planes, narrow, 0)
    copies = [
        send(k, leaving.at[ring[k]], arriving.at[k], place) for k, place in enumerate(others)
    ]
    for copy in copies:
        copy.wait_recv()

    value = own_sum[plane]
    for k in range(planes - 1):
        value = value + arriving[k].astype(jnp.float32)
    out_ref[...] = value
    for copy in copies:
        copy.wait_send()


def owner_sum(blocks, collective_id):
    members, planes, rows, columns = blocks.shape
    return pl.pallas_call(
        functools.partial(owner_sum_kernel, planes),
        out_shape=jax.ShapeDtypeStruct((rows, columns), jnp.float32),
        in_specs=[pl.BlockSpec(memory_space=pltpu.VMEM)],
        out_specs=pl.BlockSpec(memory_space=pltpu.VMEM),
        scratch_shapes=[
            pltpu.VMEM((planes, rows, columns), jnp.float32),
            pltpu.VMEM((planes, rows, columns), blocks.dtype),
            pltpu.VMEM((planes - 1, rows, columns), blocks.dtype),
            pltpu.SemaphoreType.DMA((planes - 1,)),
            pltpu.SemaphoreType.DMA((planes - 1,)),
            *plane_sum_scratch((planes, rows, columns), blocks.dtype),
        ],
        cost_estimate=busy(35),
        compiler_params=pltpu.CompilerParams(
            collective_id=collective_id, has_side_effects=True, vmem_limit_bytes=VMEM_BYTES
        ),
    )(blocks)


GAIN_SLOT = 128
TILE_ROWS, TILE_LANES = 8, 128


def packed_strips(rows, width, columns):
    across, into = width // TILE_LANES, columns // TILE_LANES
    strips, tile, tiles = [], 0, rows // TILE_ROWS * across
    while tile < tiles:
        run = min(across - tile % across, into - tile % into)
        strips.append(
            (
                tile // across * TILE_ROWS,
                tile % across * TILE_LANES,
                tile // into * TILE_ROWS,
                tile % into * TILE_LANES,
                run * TILE_LANES,
            )
        )
        tile += run
    return strips, up_to(tiles, into) // into * TILE_ROWS


def unpack_tiles(array, rows, width):
    strips, _ = packed_strips(rows, width, array.shape[1])
    lines = []
    for row in range(0, rows, TILE_ROWS):
        parts = [
            array[to : to + TILE_ROWS, at : at + n] for r, _, to, at, n in strips if r == row
        ]
        lines.append(jnp.concatenate(parts, axis=1))
    return jnp.concatenate(lines, axis=0)


def gain_places(blocks, planes, count):
    lane = lax.broadcasted_iota(jnp.int32, (GAIN_SLOT, blocks * count), 0)
    inner = lax.broadcasted_iota(jnp.int32, (GAIN_SLOT, blocks * count), 1) % count
    places = (lane == inner).astype(jnp.float32).astype(jnp.bfloat16)
    listed = lax.broadcasted_iota(jnp.int32, (blocks, blocks * count), 0)
    block = lax.broadcasted_iota(jnp.int32, (blocks, blocks * count), 1) // count
    members = blocks // planes
    block = block % members * planes + block // members
    return places, listed == block


def spread_gain(rows, planes, count):
    places, chosen = gain_places(rows.shape[0], planes, count)
    return jnp.sum(jnp.where(chosen, matmul(rows, places), 0.0), axis=0, keepdims=True)


def collect_gain(vector, blocks, planes, count):
    places, chosen = gain_places(blocks, planes, count)
    return contract_cols(jnp.where(chosen, vector, 0.0).astype(jnp.bfloat16), places)


def inverse_of(values, count):
    return lax.rsqrt(jnp.sum(values * values, axis=-1, keepdims=True) / count + epsilon)


def back_of(grad_normed, normed, inverse, count):
    inner = jnp.sum(grad_normed * normed, axis=-1, keepdims=True) / count
    return inverse * (grad_normed - normed * inner)


def turn(values, cos_table, sin_table):
    half = values.shape[1] // 2
    first, second = values[:, :half], values[:, half:]
    return first * cos_table - second * sin_table, second * cos_table + first * sin_table


def attention_forward_kernel(
    gain_widths, width_rows, padded, row_ref, hidden_ref, packed_ref, cos_ref, sin_ref, segment_column, segment_row, placing_ref,
    placed_ref, middle_ref, raw_ref, mix_ref, probs_ref, query_ref, key_ref, value_ref, query_raw_ref,
    key_raw_ref, qkv_ref, output_ref, input_scale, query_scale, key_scale, attnout_scale, ffnin_scale, ffnout_scale,
    gain_rows,
):
    bf16, f32 = jnp.bfloat16, jnp.float32
    members, planes, piece, _ = packed_ref.shape
    blocks = members * planes
    width = hidden_ref.shape[1]
    mix_rows = output_ref.shape[0] // blocks
    strips, _ = packed_strips(mix_rows, width, packed_ref.shape[3])
    local_rows, full_rows = hidden_ref.shape[0], row_ref.shape[0]
    head = key_ref.shape[1]
    heads = query_ref.shape[1] // head
    offset = pl.multiple_of(lax.axis_index("seq") * local_rows, local_rows)
    mine = pl.ds(offset, local_rows)
    for i in range(blocks):
        member, plane = i // planes, i % planes
        block = packed_ref[member, plane]
        natural = width_rows * (plane * members + member)
        qkv_ref[natural : natural + width_rows, :] = block[:width_rows]
        natural = mix_rows * (plane * members + member)
        for r, c, to, at, n in strips:
            tiles = block[padded + to : padded + to + TILE_ROWS, at : at + n]
            output_ref[natural + r : natural + r + TILE_ROWS, c : c + n] = tiles
        gain_rows[i : i + 1, :] = block[width_rows : width_rows + 1, : gain_rows.shape[1]].astype(f32)
    targets = (input_scale, query_scale, key_scale, attnout_scale, ffnin_scale, ffnout_scale)
    for k, (target, count) in enumerate(zip(targets, gain_widths)):
        rows = gain_rows[:, k * GAIN_SLOT : (k + 1) * GAIN_SLOT].astype(bf16)
        target[...] = spread_gain(rows, planes, count)

    row = row_ref[...].astype(f32)
    normed = (row * inverse_of(row, width) * input_scale[...]).astype(bf16)
    key_value = matmul(normed, qkv_ref[:, heads * head :])
    key_raw = key_value[:, :head]
    value_ref[...] = key_value[:, head:].astype(bf16)
    half = head // 2
    turned = turn(key_raw * inverse_of(key_raw, head) * key_scale[...], cos_ref[...], sin_ref[...])
    key_ref[:, :half], key_ref[:, half:] = turned[0].astype(bf16), turned[1].astype(bf16)

    row = row_ref[mine, :].astype(f32)
    normed = (row * inverse_of(row, width) * input_scale[...]).astype(bf16)
    own = matmul(normed, qkv_ref[:, : (heads + 1) * head])
    query_raw_ref[...] = own[:, : heads * head]
    key_raw_ref[...] = own[:, heads * head :]
    cos_table, sin_table = cos_ref[mine, :], sin_ref[mine, :]
    places = offset + lax.broadcasted_iota(jnp.int32, (local_rows, full_rows), 0)
    earlier = places >= lax.broadcasted_iota(jnp.int32, (local_rows, full_rows), 1)
    allowed = (segment_column[...] == segment_row[...]) & earlier
    for h in range(heads):
        at = h * head
        query_raw = query_raw_ref[:, at : at + head]
        turned = turn(
            query_raw * inverse_of(query_raw, head) * query_scale[...], cos_table, sin_table
        )
        scale = head ** (-0.5)
        query_ref[:, at : at + half] = (turned[0] * scale).astype(bf16)
        query_ref[:, at + half : at + head] = (turned[1] * scale).astype(bf16)
        scores = contract_cols(query_ref[:, at : at + head], key_ref[...])
        scores = jnp.where(allowed, scores, masked_score)
        weights = jnp.exp(scores - jnp.max(scores, axis=-1, keepdims=True))
        probs = weights / jnp.sum(weights, axis=-1, keepdims=True)
        probs_ref[h] = probs
        mix_ref[:, at : at + head] = matmul(probs.astype(bf16), value_ref[...]).astype(bf16)
    attn_raw = matmul(mix_ref[...], output_ref[...])
    raw_ref[...] = attn_raw
    middle = hidden_ref[...].astype(f32) + attn_raw * inverse_of(attn_raw, width) * attnout_scale[...]
    middle_ref[...] = middle
    ffn_in = (middle * inverse_of(middle, width) * ffnin_scale[...]).astype(bf16)
    placed_ref[...] = matmul(ffn_in, placing_ref[...]).astype(bf16)


def attention_forward(
    row_tokens, hidden, packed, cos_full, sin_full, segment_column, segment_row, placing, gain_widths, width_rows, padded,
    head_width,
):
    bf16, f32 = jnp.bfloat16, jnp.float32
    members, planes, piece, qkv_width = packed.shape
    blocks = members * planes
    local_rows, width = hidden.shape
    query_width = qkv_width - 2 * head_width
    heads = query_width // head_width
    full_rows = row_tokens.shape[0]
    depth = blocks * padded
    shape = jax.ShapeDtypeStruct
    vmem = pl.BlockSpec(memory_space=pltpu.VMEM)
    out_shape = [
        shape((local_rows, depth), bf16),
        shape((local_rows, width), f32),
        shape((local_rows, width), f32),
        shape((local_rows, query_width), bf16),
        shape((heads, local_rows, full_rows), f32),
        shape((local_rows, query_width), bf16),
        shape((full_rows, head_width), bf16),
        shape((full_rows, head_width), bf16),
        shape((local_rows, query_width), f32),
        shape((local_rows, head_width), f32),
        shape((width, qkv_width), bf16),
        shape((query_width, width), bf16),
        shape((1, width), f32),
        shape((1, head_width), f32),
        shape((1, head_width), f32),
        shape((1, width), f32),
        shape((1, width), f32),
        shape((1, width), f32),
    ]
    return pl.pallas_call(
        functools.partial(attention_forward_kernel, gain_widths, width_rows, padded),
        out_shape=out_shape,
        in_specs=[vmem] * 8,
        out_specs=[vmem] * len(out_shape),
        scratch_shapes=[pltpu.VMEM((blocks, len(gain_widths) * GAIN_SLOT), f32)],
        cost_estimate=busy(20),
        compiler_params=pltpu.CompilerParams(vmem_limit_bytes=60 * 2**20),
    )(row_tokens, hidden, packed, cos_full, sin_full, segment_column, segment_row, placing)


def attention_backward_kernel(
    gain_widths, width_rows, planes, padded, grad_ref, incoming_ref, middle_ref, raw_ref, mix_ref, probs_ref, query_ref, key_ref,
    value_ref, query_raw_ref, key_raw_ref, row_ref, qkv_ref, output_ref, cos_ref, sin_ref, input_scale,
    query_scale, key_scale, attnout_scale, ffnin_scale, ffnout_grad, by_device,
    input_grad_ref, blocks_ref, key_value, query_grad, low_ref, leaving, arriving, send_sem, recv_sem,
):
    bf16, f32 = jnp.bfloat16, jnp.float32
    members = blocks_ref.shape[0]
    blocks = members * planes
    mix_rows = output_ref.shape[0] // blocks
    local_rows, width = incoming_ref.shape
    strips, _ = packed_strips(mix_rows, width, blocks_ref.shape[3])
    head = key_ref.shape[1]
    heads = query_ref.shape[1] // head
    half = head // 2
    seq = lax.axis_index("seq")
    mine = pl.ds(pl.multiple_of(seq * local_rows, local_rows), local_rows)
    theirs = pl.ds(pl.multiple_of((1 - seq) * local_rows, local_rows), local_rows)
    partner = plane_places()[2]
    greet((partner,))

    ffn_in_grad = take_back(grad_ref[...], by_device[...])
    middle = middle_ref[...]
    inverse = inverse_of(middle, width)
    normed = middle * inverse
    ffnin_grad = jnp.sum(ffn_in_grad * normed, axis=0, keepdims=True)
    middle_grad = incoming_ref[...].astype(f32) + back_of(
        ffn_in_grad * ffnin_scale[...], normed, inverse, width
    )
    input_grad_ref[...] = middle_grad
    raw = raw_ref[...]
    inverse = inverse_of(raw, width)
    normed = raw * inverse
    attnout_grad = jnp.sum(middle_grad * normed, axis=0, keepdims=True)
    raw_grad = back_of(middle_grad * attnout_scale[...], normed, inverse, width).astype(bf16)
    mix_grad = contract_cols(raw_grad, output_ref[...]).astype(bf16)
    for h in range(heads):
        at = h * head
        grad = mix_grad[:, at : at + head]
        probs = probs_ref[h]
        prob_grad = contract_cols(grad, value_ref[...])
        delta = jnp.sum(prob_grad * probs, axis=-1, keepdims=True)
        score_grad = (probs * (prob_grad - delta)).astype(bf16)
        to_keys = contract_rows(score_grad, query_ref[:, at : at + head])
        to_values = contract_rows(probs.astype(bf16), grad)
        if h == 0:
            key_value[:, :head], key_value[:, head:] = to_keys, to_values
        else:
            key_value[:, :head] += to_keys
            key_value[:, head:] += to_values
        query_grad[:, at : at + head] = matmul(score_grad, key_ref[...])
    leaving[...] = key_value[theirs, :].astype(bf16)
    copy = sender(send_sem, recv_sem)(0, leaving, arriving, partner)

    output_grad = contract_rows(mix_ref[...], raw_grad).astype(bf16)
    cos_table, sin_table = cos_ref[mine, :], sin_ref[mine, :]

    def head_back(grad, raw, scale_ref):
        turned = jnp.concatenate(turn(grad, cos_table, -sin_table), axis=1)
        inverse = inverse_of(raw, head)
        normed = raw * inverse
        gain = jnp.sum(turned * normed, axis=0, keepdims=True)
        return back_of(turned * scale_ref[...], normed, inverse, head).astype(bf16), gain

    query_gain = jnp.zeros((1, head), f32)
    for h in range(heads):
        at = h * head
        low, gain = head_back(
            query_grad[:, at : at + head] * head ** (-0.5),
            query_raw_ref[:, at : at + head],
            query_scale,
        )
        low_ref[:, at : at + head] = low
        query_gain = query_gain + gain
    copy.wait_recv()
    total = key_value[mine, :] + arriving[...].astype(f32)
    low, key_gain = head_back(total[:, :head], key_raw_ref[...], key_scale)
    low_ref[:, heads * head : (heads + 1) * head] = low
    low_ref[:, (heads + 1) * head :] = total[:, head:].astype(bf16)

    row = row_ref[mine, :].astype(f32)
    inverse = inverse_of(row, width)
    normed = row * inverse
    normed_grad = contract_cols(low_ref[...], qkv_ref[...])
    input_gain = jnp.sum(normed_grad * normed, axis=0, keepdims=True)
    input_grad_ref[...] += back_of(normed_grad * input_scale[...], normed, inverse, width)
    vectors = (input_gain, query_gain, key_gain, attnout_grad, ffnin_grad, ffnout_grad[...])
    gains = jnp.concatenate(
        [
            collect_gain(vector, blocks, planes, count)
            for vector, count in zip(vectors, gain_widths)
        ],
        axis=1,
    )
    columns = blocks_ref.shape[3]
    gains = jnp.concatenate([gains, jnp.zeros((blocks, columns - gains.shape[1]), f32)], axis=1)
    spare = jnp.zeros((padded - width_rows - 1, columns), f32)
    normed = (normed * input_scale[...]).astype(bf16)
    weights = contract_rows(normed, low_ref[...])
    for i in range(blocks):
        member, plane = i // planes, i % planes
        natural = width_rows * (plane * members + member)
        piece = weights[natural : natural + width_rows]
        block = jnp.concatenate([piece, gains[i : i + 1], spare], axis=0)
        blocks_ref[member, plane, :padded, :] = block.astype(bf16)
        natural = mix_rows * (plane * members + member)
        for r, c, to, at, n in strips:
            tiles = output_grad[natural + r : natural + r + TILE_ROWS, c : c + n]
            blocks_ref[member, plane, padded + to : padded + to + TILE_ROWS, at : at + n] = tiles
        _, _, to, at, n = strips[-1]
        if at + n < columns:
            rest = jnp.zeros((TILE_ROWS, columns - at - n), bf16)
            blocks_ref[member, plane, padded + to : padded + to + TILE_ROWS, at + n :] = rest
    copy.wait_send()


def attention_backward(arrays, gain_widths, width_rows, planes, padded, mix_rows, collective_id):
    bf16, f32 = jnp.bfloat16, jnp.float32
    grad, incoming, query, key, qkv = arrays[0], arrays[1], arrays[6], arrays[7], arrays[12]
    local_rows, width = incoming.shape
    members = 8
    _, packed_rows = packed_strips(mix_rows, width, qkv.shape[1])
    pair = pltpu.VMEM((local_rows, 2 * key.shape[1]), bf16)
    shape = jax.ShapeDtypeStruct
    vmem = pl.BlockSpec(memory_space=pltpu.VMEM)
    return pl.pallas_call(
        functools.partial(attention_backward_kernel, gain_widths, width_rows, planes, padded),
        out_shape=[
            shape((local_rows, width), f32),
            shape((members, planes, padded + packed_rows, qkv.shape[1]), bf16),
        ],
        in_specs=[vmem] * len(arrays),
        out_specs=[vmem] * 2,
        scratch_shapes=[
            pltpu.VMEM((key.shape[0], 2 * key.shape[1]), f32),
            pltpu.VMEM(query.shape, f32),
            pltpu.VMEM((local_rows, qkv.shape[1]), bf16),
            pair,
            pair,
            pltpu.SemaphoreType.DMA((1,)),
            pltpu.SemaphoreType.DMA((1,)),
        ],
        cost_estimate=busy(30),
        compiler_params=pltpu.CompilerParams(
            collective_id=collective_id, has_side_effects=True, vmem_limit_bytes=60 * 2**20
        ),
    )(*arrays)


def body(
    tokens,
    segment_ids,
    cotangent,
    query_weight,
    key_weight,
    value_weight,
    output_weight,
    gate_weight,
    up_weight,
    down_weight,
    input_gain,
    query_gain,
    key_gain,
    attnout_gain,
    ffnin_gain,
    ffnout_gain,
):
    bf16, f32 = jnp.bfloat16, jnp.float32
    devices = lax.axis_size(ALL)
    members = lax.axis_size(PLANE)
    planes = lax.axis_size(PLANES)
    cubes = lax.axis_size("far")
    group = lax.axis_size(CUBE)
    width_rows = query_weight.shape[0]
    hidden_rows = down_weight.shape[0]
    head_width = key_weight.shape[1]
    query_width = query_weight.shape[1]
    head_count = query_width // head_width
    qkv_width = query_width + 2 * head_width
    mix_rows = output_weight.shape[0]
    padded = up_to(width_rows + 1, 8)
    width = devices * width_rows
    unit_count = cubes * hidden_rows
    unit_pad = up_to(unit_count, 128)
    by_device = place_columns(devices, width_rows, padded)

    gains = (input_gain, query_gain, key_gain, attnout_gain, ffnin_gain, ffnout_gain)
    gain_widths = [g.shape[0] for g in gains]
    packed_all = z_gather(
        query_weight, key_weight, value_weight, output_weight, gains, planes, padded, 0
    )
    other_tokens = lax.ppermute(tokens[0], "seq", [(0, 1), (1, 0)])
    packed_all, other_tokens = lax.optimization_barrier((packed_all, other_tokens))
    packed_all, down_full, gate_up = weights_gather(
        packed_all, down_weight, gate_weight, up_weight, (group, padded, 2 * unit_pad), cubes, 6
    )
    down_full = down_full.reshape(unit_count, down_weight.shape[1])
    gate_up, packed_all = lax.optimization_barrier((gate_up, packed_all))
    gate_up = gate_up.reshape(devices, padded, 2 * unit_pad)
    gate_up_full = exchange(gate_up, ALL).reshape(devices * padded, 2 * unit_pad)
    incoming = cotangent[0].astype(f32)
    local_rows = tokens.shape[1]
    offset = lax.axis_index("seq") * local_rows
    segment_row = segment_ids[0]

    def mine(rows):
        return lax.dynamic_slice_in_dim(rows, offset, local_rows)

    cos_full, sin_full = rope_tables(doc_positions(segment_row), head_width)

    first = lax.axis_index("seq") == 0
    row_tokens = jnp.concatenate(
        [
            jnp.where(first, tokens[0], other_tokens),
            jnp.where(first, other_tokens, tokens[0]),
        ]
    )
    (
        ffn_in_placed,
        middle,
        attn_raw,
        attn_flat,
        probs,
        queries,
        key_rows,
        value_rows,
        query_raw,
        key_raw,
        qkv_full,
        output_full,
        *scales,
    ) = attention_forward(
        row_tokens,
        tokens[0],
        packed_all,
        cos_full,
        sin_full,
        mine(segment_row)[:, None],
        segment_row[None],
        by_device,
        gain_widths,
        width_rows,
        padded,
        head_width,
    )
    ffnout_scale = scales.pop()

    cube_in = gather_rows(ffn_in_placed, 1)
    ffn_part, activated_low, to_gate, to_up = ffn_forward(cube_in, gate_up_full, down_full)
    ffn_part = ffn_part.reshape(group, local_rows // 16, 16, ffn_part.shape[1])
    ffn_raw = cube_scatter_sum(ffn_part, 2)
    inv_ffn = inverse_rms(ffn_raw)
    norm_ffn = ffn_raw * inv_ffn
    result = middle + norm_ffn * ffnout_scale
    ffnout_gain_grad = jnp.sum(incoming * norm_ffn, axis=0)
    ffn_raw_grad = rms_back(incoming * ffnout_scale, norm_ffn, inv_ffn).astype(bf16)

    gate_up_low, ffn_in_part, down_blocks = gather_backward(
        ffn_raw_grad, down_full, gate_up_full, to_gate, to_up, activated_low, 3
    )
    down_blocks = down_blocks.reshape(cubes, hidden_rows, down_weight.shape[1])
    ffn_in_grad, gate_up_blocks, down_wgrad = sum_gradients(
        ffn_in_part, down_blocks, cube_in, gate_up_low, 4
    )
    gate_up_terms = exchange(gate_up_blocks.reshape(devices, padded, 2 * unit_pad), ALL)
    input_grad, blocks = attention_backward(
        [
            ffn_in_grad,
            cotangent[0],
            middle,
            attn_raw,
            attn_flat,
            probs,
            queries,
            key_rows,
            value_rows,
            query_raw,
            key_raw,
            row_tokens,
            qkv_full,
            output_full,
            cos_full,
            sin_full,
            *scales,
            ffnout_gain_grad[None],
            by_device,
        ],
        gain_widths,
        width_rows,
        planes,
        padded,
        mix_rows,
        7,
    )
    share = owner_sum(blocks, 5)
    gate_wgrad, up_wgrad = unit_sum(
        gate_up_terms.reshape(cubes, group, padded, 2 * unit_pad), width_rows, gate_weight.shape[1]
    )
    qkv_share, output_share = share[:padded], unpack_tiles(share[padded:], *output_weight.shape)
    gain_shares = [
        qkv_share[width_rows, k * GAIN_SLOT : k * GAIN_SLOT + count]
        for k, count in enumerate(gain_widths)
    ]
    return (
        result.astype(bf16)[None],
        input_grad[None],
        qkv_share[:width_rows, :query_width],
        qkv_share[:width_rows, query_width : query_width + head_width],
        qkv_share[:width_rows, query_width + head_width :],
        output_share,
        gate_wgrad,
        up_wgrad,
        down_wgrad,
        *gain_shares,
    )


def solution(mesh):
    dp, seq = mesh.shape["dp"], mesh.shape["seq"]
    split = Mesh(mesh.devices.reshape(dp // 8, 2, 2, 2, seq), ALL)
    rows = P(("far", "z", "x", "core"), "seq", None)
    matrix, vector = P(ALL, None), P(ALL)
    return jax.shard_map(
        body,
        mesh=split,
        in_specs=(rows, P(("far", "z", "x", "core"), None), rows) + (matrix,) * 7 + (vector,) * 6,
        out_specs=(rows, rows) + (matrix,) * 7 + (vector,) * 6,
        check_vma=False,
    )
```

```python
import functools

import jax
import jax.numpy as jnp
import numpy as np
from jax import lax
from jax.experimental import pallas as pl
from jax.experimental.pallas import tpu as pltpu
from jax.sharding import Mesh
from jax.sharding import PartitionSpec as P

epsilon = 1e-06
rope_base = 1000000.0
masked_score = -1e30


def inverse_rms(values):
    return lax.rsqrt(jnp.mean(values * values, axis=-1, keepdims=True) + epsilon)


def rms_back(grad_normed, normed, inverse):
    return inverse * (grad_normed - normed * jnp.mean(grad_normed * normed, axis=-1, keepdims=True))


def doc_positions(segments):
    length = segments.shape[0]
    smaller = segments[None, :] < segments[:, None]
    starts = jnp.sum(smaller.astype(jnp.int32), axis=1)
    return (jnp.arange(length, dtype=jnp.int32) - starts).astype(jnp.float32)


def rope_tables(positions, head_width):
    half_width = head_width // 2
    frequency = rope_base ** (-(2.0 / head_width) * jnp.arange(half_width, dtype=jnp.float32))
    angles = positions[..., None] * frequency
    return (jnp.cos(angles), jnp.sin(angles))


def matmul(left, right):
    return jnp.dot(left, right, preferred_element_type=jnp.float32)


def contract_rows(left, right):
    return lax.dot_general(
        left, right, (((0,), (0,)), ((), ())), preferred_element_type=jnp.float32
    )


def contract_cols(left, right):
    return lax.dot_general(
        left, right, (((1,), (1,)), ((), ())), preferred_element_type=jnp.float32
    )


ALL = ("far", "z", "x", "core", "seq")
PLANES = ("far", "z")
CUBE = ("z", "x", "core", "seq")


def up_to(size, multiple):
    return (size + multiple - 1) // multiple * multiple


def place_columns(blocks, rows, padded):
    source = np.arange(blocks * rows)
    block, inner = source // rows, source % rows
    placing = np.zeros((blocks * rows, blocks * padded), np.float32)
    placing[source, block * padded + inner] = 1.0
    return jnp.asarray(placing.astype(jnp.bfloat16))


def take_back(padded_values, placing):
    high = lax.reduce_precision(padded_values, 8, 7)
    terms = jnp.concatenate([high, padded_values - high], axis=0).astype(jnp.bfloat16)
    both = contract_cols(terms, placing)
    rows = padded_values.shape[0]
    return both[:rows] + both[rows:]


PLANE = ("x", "core", "seq")

MESH_ID = pl.DeviceIdType.MESH
VMEM_BYTES = 48 * 2**20


def exchange(blocks, axes):
    return lax.all_to_all(blocks, axes, split_axis=0, concat_axis=0, tiled=True)


def busy(microseconds):
    return pl.CostEstimate(flops=0, bytes_accessed=microseconds * 3_000_000, transcendentals=0)


def shifted(flip_z, flip_x, flip_core, flip_y):
    far, *inner = (lax.axis_index(name) for name in ALL)
    flips = (flip_z, flip_x, flip_core, flip_y)
    return (far, *(1 - at if flip else at for at, flip in zip(inner, flips)))


def plane_places():
    def member(flip_x, flip_core, flip_y):
        _, _, x, core, seq = shifted(0, flip_x, flip_core, flip_y)
        return (x * 2 + core) * 2 + seq

    return shifted(0, 0, 1, 0), shifted(0, 1, 0, 0), shifted(0, 0, 0, 1), member


def cube_member(flip_z, flip_x, flip_y, flip_core):
    _, z, x, core, seq = shifted(flip_z, flip_x, flip_core, flip_y)
    return ((z * 2 + x) * 2 + core) * 2 + seq


def cube_places():
    return *plane_places()[:3], shifted(1, 0, 0, 0)


def other_planes(planes):
    far, z, x, core, seq = (lax.axis_index(name) for name in ALL)
    plane = far * 2 + z
    ring = [lax.rem(plane + k, planes) for k in range(1, planes)]
    return plane, [(at // 2, lax.rem(at, 2), x, core, seq) for at in ring], ring


def other_cubes(cubes):
    far, z, x, core, seq = (lax.axis_index(name) for name in ALL)
    return far, [(lax.rem(far + k, cubes), z, x, core, seq) for k in range(1, cubes)]


def greet(places):
    barrier = pltpu.get_barrier_semaphore()
    for place in places:
        pl.semaphore_signal(barrier, inc=1, device_id=place, device_id_type=MESH_ID)
    pl.semaphore_wait(barrier, len(places))


def sender(send_sems, recv_sems):
    def send(kind, source, target, place):
        copy = pltpu.make_async_remote_copy(
            src_ref=source,
            dst_ref=target,
            send_sem=send_sems.at[kind],
            recv_sem=recv_sems.at[kind],
            device_id=place,
            device_id_type=MESH_ID,
        )
        copy.start()
        return copy

    return send


def plane_spread(own_ref, out_ref, send_sems, recv_sems, local_sem, meanwhile=lambda: None):
    sibling, along_x, along_y, member = plane_places()
    half = own_ref.shape[0] // 2
    top, bottom = pl.ds(0, half), pl.ds(half, half)
    me = member(0, 0, 0)
    keep = pltpu.make_async_copy(own_ref, out_ref.at[me], local_sem)
    keep.start()
    send = sender(send_sems, recv_sems)

    def forward(kind, block, rows, place):
        return send(kind, out_ref.at[block, rows], out_ref.at[block, rows], place)

    own_x_top = send(1, own_ref.at[top], out_ref.at[me, top], along_x)
    own_y_bottom = send(3, own_ref.at[bottom], out_ref.at[me, bottom], along_y)
    own_sibling = send(0, own_ref, out_ref.at[me], sibling)
    own_x_bottom = send(2, own_ref.at[bottom], out_ref.at[me, bottom], along_x)
    own_y_top = send(4, own_ref.at[top], out_ref.at[me, top], along_y)
    x_block, y_block, diagonal = member(1, 0, 0), member(0, 0, 1), member(1, 0, 1)
    meanwhile()
    own_x_top.wait_recv()
    diagonal_top = forward(5, x_block, top, along_y)
    x_top = forward(7, x_block, top, sibling)
    own_y_bottom.wait_recv()
    diagonal_bottom = forward(6, y_block, bottom, along_x)
    y_bottom = forward(9, y_block, bottom, sibling)
    own_x_bottom.wait_recv()
    x_bottom = forward(8, x_block, bottom, sibling)
    own_y_top.wait_recv()
    y_top = forward(10, y_block, top, sibling)
    diagonal_top.wait_recv()
    far_top = forward(11, diagonal, top, sibling)
    diagonal_bottom.wait_recv()
    far_bottom = forward(12, diagonal, bottom, sibling)
    for copy in (own_sibling, x_top, y_bottom, x_bottom, y_top, far_top, far_bottom):
        copy.wait_recv()
    for copy in (
        own_x_top,
        own_y_bottom,
        own_sibling,
        own_x_bottom,
        own_y_top,
        diagonal_top,
        diagonal_bottom,
        x_top,
        y_bottom,
        x_bottom,
        y_top,
        far_top,
        far_bottom,
    ):
        copy.wait_send()
    keep.wait()


def cube_spread(own_ref, out_ref, send_sems, recv_sems, local_sem, compute=lambda i: None):
    sibling, along_x, along_y, along_z = cube_places()
    half = own_ref.shape[0] // 2
    top, bottom = pl.ds(0, half), pl.ds(half, half)
    me = cube_member(0, 0, 0, 0)
    keep = pltpu.make_async_copy(own_ref, out_ref.at[me], local_sem)
    keep.start()
    send = sender(send_sems, recv_sems)
    x_block, y_block, diagonal = (cube_member(0, *at, 0) for at in ((1, 0), (0, 1), (1, 1)))
    z_block, zx_block, zy_block, zd_block = (
        cube_member(1, *at, 0) for at in ((0, 0), (1, 0), (0, 1), (1, 1))
    )

    def half_on(kind, block, rows, place):
        return send(kind, out_ref.at[block, rows], out_ref.at[block, rows], place)

    def on(kind, block, place):
        return send(kind, out_ref.at[block], out_ref.at[block], place)

    own_x_top = send(1, own_ref.at[top], out_ref.at[me, top], along_x)
    own_y_bottom = send(3, own_ref.at[bottom], out_ref.at[me, bottom], along_y)
    own_z = send(13, own_ref, out_ref.at[me], along_z)
    own_sibling = send(0, own_ref, out_ref.at[me], sibling)
    own_x_bottom = send(2, own_ref.at[bottom], out_ref.at[me, bottom], along_x)
    own_y_top = send(4, own_ref.at[top], out_ref.at[me, top], along_y)
    compute(0)
    own_x_top.wait_recv()
    diagonal_top = half_on(5, x_block, top, along_y)
    x_top = half_on(7, x_block, top, sibling)
    own_y_bottom.wait_recv()
    diagonal_bottom = half_on(6, y_block, bottom, along_x)
    y_bottom = half_on(9, y_block, bottom, sibling)
    own_sibling.wait_recv()
    compute(1)
    own_z.wait_recv()
    z_to_x = on(14, z_block, along_x)
    z_to_y = on(15, z_block, along_y)
    z_near = on(16, z_block, sibling)
    own_x_bottom.wait_recv()
    x_bottom = half_on(8, x_block, bottom, sibling)
    own_y_top.wait_recv()
    y_top = half_on(10, y_block, top, sibling)
    compute(2)
    diagonal_top.wait_recv()
    far_top = half_on(11, diagonal, top, sibling)
    diagonal_bottom.wait_recv()
    far_bottom = half_on(12, diagonal, bottom, sibling)
    diagonal_z = on(17, diagonal, along_z)
    compute(3)
    compute(4)
    z_to_x.wait_recv()
    zx_near = on(18, zx_block, sibling)
    z_to_y.wait_recv()
    zy_near = on(19, zy_block, sibling)
    compute(5)
    compute(6)
    diagonal_z.wait_recv()
    zd_near = on(20, zd_block, sibling)
    compute(7)
    compute(8)
    last = (
        (x_top, x_bottom), (y_bottom, y_top), (far_top, far_bottom), (z_near,), (zx_near,), (zy_near,), (zd_near,),
    )
    for i, copies in enumerate(last):
        for copy in copies:
            copy.wait_recv()
        compute(9 + i)
    for copy in (
        own_x_top, own_y_bottom, own_z, own_sibling, own_x_bottom, own_y_top, diagonal_top, diagonal_bottom,
        z_to_x, z_to_y, diagonal_z,
    ):
        copy.wait_send()
    for copies in last:
        for copy in copies:
            copy.wait_send()
    keep.wait()


CUBE_ORDER = (
    (0, 0, 0, 0), (0, 0, 0, 1), (0, 1, 0, 0), (0, 0, 1, 0), (1, 0, 0, 0), (0, 1, 1, 0), (1, 1, 0, 0), (1, 0, 1, 0),
    (1, 1, 1, 0), (0, 1, 0, 1), (0, 0, 1, 1), (0, 1, 1, 1), (1, 0, 0, 1), (1, 1, 0, 1), (1, 0, 1, 1), (1, 1, 1, 1),
)


def cube_gather_kernel(own_ref, out_ref, *sems):
    greet(cube_places())
    cube_spread(own_ref, out_ref, *sems)


def weights_gather_kernel(
    cubes, own_hbm, down_ref, gate_hbm, up_hbm, out_ref, down_out, blocks_hbm, own_ref, gate_ref, up_ref, blocks,
    load_sems, put_sems, far_send, far_recv, own_sem, *sems
):
    group, padded, lanes = blocks.shape
    rows, hidden = gate_ref.shape
    units, half = hidden // (cubes * group), lanes // 2

    loads = [
        pltpu.make_async_copy(gate_hbm, gate_ref, load_sems.at[0]),
        pltpu.make_async_copy(up_hbm, up_ref, load_sems.at[1]),
    ]
    own_load = pltpu.make_async_copy(own_hbm, own_ref, load_sems.at[2])
    own_load.start()
    puts = [
        pltpu.make_async_copy(blocks, blocks_hbm.at[cube], put_sems.at[cube])
        for cube in range(cubes)
    ]

    def cut_blocks():
        for load in loads:
            load.wait()
        spare = jnp.zeros((rows, half - cubes * units), blocks.dtype)
        below = jnp.zeros((padded - rows, lanes), blocks.dtype)
        for member in range(group):
            for base, ref in ((0, gate_ref), (half, up_ref)):
                pieces = [
                    ref[:, (cube * group + member) * units : (cube * group + member + 1) * units]
                    for cube in range(cubes)
                ]
                piece = jnp.concatenate(pieces + [spare], axis=1)
                blocks[member, :rows, base : base + half] = piece
            blocks[member, rows:, :] = below
        for put in puts:
            put.start()

    for load in loads:
        load.start()
    far, others = other_cubes(cubes)
    greet((*plane_places()[:3], *others))
    keep = pltpu.make_async_copy(down_ref, down_out.at[far], own_sem)
    keep.start()
    send = sender(far_send, far_recv)
    copies = [send(k, down_ref, down_out.at[far], place) for k, place in enumerate(others)]
    own_load.wait()
    plane_spread(own_ref, out_ref, *sems, meanwhile=cut_blocks)
    for put in puts:
        put.wait()
    for copy in copies:
        copy.wait_recv()
    for copy in copies:
        copy.wait_send()
    keep.wait()


def z_gather_kernel(planes, padded, count, *refs):
    sources, out_ref, held = refs[:count], refs[count], refs[count + 1 : 2 * count + 1]
    own, load_sems, send_sems, recv_sems, own_sem = refs[2 * count + 1 :]
    loads = [
        pltpu.make_async_copy(source, target, load_sems.at[k])
        for k, (source, target) in enumerate(zip(sources, held))
    ]
    for load in loads:
        load.start()
    for load in loads:
        load.wait()
    query_ref, key_ref, value_ref, output_ref, *gains = held
    rows, columns = query_ref.shape[0], own.shape[1]
    plane, others, _ = other_planes(planes)
    at = 0
    for ref in (query_ref, key_ref, value_ref):
        own[:rows, at : at + ref.shape[1]] = ref[...]
        at += ref.shape[1]
    slots = [
        jnp.concatenate(
            [ref[...].astype(jnp.float32), jnp.zeros((1, GAIN_SLOT - ref.shape[1]), jnp.float32)],
            axis=1,
        )
        for ref in gains
    ]
    slots.append(jnp.zeros((1, columns - len(slots) * GAIN_SLOT), jnp.float32))
    line = jnp.concatenate(slots, axis=1)
    spare = jnp.zeros((padded - rows - 1, columns), jnp.float32)
    own[rows:padded, :] = jnp.concatenate([line, spare], axis=0).astype(own.dtype)
    strips, _ = packed_strips(*output_ref.shape, columns)
    for r, c, to, at, n in strips:
        tiles = output_ref[r : r + TILE_ROWS, c : c + n]
        own[padded + to : padded + to + TILE_ROWS, at : at + n] = tiles
    _, _, to, at, n = strips[-1]
    if at + n < columns:
        rest = jnp.zeros((TILE_ROWS, columns - at - n), own.dtype)
        own[padded + to : padded + to + TILE_ROWS, at + n :] = rest
    greet(others)
    keep = pltpu.make_async_copy(own, out_ref.at[plane], own_sem)
    keep.start()
    send = sender(send_sems, recv_sems)
    copies = [send(k, own, out_ref.at[plane], place) for k, place in enumerate(others)]
    for copy in copies:
        copy.wait_recv()
    for copy in copies:
        copy.wait_send()
    keep.wait()


def gather_sems(count):
    return [
        pltpu.SemaphoreType.DMA((count,)),
        pltpu.SemaphoreType.DMA((count,)),
        pltpu.SemaphoreType.DMA,
    ]


def z_gather(query, key, value, output, gains, planes, padded, collective_id):
    columns = query.shape[1] + key.shape[1] + value.shape[1]
    shape = (padded + packed_strips(*output.shape, columns)[1], columns)
    arrays = [query, key, value, output, *(gain[None] for gain in gains)]
    return pl.pallas_call(
        functools.partial(z_gather_kernel, planes, padded, len(arrays)),
        out_shape=jax.ShapeDtypeStruct((planes, *shape), query.dtype),
        in_specs=[pl.BlockSpec(memory_space=pltpu.HBM)] * len(arrays),
        out_specs=pl.BlockSpec(memory_space=pl.ANY),
        scratch_shapes=[
            *[pltpu.VMEM(array.shape, array.dtype) for array in arrays],
            pltpu.VMEM(shape, query.dtype),
            pltpu.SemaphoreType.DMA((len(arrays),)),
            pltpu.SemaphoreType.DMA((planes - 1,)),
            pltpu.SemaphoreType.DMA((planes - 1,)),
            pltpu.SemaphoreType.DMA,
        ],
        cost_estimate=busy(20),
        compiler_params=pltpu.CompilerParams(
            collective_id=collective_id, has_side_effects=True, vmem_limit_bytes=60 * 2**20
        ),
    )(*arrays)


def weights_gather(local, down, gate, up, block, cubes, collective_id):
    members = 8
    hbm, anywhere = pl.BlockSpec(memory_space=pltpu.HBM), pl.BlockSpec(memory_space=pl.ANY)
    return pl.pallas_call(
        functools.partial(weights_gather_kernel, cubes),
        out_shape=[
            jax.ShapeDtypeStruct((members, *local.shape), local.dtype),
            jax.ShapeDtypeStruct((cubes, *down.shape), down.dtype),
            jax.ShapeDtypeStruct((cubes, *block), gate.dtype),
        ],
        in_specs=[anywhere, hbm, hbm, hbm],
        out_specs=[anywhere, hbm, hbm],
        scratch_shapes=[
            pltpu.VMEM(local.shape, local.dtype),
            pltpu.VMEM(gate.shape, gate.dtype),
            pltpu.VMEM(up.shape, up.dtype),
            pltpu.VMEM(block, gate.dtype),
            pltpu.SemaphoreType.DMA((3,)),
            pltpu.SemaphoreType.DMA((cubes,)),
            pltpu.SemaphoreType.DMA((cubes - 1,)),
            pltpu.SemaphoreType.DMA((cubes - 1,)),
            pltpu.SemaphoreType.DMA,
            *gather_sems(13),
        ],
        cost_estimate=busy(30),
        compiler_params=pltpu.CompilerParams(
            collective_id=collective_id, has_side_effects=True, vmem_limit_bytes=60 * 2**20
        ),
    )(local, down, gate, up)


def gather_rows(local, collective_id):
    rows, columns = local.shape
    members = 16
    out = pl.pallas_call(
        cube_gather_kernel,
        out_shape=jax.ShapeDtypeStruct((members, rows // 16, 16, columns), local.dtype),
        in_specs=[pl.BlockSpec(memory_space=pl.ANY)],
        out_specs=pl.BlockSpec(memory_space=pl.ANY),
        scratch_shapes=gather_sems(21),
        cost_estimate=busy(35),
        compiler_params=pltpu.CompilerParams(
            collective_id=collective_id, has_side_effects=True, vmem_limit_bytes=VMEM_BYTES
        ),
    )(local.reshape(rows // 16, 16, columns))
    return out.reshape(-1, columns)


def add_rows(target, sources, start, count):
    def one(i, carry):
        total = sources[0][i].astype(jnp.float32)
        for source in sources[1:]:
            total = total + source[i].astype(jnp.float32)
        target[i] = total.astype(target.dtype)
        return carry

    lax.fori_loop(start, start + count, one, 0)


def plane_sum(part_ref, own_sum, near, sums, from_x, from_y, far_x, far_y, send_sems, recv_sems):
    sibling, along_x, along_y, member = plane_places()
    rows = own_sum.shape[0]
    half = rows // 2
    top, bottom = pl.ds(0, half), pl.ds(half, half)
    send = sender(send_sems, recv_sems)
    chips = ((1, 1), (1, 0), (0, 1), (0, 0))
    mine = [part_ref.at[member(at_x, 0, at_y)] for at_x, at_y in chips]
    to_sibling = [
        send(k, part_ref.at[member(at_x, 1, at_y)], near.at[k], sibling)
        for k, (at_x, at_y) in enumerate(chips)
    ]
    to_sibling[0].wait_recv()
    add_rows(sums.at[0], (mine[0], near.at[0]), 0, rows)
    diagonal_x = send(4, sums.at[0, bottom], far_x.at[bottom], along_x)
    diagonal_y = send(5, sums.at[0, top], far_y.at[top], along_y)
    to_sibling[1].wait_recv()
    add_rows(sums.at[1], (mine[1], near.at[1]), half, half)
    direct_x = send(6, sums.at[1, bottom], from_x.at[bottom], along_x)
    to_sibling[2].wait_recv()
    add_rows(sums.at[2], (mine[2], near.at[2]), 0, half)
    direct_y = send(7, sums.at[2, top], from_y.at[top], along_y)
    to_sibling[3].wait_recv()
    diagonal_y.wait_recv()
    add_rows(sums.at[1], (mine[1], near.at[1], far_y), 0, half)
    joint_x = send(8, sums.at[1, top], from_x.at[top], along_x)
    diagonal_x.wait_recv()
    add_rows(sums.at[2], (mine[2], near.at[2], far_x), half, half)
    joint_y = send(9, sums.at[2, bottom], from_y.at[bottom], along_y)
    direct_x.wait_recv()
    direct_y.wait_recv()
    joint_x.wait_recv()
    joint_y.wait_recv()
    add_rows(own_sum, (mine[3], near.at[3], from_x, from_y), 0, rows)
    for copy in (*to_sibling, diagonal_x, diagonal_y, direct_x, direct_y, joint_x, joint_y):
        copy.wait_send()


def cube_sum(
    part_hbm, own_sum, mine, near, via_z, zx_in, zy_in, far_x, far_y, from_x, from_y, from_z, load_sems, send_sems,
    recv_sems, work=lambda point: None,
):
    sibling, along_x, along_y, along_z = cube_places()
    pieces = own_sum.shape[0]
    half = pieces // 2
    top, bottom = pl.ds(0, half), pl.ds(half, half)
    send = sender(send_sems, recv_sems)
    chips = ((1, 1, 1), (1, 1, 0), (1, 0, 1), (0, 1, 0), (0, 0, 1), (0, 1, 1), (1, 0, 0), (0, 0, 0))
    z_diagonal, z_x, z_y, at_x, at_y, diagonal, at_z, here = range(8)
    to_sibling = [
        send(k, part_hbm.at[cube_member(*chip, 1)], near.at[k], sibling)
        for k, chip in enumerate(chips)
    ]
    loads = [
        pltpu.make_async_copy(part_hbm.at[cube_member(*chip, 0)], mine.at[k], load_sems.at[k])
        for k, chip in enumerate(chips)
    ]
    for load in loads:
        load.start()

    def both_in(k):
        to_sibling[k].wait_recv()
        loads[k].wait()

    def add(k, others=(), start=0, count=pieces):
        add_rows(near.at[k], (mine.at[k], near.at[k], *others), start, count)

    work(0)
    both_in(z_diagonal)
    add(z_diagonal)
    diagonal_z = send(8, near.at[z_diagonal], via_z, along_z)
    both_in(z_x)
    add(z_x)
    zx_out = send(9, near.at[z_x], zx_in, along_x)
    both_in(z_y)
    add(z_y)
    zy_out = send(10, near.at[z_y], zy_in, along_y)
    both_in(at_x)
    add(at_x, (), half, half)
    direct_x = send(13, near.at[at_x, bottom], from_x.at[bottom], along_x)
    both_in(at_y)
    add(at_y, (), 0, half)
    direct_y = send(14, near.at[at_y, top], from_y.at[top], along_y)
    both_in(diagonal)
    both_in(at_z)
    work(1)
    diagonal_z.wait_recv()
    add(diagonal, (via_z,))
    diagonal_x = send(11, near.at[diagonal, bottom], far_x.at[bottom], along_x)
    diagonal_y = send(12, near.at[diagonal, top], far_y.at[top], along_y)
    zx_out.wait_recv()
    zy_out.wait_recv()
    add(at_z, (zx_in, zy_in))
    joint_z = send(15, near.at[at_z], from_z, along_z)
    work(2)
    diagonal_y.wait_recv()
    add(at_x, (far_y,), 0, half)
    joint_x = send(16, near.at[at_x, top], from_x.at[top], along_x)
    diagonal_x.wait_recv()
    add(at_y, (far_x,), half, half)
    joint_y = send(17, near.at[at_y, bottom], from_y.at[bottom], along_y)
    both_in(here)
    work(3)
    for copy in (direct_x, direct_y, joint_z, joint_x, joint_y):
        copy.wait_recv()
    add_rows(own_sum, (mine.at[here], near.at[here], from_x, from_y, from_z), 0, pieces)
    for copy in (
        *to_sibling, diagonal_z, zx_out, zy_out, direct_x, direct_y, diagonal_x, diagonal_y, joint_z, joint_x, joint_y,
    ):
        copy.wait_send()


def cube_sum_kernel(part_ref, out_ref, *scratch):
    greet(cube_places())
    cube_sum(part_ref, out_ref, *scratch)


def cube_sum_scratch(shape, dtype):
    return [
        pltpu.VMEM((8, *shape), dtype),
        pltpu.VMEM((8, *shape), dtype),
        *[pltpu.VMEM(shape, dtype)] * 8,
        pltpu.SemaphoreType.DMA((8,)),
        pltpu.SemaphoreType.DMA((18,)),
        pltpu.SemaphoreType.DMA((18,)),
    ]


def plane_sum_scratch(shape, dtype):
    block = pltpu.VMEM(shape, dtype)
    return [
        pltpu.VMEM((4, *shape), dtype),
        pltpu.VMEM((3, *shape), dtype),
        block,
        block,
        block,
        block,
        pltpu.SemaphoreType.DMA((10,)),
        pltpu.SemaphoreType.DMA((10,)),
    ]


def cube_scatter_sum(partial, collective_id):
    shape = partial.shape[1:]
    out = pl.pallas_call(
        cube_sum_kernel,
        out_shape=jax.ShapeDtypeStruct(shape, jnp.float32),
        in_specs=[pl.BlockSpec(memory_space=pl.ANY)],
        out_specs=pl.BlockSpec(memory_space=pltpu.VMEM),
        scratch_shapes=cube_sum_scratch(shape, partial.dtype),
        cost_estimate=busy(35),
        compiler_params=pltpu.CompilerParams(
            collective_id=collective_id, has_side_effects=True, vmem_limit_bytes=VMEM_BYTES
        ),
    )(partial)
    return out.reshape(shape[0] * shape[1], shape[2])


gelu_inner = 0.7978845608028654
gelu_cubic = 0.044715


def pad_rows(target, source):
    rows = source.shape[0]
    target[pl.ds(0, rows)] = source[...]
    if target.shape[0] > rows:
        extra = target.shape[0] - rows
        target[pl.ds(rows, extra)] = jnp.zeros((extra, target.shape[1]), target.dtype)


def ffn_forward_kernel(in_ref, gate_up_ref, down_ref, part_ref, act_ref, to_gate, to_up, down, proj):
    units = act_ref.shape[1]

    @pl.when(pl.program_id(0) == 0)
    def _():
        pad_rows(down, down_ref)

    step = 64
    half_rows = in_ref.shape[0] // 2

    def mid(base):
        for i in range(half_rows // step):
            rows = pl.ds(base + i * step, step)
            gate, up = proj[rows, :units], proj[rows, units:]
            square = gate * gate
            bend = jnp.tanh(gelu_inner * gate * (1.0 + gelu_cubic * square))
            half = 0.5 * (1.0 + bend)
            value = gate * half
            slope = half + 0.5 * gate * (1.0 - bend * bend) * (
                gelu_inner * (1.0 + 3.0 * gelu_cubic * square)
            )
            to_gate[rows, :] = slope * up
            to_up[rows, :] = value
            act_ref[rows, :] = (value * up).astype(act_ref.dtype)

    first, second = pl.ds(0, half_rows), pl.ds(half_rows, half_rows)
    proj[first, :] = matmul(in_ref[first, :], gate_up_ref[...])
    proj[second, :] = matmul(in_ref[second, :], gate_up_ref[...])
    mid(0)
    part_ref[first, :] = matmul(act_ref[first, :], down[...]).astype(part_ref.dtype)
    mid(half_rows)
    part_ref[second, :] = matmul(act_ref[second, :], down[...]).astype(part_ref.dtype)


ROW_BLOCK = 512


def whole(array):
    return pl.BlockSpec(array.shape, lambda i: (0, 0), pipeline_mode=pl.Buffered(1))


def row_block(columns):
    return pl.BlockSpec((ROW_BLOCK, columns), lambda i: (i, 0))


def ffn_forward(rows_in, gate_up, down):
    rows, depth = rows_in.shape
    units, columns = gate_up.shape[1] // 2, down.shape[1]
    low = rows_in.dtype
    return pl.pallas_call(
        ffn_forward_kernel,
        grid=(rows // ROW_BLOCK,),
        in_specs=[row_block(depth), whole(gate_up), whole(down)],
        out_specs=[row_block(columns), row_block(units), row_block(units), row_block(units)],
        out_shape=[
            jax.ShapeDtypeStruct((rows, columns), low),
            jax.ShapeDtypeStruct((rows, units), low),
            jax.ShapeDtypeStruct((rows, units), jnp.float32),
            jax.ShapeDtypeStruct((rows, units), jnp.float32),
        ],
        scratch_shapes=[
            pltpu.VMEM((units, columns), low),
            pltpu.VMEM((ROW_BLOCK, 2 * units), jnp.float32),
        ],
        cost_estimate=busy(20),
        compiler_params=pltpu.CompilerParams(vmem_limit_bytes=VMEM_BYTES),
    )(rows_in, gate_up, down)


def block_order(rows):
    order = [cube_member(*flips) for flips in CUBE_ORDER]
    return order, [pl.ds(pl.multiple_of(block * rows, rows), rows) for block in order]


def gather_backward_kernel(
    own_ref, down_ref, gate_up_ref, to_gate_hbm, to_up_hbm, act_hbm, both_hbm, part_hbm, down_grad_ref,
    grad, down, to_gate, to_up, act, both, part, act_sem, load_sems, put_sems, send_sems, recv_sems, local_sem,
):
    units = down.shape[0]
    pieces, piece, columns = own_ref.shape
    rows = pieces * piece
    order, places = block_order(rows)

    def loads(i):
        slot, at = i % 2, places[i]
        return (
            pltpu.make_async_copy(to_gate_hbm.at[at], to_gate.at[slot], load_sems.at[0, slot]),
            pltpu.make_async_copy(to_up_hbm.at[at], to_up.at[slot], load_sems.at[1, slot]),
        )

    def puts(i):
        slot = i % 2
        return (
            pltpu.make_async_copy(both.at[slot], both_hbm.at[places[i]], put_sems.at[0, slot]),
            pltpu.make_async_copy(part.at[slot], part_hbm.at[order[i]], put_sems.at[1, slot]),
        )

    def compute(i):
        if i + 1 < len(order):
            for load in loads(i + 1):
                load.start()
        for load in loads(i):
            load.wait()
        if i >= 2:
            for put in puts(i - 2):
                put.wait()
        slot = i % 2
        source = own_ref if i == 0 else grad.at[order[i]]
        act_grad = contract_cols(source[...].reshape(rows, columns), down[...])
        both[slot, :, :units] = (act_grad * to_gate[slot]).astype(both.dtype)
        both[slot, :, units:] = (act_grad * to_up[slot]).astype(both.dtype)
        result = contract_cols(both[slot], gate_up_ref[...]).astype(part.dtype)
        part[slot] = result.reshape(pieces, piece, result.shape[1])
        for put in puts(i):
            put.start()

    act_load = pltpu.make_async_copy(act_hbm, act, act_sem)
    act_load.start()
    for load in loads(0):
        load.start()
    pad_rows(down, down_ref)
    greet(cube_places())
    cube_spread(own_ref, grad, send_sems, recv_sems, local_sem, compute)
    act_load.wait()
    whole = grad[...].reshape(len(order) * rows, columns)
    down_grad = contract_rows(act[...], whole)
    down_grad_ref[...] = down_grad[: down_ref.shape[0]].astype(down_grad_ref.dtype)
    for i in (len(order) - 2, len(order) - 1):
        for put in puts(i):
            put.wait()


def gather_backward(own, down, gate_up, to_gate, to_up, act, collective_id):
    rows, columns = own.shape
    members, piece = 16, 16
    pieces = rows // piece
    depth, units = gate_up.shape[0], to_gate.shape[1]
    low, wide = own.dtype, jnp.float32
    shape = jax.ShapeDtypeStruct
    vmem, anywhere = pl.BlockSpec(memory_space=pltpu.VMEM), pl.BlockSpec(memory_space=pl.ANY)
    return pl.pallas_call(
        gather_backward_kernel,
        out_shape=[
            shape((members * rows, 2 * units), low),
            shape((members, pieces, piece, depth), low),
            shape(down.shape, low),
        ],
        in_specs=[vmem, vmem, vmem, anywhere, anywhere, anywhere],
        out_specs=[anywhere, anywhere, vmem],
        scratch_shapes=[
            pltpu.VMEM((members, pieces, piece, columns), low),
            pltpu.VMEM((units, columns), low),
            pltpu.VMEM((2, rows, units), wide),
            pltpu.VMEM((2, rows, units), wide),
            pltpu.VMEM(act.shape, low),
            pltpu.VMEM((2, rows, 2 * units), low),
            pltpu.VMEM((2, pieces, piece, depth), low),
            pltpu.SemaphoreType.DMA,
            pltpu.SemaphoreType.DMA((2, 2)),
            pltpu.SemaphoreType.DMA((2, 2)),
            *gather_sems(21),
        ],
        cost_estimate=busy(45),
        compiler_params=pltpu.CompilerParams(
            collective_id=collective_id, has_side_effects=True, vmem_limit_bytes=60 * 2**20
        ),
    )(own.reshape(pieces, piece, columns), down, gate_up, to_gate, to_up, act)


def sum_gradients_kernel(
    part_ref, down_ref, in_hbm, both_hbm, sum_ref, gate_up_ref, down_sum_ref,
    columns_in, both, arriving, both_sem, in_sems, far_send, far_recv, *scratch,
):
    cubes = down_ref.shape[0]
    far, others = other_cubes(cubes)
    step = columns_in.shape[2]
    blocks = gate_up_ref.shape[0] // step

    def load(i):
        at = pl.ds(i * step, step)
        return pltpu.make_async_copy(in_hbm.at[:, at], columns_in.at[i % 2], in_sems.at[i % 2])

    both_load = pltpu.make_async_copy(both_hbm, both, both_sem)
    both_load.start()
    load(0).start()

    def rows_of(i):
        if i == 0:
            both_load.wait()
        if i + 1 < blocks:
            load(i + 1).start()
        load(i).wait()
        rows = contract_rows(columns_in[i % 2], both[...])
        gate_up_ref[pl.ds(i * step, step), :] = rows.astype(gate_up_ref.dtype)

    def work(point):
        spread = ((), (0, 1), (2, 3), tuple(range(4, blocks)))
        for i in spread[point]:
            rows_of(i)

    greet((*cube_places(), *others))
    send = sender(far_send, far_recv)
    copies = [
        send(k, down_ref.at[place[0]], arriving.at[k], place) for k, place in enumerate(others)
    ]
    cube_sum(part_ref, sum_ref, *scratch, work=work)
    down_sum = down_ref[far].astype(jnp.float32)
    for k, copy in enumerate(copies):
        copy.wait_recv()
        down_sum = down_sum + arriving[k].astype(jnp.float32)
    down_sum_ref[...] = down_sum
    for copy in copies:
        copy.wait_send()


def sum_gradients(part, down, rows_in, both, collective_id):
    members, pieces, piece, depth = part.shape
    low = part.dtype
    step = 256
    vmem, anywhere = pl.BlockSpec(memory_space=pltpu.VMEM), pl.BlockSpec(memory_space=pl.ANY)
    total, gate_up, down_sum = pl.pallas_call(
        sum_gradients_kernel,
        out_shape=[
            jax.ShapeDtypeStruct((pieces, piece, depth), jnp.float32),
            jax.ShapeDtypeStruct((depth, both.shape[1]), low),
            jax.ShapeDtypeStruct(down.shape[1:], jnp.float32),
        ],
        in_specs=[anywhere, vmem, anywhere, anywhere],
        out_specs=[vmem, vmem, vmem],
        scratch_shapes=[
            pltpu.VMEM((2, rows_in.shape[0], step), low),
            pltpu.VMEM(both.shape, low),
            pltpu.VMEM((down.shape[0] - 1, *down.shape[1:]), low),
            pltpu.SemaphoreType.DMA,
            pltpu.SemaphoreType.DMA((2,)),
            pltpu.SemaphoreType.DMA((down.shape[0] - 1,)),
            pltpu.SemaphoreType.DMA((down.shape[0] - 1,)),
            *cube_sum_scratch((pieces, piece, depth), low),
        ],
        cost_estimate=busy(35),
        compiler_params=pltpu.CompilerParams(
            collective_id=collective_id, has_side_effects=True, vmem_limit_bytes=60 * 2**20
        ),
    )(part, down, rows_in, both)
    return total.reshape(pieces * piece, depth), gate_up, down_sum


def unit_sum_kernel(terms_ref, gate_ref, up_ref):
    cubes, group, _, lanes = terms_ref.shape
    rows, hidden = gate_ref.shape
    units, half = hidden // (cubes * group), lanes // 2
    for member in range(group):
        total = terms_ref[0, member].astype(jnp.float32)
        for cube in range(1, cubes):
            total = total + terms_ref[cube, member].astype(jnp.float32)
        for cube in range(cubes):
            at = (cube * group + member) * units
            gate_ref[:, at : at + units] = total[:rows, cube * units : (cube + 1) * units]
            up_ref[:, at : at + units] = total[
                :rows, half + cube * units : half + (cube + 1) * units
            ]


def unit_sum(terms, rows, hidden):
    vmem = pl.BlockSpec(memory_space=pltpu.VMEM)
    return pl.pallas_call(
        unit_sum_kernel,
        out_shape=[jax.ShapeDtypeStruct((rows, hidden), jnp.float32)] * 2,
        in_specs=[vmem],
        out_specs=[vmem, vmem],
        cost_estimate=busy(5),
        compiler_params=pltpu.CompilerParams(vmem_limit_bytes=VMEM_BYTES),
    )(terms)


def owner_sum_kernel(planes, part_ref, out_ref, own_sum, leaving, arriving, z_send, z_recv, *scratch):
    plane, others, ring = other_planes(planes)
    greet((*plane_places()[:3], *others))
    plane_sum(part_ref, own_sum, *scratch)
    send = sender(z_send, z_recv)

    def narrow(i, carry):
        leaving[i] = own_sum[i].astype(leaving.dtype)
        return carry

    lax.fori_loop(0, planes, narrow, 0)
    copies = [
        send(k, leaving.at[ring[k]], arriving.at[k], place) for k, place in enumerate(others)
    ]
    for copy in copies:
        copy.wait_recv()

    value = own_sum[plane]
    for k in range(planes - 1):
        value = value + arriving[k].astype(jnp.float32)
    out_ref[...] = value
    for copy in copies:
        copy.wait_send()


def owner_sum(blocks, collective_id):
    members, planes, rows, columns = blocks.shape
    return pl.pallas_call(
        functools.partial(owner_sum_kernel, planes),
        out_shape=jax.ShapeDtypeStruct((rows, columns), jnp.float32),
        in_specs=[pl.BlockSpec(memory_space=pltpu.VMEM)],
        out_specs=pl.BlockSpec(memory_space=pltpu.VMEM),
        scratch_shapes=[
            pltpu.VMEM((planes, rows, columns), jnp.float32),
            pltpu.VMEM((planes, rows, columns), blocks.dtype),
            pltpu.VMEM((planes - 1, rows, columns), blocks.dtype),
            pltpu.SemaphoreType.DMA((planes - 1,)),
            pltpu.SemaphoreType.DMA((planes - 1,)),
            *plane_sum_scratch((planes, rows, columns), blocks.dtype),
        ],
        cost_estimate=busy(35),
        compiler_params=pltpu.CompilerParams(
            collective_id=collective_id, has_side_effects=True, vmem_limit_bytes=VMEM_BYTES
        ),
    )(blocks)


GAIN_SLOT = 128
TILE_ROWS, TILE_LANES = 8, 128


def packed_strips(rows, width, columns):
    across, into = width // TILE_LANES, columns // TILE_LANES
    strips, tile, tiles = [], 0, rows // TILE_ROWS * across
    while tile < tiles:
        run = min(across - tile % across, into - tile % into)
        strips.append(
            (
                tile // across * TILE_ROWS,
                tile % across * TILE_LANES,
                tile // into * TILE_ROWS,
                tile % into * TILE_LANES,
                run * TILE_LANES,
            )
        )
        tile += run
    return strips, up_to(tiles, into) // into * TILE_ROWS


def unpack_tiles(array, rows, width):
    strips, _ = packed_strips(rows, width, array.shape[1])
    lines = []
    for row in range(0, rows, TILE_ROWS):
        parts = [
            array[to : to + TILE_ROWS, at : at + n] for r, _, to, at, n in strips if r == row
        ]
        lines.append(jnp.concatenate(parts, axis=1))
    return jnp.concatenate(lines, axis=0)


def gain_places(blocks, planes, count):
    lane = lax.broadcasted_iota(jnp.int32, (GAIN_SLOT, blocks * count), 0)
    inner = lax.broadcasted_iota(jnp.int32, (GAIN_SLOT, blocks * count), 1) % count
    places = (lane == inner).astype(jnp.float32).astype(jnp.bfloat16)
    listed = lax.broadcasted_iota(jnp.int32, (blocks, blocks * count), 0)
    block = lax.broadcasted_iota(jnp.int32, (blocks, blocks * count), 1) // count
    members = blocks // planes
    block = block % members * planes + block // members
    return places, listed == block


def spread_gain(rows, planes, count):
    places, chosen = gain_places(rows.shape[0], planes, count)
    return jnp.sum(jnp.where(chosen, matmul(rows, places), 0.0), axis=0, keepdims=True)


def collect_gain(vector, blocks, planes, count):
    places, chosen = gain_places(blocks, planes, count)
    return contract_cols(jnp.where(chosen, vector, 0.0).astype(jnp.bfloat16), places)


def inverse_of(values, count):
    return lax.rsqrt(jnp.sum(values * values, axis=-1, keepdims=True) / count + epsilon)


def back_of(grad_normed, normed, inverse, count):
    inner = jnp.sum(grad_normed * normed, axis=-1, keepdims=True) / count
    return inverse * (grad_normed - normed * inner)


def turn(values, cos_table, sin_table):
    half = values.shape[1] // 2
    first, second = values[:, :half], values[:, half:]
    return first * cos_table - second * sin_table, second * cos_table + first * sin_table


def attention_forward_kernel(
    gain_widths, width_rows, padded, row_ref, hidden_ref, packed_ref, cos_ref, sin_ref, segment_column, segment_row, placing_ref,
    placed_ref, middle_ref, raw_ref, mix_ref, probs_ref, query_ref, key_ref, value_ref, query_raw_ref,
    key_raw_ref, qkv_ref, output_ref, input_scale, query_scale, key_scale, attnout_scale, ffnin_scale, ffnout_scale,
    gain_rows,
):
    bf16, f32 = jnp.bfloat16, jnp.float32
    members, planes, piece, _ = packed_ref.shape
    blocks = members * planes
    width = hidden_ref.shape[1]
    mix_rows = output_ref.shape[0] // blocks
    strips, _ = packed_strips(mix_rows, width, packed_ref.shape[3])
    local_rows, full_rows = hidden_ref.shape[0], row_ref.shape[0]
    head = key_ref.shape[1]
    heads = query_ref.shape[1] // head
    offset = pl.multiple_of(lax.axis_index("seq") * local_rows, local_rows)
    mine = pl.ds(offset, local_rows)
    for i in range(blocks):
        member, plane = i // planes, i % planes
        block = packed_ref[member, plane]
        natural = width_rows * (plane * members + member)
        qkv_ref[natural : natural + width_rows, :] = block[:width_rows]
        natural = mix_rows * (plane * members + member)
        for r, c, to, at, n in strips:
            tiles = block[padded + to : padded + to + TILE_ROWS, at : at + n]
            output_ref[natural + r : natural + r + TILE_ROWS, c : c + n] = tiles
        gain_rows[i : i + 1, :] = block[width_rows : width_rows + 1, : gain_rows.shape[1]].astype(f32)
    targets = (input_scale, query_scale, key_scale, attnout_scale, ffnin_scale, ffnout_scale)
    for k, (target, count) in enumerate(zip(targets, gain_widths)):
        rows = gain_rows[:, k * GAIN_SLOT : (k + 1) * GAIN_SLOT].astype(bf16)
        target[...] = spread_gain(rows, planes, count)

    row = row_ref[...].astype(f32)
    normed = (row * inverse_of(row, width) * input_scale[...]).astype(bf16)
    key_value = matmul(normed, qkv_ref[:, heads * head :])
    key_raw = key_value[:, :head]
    value_ref[...] = key_value[:, head:].astype(bf16)
    half = head // 2
    turned = turn(key_raw * inverse_of(key_raw, head) * key_scale[...], cos_ref[...], sin_ref[...])
    key_ref[:, :half], key_ref[:, half:] = turned[0].astype(bf16), turned[1].astype(bf16)

    row = row_ref[mine, :].astype(f32)
    normed = (row * inverse_of(row, width) * input_scale[...]).astype(bf16)
    own = matmul(normed, qkv_ref[:, : (heads + 1) * head])
    query_raw_ref[...] = own[:, : heads * head]
    key_raw_ref[...] = own[:, heads * head :]
    cos_table, sin_table = cos_ref[mine, :], sin_ref[mine, :]
    places = offset + lax.broadcasted_iota(jnp.int32, (local_rows, full_rows), 0)
    earlier = places >= lax.broadcasted_iota(jnp.int32, (local_rows, full_rows), 1)
    allowed = (segment_column[...] == segment_row[...]) & earlier
    for h in range(heads):
        at = h * head
        query_raw = query_raw_ref[:, at : at + head]
        turned = turn(
            query_raw * inverse_of(query_raw, head) * query_scale[...], cos_table, sin_table
        )
        scale = head ** (-0.5)
        query_ref[:, at : at + half] = (turned[0] * scale).astype(bf16)
        query_ref[:, at + half : at + head] = (turned[1] * scale).astype(bf16)
        scores = contract_cols(query_ref[:, at : at + head], key_ref[...])
        scores = jnp.where(allowed, scores, masked_score)
        weights = jnp.exp(scores - jnp.max(scores, axis=-1, keepdims=True))
        probs = weights / jnp.sum(weights, axis=-1, keepdims=True)
        probs_ref[h] = probs
        mix_ref[:, at : at + head] = matmul(probs.astype(bf16), value_ref[...]).astype(bf16)
    attn_raw = matmul(mix_ref[...], output_ref[...])
    raw_ref[...] = attn_raw
    middle = hidden_ref[...].astype(f32) + attn_raw * inverse_of(attn_raw, width) * attnout_scale[...]
    middle_ref[...] = middle
    ffn_in = (middle * inverse_of(middle, width) * ffnin_scale[...]).astype(bf16)
    placed_ref[...] = matmul(ffn_in, placing_ref[...]).astype(bf16)


def attention_forward(
    row_tokens, hidden, packed, cos_full, sin_full, segment_column, segment_row, placing, gain_widths, width_rows, padded,
    head_width,
):
    bf16, f32 = jnp.bfloat16, jnp.float32
    members, planes, piece, qkv_width = packed.shape
    blocks = members * planes
    local_rows, width = hidden.shape
    query_width = qkv_width - 2 * head_width
    heads = query_width // head_width
    full_rows = row_tokens.shape[0]
    depth = blocks * padded
    shape = jax.ShapeDtypeStruct
    vmem = pl.BlockSpec(memory_space=pltpu.VMEM)
    out_shape = [
        shape((local_rows, depth), bf16),
        shape((local_rows, width), f32),
        shape((local_rows, width), f32),
        shape((local_rows, query_width), bf16),
        shape((heads, local_rows, full_rows), f32),
        shape((local_rows, query_width), bf16),
        shape((full_rows, head_width), bf16),
        shape((full_rows, head_width), bf16),
        shape((local_rows, query_width), f32),
        shape((local_rows, head_width), f32),
        shape((width, qkv_width), bf16),
        shape((query_width, width), bf16),
        shape((1, width), f32),
        shape((1, head_width), f32),
        shape((1, head_width), f32),
        shape((1, width), f32),
        shape((1, width), f32),
        shape((1, width), f32),
    ]
    return pl.pallas_call(
        functools.partial(attention_forward_kernel, gain_widths, width_rows, padded),
        out_shape=out_shape,
        in_specs=[vmem] * 8,
        out_specs=[vmem] * len(out_shape),
        scratch_shapes=[pltpu.VMEM((blocks, len(gain_widths) * GAIN_SLOT), f32)],
        cost_estimate=busy(20),
        compiler_params=pltpu.CompilerParams(vmem_limit_bytes=60 * 2**20),
    )(row_tokens, hidden, packed, cos_full, sin_full, segment_column, segment_row, placing)


def attention_backward_kernel(
    gain_widths, width_rows, planes, padded, grad_ref, incoming_ref, middle_ref, raw_ref, mix_ref, probs_ref, query_ref, key_ref,
    value_ref, query_raw_ref, key_raw_ref, row_ref, qkv_ref, output_ref, cos_ref, sin_ref, input_scale,
    query_scale, key_scale, attnout_scale, ffnin_scale, ffnout_grad, by_device,
    input_grad_ref, blocks_ref, key_value, query_grad, low_ref, leaving, arriving, send_sem, recv_sem,
):
    bf16, f32 = jnp.bfloat16, jnp.float32
    members = blocks_ref.shape[0]
    blocks = members * planes
    mix_rows = output_ref.shape[0] // blocks
    local_rows, width = incoming_ref.shape
    strips, _ = packed_strips(mix_rows, width, blocks_ref.shape[3])
    head = key_ref.shape[1]
    heads = query_ref.shape[1] // head
    half = head // 2
    seq = lax.axis_index("seq")
    mine = pl.ds(pl.multiple_of(seq * local_rows, local_rows), local_rows)
    theirs = pl.ds(pl.multiple_of((1 - seq) * local_rows, local_rows), local_rows)
    partner = plane_places()[2]
    greet((partner,))

    ffn_in_grad = take_back(grad_ref[...], by_device[...])
    middle = middle_ref[...]
    inverse = inverse_of(middle, width)
    normed = middle * inverse
    ffnin_grad = jnp.sum(ffn_in_grad * normed, axis=0, keepdims=True)
    middle_grad = incoming_ref[...].astype(f32) + back_of(
        ffn_in_grad * ffnin_scale[...], normed, inverse, width
    )
    input_grad_ref[...] = middle_grad
    raw = raw_ref[...]
    inverse = inverse_of(raw, width)
    normed = raw * inverse
    attnout_grad = jnp.sum(middle_grad * normed, axis=0, keepdims=True)
    raw_grad = back_of(middle_grad * attnout_scale[...], normed, inverse, width).astype(bf16)
    mix_grad = contract_cols(raw_grad, output_ref[...]).astype(bf16)
    for h in range(heads):
        at = h * head
        grad = mix_grad[:, at : at + head]
        probs = probs_ref[h]
        prob_grad = contract_cols(grad, value_ref[...])
        delta = jnp.sum(prob_grad * probs, axis=-1, keepdims=True)
        score_grad = (probs * (prob_grad - delta)).astype(bf16)
        to_keys = contract_rows(score_grad, query_ref[:, at : at + head])
        to_values = contract_rows(probs.astype(bf16), grad)
        if h == 0:
            key_value[:, :head], key_value[:, head:] = to_keys, to_values
        else:
            key_value[:, :head] += to_keys
            key_value[:, head:] += to_values
        query_grad[:, at : at + head] = matmul(score_grad, key_ref[...])
    leaving[...] = key_value[theirs, :].astype(bf16)
    copy = sender(send_sem, recv_sem)(0, leaving, arriving, partner)

    output_grad = contract_rows(mix_ref[...], raw_grad).astype(bf16)
    cos_table, sin_table = cos_ref[mine, :], sin_ref[mine, :]

    def head_back(grad, raw, scale_ref):
        turned = jnp.concatenate(turn(grad, cos_table, -sin_table), axis=1)
        inverse = inverse_of(raw, head)
        normed = raw * inverse
        gain = jnp.sum(turned * normed, axis=0, keepdims=True)
        return back_of(turned * scale_ref[...], normed, inverse, head).astype(bf16), gain

    query_gain = jnp.zeros((1, head), f32)
    for h in range(heads):
        at = h * head
        low, gain = head_back(
            query_grad[:, at : at + head] * head ** (-0.5),
            query_raw_ref[:, at : at + head],
            query_scale,
        )
        low_ref[:, at : at + head] = low
        query_gain = query_gain + gain
    copy.wait_recv()
    total = key_value[mine, :] + arriving[...].astype(f32)
    low, key_gain = head_back(total[:, :head], key_raw_ref[...], key_scale)
    low_ref[:, heads * head : (heads + 1) * head] = low
    low_ref[:, (heads + 1) * head :] = total[:, head:].astype(bf16)

    row = row_ref[mine, :].astype(f32)
    inverse = inverse_of(row, width)
    normed = row * inverse
    normed_grad = contract_cols(low_ref[...], qkv_ref[...])
    input_gain = jnp.sum(normed_grad * normed, axis=0, keepdims=True)
    input_grad_ref[...] += back_of(normed_grad * input_scale[...], normed, inverse, width)
    vectors = (input_gain, query_gain, key_gain, attnout_grad, ffnin_grad, ffnout_grad[...])
    gains = jnp.concatenate(
        [
            collect_gain(vector, blocks, planes, count)
            for vector, count in zip(vectors, gain_widths)
        ],
        axis=1,
    )
    columns = blocks_ref.shape[3]
    gains = jnp.concatenate([gains, jnp.zeros((blocks, columns - gains.shape[1]), f32)], axis=1)
    spare = jnp.zeros((padded - width_rows - 1, columns), f32)
    normed = (normed * input_scale[...]).astype(bf16)
    weights = contract_rows(normed, low_ref[...])
    for i in range(blocks):
        member, plane = i // planes, i % planes
        natural = width_rows * (plane * members + member)
        piece = weights[natural : natural + width_rows]
        block = jnp.concatenate([piece, gains[i : i + 1], spare], axis=0)
        blocks_ref[member, plane, :padded, :] = block.astype(bf16)
        natural = mix_rows * (plane * members + member)
        for r, c, to, at, n in strips:
            tiles = output_grad[natural + r : natural + r + TILE_ROWS, c : c + n]
            blocks_ref[member, plane, padded + to : padded + to + TILE_ROWS, at : at + n] = tiles
        _, _, to, at, n = strips[-1]
        if at + n < columns:
            rest = jnp.zeros((TILE_ROWS, columns - at - n), bf16)
            blocks_ref[member, plane, padded + to : padded + to + TILE_ROWS, at + n :] = rest
    copy.wait_send()


def attention_backward(arrays, gain_widths, width_rows, planes, padded, mix_rows, collective_id):
    bf16, f32 = jnp.bfloat16, jnp.float32
    grad, incoming, query, key, qkv = arrays[0], arrays[1], arrays[6], arrays[7], arrays[12]
    local_rows, width = incoming.shape
    members = 8
    _, packed_rows = packed_strips(mix_rows, width, qkv.shape[1])
    pair = pltpu.VMEM((local_rows, 2 * key.shape[1]), bf16)
    shape = jax.ShapeDtypeStruct
    vmem = pl.BlockSpec(memory_space=pltpu.VMEM)
    return pl.pallas_call(
        functools.partial(attention_backward_kernel, gain_widths, width_rows, planes, padded),
        out_shape=[
            shape((local_rows, width), f32),
            shape((members, planes, padded + packed_rows, qkv.shape[1]), bf16),
        ],
        in_specs=[vmem] * len(arrays),
        out_specs=[vmem] * 2,
        scratch_shapes=[
            pltpu.VMEM((key.shape[0], 2 * key.shape[1]), f32),
            pltpu.VMEM(query.shape, f32),
            pltpu.VMEM((local_rows, qkv.shape[1]), bf16),
            pair,
            pair,
            pltpu.SemaphoreType.DMA((1,)),
            pltpu.SemaphoreType.DMA((1,)),
        ],
        cost_estimate=busy(30),
        compiler_params=pltpu.CompilerParams(
            collective_id=collective_id, has_side_effects=True, vmem_limit_bytes=60 * 2**20
        ),
    )(*arrays)


def body(
    tokens,
    segment_ids,
    cotangent,
    query_weight,
    key_weight,
    value_weight,
    output_weight,
    gate_weight,
    up_weight,
    down_weight,
    input_gain,
    query_gain,
    key_gain,
    attnout_gain,
    ffnin_gain,
    ffnout_gain,
):
    bf16, f32 = jnp.bfloat16, jnp.float32
    devices = lax.axis_size(ALL)
    members = lax.axis_size(PLANE)
    planes = lax.axis_size(PLANES)
    cubes = lax.axis_size("far")
    group = lax.axis_size(CUBE)
    width_rows = query_weight.shape[0]
    hidden_rows = down_weight.shape[0]
    head_width = key_weight.shape[1]
    query_width = query_weight.shape[1]
    head_count = query_width // head_width
    qkv_width = query_width + 2 * head_width
    mix_rows = output_weight.shape[0]
    padded = up_to(width_rows + 1, 8)
    width = devices * width_rows
    unit_count = cubes * hidden_rows
    unit_pad = up_to(unit_count, 128)
    by_device = place_columns(devices, width_rows, padded)

    gains = (input_gain, query_gain, key_gain, attnout_gain, ffnin_gain, ffnout_gain)
    gain_widths = [g.shape[0] for g in gains]
    packed_all = z_gather(
        query_weight, key_weight, value_weight, output_weight, gains, planes, padded, 0
    )
    other_tokens = lax.ppermute(tokens[0], "seq", [(0, 1), (1, 0)])
    packed_all, other_tokens = lax.optimization_barrier((packed_all, other_tokens))
    packed_all, down_full, gate_up = weights_gather(
        packed_all, down_weight, gate_weight, up_weight, (group, padded, 2 * unit_pad), cubes, 6
    )
    down_full = down_full.reshape(unit_count, down_weight.shape[1])
    gate_up, packed_all = lax.optimization_barrier((gate_up, packed_all))
    gate_up = gate_up.reshape(devices, padded, 2 * unit_pad)
    gate_up_full = exchange(gate_up, ALL).reshape(devices * padded, 2 * unit_pad)
    incoming = cotangent[0].astype(f32)
    local_rows = tokens.shape[1]
    offset = lax.axis_index("seq") * local_rows
    segment_row = segment_ids[0]

    def mine(rows):
        return lax.dynamic_slice_in_dim(rows, offset, local_rows)

    cos_full, sin_full = rope_tables(doc_positions(segment_row), head_width)

    first = lax.axis_index("seq") == 0
    row_tokens = jnp.concatenate(
        [
            jnp.where(first, tokens[0], other_tokens),
            jnp.where(first, other_tokens, tokens[0]),
        ]
    )
    (
        ffn_in_placed,
        middle,
        attn_raw,
        attn_flat,
        probs,
        queries,
        key_rows,
        value_rows,
        query_raw,
        key_raw,
        qkv_full,
        output_full,
        *scales,
    ) = attention_forward(
        row_tokens,
        tokens[0],
        packed_all,
        cos_full,
        sin_full,
        mine(segment_row)[:, None],
        segment_row[None],
        by_device,
        gain_widths,
        width_rows,
        padded,
        head_width,
    )
    ffnout_scale = scales.pop()

    cube_in = gather_rows(ffn_in_placed, 1)
    ffn_part, activated_low, to_gate, to_up = ffn_forward(cube_in, gate_up_full, down_full)
    ffn_part = ffn_part.reshape(group, local_rows // 16, 16, ffn_part.shape[1])
    ffn_raw = cube_scatter_sum(ffn_part, 2)
    inv_ffn = inverse_rms(ffn_raw)
    norm_ffn = ffn_raw * inv_ffn
    result = middle + norm_ffn * ffnout_scale
    ffnout_gain_grad = jnp.sum(incoming * norm_ffn, axis=0)
    ffn_raw_grad = rms_back(incoming * ffnout_scale, norm_ffn, inv_ffn).astype(bf16)

    gate_up_low, ffn_in_part, down_blocks = gather_backward(
        ffn_raw_grad, down_full, gate_up_full, to_gate, to_up, activated_low, 3
    )
    down_blocks = down_blocks.reshape(cubes, hidden_rows, down_weight.shape[1])
    ffn_in_grad, gate_up_blocks, down_wgrad = sum_gradients(
        ffn_in_part, down_blocks, cube_in, gate_up_low, 4
    )
    gate_up_terms = exchange(gate_up_blocks.reshape(devices, padded, 2 * unit_pad), ALL)
    input_grad, blocks = attention_backward(
        [
            ffn_in_grad,
            cotangent[0],
            middle,
            attn_raw,
            attn_flat,
            probs,
            queries,
            key_rows,
            value_rows,
            query_raw,
            key_raw,
            row_tokens,
            qkv_full,
            output_full,
            cos_full,
            sin_full,
            *scales,
            ffnout_gain_grad[None],
            by_device,
        ],
        gain_widths,
        width_rows,
        planes,
        padded,
        mix_rows,
        7,
    )
    share = owner_sum(blocks, 5)
    gate_wgrad, up_wgrad = unit_sum(
        gate_up_terms.reshape(cubes, group, padded, 2 * unit_pad), width_rows, gate_weight.shape[1]
    )
    qkv_share, output_share = share[:padded], unpack_tiles(share[padded:], *output_weight.shape)
    gain_shares = [
        qkv_share[width_rows, k * GAIN_SLOT : k * GAIN_SLOT + count]
        for k, count in enumerate(gain_widths)
    ]
    return (
        result.astype(bf16)[None],
        input_grad[None],
        qkv_share[:width_rows, :query_width],
        qkv_share[:width_rows, query_width : query_width + head_width],
        qkv_share[:width_rows, query_width + head_width :],
        output_share,
        gate_wgrad,
        up_wgrad,
        down_wgrad,
        *gain_shares,
    )


def solution(mesh):
    dp, seq = mesh.shape["dp"], mesh.shape["seq"]
    split = Mesh(mesh.devices.reshape(dp // 8, 2, 2, 2, seq), ALL)
    rows = P(("far", "z", "x", "core"), "seq", None)
    matrix, vector = P(ALL, None), P(ALL)
    return jax.shard_map(
        body,
        mesh=split,
        in_specs=(rows, P(("far", "z", "x", "core"), None), rows) + (matrix,) * 7 + (vector,) * 6,
        out_specs=(rows, rows) + (matrix,) * 7 + (vector,) * 6,
        check_vma=False,
    )
```
